32 devices in a mesh: dp: 8 (over y, x, core), seq: 4 (over z).
Axes of the slice: x: 2, y: 2, z: 4, core: 2. Of those that a mesh axis runs over, the one named last changes fastest.
Arguments:
- tokens: bfloat16 [24, 1024, 768], P('dp', 'seq'), may hold values from -6 to 6
- lengths: int32 [24], P('dp'), may hold values from 256 to 1024, as said below
- query_weight: float32 [768, 768], P('dp'), may hold values from -0.3125 to 0.3125
- query_shift: float32 [768], P('dp'), may hold values from -3 to 3
- key_weight: float32 [768, 768], P('dp'), may hold values from -0.3125 to 0.3125
- value_weight: float32 [768, 768], P('dp'), may hold values from -0.21875 to 0.21875
- value_shift: float32 [768], P('dp'), may hold values from -3 to 3
- merge_weight: float32 [768, 768], P('dp'), may hold values from -0.875 to 0.875
- merge_shift: float32 [768], P('dp'), may hold values from -3 to 3
- first_gain: float32 [768], P('dp'), may hold values from 0.1 to 1.9
- first_shift: float32 [768], P('dp'), may hold values from -3 to 3
- expand_weight: float32 [768, 3072], P('dp'), may hold values from -0.21875 to 0.21875
- expand_shift: float32 [3072], P('dp'), may hold values from -3 to 3
- reduce_weight: float32 [3072, 768], P('dp'), may hold values from -0.15625 to 0.15625
- reduce_shift: float32 [768], P('dp'), may hold values from -3 to 3
- second_gain: float32 [768], P('dp'), may hold values from 0.1 to 1.9
- second_shift: float32 [768], P('dp'), may hold values from -3 to 3
- upstream: bfloat16 [24, 1024, 768], P('dp', 'seq'), may hold values from -6 to 6
Outputs:
- output: bfloat16 [24, 1024, 768], P('dp', 'seq')
- token_grad: bfloat16 [24, 1024, 768], P('dp', 'seq')
- dquery_weight: float32 [768, 768], P('dp')
- dquery_shift: float32 [768], P('dp')
- dkey_weight: float32 [768, 768], P('dp')
- dvalue_weight: float32 [768, 768], P('dp')
- dvalue_shift: float32 [768], P('dp')
- dmerge_weight: float32 [768, 768], P('dp')
- dmerge_shift: float32 [768], P('dp')
- dfirst_gain: float32 [768], P('dp')
- dfirst_shift: float32 [768], P('dp')
- dexpand_weight: float32 [768, 3072], P('dp')
- dexpand_shift: float32 [3072], P('dp')
- dreduce_weight: float32 [3072, 768], P('dp')
- dreduce_shift: float32 [768], P('dp')
- dsecond_gain: float32 [768], P('dp')
- dsecond_shift: float32 [768], P('dp')
The draws below stay inside these ranges and needn't reach their ends.
Inputs may be any that keep to these rules, and one draw needn't show every extreme that they name: `lengths`: the valid length of each sequence; keys at this position or later are masked out.
All inputs are finite; a program needn't handle non-finite values.
Results may differ from the reference program's by a relative error of at most 0.018.
The reference program's roundings to bfloat16 on the way count: a program that leaves them out, or rounds other values in their place, can miss the bound.
Values may be sent and summed in bfloat16 or wider, within the bound.
A program may use at most 192 MiB of HBM per device.

```python
import math
import jax
import jax.numpy as jnp
from jax import lax

D = 768
HEAD = 64
FF = 3072
LEN = 1024
SEQS = 24


def draw_lengths(key, part):
    drawn = jax.random.randint(jax.random.fold_in(key, 11), (SEQS,), LEN // 4, LEN + 1)
    shuffled = jax.random.permutation(jax.random.fold_in(key, 12), SEQS)
    drawn = drawn.at[shuffled[0]].set(LEN)
    drawn = drawn.at[shuffled[1]].set(LEN // 4)
    return drawn.astype(jnp.int32)


def with_spikes(values, stream_key, source, target, shards_of, factor):
    owner, partner = [(jnp.arange(values.shape[dim]) // (values.shape[dim] // shards_of)).reshape([-1 if axis == dim else 1 for axis in range(values.ndim)]) for dim in (source, target)]
    chosen = jax.random.permutation(stream_key, shards_of)[partner]
    strong = (owner == chosen) | (owner == (partner + shards_of // 2) % shards_of)
    return jnp.where(strong, factor * values, values)


def block_scale(own_key, dims, shards, low, top_value):
    level = 1.0
    for dim, blocks in shards:
        heights = jax.random.uniform(jax.random.fold_in(jax.random.fold_in(own_key, 6), dim), (blocks,), jnp.float32, low / len(shards), top_value / len(shards))
        level = level * jnp.repeat(jnp.exp(heights), dims[dim] // blocks).reshape((-1,) + (1,) * (len(dims) - 1 - dim))
    return level


def normal_values(stream_key, dims, deviation, limit, cuts=(), kind=jnp.bfloat16):
    entries = jax.random.normal(stream_key, dims, jnp.float32) * deviation
    if len(cuts) > 0:
        entries = block_scale(stream_key, dims, cuts, -0.22, 0.18) * entries
    return jnp.clip(entries, min=-limit, max=limit).astype(kind)


def noise_with(rng, dims, deviation, limit, shards, heavy, held_as=jnp.bfloat16):
    values = deviation * jax.random.normal(rng, dims, jnp.float32)
    if shards:
        values = values * block_scale(rng, dims, shards, -0.22, 0.18)
    return jnp.clip(with_spikes(values, jax.random.fold_in(rng, 3), *heavy), -limit, limit).astype(held_as)


def setup_inputs(seed: int = 0) -> dict:
    arg_keys = jax.random.split(jax.random.key(seed), 19)
    return {
        "tokens": normal_values(arg_keys[0], (SEQS, LEN, D), 1.0, 6.0, ((0, 8), (1, 4))),
        "lengths": draw_lengths(jax.random.fold_in(arg_keys[18], 71), 0),
        "query_weight": normal_values(arg_keys[2], (D, D), (D // 2) ** -0.5, 0.3125, ((0, 8),), jnp.float32),
        "query_shift": normal_values(arg_keys[3], (D,), 0.5, 3.0, ((0, 8),), jnp.float32),
        "key_weight": normal_values(arg_keys[4], (D, D), (D // 2) ** -0.5, 0.3125, ((0, 8),), jnp.float32),
        "value_weight": normal_values(arg_keys[5], (D, D), D ** -0.5, 0.21875, ((0, 8),), jnp.float32),
        "value_shift": normal_values(arg_keys[6], (D,), 0.5, 3.0, ((0, 8),), jnp.float32),
        "merge_weight": normal_values(arg_keys[7], (D, D), (D // 16) ** -0.5, 0.875, ((0, 8),), jnp.float32),
        "merge_shift": normal_values(arg_keys[8], (D,), 0.5, 3.0, ((0, 8),), jnp.float32),
        "first_gain": jnp.clip(1.0 + 0.18 * jax.random.normal(arg_keys[9], (D,), jnp.float32), 0.1, 1.9),
        "first_shift": normal_values(arg_keys[10], (D,), 0.5, 3.0, ((0, 8),), jnp.float32),
        "expand_weight": normal_values(arg_keys[11], (D, FF), D ** -0.5, 0.21875, ((0, 8),), jnp.float32),
        "expand_shift": normal_values(arg_keys[12], (FF,), 0.5, 3.0, ((0, 8),), jnp.float32),
        "reduce_weight": normal_values(arg_keys[13], (FF, D), (FF // 2) ** -0.5, 0.15625, ((0, 8),), jnp.float32),
        "reduce_shift": normal_values(arg_keys[14], (D,), 0.5, 3.0, ((0, 8),), jnp.float32),
        "second_gain": jnp.clip(1.0 + 0.18 * jax.random.normal(arg_keys[15], (D,), jnp.float32), 0.1, 1.9),
        "second_shift": normal_values(arg_keys[16], (D,), 0.5, 3.0, ((0, 8),), jnp.float32),
        "upstream": noise_with(arg_keys[17], (SEQS, LEN, D), 1.0, 6.0, ((0, 8), (1, 4)), (0, 2, 8, 2.0)),
    }


EPS = 1e-12
NEG_FILL = -1000000000.0

@jax.custom_vjp
def low(v):
    return lax.optimization_barrier(v.astype(jnp.bfloat16)).astype(jnp.float32)

@jax.custom_vjp
def low_back(v):
    return v

def low_keep(v):
    return (low(v), None)

def low_pass(kept, grad):
    return (grad,)

def back_keep(v):
    return (v, None)

def back_low(kept, grad):
    return (low(grad),)
low.defvjp(low_keep, low_pass)
low_back.defvjp(back_keep, back_low)

def matmul(left, right):
    return jnp.einsum('gld,de->gle', left, right, precision=lax.Precision.HIGHEST)

def layer_norm(resid, gain, shift):
    centre = resid - lax.optimization_barrier(jnp.mean(resid, axis=-1, keepdims=True))
    spread = lax.optimization_barrier(jnp.mean(centre * centre, axis=-1, keepdims=True))
    return centre * lax.rsqrt(spread + EPS) * gain + shift

def forward(inputs, valid_lens, params):
    query_mat, query_vec, key_mat, value_mat, value_vec, merge_mat, merge_vec, first_scale, first_offset, expand_mat, expand_vec, reduce_mat, reduce_vec, second_scale, second_offset = [low(item) for item in params]
    groups, seq_len, features = inputs.shape
    head_count = features // HEAD

    def per_head(array):
        return array.reshape(groups, seq_len, head_count, HEAD)
    queries = low_back(low(matmul(inputs, query_mat) + query_vec))
    key_rows = low_back(low(matmul(inputs, key_mat)))
    value_rows = low_back(low(matmul(inputs, value_mat) + value_vec))
    raw_scores = jnp.einsum('gqhd,gkhd->ghqk', per_head(queries), per_head(key_rows), precision=lax.Precision.HIGHEST)
    key_ok = lax.iota(jnp.int32, seq_len)[None, :] < valid_lens[:, None]
    scores = low_back(jnp.where(key_ok[:, None, None, :], 0.125 * raw_scores, NEG_FILL))
    row_max = lax.optimization_barrier(jnp.max(scores, axis=-1, keepdims=True))
    expo_vals = jnp.exp(scores - row_max)
    probs_low = low(expo_vals / lax.optimization_barrier(jnp.sum(expo_vals, axis=-1, keepdims=True)))
    context = jnp.einsum('ghqk,gkhd->gqhd', probs_low, per_head(value_rows), precision=lax.Precision.HIGHEST)
    context = low_back(low(context.reshape(groups, seq_len, features)))
    attended = low_back(matmul(context, merge_mat) + merge_vec)
    hidden = layer_norm(inputs + attended, first_scale, first_offset)
    pre_act = low_back(matmul(low(hidden), expand_mat) + expand_vec)
    act_low = low(jax.nn.gelu(pre_act, approximate=False))
    ffn_out = low_back(matmul(act_low, reduce_mat) + reduce_vec)
    return layer_norm(hidden + ffn_out, second_scale, second_offset)

def reference(tokens, lengths, query_weight, query_shift, key_weight, value_weight, value_shift, merge_weight, merge_shift, first_gain, first_shift, expand_weight, expand_shift, reduce_weight, reduce_shift, second_gain, second_shift, upstream):
    params = (query_weight, query_shift, key_weight, value_weight, value_shift, merge_weight, merge_shift, first_gain, first_shift, expand_weight, expand_shift, reduce_weight, reduce_shift, second_gain, second_shift)
    seq_total, seq_len, features = tokens.shape
    group_size = math.gcd(seq_total, max(1, 4096 // seq_len))
    group_count = seq_total // group_size
    inputs = tokens.astype(jnp.float32).reshape(group_count, group_size, seq_len, features)
    cotangent = upstream.astype(jnp.float32).reshape(group_count, group_size, seq_len, features)
    grouped_lens = lengths.reshape(group_count, group_size).astype(jnp.int32)

    def scan_step(totals, pieces):
        block_in, block_lens, block_cot = pieces

        def run_layer(layer_in, *weights):
            return forward(layer_in, block_lens, weights)
        result, pullback = jax.vjp(run_layer, block_in, *params)
        grads = pullback(block_cot)
        totals = tuple((total + grad for total, grad in zip(totals, grads[1:])))
        return (totals, (result.astype(jnp.bfloat16), grads[0].astype(jnp.bfloat16)))
    start = tuple((jnp.zeros(item.shape, jnp.float32) for item in params))
    totals, (outputs, input_grads) = lax.scan(scan_step, start, (inputs, grouped_lens, cotangent))
    output = outputs.reshape(seq_total, seq_len, features)
    token_grad = input_grads.reshape(seq_total, seq_len, features)
    return (output, token_grad, totals[0], totals[1], totals[2], totals[3], totals[4], totals[5], totals[6], totals[7], totals[8], totals[9], totals[10], totals[11], totals[12], totals[13], totals[14])
```

```python
import functools

import jax
import jax.numpy as jnp
from jax import lax
from jax.experimental import pallas as pl
from jax.experimental.pallas import tpu as pltpu
from jax.sharding import PartitionSpec as P

HEAD = 64
LANES = 128
EPS = 1e-12
NEG_FILL = -1000000000.0
SCALE2 = 0.125 * 1.4426950408889634
F32 = jnp.float32
BF16 = jnp.bfloat16
VMEM_LIMIT = 60 * 1024 * 1024


def dot(left, right, left_dim, right_dim):
    return lax.dot_general(
        left, right, (((left_dim,), (right_dim,)), ((), ())), preferred_element_type=F32
    )


def attend_kernel(bias_ref, q_ref, k_ref, v_ref, ctx_ref, probs_ref, *, rows_blk):
    seq_len = q_ref.shape[0]
    lane = lax.broadcasted_iota(jnp.int32, (1, LANES), 1)
    bias = bias_ref[...]
    for blk in range(seq_len // rows_blk):
        rows = pl.ds(blk * rows_blk, rows_blk)
        query = q_ref[rows, :]
        mixed = []
        for head in range(2):
            mine = (lane < HEAD) if head == 0 else (lane >= HEAD)
            query_h = jnp.where(mine, query, jnp.zeros_like(query))
            score = dot(query_h, k_ref[...], 1, 1) + bias
            top = jnp.max(score, axis=1, keepdims=True)
            expo = jnp.exp2((score - top) * SCALE2)
            total = jnp.sum(expo, axis=1, keepdims=True)
            probs = (expo * (1.0 / total)).astype(BF16)
            probs_ref[head, rows, :] = probs
            mixed.append(dot(probs, v_ref[...], 1, 0))
        ctx_ref[rows, :] = jnp.where(lane < HEAD, mixed[0], mixed[1]).astype(BF16)


def attend(bias, qkv):
    seq_len, width = qkv.shape
    feats = width // 3
    pairs = feats // LANES

    def part(which):
        return pl.BlockSpec((seq_len, LANES), lambda g, w=which: (0, w * pairs + g))

    return pl.pallas_call(
        functools.partial(attend_kernel, rows_blk=min(512, seq_len)),
        grid=(pairs,),
        in_specs=[pl.BlockSpec((1, seq_len), lambda g: (0, 0)), part(0), part(1), part(2)],
        out_specs=[
            pl.BlockSpec((seq_len, LANES), lambda g: (0, g)),
            pl.BlockSpec((2, seq_len, seq_len), lambda g: (g, 0, 0)),
        ],
        out_shape=[
            jax.ShapeDtypeStruct((seq_len, feats), BF16),
            jax.ShapeDtypeStruct((feats // HEAD, seq_len, seq_len), BF16),
        ],
        compiler_params=pltpu.CompilerParams(vmem_limit_bytes=VMEM_LIMIT),
        cost_estimate=pl.CostEstimate(
            flops=16 * feats // HEAD * seq_len * seq_len * HEAD,
            bytes_accessed=2 * seq_len * (4 * feats + feats // HEAD * seq_len),
            transcendentals=0,
        ),
    )(bias, qkv, qkv, qkv)


def attend_back_kernel(
    q_ref, k_ref, v_ref, ctx_ref, grad_ref, probs_ref, out_ref, key_acc, value_acc, *, rows_blk
):
    seq_len = q_ref.shape[0]
    lane = lax.broadcasted_iota(jnp.int32, (1, LANES), 1)
    for blk in range(seq_len // rows_blk):
        rows = pl.ds(blk * rows_blk, rows_blk)
        query = q_ref[rows, :]
        grad = grad_ref[rows, :]
        overlap = ctx_ref[rows, :].astype(F32) * grad.astype(F32)
        query_t = query.T
        grad_t = grad.T
        grad_query = []
        for head in range(2):
            mine = (lane < HEAD) if head == 0 else (lane >= HEAD)
            part = slice(head * HEAD, (head + 1) * HEAD)
            grad_h = jnp.where(mine, grad, jnp.zeros_like(grad))
            inner = jnp.sum(jnp.where(mine, overlap, 0.0), axis=1, keepdims=True)
            probs = probs_ref[head, rows, :]
            grad_probs = dot(grad_h, v_ref[...], 1, 1)
            grad_score = (probs.astype(F32) * (grad_probs - inner)).astype(BF16)
            grad_query.append(dot(grad_score, k_ref[...], 1, 0))
            grad_key = dot(query_t[part], grad_score, 1, 0)
            grad_value = dot(grad_t[part], probs, 1, 0)
            if blk == 0:
                key_acc[head] = grad_key
                value_acc[head] = grad_value
            else:
                key_acc[head] += grad_key
                value_acc[head] += grad_value
        out_ref[0, rows, :] = (0.125 * jnp.where(lane < HEAD, grad_query[0], grad_query[1])).astype(
            BF16
        )
    out_ref[1] = (0.125 * jnp.concatenate([key_acc[0], key_acc[1]], axis=0)).T.astype(BF16)
    out_ref[2] = jnp.concatenate([value_acc[0], value_acc[1]], axis=0).T.astype(BF16)


def attend_back(qkv, ctx, grad_ctx, probs):
    seq_len, feats = ctx.shape
    pairs = feats // LANES

    def part(which):
        return pl.BlockSpec((seq_len, LANES), lambda g, w=which: (0, w * pairs + g))

    return pl.pallas_call(
        functools.partial(attend_back_kernel, rows_blk=min(512, seq_len)),
        grid=(pairs,),
        in_specs=[part(0), part(1), part(2), part(0), part(0)]
        + [pl.BlockSpec((2, seq_len, seq_len), lambda g: (g, 0, 0))],
        out_specs=pl.BlockSpec((3, seq_len, LANES), lambda g: (0, 0, g)),
        out_shape=jax.ShapeDtypeStruct((3, seq_len, feats), BF16),
        scratch_shapes=[pltpu.VMEM((2, HEAD, seq_len), F32)] * 2,
        compiler_params=pltpu.CompilerParams(vmem_limit_bytes=VMEM_LIMIT),
        cost_estimate=pl.CostEstimate(
            flops=16 * feats // HEAD * seq_len * seq_len * HEAD,
            bytes_accessed=2 * seq_len * (8 * feats + feats // HEAD * seq_len),
            transcendentals=0,
        ),
    )(qkv, qkv, qkv, ctx, grad_ctx, probs)


def normalize(resid):
    centre = resid - jnp.mean(resid, axis=-1, keepdims=True)
    inv = lax.rsqrt(jnp.mean(centre * centre, axis=-1, keepdims=True) + EPS)
    return centre * inv, inv


def normalize_back(normed, inv, grad_normed):
    mean_grad = jnp.mean(grad_normed, axis=-1, keepdims=True)
    mean_both = jnp.mean(grad_normed * normed, axis=-1, keepdims=True)
    return inv * (grad_normed - mean_grad - normed * mean_both)


def column_sum(rows):
    return jnp.sum(rows, axis=0, dtype=F32)


INV_SQRT2 = 0.7071067811865476
INV_SQRT_2PI = 0.3989422804014327


def per_device(mesh_shape, tokens, lengths, *rest):
    weights, upstream = rest[:15], rest[15]
    dp_size, seq_size = mesh_shape
    seq_count, row_count, feats = tokens.shape
    dp_index = lax.axis_index("dp")
    here = lax.axis_index("seq")
    spare = seq_size - seq_count

    def owner_shift(dp):
        return spare * (dp % 2)

    my_seq = jnp.clip(here - owner_shift(dp_index), 0, seq_count - 1)

    def owned_by(dp, pos):
        seq = pos - owner_shift(dp)
        return 0 <= seq < seq_count

    def shift_pairs(step, to_owner):
        pairs = []
        for dp in range(dp_size):
            for pos in range(seq_size):
                dest = (pos + step) % seq_size
                if owned_by(dp, dest if to_owner else pos):
                    pairs.append((dp * seq_size + pos, dp * seq_size + dest))
        return pairs

    def to_owners(blocks):
        pieces = []
        for step in range(seq_size):
            dest = (here + step) % seq_size
            seq = jnp.clip(dest - owner_shift(dp_index), 0, seq_count - 1)
            piece = lax.dynamic_index_in_dim(blocks, seq, 0, keepdims=False)
            if step == 0:
                owner = (here >= owner_shift(dp_index)) & (here < owner_shift(dp_index) + seq_count)
                piece = jnp.where(owner, piece, jnp.zeros_like(piece))
            else:
                piece = lax.ppermute(piece, ("dp", "seq"), shift_pairs(step, True))
            pieces.append(piece)
        return jnp.concatenate(pieces, axis=0)

    def from_owners(rows):
        pieces = rows.reshape(seq_size, row_count, feats)
        arrived = []
        for step in range(seq_size):
            piece = pieces[step]
            if step:
                piece = lax.ppermute(piece, ("dp", "seq"), shift_pairs(seq_size - step, False))
            arrived.append(piece)
        stack = jnp.stack(arrived)
        order = (jnp.arange(seq_count) + owner_shift(dp_index) - here) % seq_size
        return jnp.take(stack, order, axis=0)

    low = [item.astype(BF16) for item in weights]
    wq, bq, wk, wv, bv, wo, bo, g1, b1, w1, c1, w2, c2, g2, b2 = low

    def gather(piece):
        return lax.all_gather(piece, "dp", axis=0, tiled=True)

    qkv_mat = gather(jnp.concatenate([wq, wk, wv], axis=1))
    vec_sizes = [item.shape[0] for item in (bq, bv, bo, g1, b1, c1, c2, g2, b2)]
    packed = lax.all_gather(
        jnp.concatenate([bq, bv, bo, g1, b1, c1, c2, g2, b2]), "dp", axis=0, tiled=False
    )
    vecs = []
    start = 0
    for size in vec_sizes:
        vecs.append(packed[:, start : start + size].reshape(1, -1).astype(F32))
        start += size
    bq, bv, bo, g1, b1, c1, c2, g2, b2 = vecs
    merge_mat = gather(wo)
    expand_mat = gather(w1)
    reduce_mat = gather(w2)

    inputs = to_owners(tokens)
    seq_len = inputs.shape[0]
    dy = to_owners(upstream).astype(F32)

    spot = lax.iota(jnp.int32, seq_len)
    position = ((here - spot // row_count) % seq_size) * row_count + spot % row_count
    valid_len = lax.dynamic_index_in_dim(lengths, my_seq, 0, keepdims=False)
    key_bias = jnp.where(position < valid_len, 0.0, 8.0 * NEG_FILL).astype(F32).reshape(1, seq_len)

    qkv_bias = jnp.concatenate([bq, jnp.zeros_like(bq), bv], axis=1)
    qkv = (dot(inputs, qkv_mat, 1, 0) + qkv_bias).astype(BF16)
    ctx, probs = attend(key_bias, qkv)
    normed1, inv1 = normalize(inputs.astype(F32) + dot(ctx, merge_mat, 1, 0) + bo)
    hidden = normed1 * g1 + b1
    hidden_low = hidden.astype(BF16)
    pre = dot(hidden_low, expand_mat, 1, 0) + c1
    phi_cum = 0.5 * (1.0 + lax.erf(pre * INV_SQRT2))
    act = (pre * phi_cum).astype(BF16)
    slope = (phi_cum + pre * (INV_SQRT_2PI * jnp.exp(-0.5 * pre * pre))).astype(BF16)
    normed2, inv2 = normalize(hidden + dot(act, reduce_mat, 1, 0) + c2)
    result = (normed2 * g2 + b2).astype(BF16)
    output = from_owners(result)

    d_g2 = column_sum(dy * normed2)
    d_b2 = column_sum(dy)
    grad_resid2 = normalize_back(normed2, inv2, g2 * dy)
    grad_ffn = grad_resid2.astype(BF16)
    d_w2 = dot(act, grad_ffn, 0, 0).astype(BF16)
    d_c2 = column_sum(grad_ffn)
    grad_pre = (dot(grad_ffn, reduce_mat, 1, 1) * slope.astype(F32)).astype(BF16)
    d_w1 = dot(hidden_low, grad_pre, 0, 0).astype(BF16)
    d_c1 = column_sum(grad_pre)
    grad_hidden = grad_resid2 + dot(grad_pre, expand_mat, 1, 1)
    d_g1 = column_sum(grad_hidden * normed1)
    d_b1 = column_sum(grad_hidden)
    grad_resid1 = normalize_back(normed1, inv1, g1 * grad_hidden)
    grad_att = grad_resid1.astype(BF16)
    d_wo = dot(ctx, grad_att, 0, 0).astype(BF16)
    d_bo = column_sum(grad_att)
    grad_ctx = dot(grad_att, merge_mat, 1, 1).astype(BF16)
    grad_qkv = attend_back(qkv, ctx, grad_ctx, probs)
    token_rows = grad_resid1
    d_qkv = []
    for which in range(3):
        mat = qkv_mat[:, which * feats : (which + 1) * feats]
        token_rows = token_rows + dot(grad_qkv[which], mat, 1, 1)
        d_qkv.append(dot(inputs, grad_qkv[which], 0, 0).astype(BF16))
    d_bq = column_sum(grad_qkv[0])
    d_bv = column_sum(grad_qkv[2])
    token_grad = from_owners(token_rows.astype(BF16))

    def reduce(full):
        return lax.psum_scatter(full, "dp", scatter_dimension=0, tiled=True)

    vec_grads = (d_bq, d_bv, d_bo, d_g1, d_b1, d_c1, d_c2, d_g2, d_b2)
    vec_pack = jnp.concatenate([item.reshape(dp_size, -1) for item in vec_grads], axis=1)
    vec_len = vec_pack.shape[1]
    shard_rows = feats // dp_size
    vec_cols = -(-vec_len // (shard_rows * LANES)) * LANES
    vec_pack = jnp.pad(vec_pack, ((0, 0), (0, shard_rows * vec_cols - vec_len)))
    vec_pack = vec_pack.reshape(feats, vec_cols).astype(BF16)
    own_w2 = reduce(d_w2)
    own_w1 = reduce(d_w1)
    own_rest = reduce(jnp.concatenate([d_wo] + d_qkv + [vec_pack], axis=1))
    sum_w2 = lax.psum(own_w2, "seq").astype(F32)
    sum_w1 = lax.psum(own_w1, "seq").astype(F32)
    sum_rest = lax.psum(own_rest, "seq").astype(F32)
    s_wo, s_wq, s_wk, s_wv = [sum_rest[:, i * feats : (i + 1) * feats] for i in range(4)]
    flat = sum_rest[:, 4 * feats :].reshape(-1)
    out_vecs = []
    start = 0
    for size in vec_sizes:
        out_vecs.append(flat[start : start + size])
        start += size
    s_bq, s_bv, s_bo, s_g1, s_b1, s_c1, s_c2, s_g2, s_b2 = out_vecs
    return (
        output,
        token_grad,
        s_wq,
        s_bq,
        s_wk,
        s_wv,
        s_bv,
        s_wo,
        s_bo,
        s_g1,
        s_b1,
        sum_w1,
        s_c1,
        sum_w2,
        s_c2,
        s_g2,
        s_b2,
    )


def solution(mesh):
    rows, mat, vec = P("dp", "seq", None), P("dp", None), P("dp")
    params = (mat, vec, mat, mat, vec, mat, vec, vec, vec, mat, vec, mat, vec, vec, vec)
    return jax.shard_map(
        functools.partial(per_device, (mesh.shape["dp"], mesh.shape["seq"])),
        mesh=mesh,
        in_specs=(rows, vec) + params + (rows,),
        out_specs=(rows, rows) + params,
        check_vma=False,
    )
```

```python
import functools

import jax
import jax.numpy as jnp
from jax import lax
from jax.experimental import pallas as pl
from jax.experimental.pallas import tpu as pltpu
from jax.sharding import PartitionSpec as P

HEAD = 64
LANES = 128
EPS = 1e-12
NEG_FILL = -1000000000.0
SCALE2 = 0.125 * 1.4426950408889634
F32 = jnp.float32
BF16 = jnp.bfloat16
VMEM_LIMIT = 60 * 1024 * 1024


def dot(left, right, left_dim, right_dim):
    return lax.dot_general(
        left, right, (((left_dim,), (right_dim,)), ((), ())), preferred_element_type=F32
    )


def attend_kernel(bias_ref, q_ref, k_ref, v_ref, ctx_ref, probs_ref, *, rows_blk):
    seq_len = q_ref.shape[0]
    lane = lax.broadcasted_iota(jnp.int32, (1, LANES), 1)
    bias = bias_ref[...]
    for blk in range(seq_len // rows_blk):
        rows = pl.ds(blk * rows_blk, rows_blk)
        query = q_ref[rows, :]
        mixed = []
        for head in range(2):
            mine = (lane < HEAD) if head == 0 else (lane >= HEAD)
            query_h = jnp.where(mine, query, jnp.zeros_like(query))
            score = dot(query_h, k_ref[...], 1, 1) + bias
            top = jnp.max(score, axis=1, keepdims=True)
            expo = jnp.exp2((score - top) * SCALE2)
            total = jnp.sum(expo, axis=1, keepdims=True)
            probs = (expo * (1.0 / total)).astype(BF16)
            probs_ref[head, rows, :] = probs
            mixed.append(dot(probs, v_ref[...], 1, 0))
        ctx_ref[rows, :] = jnp.where(lane < HEAD, mixed[0], mixed[1]).astype(BF16)


def attend(bias, qkv):
    seq_len, width = qkv.shape
    feats = width // 3
    pairs = feats // LANES

    def part(which):
        return pl.BlockSpec((seq_len, LANES), lambda g, w=which: (0, w * pairs + g))

    return pl.pallas_call(
        functools.partial(attend_kernel, rows_blk=min(512, seq_len)),
        grid=(pairs,),
        in_specs=[pl.BlockSpec((1, seq_len), lambda g: (0, 0)), part(0), part(1), part(2)],
        out_specs=[
            pl.BlockSpec((seq_len, LANES), lambda g: (0, g)),
            pl.BlockSpec((2, seq_len, seq_len), lambda g: (g, 0, 0)),
        ],
        out_shape=[
            jax.ShapeDtypeStruct((seq_len, feats), BF16),
            jax.ShapeDtypeStruct((feats // HEAD, seq_len, seq_len), BF16),
        ],
        compiler_params=pltpu.CompilerParams(vmem_limit_bytes=VMEM_LIMIT),
        cost_estimate=pl.CostEstimate(
            flops=16 * feats // HEAD * seq_len * seq_len * HEAD,
            bytes_accessed=2 * seq_len * (4 * feats + feats // HEAD * seq_len),
            transcendentals=0,
        ),
    )(bias, qkv, qkv, qkv)


def attend_back_kernel(
    q_ref, k_ref, v_ref, ctx_ref, grad_ref, probs_ref, out_ref, key_acc, value_acc, *, rows_blk
):
    seq_len = q_ref.shape[0]
    lane = lax.broadcasted_iota(jnp.int32, (1, LANES), 1)
    for blk in range(seq_len // rows_blk):
        rows = pl.ds(blk * rows_blk, rows_blk)
        query = q_ref[rows, :]
        grad = grad_ref[rows, :]
        overlap = ctx_ref[rows, :].astype(F32) * grad.astype(F32)
        query_t = query.T
        grad_t = grad.T
        grad_query = []
        for head in range(2):
            mine = (lane < HEAD) if head == 0 else (lane >= HEAD)
            part = slice(head * HEAD, (head + 1) * HEAD)
            grad_h = jnp.where(mine, grad, jnp.zeros_like(grad))
            inner = jnp.sum(jnp.where(mine, overlap, 0.0), axis=1, keepdims=True)
            probs = probs_ref[head, rows, :]
            grad_probs = dot(grad_h, v_ref[...], 1, 1)
            grad_score = (probs.astype(F32) * (grad_probs - inner)).astype(BF16)
            grad_query.append(dot(grad_score, k_ref[...], 1, 0))
            grad_key = dot(query_t[part], grad_score, 1, 0)
            grad_value = dot(grad_t[part], probs, 1, 0)
            if blk == 0:
                key_acc[head] = grad_key
                value_acc[head] = grad_value
            else:
                key_acc[head] += grad_key
                value_acc[head] += grad_value
        out_ref[0, rows, :] = (0.125 * jnp.where(lane < HEAD, grad_query[0], grad_query[1])).astype(
            BF16
        )
    out_ref[1] = (0.125 * jnp.concatenate([key_acc[0], key_acc[1]], axis=0)).T.astype(BF16)
    out_ref[2] = jnp.concatenate([value_acc[0], value_acc[1]], axis=0).T.astype(BF16)


def attend_back(qkv, ctx, grad_ctx, probs):
    seq_len, feats = ctx.shape
    pairs = feats // LANES

    def part(which):
        return pl.BlockSpec((seq_len, LANES), lambda g, w=which: (0, w * pairs + g))

    return pl.pallas_call(
        functools.partial(attend_back_kernel, rows_blk=min(512, seq_len)),
        grid=(pairs,),
        in_specs=[part(0), part(1), part(2), part(0), part(0)]
        + [pl.BlockSpec((2, seq_len, seq_len), lambda g: (g, 0, 0))],
        out_specs=pl.BlockSpec((3, seq_len, LANES), lambda g: (0, 0, g)),
        out_shape=jax.ShapeDtypeStruct((3, seq_len, feats), BF16),
        scratch_shapes=[pltpu.VMEM((2, HEAD, seq_len), F32)] * 2,
        compiler_params=pltpu.CompilerParams(vmem_limit_bytes=VMEM_LIMIT),
        cost_estimate=pl.CostEstimate(
            flops=16 * feats // HEAD * seq_len * seq_len * HEAD,
            bytes_accessed=2 * seq_len * (8 * feats + feats // HEAD * seq_len),
            transcendentals=0,
        ),
    )(qkv, qkv, qkv, ctx, grad_ctx, probs)


MESH = pl.DeviceIdType.MESH


def add_rows(dest, other, start, count, step=16):
    def body(i, carry):
        to = pl.ds(pl.multiple_of(start + i * step, step), step)
        frm = pl.ds(pl.multiple_of(i * step, step), step)
        dest[to, :] = (dest[to, :].astype(F32) + other[frm, :].astype(F32)).astype(BF16)
        return carry

    lax.fori_loop(0, count // step, body, 0)


def reduce_kernel(seq_size, seq_count, chunk_count, *refs):
    refs = list(refs)

    def take(count):
        got = refs[:count]
        del refs[:count]
        return got

    grads = take(chunk_count)
    (token_rows,) = take(1)
    sums = take(chunk_count)
    (token_out,) = take(1)
    own, other, first_x, first_y, second, from_left, from_right, passed = [
        take(chunk_count) for _ in range(8)
    ]
    (token_buf,) = take(1)
    own_sem, core_send, core_recv, one_send, one_recv, two_send, two_recv = take(7)
    z_send, z_recv, token_send, token_recv, token_local = take(5)

    me = lax.axis_index("dp")
    here = lax.axis_index("seq")
    core, x_at, y_at = me % 2, (me // 2) % 2, (me // 4) % 2
    to_core, to_x, to_y = 1 - 2 * core, 2 - 4 * x_at, 4 - 8 * y_at
    shift = (seq_size - seq_count) * core
    my_seq = here - shift
    is_owner = (my_seq >= 0) & (my_seq < seq_count)
    rows = token_out.shape[1]

    barrier = pltpu.get_barrier_semaphore()
    for away in (to_core, to_x, to_y):
        pl.semaphore_signal(barrier, inc=1, device_id=(me + away, here), device_id_type=MESH)
    for step in range(1, seq_size):
        pl.semaphore_signal(
            barrier, inc=1, device_id=(me, (here + step) % seq_size), device_id_type=MESH
        )
    pl.semaphore_wait(barrier, 3 + seq_size - 1)

    def remote(src, dst, send, recv, device):
        return pltpu.make_async_remote_copy(
            src_ref=src, dst_ref=dst, send_sem=send, recv_sem=recv,
            device_id=device, device_id_type=MESH,
        )

    apart = [(r % 2) * to_x + (r // 2) * to_y for r in range(4)]
    core_dev, x_dev, y_dev = (me + to_core, here), (me + to_x, here), (me + to_y, here)

    def keep_copy(c, r):
        return pltpu.make_async_copy(grads[c].at[me + apart[r]], own[c].at[r], own_sem.at[c, r])

    def core_copy(c, r):
        return remote(
            grads[c].at[me + to_core + apart[r]], other[c].at[r],
            core_send.at[c, r], core_recv.at[c, r], core_dev,
        )

    def one_copy(c, way, k):
        half = own[c].shape[1] // 2
        if way == 0:
            src, dst, dev = own[c].at[(1, 3)[k], pl.ds(0, half)], first_x[c].at[k], x_dev
        else:
            src, dst, dev = own[c].at[(2, 3)[k], pl.ds(half, half)], first_y[c].at[k], y_dev
        return remote(src, dst, one_send.at[c, way, k], one_recv.at[c, way, k], dev)

    def two_copy(c, way):
        half = own[c].shape[1] // 2
        if way == 0:
            src, dst, dev = own[c].at[2, pl.ds(0, half)], second[c].at[0], y_dev
        else:
            src, dst, dev = own[c].at[1, pl.ds(half, half)], second[c].at[1], x_dev
        return remote(src, dst, two_send.at[c, way], two_recv.at[c, way], dev)

    def z_copy(c, way, src):
        dst = (from_left, from_right)[way][c]
        dev = (me, here + (1, -1)[way])
        return remote(src, dst, z_send.at[c, way], z_recv.at[c, way], dev)

    def token_copy(pos):
        return remote(
            token_rows.at[pl.ds(pos * rows, rows)], token_out.at[my_seq],
            token_send.at[pos], token_recv.at[my_seq], (me, pos),
        )

    for c in range(chunk_count):
        for r in (3, 1, 2, 0):
            core_copy(c, r).start()
            keep_copy(c, r).start()

    @pl.when(is_owner)
    def _():
        for pos in range(seq_size):
            @pl.when(here != pos)
            def _():
                token_copy(pos).start()
        load = pltpu.make_async_copy(
            token_rows.at[pl.ds(here * rows, rows)], token_buf, token_local.at[0]
        )
        load.start()
        load.wait()
        store = pltpu.make_async_copy(token_buf, token_out.at[my_seq], token_local.at[1])
        store.start()
        store.wait()

    def core_stage(c):
        for r in (3, 1, 2, 0):
            keep_copy(c, r).wait()
            core_copy(c, r).wait_recv()
            add_rows(own[c].at[r], other[c].at[r], 0, own[c].shape[1])
            if r == 3:
                one_copy(c, 0, 1).start()
                one_copy(c, 1, 1).start()
            elif r == 1:
                one_copy(c, 0, 0).start()
            elif r == 2:
                one_copy(c, 1, 0).start()

    def one_stage(c):
        half = own[c].shape[1] // 2
        for way, base in ((0, 0), (1, half)):
            one_copy(c, way, 1).wait_recv()
            add_rows(own[c].at[(2, 1)[way]], (first_x, first_y)[way][c].at[1], base, half)
            two_copy(c, way).start()
        for way, base in ((0, 0), (1, half)):
            one_copy(c, way, 0).wait_recv()
            add_rows(own[c].at[0], (first_x, first_y)[way][c].at[0], base, half)

    def two_stage(c):
        half = own[c].shape[1] // 2
        for way, base in ((0, 0), (1, half)):
            two_copy(c, way).wait_recv()
            add_rows(own[c].at[0], second[c].at[way], base, half)

    def z_hop(c, hop):
        mine = own[c].at[0]
        for way in range(2):
            at = here if way == 0 else seq_size - 1 - here
            buf = passed[c].at[way]

            @pl.when(at == hop)
            def _():
                if hop == 0:
                    z_copy(c, way, mine).start()
                else:
                    arrived = (from_left, from_right)[way][c]
                    z_copy(c, way, buf).wait_recv()
                    if hop < seq_size - 1:
                        def body(i, carry):
                            at_rows = pl.ds(pl.multiple_of(i * 16, 16), 16)
                            buf[at_rows, :] = (
                                mine[at_rows, :].astype(F32) + arrived[at_rows, :].astype(F32)
                            ).astype(BF16)
                            return carry

                        lax.fori_loop(0, mine.shape[0] // 16, body, 0)
                        z_copy(c, way, buf).start()

    def finish(c):
        mine = own[c].at[0]
        total = sums[c]

        def body(i, carry):
            at_rows = pl.ds(pl.multiple_of(i * 16, 16), 16)
            total[at_rows, :] = mine[at_rows, :].astype(F32)
            return carry

        lax.fori_loop(0, mine.shape[0] // 16, body, 0)
        for way in range(2):
            arrived = (from_left, from_right)[way][c]
            at = here if way == 0 else seq_size - 1 - here

            @pl.when(at > 0)
            def _():
                def more(i, carry):
                    at_rows = pl.ds(pl.multiple_of(i * 16, 16), 16)
                    total[at_rows, :] += arrived[at_rows, :].astype(F32)
                    return carry

                lax.fori_loop(0, mine.shape[0] // 16, more, 0)

    depth = 3 + seq_size
    for time in range(chunk_count + depth):
        for stage in range(depth):
            c = time - stage
            if 0 <= c < chunk_count:
                if stage == 0:
                    core_stage(c)
                elif stage == 1:
                    one_stage(c)
                elif stage == 2:
                    two_stage(c)
                    z_hop(c, 0)
                elif stage < 2 + seq_size:
                    z_hop(c, stage - 2)
                else:
                    finish(c)

    for c in range(chunk_count):
        for r in range(4):
            core_copy(c, r).wait_send()
        for way in range(2):
            for k in range(2):
                one_copy(c, way, k).wait_send()
            two_copy(c, way).wait_send()
            at = here if way == 0 else seq_size - 1 - here

            @pl.when(at < seq_size - 1)
            def _():
                z_copy(c, way, own[c].at[0]).wait_send()

    for seq in range(seq_count):
        @pl.when(here != seq + shift)
        def _():
            remote(
                token_rows.at[pl.ds(0, rows)], token_out.at[seq],
                token_send.at[0], token_recv.at[seq], (me, (here + 1) % seq_size),
            ).wait_recv()

    @pl.when(is_owner)
    def _():
        for pos in range(seq_size):
            @pl.when(here != pos)
            def _():
                token_copy(pos).wait_send()


def reduce_all(seq_size, seq_count, chunks, token_rows):
    count = len(chunks)
    seq_len, feats = token_rows.shape
    blk = seq_len // seq_size
    any_spec = pl.BlockSpec(memory_space=pl.ANY)
    vmem_spec = pl.BlockSpec(memory_space=pltpu.VMEM)

    def bufs(lead, split):
        return [
            pltpu.VMEM(lead + (item.shape[1] // split, item.shape[2]), BF16) for item in chunks
        ]

    dma = pltpu.SemaphoreType.DMA
    return pl.pallas_call(
        functools.partial(reduce_kernel, seq_size, seq_count, count),
        in_specs=[any_spec] * (count + 1),
        out_specs=[vmem_spec] * count + [any_spec],
        out_shape=[jax.ShapeDtypeStruct(item.shape[1:], F32) for item in chunks]
        + [jax.ShapeDtypeStruct((seq_count, blk, feats), BF16)],
        scratch_shapes=bufs((4,), 1) + bufs((4,), 1) + bufs((2,), 2) + bufs((2,), 2) + bufs((2,), 2)
        + bufs((), 1) + bufs((), 1) + bufs((2,), 1)
        + [
            pltpu.VMEM((blk, feats), BF16),
            dma((count, 4)), dma((count, 4)), dma((count, 4)),
            dma((count, 2, 2)), dma((count, 2, 2)), dma((count, 2)), dma((count, 2)),
            dma((count, 2)), dma((count, 2)), dma((seq_size,)), dma((seq_count,)), dma((2,)),
        ],
        compiler_params=pltpu.CompilerParams(
            collective_id=1, has_side_effects=True, vmem_limit_bytes=VMEM_LIMIT
        ),
    )(*chunks, token_rows)


def normalize(resid):
    centre = resid - jnp.mean(resid, axis=-1, keepdims=True)
    inv = lax.rsqrt(jnp.mean(centre * centre, axis=-1, keepdims=True) + EPS)
    return centre * inv, inv


def normalize_back(normed, inv, grad_normed):
    mean_grad = jnp.mean(grad_normed, axis=-1, keepdims=True)
    mean_both = jnp.mean(grad_normed * normed, axis=-1, keepdims=True)
    return inv * (grad_normed - mean_grad - normed * mean_both)


def column_sum(rows):
    return jnp.sum(rows, axis=0, dtype=F32)


INV_SQRT2 = 0.7071067811865476
INV_SQRT_2PI = 0.3989422804014327


def per_device(mesh_shape, tokens, lengths, *rest):
    weights, upstream = rest[:15], rest[15]
    dp_size, seq_size = mesh_shape
    seq_count, row_count, feats = tokens.shape
    dp_index = lax.axis_index("dp")
    here = lax.axis_index("seq")
    spare = seq_size - seq_count

    def owner_shift(dp):
        return spare * (dp % 2)

    my_seq = jnp.clip(here - owner_shift(dp_index), 0, seq_count - 1)

    def owned_by(dp, pos):
        seq = pos - owner_shift(dp)
        return 0 <= seq < seq_count

    def shift_pairs(step, to_owner):
        pairs = []
        for dp in range(dp_size):
            for pos in range(seq_size):
                dest = (pos + step) % seq_size
                if owned_by(dp, dest if to_owner else pos):
                    pairs.append((dp * seq_size + pos, dp * seq_size + dest))
        return pairs

    def to_owners(blocks):
        pieces = []
        for step in range(seq_size):
            dest = (here + step) % seq_size
            seq = jnp.clip(dest - owner_shift(dp_index), 0, seq_count - 1)
            piece = lax.dynamic_index_in_dim(blocks, seq, 0, keepdims=False)
            if step == 0:
                owner = (here >= owner_shift(dp_index)) & (here < owner_shift(dp_index) + seq_count)
                piece = jnp.where(owner, piece, jnp.zeros_like(piece))
            else:
                piece = lax.ppermute(piece, ("dp", "seq"), shift_pairs(step, True))
            pieces.append(piece)
        order = (here - jnp.arange(seq_size)) % seq_size
        return jnp.take(jnp.stack(pieces), order, axis=0).reshape(-1, feats)

    def from_owners(rows):
        pieces = rows.reshape(seq_size, row_count, feats)
        arrived = []
        for step in range(seq_size):
            piece = lax.dynamic_index_in_dim(pieces, (here - step) % seq_size, 0, keepdims=False)
            if step:
                piece = lax.ppermute(piece, ("dp", "seq"), shift_pairs(seq_size - step, False))
            arrived.append(piece)
        stack = jnp.stack(arrived)
        order = (jnp.arange(seq_count) + owner_shift(dp_index) - here) % seq_size
        return jnp.take(stack, order, axis=0)

    low = [item.astype(BF16) for item in weights]
    wq, bq, wk, wv, bv, wo, bo, g1, b1, w1, c1, w2, c2, g2, b2 = low

    def gather(piece):
        return lax.all_gather(piece, "dp", axis=0, tiled=True)

    qkv_mat = gather(jnp.concatenate([wq, wk, wv], axis=1))
    vec_sizes = [item.shape[0] for item in (bq, bv, bo, g1, b1, c1, c2, g2, b2)]
    packed = lax.all_gather(
        jnp.concatenate([bq, bv, bo, g1, b1, c1, c2, g2, b2]), "dp", axis=0, tiled=False
    )
    vecs = []
    start = 0
    for size in vec_sizes:
        vecs.append(packed[:, start : start + size].reshape(1, -1).astype(F32))
        start += size
    bq, bv, bo, g1, b1, c1, c2, g2, b2 = vecs
    merge_mat = gather(wo)
    expand_mat = gather(w1)
    reduce_mat = gather(w2)

    inputs = to_owners(tokens)
    seq_len = inputs.shape[0]
    dy = to_owners(upstream).astype(F32)

    position = lax.iota(jnp.int32, seq_len)
    valid_len = lax.dynamic_index_in_dim(lengths, my_seq, 0, keepdims=False)
    key_bias = jnp.where(position < valid_len, 0.0, 8.0 * NEG_FILL).astype(F32).reshape(1, seq_len)

    qkv_bias = jnp.concatenate([bq, jnp.zeros_like(bq), bv], axis=1)
    qkv = (dot(inputs, qkv_mat, 1, 0) + qkv_bias).astype(BF16)
    ctx, probs = attend(key_bias, qkv)
    normed1, inv1 = normalize(inputs.astype(F32) + dot(ctx, merge_mat, 1, 0) + bo)
    hidden = normed1 * g1 + b1
    hidden_low = hidden.astype(BF16)
    pre = dot(hidden_low, expand_mat, 1, 0) + c1
    phi_cum = 0.5 * (1.0 + lax.erf(pre * INV_SQRT2))
    act = (pre * phi_cum).astype(BF16)
    slope = (phi_cum + pre * (INV_SQRT_2PI * jnp.exp(-0.5 * pre * pre))).astype(BF16)
    normed2, inv2 = normalize(hidden + dot(act, reduce_mat, 1, 0) + c2)
    result = (normed2 * g2 + b2).astype(BF16)
    output = from_owners(result)

    d_g2 = column_sum(dy * normed2)
    d_b2 = column_sum(dy)
    grad_resid2 = normalize_back(normed2, inv2, g2 * dy)
    grad_ffn = grad_resid2.astype(BF16)
    d_w2 = dot(act, grad_ffn, 0, 0).astype(BF16)
    d_c2 = column_sum(grad_ffn)
    grad_pre = (dot(grad_ffn, reduce_mat, 1, 1) * slope.astype(F32)).astype(BF16)
    d_w1 = dot(hidden_low, grad_pre, 0, 0).astype(BF16)
    d_c1 = column_sum(grad_pre)
    grad_hidden = grad_resid2 + dot(grad_pre, expand_mat, 1, 1)
    d_g1 = column_sum(grad_hidden * normed1)
    d_b1 = column_sum(grad_hidden)
    grad_resid1 = normalize_back(normed1, inv1, g1 * grad_hidden)
    grad_att = grad_resid1.astype(BF16)
    d_wo = dot(ctx, grad_att, 0, 0).astype(BF16)
    d_bo = column_sum(grad_att)
    grad_ctx = dot(grad_att, merge_mat, 1, 1).astype(BF16)
    grad_qkv = attend_back(qkv, ctx, grad_ctx, probs)
    token_rows = grad_resid1
    d_qkv = []
    for which in range(3):
        mat = qkv_mat[:, which * feats : (which + 1) * feats]
        token_rows = token_rows + dot(grad_qkv[which], mat, 1, 1)
        d_qkv.append(dot(inputs, grad_qkv[which], 0, 0).astype(BF16))
    d_bq = column_sum(grad_qkv[0])
    d_bv = column_sum(grad_qkv[2])
    vec_grads = (d_bq, d_bv, d_bo, d_g1, d_b1, d_c1, d_c2, d_g2, d_b2)
    vec_pack = jnp.concatenate([item.reshape(dp_size, -1) for item in vec_grads], axis=1)
    vec_len = vec_pack.shape[1]
    shard_rows = feats // dp_size
    token_rows = token_rows.astype(BF16)
    if dp_size == 8 and shard_rows % 32 == 0:
        vec_rows = -(-vec_len // (32 * LANES)) * 32
        vec_pack = jnp.pad(vec_pack, ((0, 0), (0, vec_rows * LANES - vec_len)))
        mats = [d_w2, d_w1, d_wo] + d_qkv
        chunks = [item.reshape(dp_size, item.shape[0] // dp_size, item.shape[1]) for item in mats]
        chunks.append(vec_pack.reshape(dp_size, vec_rows, LANES).astype(BF16))
        sum_w2, sum_w1, s_wo, s_wq, s_wk, s_wv, flat, token_grad = reduce_all(
            seq_size, seq_count, chunks, token_rows
        )
        flat = flat.reshape(-1)
    else:
        token_grad = from_owners(token_rows)
        vec_cols = -(-vec_len // (shard_rows * LANES)) * LANES
        vec_pack = jnp.pad(vec_pack, ((0, 0), (0, shard_rows * vec_cols - vec_len)))
        vec_pack = vec_pack.reshape(feats, vec_cols).astype(BF16)

        def reduce(full):
            own = lax.psum_scatter(full, "dp", scatter_dimension=0, tiled=True)
            return lax.psum(own, "seq").astype(F32)

        sum_w2 = reduce(d_w2)
        sum_w1 = reduce(d_w1)
        sum_rest = reduce(jnp.concatenate([d_wo] + d_qkv + [vec_pack], axis=1))
        s_wo, s_wq, s_wk, s_wv = [sum_rest[:, i * feats : (i + 1) * feats] for i in range(4)]
        flat = sum_rest[:, 4 * feats :].reshape(-1)
    out_vecs = []
    start = 0
    for size in vec_sizes:
        out_vecs.append(flat[start : start + size])
        start += size
    s_bq, s_bv, s_bo, s_g1, s_b1, s_c1, s_c2, s_g2, s_b2 = out_vecs
    return (
        output,
        token_grad,
        s_wq,
        s_bq,
        s_wk,
        s_wv,
        s_bv,
        s_wo,
        s_bo,
        s_g1,
        s_b1,
        sum_w1,
        s_c1,
        sum_w2,
        s_c2,
        s_g2,
        s_b2,
    )


def solution(mesh):
    rows, mat, vec = P("dp", "seq", None), P("dp", None), P("dp")
    params = (mat, vec, mat, mat, vec, mat, vec, vec, vec, mat, vec, mat, vec, vec, vec)
    return jax.shard_map(
        functools.partial(per_device, (mesh.shape["dp"], mesh.shape["seq"])),
        mesh=mesh,
        in_specs=(rows, vec) + params + (rows,),
        out_specs=(rows, rows) + params,
        check_vma=False,
    )
```

```python
import functools

import jax
import jax.numpy as jnp
from jax import lax
from jax.experimental import pallas as pl
from jax.experimental.pallas import tpu as pltpu
from jax.sharding import PartitionSpec as P

HEAD = 64
LANES = 128
EPS = 1e-12
NEG_FILL = -1000000000.0
SCALE2 = 0.125 * 1.4426950408889634
F32 = jnp.float32
BF16 = jnp.bfloat16
VMEM_LIMIT = 60 * 1024 * 1024


def dot(left, right, left_dim, right_dim):
    return lax.dot_general(
        left, right, (((left_dim,), (right_dim,)), ((), ())), preferred_element_type=F32
    )


def attend_kernel(bias_ref, q_ref, k_ref, v_ref, ctx_ref, probs_ref, *, rows_blk):
    seq_len = q_ref.shape[0]
    lane = lax.broadcasted_iota(jnp.int32, (1, LANES), 1)
    bias = bias_ref[...]
    for blk in range(seq_len // rows_blk):
        rows = pl.ds(blk * rows_blk, rows_blk)
        query = q_ref[rows, :]
        mixed = []
        for head in range(2):
            mine = (lane < HEAD) if head == 0 else (lane >= HEAD)
            query_h = jnp.where(mine, query, jnp.zeros_like(query))
            score = dot(query_h, k_ref[...], 1, 1) + bias
            top = jnp.max(score, axis=1, keepdims=True)
            expo = jnp.exp2((score - top) * SCALE2)
            total = jnp.sum(expo, axis=1, keepdims=True)
            probs = (expo * (1.0 / total)).astype(BF16)
            probs_ref[head, rows, :] = probs
            mixed.append(dot(probs, v_ref[...], 1, 0))
        ctx_ref[rows, :] = jnp.where(lane < HEAD, mixed[0], mixed[1]).astype(BF16)


def attend(bias, query, key, value):
    seq_len, feats = query.shape
    cols = pl.BlockSpec((seq_len, LANES), lambda g: (0, g))
    return pl.pallas_call(
        functools.partial(attend_kernel, rows_blk=min(512, seq_len)),
        grid=(feats // LANES,),
        in_specs=[pl.BlockSpec((1, seq_len), lambda g: (0, 0)), cols, cols, cols],
        out_specs=[cols, pl.BlockSpec((2, seq_len, seq_len), lambda g: (g, 0, 0))],
        out_shape=[
            jax.ShapeDtypeStruct((seq_len, feats), BF16),
            jax.ShapeDtypeStruct((feats // HEAD, seq_len, seq_len), BF16),
        ],
        compiler_params=pltpu.CompilerParams(vmem_limit_bytes=VMEM_LIMIT),
    )(bias, query, key, value)


def attend_back_kernel(
    q_ref, k_ref, v_ref, ctx_ref, grad_ref, probs_ref, out_ref, key_acc, value_acc, *, rows_blk
):
    seq_len = q_ref.shape[0]
    lane = lax.broadcasted_iota(jnp.int32, (1, LANES), 1)
    for blk in range(seq_len // rows_blk):
        rows = pl.ds(blk * rows_blk, rows_blk)
        query = q_ref[rows, :]
        grad = grad_ref[rows, :]
        overlap = ctx_ref[rows, :].astype(F32) * grad.astype(F32)
        query_t = query.T
        grad_t = grad.T
        grad_query = []
        for head in range(2):
            mine = (lane < HEAD) if head == 0 else (lane >= HEAD)
            part = slice(head * HEAD, (head + 1) * HEAD)
            grad_h = jnp.where(mine, grad, jnp.zeros_like(grad))
            inner = jnp.sum(jnp.where(mine, overlap, 0.0), axis=1, keepdims=True)
            probs = probs_ref[head, rows, :]
            grad_probs = dot(grad_h, v_ref[...], 1, 1)
            grad_score = (probs.astype(F32) * (grad_probs - inner)).astype(BF16)
            grad_query.append(dot(grad_score, k_ref[...], 1, 0))
            grad_key = dot(query_t[part], grad_score, 1, 0)
            grad_value = dot(grad_t[part], probs, 1, 0)
            if blk == 0:
                key_acc[head] = grad_key
                value_acc[head] = grad_value
            else:
                key_acc[head] += grad_key
                value_acc[head] += grad_value
        out_ref[0, rows, :] = (0.125 * jnp.where(lane < HEAD, grad_query[0], grad_query[1])).astype(
            BF16
        )
    out_ref[1] = (0.125 * jnp.concatenate([key_acc[0], key_acc[1]], axis=0)).T.astype(BF16)
    out_ref[2] = jnp.concatenate([value_acc[0], value_acc[1]], axis=0).T.astype(BF16)


def attend_back(query, key, value, ctx, grad_ctx, probs):
    seq_len, feats = ctx.shape
    cols = pl.BlockSpec((seq_len, LANES), lambda g: (0, g))
    return pl.pallas_call(
        functools.partial(attend_back_kernel, rows_blk=min(512, seq_len)),
        grid=(feats // LANES,),
        in_specs=[cols] * 5 + [pl.BlockSpec((2, seq_len, seq_len), lambda g: (g, 0, 0))],
        out_specs=pl.BlockSpec((3, seq_len, LANES), lambda g: (0, 0, g)),
        out_shape=jax.ShapeDtypeStruct((3, seq_len, feats), BF16),
        scratch_shapes=[pltpu.VMEM((2, HEAD, seq_len), F32)] * 2,
        compiler_params=pltpu.CompilerParams(vmem_limit_bytes=VMEM_LIMIT),
    )(query, key, value, ctx, grad_ctx, probs)


MESH = pl.DeviceIdType.MESH


def remote(src, dst, send, recv, device):
    return pltpu.make_async_remote_copy(
        src_ref=src, dst_ref=dst, send_sem=send, recv_sem=recv,
        device_id=device, device_id_type=MESH,
    )


class Place:
    def __init__(self, seq_size, seq_count):
        self.me = me = lax.axis_index("dp")
        self.here = here = lax.axis_index("seq")
        core, x_at, y_at = me % 2, (me // 2) % 2, (me // 4) % 2
        self.to_core, self.to_x, self.to_y = 1 - 2 * core, 2 - 4 * x_at, 4 - 8 * y_at
        self.core_dev = (me + self.to_core, here)
        self.x_dev = (me + self.to_x, here)
        self.y_dev = (me + self.to_y, here)
        self.shift = (seq_size - seq_count) * core
        self.my_seq = here - self.shift
        self.is_owner = (self.my_seq >= 0) & (self.my_seq < seq_count)
        self.seq_size, self.seq_count = seq_size, seq_count

    def barrier(self):
        barrier = pltpu.get_barrier_semaphore()
        for device in (self.core_dev, self.x_dev, self.y_dev):
            pl.semaphore_signal(barrier, inc=1, device_id=device, device_id_type=MESH)
        for step in range(1, self.seq_size):
            pl.semaphore_signal(
                barrier, inc=1, device_id=(self.me, (self.here + step) % self.seq_size),
                device_id_type=MESH,
            )
        pl.semaphore_wait(barrier, 3 + self.seq_size - 1)


class Gather:
    def __init__(self, place, full, own, sems, index):
        self.place, self.full, self.own, self.index = place, full, own, index
        self.send_sem, self.recv_sem, self.core_send, self.core_recv = sems

    def half(self, which):
        count = self.full.shape[1] // 2
        return pl.ds(which * count, count)

    def piece(self, p):
        at = self.place
        rows = self.half(p % 2)
        shard = at.me + (0, 0, 0, 0, at.to_x, at.to_y)[p]
        src = self.own.at[rows] if p < 4 else self.full.at[shard, rows]
        device = (at.x_dev, at.y_dev, at.y_dev, at.x_dev, at.y_dev, at.x_dev)[p]
        return remote(
            src, self.full.at[shard, rows],
            self.send_sem.at[self.index, p], self.recv_sem.at[self.index, p], device,
        )

    def core_piece(self, p):
        at = self.place
        if p == 6:
            src, dst = self.own, self.full.at[at.me]
        else:
            across = at.to_x + at.to_y
            shard = at.me + (at.to_x, at.to_y, at.to_y, at.to_x, across, across)[p]
            src = dst = self.full.at[shard, self.half(p % 2)]
        return remote(
            src, dst, self.core_send.at[self.index, p], self.core_recv.at[self.index, p],
            at.core_dev,
        )

    def start(self, *pieces):
        for p in pieces:
            self.piece(p).start()

    def arrive(self, *pieces):
        for p in pieces:
            self.piece(p).wait_recv()

    def to_core(self, *pieces):
        for p in pieces:
            self.core_piece(p).start()

    def finish(self, pieces, core_pieces):
        for p in core_pieces:
            self.core_piece(p).wait_recv()
        for p in pieces:
            self.piece(p).wait_send()
        for p in core_pieces:
            self.core_piece(p).wait_send()


class RowsIn:
    def __init__(self, place, blocks, whole, buf, sems):
        self.place, self.blocks, self.whole, self.buf = place, blocks, whole, buf
        self.send_sem, self.recv_sem, self.local_sem = sems
        self.rows = blocks.shape[1]

    def to(self, seq, source):
        at = self.place
        return remote(
            self.blocks.at[seq], self.whole.at[pl.ds(source * self.rows, self.rows)],
            self.send_sem.at[seq], self.recv_sem.at[source], (at.me, seq + at.shift),
        )

    def own(self, count):
        at = self.place

        def out(pos, k):
            return pltpu.make_async_copy(
                self.buf, self.whole.at[pl.ds(pos * self.rows, self.rows)], self.local_sem.at[k]
            )

        @pl.when(at.is_owner)
        def _():
            load = pltpu.make_async_copy(self.blocks.at[at.my_seq], self.buf, self.local_sem.at[0])
            load.start()
            load.wait()
            out(at.here, 1).start()
            out(at.here, 1).wait()

        @pl.when(jnp.logical_not(at.is_owner))
        def _():
            self.buf[...] = jnp.zeros_like(self.buf)
            for pos in range(at.seq_size):
                out(pos, pos).start()
            for pos in range(at.seq_size):
                out(pos, pos).wait()

    def start(self):
        at = self.place
        for seq in range(at.seq_count):

            @pl.when(at.here != seq + at.shift)
            def _():
                self.to(seq, at.here).start()

    def finish(self):
        at = self.place

        @pl.when(at.is_owner)
        def _():
            for pos in range(at.seq_size):

                @pl.when(at.here != pos)
                def _():
                    remote(
                        self.blocks.at[0], self.whole.at[pl.ds(pos * self.rows, self.rows)],
                        self.send_sem.at[0], self.recv_sem.at[pos],
                        (at.me, (at.here + 1) % at.seq_size),
                    ).wait_recv()

        for seq in range(at.seq_count):

            @pl.when(at.here != seq + at.shift)
            def _():
                self.to(seq, at.here).wait_send()


def start_kernel(
    seq_size, seq_count, tokens, wq, wk, wv, vecs, w2, w1, wo,
    rows_out, qkv_full, vec_full, w2_full, w1_full, wo_full,
    qkv_low, w2_low, w1_low, wo_low, row_buf,
    row_send, row_recv, row_local, sem_a, sem_b, sem_c, sem_d, own_sem,
):
    place = Place(seq_size, seq_count)
    sems = (sem_a, sem_b, sem_c, sem_d)
    rows = RowsIn(place, tokens, rows_out, row_buf, (row_send, row_recv, row_local))
    first = [
        Gather(place, qkv_full, qkv_low, sems, 0),
        Gather(place, vec_full, vecs, sems, 1),
    ]
    later = [
        Gather(place, w2_full, w2_low, sems, 2),
        Gather(place, w1_full, w1_low, sems, 3),
        Gather(place, wo_full, wo_low, sems, 4),
    ]
    place.barrier()
    rows.start()
    feats = wq.shape[1]
    for k, item in enumerate((wq, wk, wv)):
        qkv_low[:, k * feats : (k + 1) * feats] = item[...].astype(BF16)
    for item in first:
        item.start(0, 1)
    for item in first:
        item.start(2, 3)
        item.to_core(6)
    w2_low[...] = w2[...].astype(BF16)
    w1_low[...] = w1[...].astype(BF16)
    wo_low[...] = wo[...].astype(BF16)
    keep = [
        pltpu.make_async_copy(item.own, item.full.at[place.me], own_sem.at[item.index])
        for item in first + later
    ]
    for copy in keep:
        copy.start()
    for item in first:
        item.arrive(0, 1)
        item.start(4, 5)
        item.to_core(0, 1)
    for item in later:
        item.start(0, 1)
    rows.own(seq_size)
    for item in first:
        item.arrive(2, 3)
        item.to_core(2, 3)
    for item in first:
        item.arrive(4, 5)
        item.to_core(4, 5)
    for item in first:
        item.finish(range(6), range(7))
    for item in later:
        item.arrive(0, 1)
        for p in (0, 1):
            item.piece(p).wait_send()
    for copy in keep:
        copy.wait()
    rows.finish()


def start_all(seq_size, tokens, qkv_parts, vecs, w2, w1, wo):
    seq_count, blk, feats = tokens.shape
    any_spec = pl.BlockSpec(memory_space=pl.ANY)
    vmem_spec = pl.BlockSpec(memory_space=pltpu.VMEM)
    dma = pltpu.SemaphoreType.DMA
    shard = qkv_parts[0].shape[0]

    def full(rows, cols):
        return jax.ShapeDtypeStruct((8, rows, cols), BF16)

    return pl.pallas_call(
        functools.partial(start_kernel, seq_size, seq_count),
        in_specs=[any_spec] + [vmem_spec] * 7,
        out_specs=[any_spec] * 6,
        out_shape=[
            jax.ShapeDtypeStruct((seq_size * blk, feats), BF16),
            full(shard, 3 * feats), full(*vecs.shape), full(*w2.shape), full(*w1.shape),
            full(*wo.shape),
        ],
        scratch_shapes=[
            pltpu.VMEM((shard, 3 * feats), BF16), pltpu.VMEM(w2.shape, BF16),
            pltpu.VMEM(w1.shape, BF16), pltpu.VMEM(wo.shape, BF16), pltpu.VMEM((blk, feats), BF16),
            dma((seq_count,)), dma((seq_size,)), dma((seq_size,)),
            dma((5, 6)), dma((5, 6)), dma((5, 7)), dma((5, 7)), dma((5,)),
        ],
        compiler_params=pltpu.CompilerParams(
            collective_id=2, has_side_effects=True, vmem_limit_bytes=VMEM_LIMIT
        ),
    )(tokens, *qkv_parts, vecs, w2, w1, wo)


def forward_kernel(
    seq_size, seq_count, rows_blk,
    bias_ref, x_ref, wq_ref, wk_ref, wv_ref, bq_ref, bv_ref, upstream, w2_in, w1_in, wo_in,
    q_ref, k_ref, v_ref, ctx_ref, probs_ref, dy_out, w2_full, w1_full, wo_full,
    row_buf, row_send, row_recv, row_local, sem_a, sem_b, sem_c, sem_d,
):
    step = pl.program_id(0)
    last = pl.num_programs(0) - 1
    place = Place(seq_size, seq_count)
    sems = (sem_a, sem_b, sem_c, sem_d)
    rows = RowsIn(place, upstream, dy_out, row_buf, (row_send, row_recv, row_local))
    later = [
        Gather(place, full, full.at[place.me], sems, k)
        for k, full in enumerate((w2_full, w1_full, wo_full))
    ]

    @pl.when(step == 0)
    def _():
        place.barrier()
        for item in later:
            item.start(2, 3)
        for item in later:
            item.start(4, 5)
        rows.start()
        for item in later:
            item.to_core(6, 0, 1)
        rows.own(seq_size)

    x_rows = x_ref[...]
    depth = x_rows.shape[1]
    mats = [ref[...].reshape(depth, LANES) for ref in (wq_ref, wk_ref, wv_ref)]
    both = dot(x_rows, jnp.concatenate(mats, axis=1), 1, 0)
    q_ref[...] = (both[:, :LANES] + bq_ref[...]).astype(BF16)
    k_ref[...] = both[:, LANES : 2 * LANES].astype(BF16)
    v_ref[...] = (both[:, 2 * LANES :] + bv_ref[...]).astype(BF16)
    attend_kernel(bias_ref, q_ref, k_ref, v_ref, ctx_ref, probs_ref, rows_blk=rows_blk)

    @pl.when(step == last - 1)
    def _():
        for item in later:
            item.arrive(2, 3)
            item.to_core(2, 3)

    @pl.when(step == last)
    def _():
        for item in later:
            item.arrive(4, 5)
            item.to_core(4, 5)
        for item in later:
            item.finish(range(2, 6), range(7))
        rows.finish()


def forward_all(seq_size, bias, rows, qkv_full, bq, bv, upstream, w2_full, w1_full, wo_full):
    seq_len, feats = rows.shape
    seq_count, blk, _ = upstream.shape
    pairs = feats // LANES
    shard = qkv_full.shape[1]
    any_spec = pl.BlockSpec(memory_space=pl.ANY)
    dma = pltpu.SemaphoreType.DMA
    cols = pl.BlockSpec((seq_len, LANES), lambda g: (0, g))

    def mat(which):
        return pl.BlockSpec((8, shard, LANES), lambda g, w=which: (0, 0, w * pairs + g))

    vec = pl.BlockSpec((1, LANES), lambda g: (0, g))
    fulls = [w2_full, w1_full, wo_full]
    flat = jax.ShapeDtypeStruct((seq_len, feats), BF16)
    return pl.pallas_call(
        functools.partial(forward_kernel, seq_size, seq_count, min(512, seq_len)),
        grid=(pairs,),
        in_specs=[
            pl.BlockSpec((1, seq_len), lambda g: (0, 0)),
            pl.BlockSpec((seq_len, feats), lambda g: (0, 0)),
            mat(0), mat(1), mat(2), vec, vec,
        ]
        + [any_spec] * 4,
        out_specs=[cols] * 4
        + [pl.BlockSpec((2, seq_len, seq_len), lambda g: (g, 0, 0))]
        + [any_spec] * 4,
        out_shape=[flat] * 4
        + [jax.ShapeDtypeStruct((feats // HEAD, seq_len, seq_len), BF16), flat]
        + [jax.ShapeDtypeStruct(item.shape, BF16) for item in fulls],
        scratch_shapes=[
            pltpu.VMEM((blk, feats), BF16),
            dma((seq_count,)), dma((seq_size,)), dma((seq_size,)),
            dma((3, 6)), dma((3, 6)), dma((3, 7)), dma((3, 7)),
        ],
        input_output_aliases={8: 6, 9: 7, 10: 8},
        compiler_params=pltpu.CompilerParams(
            collective_id=3, has_side_effects=True, vmem_limit_bytes=VMEM_LIMIT
        ),
    )(bias, rows, qkv_full, qkv_full, qkv_full, bq, bv, upstream, *fulls)


def add_rows(dest, other, start, count, step=16):
    def body(i, carry):
        to = pl.ds(pl.multiple_of(start + i * step, step), step)
        frm = pl.ds(pl.multiple_of(i * step, step), step)
        dest[to, :] = (dest[to, :].astype(F32) + other[frm, :].astype(F32)).astype(BF16)
        return carry

    lax.fori_loop(0, count // step, body, 0)


def reduce_kernel(seq_size, seq_count, chunk_count, *refs):
    refs = list(refs)

    def take(count):
        got = refs[:count]
        del refs[:count]
        return got

    grads = take(chunk_count)
    (token_rows,) = take(1)
    sums = take(chunk_count)
    (token_out,) = take(1)
    own, other, first_x, first_y, second, from_left, from_right, passed = [
        take(chunk_count) for _ in range(8)
    ]
    (token_buf,) = take(1)
    own_sem, core_send, core_recv, one_send, one_recv, two_send, two_recv = take(7)
    z_send, z_recv, token_send, token_recv, token_local = take(5)

    place = Place(seq_size, seq_count)
    me, here, shift = place.me, place.here, place.shift
    my_seq, is_owner = place.my_seq, place.is_owner
    to_core, to_x, to_y = place.to_core, place.to_x, place.to_y
    rows = token_out.shape[1]
    place.barrier()

    apart = [(r % 2) * to_x + (r // 2) * to_y for r in range(4)]
    core_dev, x_dev, y_dev = (me + to_core, here), (me + to_x, here), (me + to_y, here)

    def keep_copy(c, r):
        return pltpu.make_async_copy(grads[c].at[me + apart[r]], own[c].at[r], own_sem.at[c, r])

    def core_copy(c, r):
        return remote(
            grads[c].at[me + to_core + apart[r]], other[c].at[r],
            core_send.at[c, r], core_recv.at[c, r], core_dev,
        )

    def one_copy(c, way, k):
        half = own[c].shape[1] // 2
        if way == 0:
            src, dst, dev = own[c].at[(1, 3)[k], pl.ds(0, half)], first_x[c].at[k], x_dev
        else:
            src, dst, dev = own[c].at[(2, 3)[k], pl.ds(half, half)], first_y[c].at[k], y_dev
        return remote(src, dst, one_send.at[c, way, k], one_recv.at[c, way, k], dev)

    def two_copy(c, way):
        half = own[c].shape[1] // 2
        if way == 0:
            src, dst, dev = own[c].at[2, pl.ds(0, half)], second[c].at[0], y_dev
        else:
            src, dst, dev = own[c].at[1, pl.ds(half, half)], second[c].at[1], x_dev
        return remote(src, dst, two_send.at[c, way], two_recv.at[c, way], dev)

    def z_copy(c, way, src):
        dst = (from_left, from_right)[way][c]
        dev = (me, here + (1, -1)[way])
        return remote(src, dst, z_send.at[c, way], z_recv.at[c, way], dev)

    def token_copy(pos):
        return remote(
            token_rows.at[pl.ds(pos * rows, rows)], token_out.at[my_seq],
            token_send.at[pos], token_recv.at[my_seq], (me, pos),
        )

    for c in range(chunk_count):
        for r in (3, 1, 2, 0):
            core_copy(c, r).start()
            keep_copy(c, r).start()

    @pl.when(is_owner)
    def _():
        for pos in range(seq_size):
            @pl.when(here != pos)
            def _():
                token_copy(pos).start()
        load = pltpu.make_async_copy(
            token_rows.at[pl.ds(here * rows, rows)], token_buf, token_local.at[0]
        )
        load.start()
        load.wait()
        store = pltpu.make_async_copy(token_buf, token_out.at[my_seq], token_local.at[1])
        store.start()
        store.wait()

    def core_stage(c):
        for r in (3, 1, 2, 0):
            keep_copy(c, r).wait()
            core_copy(c, r).wait_recv()
            add_rows(own[c].at[r], other[c].at[r], 0, own[c].shape[1])
            if r == 3:
                one_copy(c, 0, 1).start()
                one_copy(c, 1, 1).start()
            elif r == 1:
                one_copy(c, 0, 0).start()
            elif r == 2:
                one_copy(c, 1, 0).start()

    def one_stage(c):
        half = own[c].shape[1] // 2
        for way, base in ((0, 0), (1, half)):
            one_copy(c, way, 1).wait_recv()
            add_rows(own[c].at[(2, 1)[way]], (first_x, first_y)[way][c].at[1], base, half)
            two_copy(c, way).start()
        for way, base in ((0, 0), (1, half)):
            one_copy(c, way, 0).wait_recv()
            add_rows(own[c].at[0], (first_x, first_y)[way][c].at[0], base, half)

    def two_stage(c):
        half = own[c].shape[1] // 2
        for way, base in ((0, 0), (1, half)):
            two_copy(c, way).wait_recv()
            add_rows(own[c].at[0], second[c].at[way], base, half)

    def z_hop(c, hop):
        mine = own[c].at[0]
        for way in range(2):
            at = here if way == 0 else seq_size - 1 - here
            buf = passed[c].at[way]

            @pl.when(at == hop)
            def _():
                if hop == 0:
                    z_copy(c, way, mine).start()
                else:
                    arrived = (from_left, from_right)[way][c]
                    z_copy(c, way, buf).wait_recv()
                    if hop < seq_size - 1:
                        def body(i, carry):
                            at_rows = pl.ds(pl.multiple_of(i * 16, 16), 16)
                            buf[at_rows, :] = (
                                mine[at_rows, :].astype(F32) + arrived[at_rows, :].astype(F32)
                            ).astype(BF16)
                            return carry

                        lax.fori_loop(0, mine.shape[0] // 16, body, 0)
                        z_copy(c, way, buf).start()

    def finish(c):
        mine = own[c].at[0]
        total = sums[c]

        def body(i, carry):
            at_rows = pl.ds(pl.multiple_of(i * 16, 16), 16)
            total[at_rows, :] = mine[at_rows, :].astype(F32)
            return carry

        lax.fori_loop(0, mine.shape[0] // 16, body, 0)
        for way in range(2):
            arrived = (from_left, from_right)[way][c]
            at = here if way == 0 else seq_size - 1 - here

            @pl.when(at > 0)
            def _():
                def more(i, carry):
                    at_rows = pl.ds(pl.multiple_of(i * 16, 16), 16)
                    total[at_rows, :] += arrived[at_rows, :].astype(F32)
                    return carry

                lax.fori_loop(0, mine.shape[0] // 16, more, 0)

    depth = 3 + seq_size
    for time in range(chunk_count + depth):
        for stage in range(depth):
            c = time - stage
            if 0 <= c < chunk_count:
                if stage == 0:
                    core_stage(c)
                elif stage == 1:
                    one_stage(c)
                elif stage == 2:
                    two_stage(c)
                    z_hop(c, 0)
                elif stage < 2 + seq_size:
                    z_hop(c, stage - 2)
                else:
                    finish(c)

    for c in range(chunk_count):
        for r in range(4):
            core_copy(c, r).wait_send()
        for way in range(2):
            for k in range(2):
                one_copy(c, way, k).wait_send()
            two_copy(c, way).wait_send()
            at = here if way == 0 else seq_size - 1 - here

            @pl.when(at < seq_size - 1)
            def _():
                z_copy(c, way, own[c].at[0]).wait_send()

    for seq in range(seq_count):
        @pl.when(here != seq + shift)
        def _():
            remote(
                token_rows.at[pl.ds(0, rows)], token_out.at[seq],
                token_send.at[0], token_recv.at[seq], (me, (here + 1) % seq_size),
            ).wait_recv()

    @pl.when(is_owner)
    def _():
        for pos in range(seq_size):
            @pl.when(here != pos)
            def _():
                token_copy(pos).wait_send()


def reduce_all(seq_size, seq_count, chunks, token_rows):
    count = len(chunks)
    seq_len, feats = token_rows.shape
    blk = seq_len // seq_size
    any_spec = pl.BlockSpec(memory_space=pl.ANY)
    vmem_spec = pl.BlockSpec(memory_space=pltpu.VMEM)

    def bufs(lead, split):
        return [
            pltpu.VMEM(lead + (item.shape[1] // split, item.shape[2]), BF16) for item in chunks
        ]

    dma = pltpu.SemaphoreType.DMA
    return pl.pallas_call(
        functools.partial(reduce_kernel, seq_size, seq_count, count),
        in_specs=[any_spec] * (count + 1),
        out_specs=[vmem_spec] * count + [any_spec],
        out_shape=[jax.ShapeDtypeStruct(item.shape[1:], F32) for item in chunks]
        + [jax.ShapeDtypeStruct((seq_count, blk, feats), BF16)],
        scratch_shapes=bufs((4,), 1) + bufs((4,), 1) + bufs((2,), 2) + bufs((2,), 2) + bufs((2,), 2)
        + bufs((), 1) + bufs((), 1) + bufs((2,), 1)
        + [
            pltpu.VMEM((blk, feats), BF16),
            dma((count, 4)), dma((count, 4)), dma((count, 4)),
            dma((count, 2, 2)), dma((count, 2, 2)), dma((count, 2)), dma((count, 2)),
            dma((count, 2)), dma((count, 2)), dma((seq_size,)), dma((seq_count,)), dma((2,)),
        ],
        compiler_params=pltpu.CompilerParams(
            collective_id=1, has_side_effects=True, vmem_limit_bytes=VMEM_LIMIT
        ),
    )(*chunks, token_rows)


def normalize(resid):
    centre = resid - jnp.mean(resid, axis=-1, keepdims=True)
    inv = lax.rsqrt(jnp.mean(centre * centre, axis=-1, keepdims=True) + EPS)
    return centre * inv, inv


def normalize_back(normed, inv, grad_normed):
    mean_grad = jnp.mean(grad_normed, axis=-1, keepdims=True)
    mean_both = jnp.mean(grad_normed * normed, axis=-1, keepdims=True)
    return inv * (grad_normed - mean_grad - normed * mean_both)


def column_sum(rows):
    return jnp.sum(rows, axis=0, dtype=F32)


INV_SQRT2 = 0.7071067811865476
INV_SQRT_2PI = 0.3989422804014327


def per_device(mesh_shape, tokens, lengths, *rest):
    weights, upstream = rest[:15], rest[15]
    dp_size, seq_size = mesh_shape
    seq_count, row_count, feats = tokens.shape
    dp_index = lax.axis_index("dp")
    here = lax.axis_index("seq")
    spare = seq_size - seq_count

    def owner_shift(dp):
        return spare * (dp % 2)

    my_seq = jnp.clip(here - owner_shift(dp_index), 0, seq_count - 1)

    def owned_by(dp, pos):
        seq = pos - owner_shift(dp)
        return 0 <= seq < seq_count

    def shift_pairs(step, to_owner):
        pairs = []
        for dp in range(dp_size):
            for pos in range(seq_size):
                dest = (pos + step) % seq_size
                if owned_by(dp, dest if to_owner else pos):
                    pairs.append((dp * seq_size + pos, dp * seq_size + dest))
        return pairs

    def gather(piece):
        return lax.all_gather(piece, "dp", axis=0, tiled=True)

    def to_owners(blocks):
        pieces = []
        for step in range(seq_size):
            dest = (here + step) % seq_size
            seq = jnp.clip(dest - owner_shift(dp_index), 0, seq_count - 1)
            piece = lax.dynamic_index_in_dim(blocks, seq, 0, keepdims=False)
            if step == 0:
                owner = (here >= owner_shift(dp_index)) & (here < owner_shift(dp_index) + seq_count)
                piece = jnp.where(owner, piece, jnp.zeros_like(piece))
            else:
                piece = lax.ppermute(piece, ("dp", "seq"), shift_pairs(step, True))
            pieces.append(piece)
        order = (here - jnp.arange(seq_size)) % seq_size
        return jnp.take(jnp.stack(pieces), order, axis=0).reshape(-1, feats)

    def from_owners(rows):
        pieces = rows.reshape(seq_size, row_count, feats)
        arrived = []
        for step in range(seq_size):
            piece = lax.dynamic_index_in_dim(pieces, (here - step) % seq_size, 0, keepdims=False)
            if step:
                piece = lax.ppermute(piece, ("dp", "seq"), shift_pairs(seq_size - step, False))
            arrived.append(piece)
        stack = jnp.stack(arrived)
        order = (jnp.arange(seq_count) + owner_shift(dp_index) - here) % seq_size
        return jnp.take(stack, order, axis=0)

    wq, bq, wk, wv, bv, wo, bo, g1, b1, w1, c1, w2, c2, g2, b2 = weights
    shard_rows = feats // dp_size
    direct = dp_size == 8 and shard_rows % 32 == 0
    vec_parts = (bq, bv, bo, g1, b1, c1, c2, g2, b2)
    vec_sizes = [item.shape[0] for item in vec_parts]
    vec_len = sum(vec_sizes)
    vec_rows = -(-vec_len // (32 * LANES)) * 32
    packed = jnp.concatenate(vec_parts).astype(BF16)
    seq_len = seq_size * row_count
    position = lax.iota(jnp.int32, seq_len)
    valid_len = lax.dynamic_index_in_dim(lengths, my_seq, 0, keepdims=False)
    key_bias = jnp.where(position < valid_len, 0.0, 8.0 * NEG_FILL).astype(F32).reshape(1, seq_len)

    if direct:
        packed = jnp.pad(packed, (0, vec_rows * LANES - vec_len)).reshape(vec_rows, LANES)
        inputs, qkv_full, packed, w2_part, w1_part, wo_part = start_all(
            seq_size, tokens, (wq, wk, wv), packed, w2, w1, wo
        )
        packed = packed.reshape(dp_size, vec_rows * LANES)
        qkv_mat = qkv_full.reshape(feats, 3 * feats)
    else:
        qkv_mat = gather(jnp.concatenate([wq, wk, wv], axis=1).astype(BF16))
        packed = lax.all_gather(packed, "dp", axis=0, tiled=False)
        merge_mat, expand_mat, reduce_mat = [gather(item.astype(BF16)) for item in (wo, w1, w2)]
    vecs = []
    start = 0
    for size in vec_sizes:
        vecs.append(packed[:, start : start + size].reshape(1, -1).astype(F32))
        start += size
    bq, bv, bo, g1, b1, c1, c2, g2, b2 = vecs

    if direct:
        query, key, value, ctx, probs, dy, reduce_mat, expand_mat, merge_mat = forward_all(
            seq_size, key_bias, inputs, qkv_full, bq, bv, upstream, w2_part, w1_part, wo_part
        )
        reduce_mat, expand_mat, merge_mat = [
            item.reshape(-1, item.shape[2]) for item in (reduce_mat, expand_mat, merge_mat)
        ]
        dy = dy.astype(F32)
    else:
        inputs = to_owners(tokens)
        dy = to_owners(upstream).astype(F32)
        qkv = dot(inputs, qkv_mat, 1, 0)
        query = (qkv[:, :feats] + bq).astype(BF16)
        key = qkv[:, feats : 2 * feats].astype(BF16)
        value = (qkv[:, 2 * feats :] + bv).astype(BF16)
        ctx, probs = attend(key_bias, query, key, value)
    normed1, inv1 = normalize(inputs.astype(F32) + dot(ctx, merge_mat, 1, 0) + bo)
    hidden = normed1 * g1 + b1
    hidden_low = hidden.astype(BF16)
    pre = dot(hidden_low, expand_mat, 1, 0) + c1
    phi_cum = 0.5 * (1.0 + lax.erf(pre * INV_SQRT2))
    act = (pre * phi_cum).astype(BF16)
    slope = (phi_cum + pre * (INV_SQRT_2PI * jnp.exp(-0.5 * pre * pre))).astype(BF16)
    normed2, inv2 = normalize(hidden + dot(act, reduce_mat, 1, 0) + c2)
    result = (normed2 * g2 + b2).astype(BF16)
    output = from_owners(result)

    d_g2 = column_sum(dy * normed2)
    d_b2 = column_sum(dy)
    grad_resid2 = normalize_back(normed2, inv2, g2 * dy)
    grad_ffn = grad_resid2.astype(BF16)
    d_w2 = dot(act, grad_ffn, 0, 0).astype(BF16)
    d_c2 = column_sum(grad_ffn)
    grad_pre = (dot(grad_ffn, reduce_mat, 1, 1) * slope.astype(F32)).astype(BF16)
    d_w1 = dot(hidden_low, grad_pre, 0, 0).astype(BF16)
    d_c1 = column_sum(grad_pre)
    grad_hidden = grad_resid2 + dot(grad_pre, expand_mat, 1, 1)
    d_g1 = column_sum(grad_hidden * normed1)
    d_b1 = column_sum(grad_hidden)
    grad_resid1 = normalize_back(normed1, inv1, g1 * grad_hidden)
    grad_att = grad_resid1.astype(BF16)
    d_wo = dot(ctx, grad_att, 0, 0).astype(BF16)
    d_bo = column_sum(grad_att)
    grad_ctx = dot(grad_att, merge_mat, 1, 1).astype(BF16)
    grad_qkv = attend_back(query, key, value, ctx, grad_ctx, probs)
    token_rows = grad_resid1
    d_qkv = []
    for which in range(3):
        mat = qkv_mat[:, which * feats : (which + 1) * feats]
        token_rows = token_rows + dot(grad_qkv[which], mat, 1, 1)
        d_qkv.append(dot(inputs, grad_qkv[which], 0, 0).astype(BF16))
    d_bq = column_sum(grad_qkv[0])
    d_bv = column_sum(grad_qkv[2])
    vec_grads = (d_bq, d_bv, d_bo, d_g1, d_b1, d_c1, d_c2, d_g2, d_b2)
    vec_pack = jnp.concatenate([item.reshape(dp_size, -1) for item in vec_grads], axis=1)
    token_rows = token_rows.astype(BF16)
    if direct:
        vec_pack = jnp.pad(vec_pack, ((0, 0), (0, vec_rows * LANES - vec_len)))
        mats = [d_w2, d_w1, d_wo] + d_qkv
        chunks = [item.reshape(dp_size, item.shape[0] // dp_size, item.shape[1]) for item in mats]
        chunks.append(vec_pack.reshape(dp_size, vec_rows, LANES).astype(BF16))
        sum_w2, sum_w1, s_wo, s_wq, s_wk, s_wv, flat, token_grad = reduce_all(
            seq_size, seq_count, chunks, token_rows
        )
        flat = flat.reshape(-1)
    else:
        token_grad = from_owners(token_rows)
        vec_cols = -(-vec_len // (shard_rows * LANES)) * LANES
        vec_pack = jnp.pad(vec_pack, ((0, 0), (0, shard_rows * vec_cols - vec_len)))
        vec_pack = vec_pack.reshape(feats, vec_cols).astype(BF16)

        def reduce(full):
            own = lax.psum_scatter(full, "dp", scatter_dimension=0, tiled=True)
            return lax.psum(own, "seq").astype(F32)

        sum_w2 = reduce(d_w2)
        sum_w1 = reduce(d_w1)
        sum_rest = reduce(jnp.concatenate([d_wo] + d_qkv + [vec_pack], axis=1))
        s_wo, s_wq, s_wk, s_wv = [sum_rest[:, i * feats : (i + 1) * feats] for i in range(4)]
        flat = sum_rest[:, 4 * feats :].reshape(-1)
    out_vecs = []
    start = 0
    for size in vec_sizes:
        out_vecs.append(flat[start : start + size])
        start += size
    s_bq, s_bv, s_bo, s_g1, s_b1, s_c1, s_c2, s_g2, s_b2 = out_vecs
    return (
        output,
        token_grad,
        s_wq,
        s_bq,
        s_wk,
        s_wv,
        s_bv,
        s_wo,
        s_bo,
        s_g1,
        s_b1,
        sum_w1,
        s_c1,
        sum_w2,
        s_c2,
        s_g2,
        s_b2,
    )


def solution(mesh):
    rows, mat, vec = P("dp", "seq", None), P("dp", None), P("dp")
    params = (mat, vec, mat, mat, vec, mat, vec, vec, vec, mat, vec, mat, vec, vec, vec)
    return jax.shard_map(
        functools.partial(per_device, (mesh.shape["dp"], mesh.shape["seq"])),
        mesh=mesh,
        in_specs=(rows, vec) + params + (rows,),
        out_specs=(rows, rows) + params,
        check_vma=False,
    )
```

```python
import functools

import jax
import jax.numpy as jnp
from jax import lax
from jax.experimental import pallas as pl
from jax.experimental.pallas import tpu as pltpu
from jax.sharding import PartitionSpec as P

HEAD = 64
LANES = 128
EPS = 1e-12
NEG_FILL = -1000000000.0
SCALE2 = 0.125 * 1.4426950408889634
F32 = jnp.float32
BF16 = jnp.bfloat16
VMEM_LIMIT = 60 * 1024 * 1024
VMEM_MAX = 67043328


def dot(left, right, left_dim, right_dim):
    return lax.dot_general(
        left, right, (((left_dim,), (right_dim,)), ((), ())), preferred_element_type=F32
    )


def attend_kernel(bias_ref, q_ref, k_ref, v_ref, ctx_ref, probs_ref, *, rows_blk):
    seq_len = q_ref.shape[0]
    lane = lax.broadcasted_iota(jnp.int32, (1, LANES), 1)
    bias = bias_ref[...]
    for blk in range(seq_len // rows_blk):
        rows = pl.ds(blk * rows_blk, rows_blk)
        query = q_ref[rows, :]
        mixed = []
        for head in range(2):
            mine = (lane < HEAD) if head == 0 else (lane >= HEAD)
            query_h = jnp.where(mine, query, jnp.zeros_like(query))
            score = dot(query_h, k_ref[...], 1, 1) + bias
            top = jnp.max(score, axis=1, keepdims=True)
            expo = jnp.exp2((score - top) * SCALE2)
            total = jnp.sum(expo, axis=1, keepdims=True)
            probs = (expo * (1.0 / total)).astype(BF16)
            probs_ref[head, rows, :] = probs
            mixed.append(dot(probs, v_ref[...], 1, 0))
        ctx_ref[rows, :] = jnp.where(lane < HEAD, mixed[0], mixed[1]).astype(BF16)


def attend(bias, query, key, value):
    seq_len, feats = query.shape
    cols = pl.BlockSpec((seq_len, LANES), lambda g: (0, g))
    return pl.pallas_call(
        functools.partial(attend_kernel, rows_blk=min(512, seq_len)),
        grid=(feats // LANES,),
        in_specs=[pl.BlockSpec((1, seq_len), lambda g: (0, 0)), cols, cols, cols],
        out_specs=[cols, pl.BlockSpec((2, seq_len, seq_len), lambda g: (g, 0, 0))],
        out_shape=[
            jax.ShapeDtypeStruct((seq_len, feats), BF16),
            jax.ShapeDtypeStruct((feats // HEAD, seq_len, seq_len), BF16),
        ],
        compiler_params=pltpu.CompilerParams(vmem_limit_bytes=VMEM_LIMIT),
    )(bias, query, key, value)


def attend_back_pair(
    q_ref, k_ref, v_ref, ctx_ref, grad_ref, probs_ref, store, key_acc, value_acc, rows_blk
):
    seq_len = q_ref.shape[0]
    lane = lax.broadcasted_iota(jnp.int32, (1, LANES), 1)
    for blk in range(seq_len // rows_blk):
        rows = pl.ds(blk * rows_blk, rows_blk)
        query = q_ref[rows, :]
        grad = grad_ref[rows, :]
        overlap = ctx_ref[rows, :].astype(F32) * grad.astype(F32)
        query_t = query.T
        grad_t = grad.T
        grad_query = []
        for head in range(2):
            mine = (lane < HEAD) if head == 0 else (lane >= HEAD)
            part = slice(head * HEAD, (head + 1) * HEAD)
            grad_h = jnp.where(mine, grad, jnp.zeros_like(grad))
            inner = jnp.sum(jnp.where(mine, overlap, 0.0), axis=1, keepdims=True)
            probs = probs_ref[head, rows, :]
            grad_probs = dot(grad_h, v_ref[...], 1, 1)
            grad_score = (probs.astype(F32) * (grad_probs - inner)).astype(BF16)
            grad_query.append(dot(grad_score, k_ref[...], 1, 0))
            grad_key = dot(query_t[part], grad_score, 1, 0)
            grad_value = dot(grad_t[part], probs, 1, 0)
            if blk == 0:
                key_acc[head] = grad_key
                value_acc[head] = grad_value
            else:
                key_acc[head] += grad_key
                value_acc[head] += grad_value
        mixed = jnp.where(lane < HEAD, grad_query[0], grad_query[1])
        store(0, rows, (0.125 * mixed).astype(BF16))
    everything = pl.ds(0, seq_len)
    grad_key = jnp.concatenate([key_acc[0], key_acc[1]], axis=0)
    store(1, everything, (0.125 * grad_key).T.astype(BF16))
    grad_value = jnp.concatenate([value_acc[0], value_acc[1]], axis=0)
    store(2, everything, grad_value.T.astype(BF16))


def attend_back_kernel(
    q_ref, k_ref, v_ref, ctx_ref, grad_ref, probs_ref, out_ref, key_acc, value_acc, *, rows_blk
):
    def store(which, rows, values):
        out_ref[which, rows, :] = values

    attend_back_pair(
        q_ref, k_ref, v_ref, ctx_ref, grad_ref, probs_ref, store, key_acc, value_acc, rows_blk
    )


def attend_back(query, key, value, ctx, grad_ctx, probs):
    seq_len, feats = ctx.shape
    cols = pl.BlockSpec((seq_len, LANES), lambda g: (0, g))
    return pl.pallas_call(
        functools.partial(attend_back_kernel, rows_blk=min(512, seq_len)),
        grid=(feats // LANES,),
        in_specs=[cols] * 5 + [pl.BlockSpec((2, seq_len, seq_len), lambda g: (g, 0, 0))],
        out_specs=pl.BlockSpec((3, seq_len, LANES), lambda g: (0, 0, g)),
        out_shape=jax.ShapeDtypeStruct((3, seq_len, feats), BF16),
        scratch_shapes=[pltpu.VMEM((2, HEAD, seq_len), F32)] * 2,
        compiler_params=pltpu.CompilerParams(vmem_limit_bytes=VMEM_LIMIT),
    )(query, key, value, ctx, grad_ctx, probs)


MESH = pl.DeviceIdType.MESH


def remote(src, dst, send, recv, device):
    return pltpu.make_async_remote_copy(
        src_ref=src, dst_ref=dst, send_sem=send, recv_sem=recv,
        device_id=device, device_id_type=MESH,
    )


class Place:
    def __init__(self, seq_size, seq_count):
        self.me = me = lax.axis_index("dp")
        self.here = here = lax.axis_index("seq")
        core, x_at, y_at = me % 2, (me // 2) % 2, (me // 4) % 2
        self.to_core, self.to_x, self.to_y = 1 - 2 * core, 2 - 4 * x_at, 4 - 8 * y_at
        self.core_dev = (me + self.to_core, here)
        self.x_dev = (me + self.to_x, here)
        self.y_dev = (me + self.to_y, here)
        self.shift = (seq_size - seq_count) * core
        self.my_seq = here - self.shift
        self.is_owner = (self.my_seq >= 0) & (self.my_seq < seq_count)
        self.seq_size, self.seq_count = seq_size, seq_count

    def barrier(self):
        barrier = pltpu.get_barrier_semaphore()
        for device in (self.core_dev, self.x_dev, self.y_dev):
            pl.semaphore_signal(barrier, inc=1, device_id=device, device_id_type=MESH)
        for step in range(1, self.seq_size):
            pl.semaphore_signal(
                barrier, inc=1, device_id=(self.me, (self.here + step) % self.seq_size),
                device_id_type=MESH,
            )
        pl.semaphore_wait(barrier, 3 + self.seq_size - 1)


class Gather:
    def __init__(self, place, full, own, sems, index):
        self.place, self.full, self.own, self.index = place, full, own, index
        self.send_sem, self.recv_sem, self.core_send, self.core_recv = sems

    def half(self, which):
        count = self.full.shape[1] // 2
        return pl.ds(which * count, count)

    def piece(self, p):
        at = self.place
        rows = self.half(p % 2)
        shard = at.me + (0, 0, 0, 0, at.to_x, at.to_y)[p]
        src = self.own.at[rows] if p < 4 else self.full.at[shard, rows]
        device = (at.x_dev, at.y_dev, at.y_dev, at.x_dev, at.y_dev, at.x_dev)[p]
        return remote(
            src, self.full.at[shard, rows],
            self.send_sem.at[self.index, p], self.recv_sem.at[self.index, p], device,
        )

    def core_piece(self, p):
        at = self.place
        if p == 6:
            src, dst = self.own, self.full.at[at.me]
        else:
            across = at.to_x + at.to_y
            shard = at.me + (at.to_x, at.to_y, at.to_y, at.to_x, across, across)[p]
            src = dst = self.full.at[shard, self.half(p % 2)]
        return remote(
            src, dst, self.core_send.at[self.index, p], self.core_recv.at[self.index, p],
            at.core_dev,
        )

    def start(self, *pieces):
        for p in pieces:
            self.piece(p).start()

    def arrive(self, *pieces):
        for p in pieces:
            self.piece(p).wait_recv()

    def to_core(self, *pieces):
        for p in pieces:
            self.core_piece(p).start()

    def finish(self, pieces, core_pieces):
        for p in core_pieces:
            self.core_piece(p).wait_recv()
        for p in pieces:
            self.piece(p).wait_send()
        for p in core_pieces:
            self.core_piece(p).wait_send()


class RowsIn:
    def __init__(self, place, blocks, whole, buf, sems):
        self.place, self.blocks, self.whole, self.buf = place, blocks, whole, buf
        self.send_sem, self.recv_sem, self.local_sem = sems
        self.rows = blocks.shape[1]

    def to(self, seq, source):
        at = self.place
        return remote(
            self.blocks.at[seq], self.whole.at[pl.ds(source * self.rows, self.rows)],
            self.send_sem.at[seq], self.recv_sem.at[source], (at.me, seq + at.shift),
        )

    def own(self, count):
        at = self.place

        def out(pos, k):
            return pltpu.make_async_copy(
                self.buf, self.whole.at[pl.ds(pos * self.rows, self.rows)], self.local_sem.at[k]
            )

        @pl.when(at.is_owner)
        def _():
            load = pltpu.make_async_copy(self.blocks.at[at.my_seq], self.buf, self.local_sem.at[0])
            load.start()
            load.wait()
            out(at.here, 1).start()
            out(at.here, 1).wait()

        @pl.when(jnp.logical_not(at.is_owner))
        def _():
            self.buf[...] = jnp.zeros_like(self.buf)
            for pos in range(at.seq_size):
                out(pos, pos).start()
            for pos in range(at.seq_size):
                out(pos, pos).wait()

    def start(self):
        at = self.place
        for seq in range(at.seq_count):

            @pl.when(at.here != seq + at.shift)
            def _():
                self.to(seq, at.here).start()

    def finish(self):
        at = self.place

        @pl.when(at.is_owner)
        def _():
            for pos in range(at.seq_size):

                @pl.when(at.here != pos)
                def _():
                    remote(
                        self.blocks.at[0], self.whole.at[pl.ds(pos * self.rows, self.rows)],
                        self.send_sem.at[0], self.recv_sem.at[pos],
                        (at.me, (at.here + 1) % at.seq_size),
                    ).wait_recv()

        for seq in range(at.seq_count):

            @pl.when(at.here != seq + at.shift)
            def _():
                self.to(seq, at.here).wait_send()


def start_kernel(
    seq_size, seq_count, tokens, wq, wk, wv, vecs, w2, w1, wo,
    rows_out, qkv_full, vec_full, w2_full, w1_full, wo_full,
    qkv_low, w2_low, w1_low, wo_low, row_buf,
    row_send, row_recv, row_local, sem_a, sem_b, sem_c, sem_d, own_sem,
):
    place = Place(seq_size, seq_count)
    sems = (sem_a, sem_b, sem_c, sem_d)
    rows = RowsIn(place, tokens, rows_out, row_buf, (row_send, row_recv, row_local))
    first = [
        Gather(place, qkv_full, qkv_low, sems, 0),
        Gather(place, vec_full, vecs, sems, 1),
    ]
    later = [
        Gather(place, w2_full, w2_low, sems, 2),
        Gather(place, w1_full, w1_low, sems, 3),
        Gather(place, wo_full, wo_low, sems, 4),
    ]
    place.barrier()
    rows.start()
    feats = wq.shape[1]
    for k, item in enumerate((wq, wk, wv)):
        qkv_low[:, k * feats : (k + 1) * feats] = item[...].astype(BF16)
    for item in first:
        item.start(0, 1)
    for item in first:
        item.start(2, 3)
        item.to_core(6)
    w2_low[...] = w2[...].astype(BF16)
    w1_low[...] = w1[...].astype(BF16)
    wo_low[...] = wo[...].astype(BF16)
    keep = [
        pltpu.make_async_copy(item.own, item.full.at[place.me], own_sem.at[item.index])
        for item in first + later
    ]
    for copy in keep:
        copy.start()
    for item in first:
        item.arrive(0, 1)
        item.start(4, 5)
        item.to_core(0, 1)
    for item in later:
        item.start(0, 1)
    rows.own(seq_size)
    for item in first:
        item.arrive(2, 3)
        item.to_core(2, 3)
    for item in first:
        item.arrive(4, 5)
        item.to_core(4, 5)
    for item in first:
        item.finish(range(6), range(7))
    for item in later:
        item.arrive(0, 1)
        for p in (0, 1):
            item.piece(p).wait_send()
    for copy in keep:
        copy.wait()
    rows.finish()


def start_all(seq_size, tokens, qkv_parts, vecs, w2, w1, wo):
    seq_count, blk, feats = tokens.shape
    any_spec = pl.BlockSpec(memory_space=pl.ANY)
    vmem_spec = pl.BlockSpec(memory_space=pltpu.VMEM)
    dma = pltpu.SemaphoreType.DMA
    shard = qkv_parts[0].shape[0]

    def full(rows, cols):
        return jax.ShapeDtypeStruct((8, rows, cols), BF16)

    return pl.pallas_call(
        functools.partial(start_kernel, seq_size, seq_count),
        in_specs=[any_spec] + [vmem_spec] * 7,
        out_specs=[any_spec] * 6,
        out_shape=[
            jax.ShapeDtypeStruct((seq_size * blk, feats), BF16),
            full(shard, 3 * feats), full(*vecs.shape), full(*w2.shape), full(*w1.shape),
            full(*wo.shape),
        ],
        scratch_shapes=[
            pltpu.VMEM((shard, 3 * feats), BF16), pltpu.VMEM(w2.shape, BF16),
            pltpu.VMEM(w1.shape, BF16), pltpu.VMEM(wo.shape, BF16), pltpu.VMEM((blk, feats), BF16),
            dma((seq_count,)), dma((seq_size,)), dma((seq_size,)),
            dma((5, 6)), dma((5, 6)), dma((5, 7)), dma((5, 7)), dma((5,)),
        ],
        compiler_params=pltpu.CompilerParams(
            collective_id=2, has_side_effects=True, vmem_limit_bytes=VMEM_LIMIT
        ),
    )(tokens, *qkv_parts, vecs, w2, w1, wo)


def forward_kernel(
    seq_size, seq_count, rows_blk,
    bias_ref, x_ref, wq_ref, wk_ref, wv_ref, bq_ref, bv_ref, upstream, w2_in, w1_in, wo_in,
    q_ref, k_ref, v_ref, ctx_ref, probs_ref, dy_out, w2_full, w1_full, wo_full,
    row_buf, row_send, row_recv, row_local, sem_a, sem_b, sem_c, sem_d,
):
    step = pl.program_id(0)
    last = pl.num_programs(0) - 1
    place = Place(seq_size, seq_count)
    sems = (sem_a, sem_b, sem_c, sem_d)
    rows = RowsIn(place, upstream, dy_out, row_buf, (row_send, row_recv, row_local))
    later = [
        Gather(place, full, full.at[place.me], sems, k)
        for k, full in enumerate((w2_full, w1_full, wo_full))
    ]

    @pl.when(step == 0)
    def _():
        place.barrier()
        for item in later:
            item.start(2, 3)
        for item in later:
            item.start(4, 5)
        rows.start()
        for item in later:
            item.to_core(6, 0, 1)
        rows.own(seq_size)

    x_rows = x_ref[...]
    depth = x_rows.shape[1]
    mats = [ref[...].reshape(depth, LANES) for ref in (wq_ref, wk_ref, wv_ref)]
    both = dot(x_rows, jnp.concatenate(mats, axis=1), 1, 0)
    q_ref[...] = (both[:, :LANES] + bq_ref[...]).astype(BF16)
    k_ref[...] = both[:, LANES : 2 * LANES].astype(BF16)
    v_ref[...] = (both[:, 2 * LANES :] + bv_ref[...]).astype(BF16)
    attend_kernel(bias_ref, q_ref, k_ref, v_ref, ctx_ref, probs_ref, rows_blk=rows_blk)

    @pl.when(step == last - 1)
    def _():
        for item in later:
            item.arrive(2, 3)
            item.to_core(2, 3)

    @pl.when(step == last)
    def _():
        for item in later:
            item.arrive(4, 5)
            item.to_core(4, 5)
        for item in later:
            item.finish(range(2, 6), range(7))
        rows.finish()


def forward_all(seq_size, bias, rows, qkv_full, bq, bv, upstream, w2_full, w1_full, wo_full):
    seq_len, feats = rows.shape
    seq_count, blk, _ = upstream.shape
    pairs = feats // LANES
    shard = qkv_full.shape[1]
    any_spec = pl.BlockSpec(memory_space=pl.ANY)
    dma = pltpu.SemaphoreType.DMA
    cols = pl.BlockSpec((seq_len, LANES), lambda g: (0, g))

    def mat(which):
        return pl.BlockSpec((8, shard, LANES), lambda g, w=which: (0, 0, w * pairs + g))

    vec = pl.BlockSpec((1, LANES), lambda g: (0, g))
    fulls = [w2_full, w1_full, wo_full]
    flat = jax.ShapeDtypeStruct((seq_len, feats), BF16)
    return pl.pallas_call(
        functools.partial(forward_kernel, seq_size, seq_count, min(512, seq_len)),
        grid=(pairs,),
        in_specs=[
            pl.BlockSpec((1, seq_len), lambda g: (0, 0)),
            pl.BlockSpec((seq_len, feats), lambda g: (0, 0)),
            mat(0), mat(1), mat(2), vec, vec,
        ]
        + [any_spec] * 4,
        out_specs=[cols] * 4
        + [pl.BlockSpec((2, seq_len, seq_len), lambda g: (g, 0, 0))]
        + [any_spec] * 4,
        out_shape=[flat] * 4
        + [jax.ShapeDtypeStruct((feats // HEAD, seq_len, seq_len), BF16), flat]
        + [jax.ShapeDtypeStruct(item.shape, BF16) for item in fulls],
        scratch_shapes=[
            pltpu.VMEM((blk, feats), BF16),
            dma((seq_count,)), dma((seq_size,)), dma((seq_size,)),
            dma((3, 6)), dma((3, 6)), dma((3, 7)), dma((3, 7)),
        ],
        input_output_aliases={8: 6, 9: 7, 10: 8},
        compiler_params=pltpu.CompilerParams(
            collective_id=3, has_side_effects=True, vmem_limit_bytes=VMEM_LIMIT
        ),
    )(bias, rows, qkv_full, qkv_full, qkv_full, bq, bv, upstream, *fulls)


class Reduce:
    def __init__(self, place, grads, total, bufs, sems, index):
        self.place, self.grads, self.total, self.index = place, grads, total, index
        self.own, self.other, self.first_x, self.first_y, self.second, self.arrived = bufs
        (
            self.own_sem, self.core_send, self.core_recv, self.one_send, self.one_recv,
            self.two_send, self.two_recv, self.z_send, self.z_recv,
        ) = sems
        at = place
        self.apart = [(r % 2) * at.to_x + (r // 2) * at.to_y for r in range(4)]
        self.rows = self.own.shape[1]
        self.half = self.rows // 2

    def keep_copy(self, r):
        return pltpu.make_async_copy(
            self.grads.at[self.place.me + self.apart[r]], self.own.at[r],
            self.own_sem.at[self.index, r],
        )

    def core_copy(self, r):
        at = self.place
        return remote(
            self.grads.at[at.me + at.to_core + self.apart[r]], self.other.at[r],
            self.core_send.at[self.index, r], self.core_recv.at[self.index, r], at.core_dev,
        )

    def one_copy(self, way, k):
        half = self.half
        if way == 0:
            src, dst = self.own.at[(1, 3)[k], pl.ds(0, half)], self.first_x.at[k]
        else:
            src, dst = self.own.at[(2, 3)[k], pl.ds(half, half)], self.first_y.at[k]
        return remote(
            src, dst, self.one_send.at[self.index, way, k], self.one_recv.at[self.index, way, k],
            (self.place.x_dev, self.place.y_dev)[way],
        )

    def two_copy(self, way):
        src = self.own.at[(2, 1)[way], pl.ds(way * self.half, self.half)]
        return remote(
            src, self.second.at[way], self.two_send.at[self.index, way],
            self.two_recv.at[self.index, way], (self.place.y_dev, self.place.x_dev)[way],
        )

    def z_copy(self, way, src):
        at = self.place
        return remote(
            src, self.arrived.at[way], self.z_send.at[self.index, way],
            self.z_recv.at[self.index, way], (at.me, at.here + (1, -1)[way]),
        )

    def hops(self, way):
        at = self.place
        return at.here if way == 0 else at.seq_size - 1 - at.here

    def add(self, dest, first, other, start, count):
        def body(i, carry):
            to = pl.ds(pl.multiple_of(start + i * 16, 16), 16)
            frm = pl.ds(pl.multiple_of(i * 16, 16), 16)
            dest[to, :] = (first[to, :].astype(F32) + other[frm, :].astype(F32)).astype(BF16)
            return carry

        lax.fori_loop(0, count // 16, body, 0)

    def begin(self):
        for r in (3, 1, 2, 0):
            self.core_copy(r).start()
            self.keep_copy(r).start()

    def core_stage(self):
        for r in (3, 1, 2, 0):
            self.keep_copy(r).wait()
            self.core_copy(r).wait_recv()
            self.add(self.own.at[r], self.own.at[r], self.other.at[r], 0, self.rows)
            if r == 3:
                self.one_copy(0, 1).start()
                self.one_copy(1, 1).start()
            elif r == 1:
                self.one_copy(0, 0).start()
            elif r == 2:
                self.one_copy(1, 0).start()

    def one_stage(self):
        firsts = (self.first_x, self.first_y)
        for k in (1, 0):
            for way in range(2):
                self.one_copy(way, k).wait_recv()
                dest = self.own.at[(2, 1)[way] if k else 0]
                self.add(dest, dest, firsts[way].at[k], way * self.half, self.half)
                if k:
                    self.two_copy(way).start()

    def two_stage(self):
        mine = self.own.at[0]
        for way in range(2):
            self.two_copy(way).wait_recv()
            self.add(mine, mine, self.second.at[way], way * self.half, self.half)
        self.z_hop(0)

    def z_hop(self, hop):
        mine = self.own.at[0]
        for way in range(2):
            passed = self.other.at[way]

            @pl.when(self.hops(way) == hop)
            def _():
                if hop == 0:
                    self.z_copy(way, mine).start()
                else:
                    self.z_copy(way, passed).wait_recv()
                    if hop < self.place.seq_size - 1:
                        self.add(passed, mine, self.arrived.at[way], 0, self.rows)
                        self.z_copy(way, passed).start()

    def finish(self):
        total = self.own.at[3]
        last = self.place.seq_size - 1
        mine = self.own.at[0]
        up, down = self.arrived.at[0], self.arrived.at[1]
        here = self.place.here
        self.one_copy(0, 1).wait_send()
        self.one_copy(1, 1).wait_send()

        @pl.when(here == 0)
        def _():
            self.add(total, mine, down, 0, self.rows)

        @pl.when(here == last)
        def _():
            self.add(total, mine, up, 0, self.rows)

        @pl.when((here > 0) & (here < last))
        def _():
            def body(i, carry):
                at = pl.ds(pl.multiple_of(i * 16, 16), 16)
                total[at, :] = (
                    mine[at, :].astype(F32) + up[at, :].astype(F32) + down[at, :].astype(F32)
                ).astype(BF16)
                return carry

            lax.fori_loop(0, self.rows // 16, body, 0)

        self.total_copy().start()

    def total_copy(self):
        return pltpu.make_async_copy(
            self.own.at[3], self.total, self.own_sem.at[self.index, 3]
        )

    def drain(self):
        for r in range(4):
            self.core_copy(r).wait_send()
        for way in range(2):
            self.one_copy(way, 0).wait_send()
            self.two_copy(way).wait_send()

            @pl.when(self.hops(way) < self.place.seq_size - 1)
            def _():
                self.z_copy(way, self.own.at[0]).wait_send()

        self.total_copy().wait()


def backward_kernel(seq_size, seq_count, rows_blk, outer_count, *refs):
    refs = list(refs)

    def take(count):
        got = refs[:count]
        del refs[:count]
        return got

    count = outer_count + 4
    q_ref, k_ref, v_ref, ctx_ref, grad_ref, probs_ref, vec_ref = take(7)
    x_in, qkv_in, resid_in = take(3)
    outer = take(outer_count)
    totals = take(count)
    (token_out,) = take(1)
    key_acc, value_acc, grads_all, x_rows, qkv_mat, resid, token_rows = take(7)
    mats = take(3)
    (vec_src,) = take(1)
    bufs = [take(count) for _ in range(6)]
    sems = take(9)
    load_sem, token_send, token_recv, token_local = take(4)

    step = pl.program_id(0)
    place = Place(seq_size, seq_count)
    here = place.here
    sources = outer + mats + [vec_src]
    jobs = [
        Reduce(place, sources[c], totals[c], [buf[c] for buf in bufs], sems, c)
        for c in range(count)
    ]
    seq_len, feats = x_rows.shape
    blk = seq_len // seq_size
    loads = [
        pltpu.make_async_copy(src, dst, load_sem.at[k])
        for k, (src, dst) in enumerate(((x_in, x_rows), (qkv_in, qkv_mat), (resid_in, resid)))
    ]

    def token_copy(pos):
        return remote(
            token_rows.at[pl.ds(pos * blk, blk)], token_out.at[place.my_seq],
            token_send.at[pos], token_recv.at[place.my_seq], (place.me, pos),
        )

    def token_keep(pos):
        return pltpu.make_async_copy(
            token_rows.at[pl.ds(pos * blk, blk)], token_out.at[place.my_seq], token_local.at[0]
        )

    @pl.when(step == 0)
    def _():
        place.barrier()
        for job in jobs[:outer_count]:
            job.begin()
        for load in loads:
            load.start()
        jobs[0].core_stage()

    column = pl.multiple_of(step * LANES, LANES)

    def store(which, rows, values):
        grads_all[which, rows, pl.ds(column, LANES)] = values

    attend_back_pair(
        q_ref, k_ref, v_ref, ctx_ref, grad_ref, probs_ref, store, key_acc, value_acc, rows_blk
    )

    @pl.when(step == 0)
    def _():
        for job in jobs[1:outer_count]:
            job.core_stage()

    @pl.when(step == 3)
    def _():
        jobs[0].one_stage()

    @pl.when(step == pl.num_programs(0) - 1)
    def _():
        for load in loads:
            load.wait()
        for pos in range(seq_size):
            rows = pl.ds(pos * blk, blk)
            part = resid[rows, :]
            for which in range(3):
                mat = qkv_mat[:, :, which * feats : (which + 1) * feats].reshape(feats, feats)
                part = part + dot(grads_all[which, rows, :], mat, 1, 1)
            token_rows[rows, :] = part.astype(BF16)

            @pl.when(place.is_owner & (here != pos))
            def _():
                token_copy(pos).start()

            @pl.when(place.is_owner & (here == pos))
            def _():
                token_keep(pos).start()

        for job in jobs[1:outer_count]:
            job.one_stage()
        jobs[0].two_stage()
        for which in range(3):
            outer_sum = dot(x_rows[...], grads_all[which], 0, 0).astype(BF16)
            mats[which][...] = outer_sum.reshape(mats[which].shape)
            jobs[outer_count + which].begin()
            if which:
                jobs[outer_count + which - 1].core_stage()
        ones = jnp.ones((16, seq_len), BF16)
        grad_bq = dot(ones, grads_all[0], 1, 0)
        grad_bv = dot(ones, grads_all[2], 1, 0)
        row = lax.broadcasted_iota(jnp.int32, (16, 1), 0)
        biases = jnp.where(row == 0, grad_bq, grad_bv).astype(BF16)
        for shard in range(8):
            vec_src[shard, 0:16, :] = vec_ref[...]
            vec_src[shard, 16:32, :] = biases
        jobs[-1].begin()
        jobs[-2].core_stage()
        jobs[-1].core_stage()

        hops = [functools.partial(Reduce.z_hop, hop=hop) for hop in range(1, seq_size)]
        tail = hops + [Reduce.finish]
        plan = [(jobs[0], 0, tail)]
        for k, job in enumerate(jobs[1:outer_count]):
            plan.append((job, k, [Reduce.two_stage] + tail))
        for k, job in enumerate(jobs[outer_count:]):
            plan.append((job, 1 + k, [Reduce.one_stage, Reduce.two_stage] + tail))
        for time in range(max(wait + len(stages) for _, wait, stages in plan)):
            for job, wait, stages in plan:
                if 0 <= time - wait < len(stages):
                    stages[time - wait](job)
        for job in jobs:
            job.drain()

        for seq in range(seq_count):

            @pl.when(here != seq + place.shift)
            def _():
                remote(
                    token_rows.at[pl.ds(0, blk)], token_out.at[seq], token_send.at[0],
                    token_recv.at[seq], (place.me, (here + 1) % seq_size),
                ).wait_recv()

        @pl.when(place.is_owner)
        def _():
            token_keep(0).wait()
            for pos in range(seq_size):

                @pl.when(here != pos)
                def _():
                    token_copy(pos).wait_send()


def backward_all(
    seq_size, seq_count, query, key, value, ctx, grad_ctx, probs, vecs, inputs, qkv_full, resid, outer
):
    seq_len, feats = ctx.shape
    blk = seq_len // seq_size
    shard = qkv_full.shape[1]
    any_spec = pl.BlockSpec(memory_space=pl.ANY)
    cols = pl.BlockSpec((seq_len, LANES), lambda g: (0, g))
    shapes = [item.shape[1:] for item in outer] + [(shard, feats)] * 3 + [(32, feats)]
    count = len(shapes)
    dma = pltpu.SemaphoreType.DMA

    def bufs(lead, split):
        return [pltpu.VMEM((lead, rows // split, width), BF16) for rows, width in shapes]

    return pl.pallas_call(
        functools.partial(backward_kernel, seq_size, seq_count, min(512, seq_len), len(outer)),
        grid=(feats // LANES,),
        in_specs=[cols] * 5
        + [
            pl.BlockSpec((2, seq_len, seq_len), lambda g: (g, 0, 0)),
            pl.BlockSpec(vecs.shape, lambda g: (0, 0)),
        ]
        + [any_spec] * (3 + len(outer)),
        out_specs=[any_spec] * (count + 1),
        out_shape=[jax.ShapeDtypeStruct(shape, BF16) for shape in shapes]
        + [jax.ShapeDtypeStruct((seq_count, blk, feats), BF16)],
        scratch_shapes=[pltpu.VMEM((2, HEAD, seq_len), F32)] * 2
        + [
            pltpu.VMEM((3, seq_len, feats), BF16),
            pltpu.VMEM((seq_len, feats), BF16),
            pltpu.VMEM(qkv_full.shape, BF16),
            pltpu.VMEM((seq_len, feats), F32),
            pltpu.VMEM((seq_len, feats), BF16),
        ]
        + [pltpu.VMEM((8, shard, feats), BF16)] * 3
        + [pltpu.VMEM((8, 32, feats), BF16)]
        + bufs(4, 1) + bufs(4, 1) + bufs(2, 2) + bufs(2, 2) + bufs(2, 2) + bufs(2, 1)
        + [
            dma((count, 4)), dma((count, 4)), dma((count, 4)),
            dma((count, 2, 2)), dma((count, 2, 2)), dma((count, 2)), dma((count, 2)),
            dma((count, 2)), dma((count, 2)),
            dma((3,)), dma((seq_size,)), dma((seq_count,)), dma((1,)),
        ],
        compiler_params=pltpu.CompilerParams(
            collective_id=1, has_side_effects=True, vmem_limit_bytes=VMEM_MAX
        ),
    )(query, key, value, ctx, grad_ctx, probs, vecs, inputs, qkv_full, resid, *outer)


def normalize(resid):
    centre = resid - jnp.mean(resid, axis=-1, keepdims=True)
    inv = lax.rsqrt(jnp.mean(centre * centre, axis=-1, keepdims=True) + EPS)
    return centre * inv, inv


def normalize_back(normed, inv, grad_normed):
    mean_grad = jnp.mean(grad_normed, axis=-1, keepdims=True)
    mean_both = jnp.mean(grad_normed * normed, axis=-1, keepdims=True)
    return inv * (grad_normed - mean_grad - normed * mean_both)


def column_sum(rows):
    return jnp.sum(rows, axis=0, dtype=F32)


INV_SQRT2 = 0.7071067811865476
INV_SQRT_2PI = 0.3989422804014327


def per_device(mesh_shape, tokens, lengths, *rest):
    weights, upstream = rest[:15], rest[15]
    dp_size, seq_size = mesh_shape
    seq_count, row_count, feats = tokens.shape
    dp_index = lax.axis_index("dp")
    here = lax.axis_index("seq")
    spare = seq_size - seq_count

    def owner_shift(dp):
        return spare * (dp % 2)

    my_seq = jnp.clip(here - owner_shift(dp_index), 0, seq_count - 1)

    def owned_by(dp, pos):
        seq = pos - owner_shift(dp)
        return 0 <= seq < seq_count

    def shift_pairs(step, to_owner):
        pairs = []
        for dp in range(dp_size):
            for pos in range(seq_size):
                dest = (pos + step) % seq_size
                if owned_by(dp, dest if to_owner else pos):
                    pairs.append((dp * seq_size + pos, dp * seq_size + dest))
        return pairs

    def gather(piece):
        return lax.all_gather(piece, "dp", axis=0, tiled=True)

    def to_owners(blocks):
        pieces = []
        for step in range(seq_size):
            dest = (here + step) % seq_size
            seq = jnp.clip(dest - owner_shift(dp_index), 0, seq_count - 1)
            piece = lax.dynamic_index_in_dim(blocks, seq, 0, keepdims=False)
            if step == 0:
                owner = (here >= owner_shift(dp_index)) & (here < owner_shift(dp_index) + seq_count)
                piece = jnp.where(owner, piece, jnp.zeros_like(piece))
            else:
                piece = lax.ppermute(piece, ("dp", "seq"), shift_pairs(step, True))
            pieces.append(piece)
        order = (here - jnp.arange(seq_size)) % seq_size
        return jnp.take(jnp.stack(pieces), order, axis=0).reshape(-1, feats)

    def from_owners(rows):
        pieces = rows.reshape(seq_size, row_count, feats)
        arrived = []
        for step in range(seq_size):
            piece = lax.dynamic_index_in_dim(pieces, (here - step) % seq_size, 0, keepdims=False)
            if step:
                piece = lax.ppermute(piece, ("dp", "seq"), shift_pairs(seq_size - step, False))
            arrived.append(piece)
        stack = jnp.stack(arrived)
        order = (jnp.arange(seq_count) + owner_shift(dp_index) - here) % seq_size
        return jnp.take(stack, order, axis=0)

    wq, bq, wk, wv, bv, wo, bo, g1, b1, w1, c1, w2, c2, g2, b2 = weights
    shard_rows = feats // dp_size
    direct = dp_size == 8 and shard_rows % 32 == 0
    vec_parts = (bq, bv, bo, g1, b1, c1, c2, g2, b2)
    vec_sizes = [item.shape[0] for item in vec_parts]
    vec_len = sum(vec_sizes)
    vec_rows = -(-vec_len // (32 * LANES)) * 32
    packed = jnp.concatenate(vec_parts).astype(BF16)
    seq_len = seq_size * row_count
    position = lax.iota(jnp.int32, seq_len)
    valid_len = lax.dynamic_index_in_dim(lengths, my_seq, 0, keepdims=False)
    key_bias = jnp.where(position < valid_len, 0.0, 8.0 * NEG_FILL).astype(F32).reshape(1, seq_len)

    if direct:
        packed = jnp.pad(packed, (0, vec_rows * LANES - vec_len)).reshape(vec_rows, LANES)
        inputs, qkv_full, packed, w2_part, w1_part, wo_part = start_all(
            seq_size, tokens, (wq, wk, wv), packed, w2, w1, wo
        )
        packed = packed.reshape(dp_size, vec_rows * LANES)
        qkv_mat = qkv_full.reshape(feats, 3 * feats)
    else:
        qkv_mat = gather(jnp.concatenate([wq, wk, wv], axis=1).astype(BF16))
        packed = lax.all_gather(packed, "dp", axis=0, tiled=False)
        merge_mat, expand_mat, reduce_mat = [gather(item.astype(BF16)) for item in (wo, w1, w2)]
    vecs = []
    start = 0
    for size in vec_sizes:
        vecs.append(packed[:, start : start + size].reshape(1, -1).astype(F32))
        start += size
    bq, bv, bo, g1, b1, c1, c2, g2, b2 = vecs

    if direct:
        query, key, value, ctx, probs, dy, reduce_mat, expand_mat, merge_mat = forward_all(
            seq_size, key_bias, inputs, qkv_full, bq, bv, upstream, w2_part, w1_part, wo_part
        )
        reduce_mat, expand_mat, merge_mat = [
            item.reshape(-1, item.shape[2]) for item in (reduce_mat, expand_mat, merge_mat)
        ]
        dy = dy.astype(F32)
    else:
        inputs = to_owners(tokens)
        dy = to_owners(upstream).astype(F32)
        qkv = dot(inputs, qkv_mat, 1, 0)
        query = (qkv[:, :feats] + bq).astype(BF16)
        key = qkv[:, feats : 2 * feats].astype(BF16)
        value = (qkv[:, 2 * feats :] + bv).astype(BF16)
        ctx, probs = attend(key_bias, query, key, value)
    normed1, inv1 = normalize(inputs.astype(F32) + dot(ctx, merge_mat, 1, 0) + bo)
    hidden = normed1 * g1 + b1
    hidden_low = hidden.astype(BF16)
    pre = dot(hidden_low, expand_mat, 1, 0) + c1
    phi_cum = 0.5 * (1.0 + lax.erf(pre * INV_SQRT2))
    act = (pre * phi_cum).astype(BF16)
    slope = (phi_cum + pre * (INV_SQRT_2PI * jnp.exp(-0.5 * pre * pre))).astype(BF16)
    normed2, inv2 = normalize(hidden + dot(act, reduce_mat, 1, 0) + c2)
    result = (normed2 * g2 + b2).astype(BF16)
    output = from_owners(result)

    d_g2 = column_sum(dy * normed2)
    d_b2 = column_sum(dy)
    grad_resid2 = normalize_back(normed2, inv2, g2 * dy)
    grad_ffn = grad_resid2.astype(BF16)
    d_w2 = dot(act, grad_ffn, 0, 0).astype(BF16)
    d_c2 = column_sum(grad_ffn)
    grad_pre = (dot(grad_ffn, reduce_mat, 1, 1) * slope.astype(F32)).astype(BF16)
    d_w1 = dot(hidden_low, grad_pre, 0, 0).astype(BF16)
    d_c1 = column_sum(grad_pre)
    grad_hidden = grad_resid2 + dot(grad_pre, expand_mat, 1, 1)
    d_g1 = column_sum(grad_hidden * normed1)
    d_b1 = column_sum(grad_hidden)
    grad_resid1 = normalize_back(normed1, inv1, g1 * grad_hidden)
    grad_att = grad_resid1.astype(BF16)
    d_wo = dot(ctx, grad_att, 0, 0).astype(BF16)
    d_bo = column_sum(grad_att)
    grad_ctx = dot(grad_att, merge_mat, 1, 1).astype(BF16)
    if direct:
        wide = jnp.concatenate(
            [item.reshape(-1, feats) for item in (d_bo, d_g1, d_b1, d_c2, d_g2, d_b2, d_c1)]
        )
        wide = jnp.pad(wide, ((0, 16 - wide.shape[0]), (0, 0))).astype(BF16)
        outer = [
            item.reshape(dp_size, item.shape[0] // dp_size, item.shape[1])
            for item in (d_w2, d_w1, d_wo)
        ]
        *sums, vec_sum, token_grad = backward_all(
            seq_size, seq_count, query, key, value, ctx, grad_ctx, probs, wide, inputs, qkv_full,
            grad_resid1, outer,
        )
        sum_w2, sum_w1, s_wo, s_wq, s_wk, s_wv = [item.astype(F32) for item in sums]
        vec_sum = vec_sum.astype(F32)

        def own_part(first, length):
            rows = vec_sum[first : first + -(-length * dp_size // feats)].reshape(-1)
            return lax.dynamic_slice(rows, (dp_index * length,), (length,))

        s_bo, s_g1, s_b1, s_c2, s_g2, s_b2 = [own_part(k, shard_rows) for k in range(6)]
        s_c1 = own_part(6, c1.shape[1] // dp_size)
        s_bq, s_bv = own_part(16, shard_rows), own_part(17, shard_rows)
    else:
        grad_qkv = attend_back(query, key, value, ctx, grad_ctx, probs)
        token_rows = grad_resid1
        d_qkv = []
        for which in range(3):
            mat = qkv_mat[:, which * feats : (which + 1) * feats]
            token_rows = token_rows + dot(grad_qkv[which], mat, 1, 1)
            d_qkv.append(dot(inputs, grad_qkv[which], 0, 0).astype(BF16))
        d_bq = column_sum(grad_qkv[0])
        d_bv = column_sum(grad_qkv[2])
        token_grad = from_owners(token_rows.astype(BF16))
        vec_grads = (d_bq, d_bv, d_bo, d_g1, d_b1, d_c1, d_c2, d_g2, d_b2)
        vec_pack = jnp.concatenate([item.reshape(dp_size, -1) for item in vec_grads], axis=1)
        vec_cols = -(-vec_len // (shard_rows * LANES)) * LANES
        vec_pack = jnp.pad(vec_pack, ((0, 0), (0, shard_rows * vec_cols - vec_len)))
        vec_pack = vec_pack.reshape(feats, vec_cols).astype(BF16)

        def reduce(full):
            own = lax.psum_scatter(full, "dp", scatter_dimension=0, tiled=True)
            return lax.psum(own, "seq").astype(F32)

        sum_w2 = reduce(d_w2)
        sum_w1 = reduce(d_w1)
        sum_rest = reduce(jnp.concatenate([d_wo] + d_qkv + [vec_pack], axis=1))
        s_wo, s_wq, s_wk, s_wv = [sum_rest[:, i * feats : (i + 1) * feats] for i in range(4)]
        flat = sum_rest[:, 4 * feats :].reshape(-1)
        out_vecs = []
        start = 0
        for size in vec_sizes:
            out_vecs.append(flat[start : start + size])
            start += size
        s_bq, s_bv, s_bo, s_g1, s_b1, s_c1, s_c2, s_g2, s_b2 = out_vecs
    return (
        output,
        token_grad,
        s_wq,
        s_bq,
        s_wk,
        s_wv,
        s_bv,
        s_wo,
        s_bo,
        s_g1,
        s_b1,
        sum_w1,
        s_c1,
        sum_w2,
        s_c2,
        s_g2,
        s_b2,
    )


def solution(mesh):
    rows, mat, vec = P("dp", "seq", None), P("dp", None), P("dp")
    params = (mat, vec, mat, mat, vec, mat, vec, vec, vec, mat, vec, mat, vec, vec, vec)
    return jax.shard_map(
        functools.partial(per_device, (mesh.shape["dp"], mesh.shape["seq"])),
        mesh=mesh,
        in_specs=(rows, vec) + params + (rows,),
        out_specs=(rows, rows) + params,
        check_vma=False,
    )
```

```python
import functools

import jax
import jax.numpy as jnp
from jax import lax
from jax.experimental import pallas as pl
from jax.experimental.pallas import tpu as pltpu
from jax.sharding import PartitionSpec as P

HEAD = 64
LANES = 128
EPS = 1e-12
NEG_FILL = -1000000000.0
SCALE2 = 0.125 * 1.4426950408889634
F32 = jnp.float32
BF16 = jnp.bfloat16
VMEM_LIMIT = 60 * 1024 * 1024
VMEM_MAX = 67043328


def dot(left, right, left_dim, right_dim):
    return lax.dot_general(
        left, right, (((left_dim,), (right_dim,)), ((), ())), preferred_element_type=F32
    )


def attend_kernel(bias_ref, q_ref, k_ref, v_ref, ctx_ref, probs_ref, *, rows_blk):
    seq_len = q_ref.shape[0]
    lane = lax.broadcasted_iota(jnp.int32, (1, LANES), 1)
    bias = bias_ref[...]
    for blk in range(seq_len // rows_blk):
        rows = pl.ds(blk * rows_blk, rows_blk)
        query = q_ref[rows, :]
        mixed = []
        for head in range(2):
            mine = (lane < HEAD) if head == 0 else (lane >= HEAD)
            query_h = jnp.where(mine, query, jnp.zeros_like(query))
            score = dot(query_h, k_ref[...], 1, 1) + bias
            top = jnp.max(score, axis=1, keepdims=True)
            expo = jnp.exp2((score - top) * SCALE2)
            total = jnp.sum(expo, axis=1, keepdims=True)
            probs = (expo * (1.0 / total)).astype(BF16)
            probs_ref[head, rows, :] = probs
            mixed.append(dot(probs, v_ref[...], 1, 0))
        ctx_ref[rows, :] = jnp.where(lane < HEAD, mixed[0], mixed[1]).astype(BF16)


def attend(bias, query, key, value):
    seq_len, feats = query.shape
    cols = pl.BlockSpec((seq_len, LANES), lambda g: (0, g))
    return pl.pallas_call(
        functools.partial(attend_kernel, rows_blk=min(512, seq_len)),
        grid=(feats // LANES,),
        in_specs=[pl.BlockSpec((1, seq_len), lambda g: (0, 0)), cols, cols, cols],
        out_specs=[cols, pl.BlockSpec((2, seq_len, seq_len), lambda g: (g, 0, 0))],
        out_shape=[
            jax.ShapeDtypeStruct((seq_len, feats), BF16),
            jax.ShapeDtypeStruct((feats // HEAD, seq_len, seq_len), BF16),
        ],
        compiler_params=pltpu.CompilerParams(vmem_limit_bytes=VMEM_LIMIT),
    )(bias, query, key, value)


def attend_back_pair(
    q_ref, k_ref, v_ref, ctx_ref, grad_ref, probs_ref, store, key_acc, value_acc, rows_blk
):
    seq_len = q_ref.shape[0]
    lane = lax.broadcasted_iota(jnp.int32, (1, LANES), 1)
    for blk in range(seq_len // rows_blk):
        rows = pl.ds(blk * rows_blk, rows_blk)
        query = q_ref[rows, :]
        grad = grad_ref[rows, :]
        overlap = ctx_ref[rows, :].astype(F32) * grad.astype(F32)
        query_t = query.T
        grad_t = grad.T
        grad_query = []
        for head in range(2):
            mine = (lane < HEAD) if head == 0 else (lane >= HEAD)
            part = slice(head * HEAD, (head + 1) * HEAD)
            grad_h = jnp.where(mine, grad, jnp.zeros_like(grad))
            inner = jnp.sum(jnp.where(mine, overlap, 0.0), axis=1, keepdims=True)
            probs = probs_ref[head, rows, :]
            grad_probs = dot(grad_h, v_ref[...], 1, 1)
            grad_score = (probs.astype(F32) * (grad_probs - inner)).astype(BF16)
            grad_query.append(dot(grad_score, k_ref[...], 1, 0))
            grad_key = dot(query_t[part], grad_score, 1, 0)
            grad_value = dot(grad_t[part], probs, 1, 0)
            if blk == 0:
                key_acc[head] = grad_key
                value_acc[head] = grad_value
            else:
                key_acc[head] += grad_key
                value_acc[head] += grad_value
        mixed = jnp.where(lane < HEAD, grad_query[0], grad_query[1])
        store(0, rows, (0.125 * mixed).astype(BF16))
    everything = pl.ds(0, seq_len)
    grad_key = jnp.concatenate([key_acc[0], key_acc[1]], axis=0)
    store(1, everything, (0.125 * grad_key).T.astype(BF16))
    grad_value = jnp.concatenate([value_acc[0], value_acc[1]], axis=0)
    store(2, everything, grad_value.T.astype(BF16))


def attend_back_kernel(
    q_ref, k_ref, v_ref, ctx_ref, grad_ref, probs_ref, out_ref, key_acc, value_acc, *, rows_blk
):
    def store(which, rows, values):
        out_ref[which, rows, :] = values

    attend_back_pair(
        q_ref, k_ref, v_ref, ctx_ref, grad_ref, probs_ref, store, key_acc, value_acc, rows_blk
    )


def attend_back(query, key, value, ctx, grad_ctx, probs):
    seq_len, feats = ctx.shape
    cols = pl.BlockSpec((seq_len, LANES), lambda g: (0, g))
    return pl.pallas_call(
        functools.partial(attend_back_kernel, rows_blk=min(512, seq_len)),
        grid=(feats // LANES,),
        in_specs=[cols] * 5 + [pl.BlockSpec((2, seq_len, seq_len), lambda g: (g, 0, 0))],
        out_specs=pl.BlockSpec((3, seq_len, LANES), lambda g: (0, 0, g)),
        out_shape=jax.ShapeDtypeStruct((3, seq_len, feats), BF16),
        scratch_shapes=[pltpu.VMEM((2, HEAD, seq_len), F32)] * 2,
        compiler_params=pltpu.CompilerParams(vmem_limit_bytes=VMEM_LIMIT),
    )(query, key, value, ctx, grad_ctx, probs)


MESH = pl.DeviceIdType.MESH


def remote(src, dst, send, recv, device):
    return pltpu.make_async_remote_copy(
        src_ref=src, dst_ref=dst, send_sem=send, recv_sem=recv,
        device_id=device, device_id_type=MESH,
    )


class Place:
    def __init__(self, seq_size, seq_count):
        self.me = me = lax.axis_index("dp")
        self.here = here = lax.axis_index("seq")
        core, x_at, y_at = me % 2, (me // 2) % 2, (me // 4) % 2
        self.to_core, self.to_x, self.to_y = 1 - 2 * core, 2 - 4 * x_at, 4 - 8 * y_at
        self.core_dev = (me + self.to_core, here)
        self.x_dev = (me + self.to_x, here)
        self.y_dev = (me + self.to_y, here)
        self.shift = (seq_size - seq_count) * core
        self.my_seq = here - self.shift
        self.is_owner = (self.my_seq >= 0) & (self.my_seq < seq_count)
        self.seq_size, self.seq_count = seq_size, seq_count

    def barrier(self):
        barrier = pltpu.get_barrier_semaphore()
        for device in (self.core_dev, self.x_dev, self.y_dev):
            pl.semaphore_signal(barrier, inc=1, device_id=device, device_id_type=MESH)
        for step in range(1, self.seq_size):
            pl.semaphore_signal(
                barrier, inc=1, device_id=(self.me, (self.here + step) % self.seq_size),
                device_id_type=MESH,
            )
        pl.semaphore_wait(barrier, 3 + self.seq_size - 1)


class Gather:
    def __init__(self, place, full, own, sems, index):
        self.place, self.full, self.own, self.index = place, full, own, index
        self.send_sem, self.recv_sem, self.core_send, self.core_recv = sems

    def half(self, which):
        count = self.full.shape[1] // 2
        return pl.ds(which * count, count)

    def piece(self, p):
        at = self.place
        rows = self.half(p % 2)
        shard = at.me + (0, 0, 0, 0, at.to_x, at.to_y)[p]
        src = self.own.at[rows] if p < 4 else self.full.at[shard, rows]
        device = (at.x_dev, at.y_dev, at.y_dev, at.x_dev, at.y_dev, at.x_dev)[p]
        return remote(
            src, self.full.at[shard, rows],
            self.send_sem.at[self.index, p], self.recv_sem.at[self.index, p], device,
        )

    def core_piece(self, p):
        at = self.place
        if p == 6:
            src, dst = self.own, self.full.at[at.me]
        else:
            across = at.to_x + at.to_y
            shard = at.me + (at.to_x, at.to_y, at.to_y, at.to_x, across, across)[p]
            src = dst = self.full.at[shard, self.half(p % 2)]
        return remote(
            src, dst, self.core_send.at[self.index, p], self.core_recv.at[self.index, p],
            at.core_dev,
        )

    def start(self, *pieces):
        for p in pieces:
            self.piece(p).start()

    def arrive(self, *pieces):
        for p in pieces:
            self.piece(p).wait_recv()

    def to_core(self, *pieces):
        for p in pieces:
            self.core_piece(p).start()

    def finish(self, pieces, core_pieces):
        for p in core_pieces:
            self.core_piece(p).wait_recv()
        for p in pieces:
            self.piece(p).wait_send()
        for p in core_pieces:
            self.core_piece(p).wait_send()


class RowsIn:
    def __init__(self, place, blocks, whole, buf, sems):
        self.place, self.blocks, self.whole, self.buf = place, blocks, whole, buf
        self.send_sem, self.recv_sem, self.local_sem = sems
        self.rows = blocks.shape[1]

    def to(self, seq, source):
        at = self.place
        return remote(
            self.blocks.at[seq], self.whole.at[pl.ds(source * self.rows, self.rows)],
            self.send_sem.at[seq], self.recv_sem.at[source], (at.me, seq + at.shift),
        )

    def own(self, count):
        at = self.place

        def out(pos, k):
            return pltpu.make_async_copy(
                self.buf, self.whole.at[pl.ds(pos * self.rows, self.rows)], self.local_sem.at[k]
            )

        @pl.when(at.is_owner)
        def _():
            load = pltpu.make_async_copy(self.blocks.at[at.my_seq], self.buf, self.local_sem.at[0])
            load.start()
            load.wait()
            out(at.here, 1).start()
            out(at.here, 1).wait()

        @pl.when(jnp.logical_not(at.is_owner))
        def _():
            self.buf[...] = jnp.zeros_like(self.buf)
            for pos in range(at.seq_size):
                out(pos, pos).start()
            for pos in range(at.seq_size):
                out(pos, pos).wait()

    def start(self):
        at = self.place
        for seq in range(at.seq_count):

            @pl.when(at.here != seq + at.shift)
            def _():
                self.to(seq, at.here).start()

    def finish(self):
        at = self.place

        @pl.when(at.is_owner)
        def _():
            for pos in range(at.seq_size):

                @pl.when(at.here != pos)
                def _():
                    remote(
                        self.blocks.at[0], self.whole.at[pl.ds(pos * self.rows, self.rows)],
                        self.send_sem.at[0], self.recv_sem.at[pos],
                        (at.me, (at.here + 1) % at.seq_size),
                    ).wait_recv()

        for seq in range(at.seq_count):

            @pl.when(at.here != seq + at.shift)
            def _():
                self.to(seq, at.here).wait_send()


def start_kernel(
    seq_size, seq_count, tokens, wq, wk, wv, vecs, w2, w1, wo,
    rows_out, qkv_full, vec_full, w2_full, w1_full, wo_full,
    qkv_low, w2_low, w1_low, wo_low, row_buf,
    row_send, row_recv, row_local, sem_a, sem_b, sem_c, sem_d, own_sem,
):
    place = Place(seq_size, seq_count)
    sems = (sem_a, sem_b, sem_c, sem_d)
    rows = RowsIn(place, tokens, rows_out, row_buf, (row_send, row_recv, row_local))
    first = [
        Gather(place, qkv_full, qkv_low, sems, 0),
        Gather(place, vec_full, vecs, sems, 1),
    ]
    later = [
        Gather(place, w2_full, w2_low, sems, 2),
        Gather(place, w1_full, w1_low, sems, 3),
        Gather(place, wo_full, wo_low, sems, 4),
    ]
    place.barrier()
    rows.start()
    feats = wq.shape[1]
    for k, item in enumerate((wq, wk, wv)):
        qkv_low[:, k * feats : (k + 1) * feats] = item[...].astype(BF16)
    for item in first:
        item.start(0, 1)
    for item in first:
        item.start(2, 3)
        item.to_core(6)
    w2_low[...] = w2[...].astype(BF16)
    w1_low[...] = w1[...].astype(BF16)
    wo_low[...] = wo[...].astype(BF16)
    keep = [
        pltpu.make_async_copy(item.own, item.full.at[place.me], own_sem.at[item.index])
        for item in first + later
    ]
    for copy in keep:
        copy.start()
    for item in first:
        item.arrive(0, 1)
        item.start(4, 5)
        item.to_core(0, 1)
    for item in later:
        item.start(0, 1)
    rows.own(seq_size)
    for item in first:
        item.arrive(2, 3)
        item.to_core(2, 3)
    for item in first:
        item.arrive(4, 5)
        item.to_core(4, 5)
    for item in first:
        item.finish(range(6), range(7))
    for item in later:
        item.arrive(0, 1)
        for p in (0, 1):
            item.piece(p).wait_send()
    for copy in keep:
        copy.wait()
    rows.finish()


def start_all(seq_size, tokens, qkv_parts, vecs, w2, w1, wo):
    seq_count, blk, feats = tokens.shape
    any_spec = pl.BlockSpec(memory_space=pl.ANY)
    vmem_spec = pl.BlockSpec(memory_space=pltpu.VMEM)
    dma = pltpu.SemaphoreType.DMA
    shard = qkv_parts[0].shape[0]

    def full(rows, cols):
        return jax.ShapeDtypeStruct((8, rows, cols), BF16)

    return pl.pallas_call(
        functools.partial(start_kernel, seq_size, seq_count),
        in_specs=[any_spec] + [vmem_spec] * 7,
        out_specs=[any_spec] * 6,
        out_shape=[
            jax.ShapeDtypeStruct((seq_size * blk, feats), BF16),
            full(shard, 3 * feats), full(*vecs.shape), full(*w2.shape), full(*w1.shape),
            full(*wo.shape),
        ],
        scratch_shapes=[
            pltpu.VMEM((shard, 3 * feats), BF16), pltpu.VMEM(w2.shape, BF16),
            pltpu.VMEM(w1.shape, BF16), pltpu.VMEM(wo.shape, BF16), pltpu.VMEM((blk, feats), BF16),
            dma((seq_count,)), dma((seq_size,)), dma((seq_size,)),
            dma((5, 6)), dma((5, 6)), dma((5, 7)), dma((5, 7)), dma((5,)),
        ],
        compiler_params=pltpu.CompilerParams(
            collective_id=2, has_side_effects=True, vmem_limit_bytes=VMEM_LIMIT
        ),
    )(tokens, *qkv_parts, vecs, w2, w1, wo)


def forward_kernel(
    seq_size, seq_count, rows_blk,
    bias_ref, x_ref, wq_ref, wk_ref, wv_ref, bq_ref, bv_ref, upstream, w2_in, w1_in, wo_in,
    q_ref, k_ref, v_ref, ctx_ref, probs_ref, dy_out, w2_full, w1_full, wo_full,
    row_buf, row_send, row_recv, row_local, sem_a, sem_b, sem_c, sem_d,
):
    step = pl.program_id(0)
    last = pl.num_programs(0) - 1
    place = Place(seq_size, seq_count)
    sems = (sem_a, sem_b, sem_c, sem_d)
    rows = RowsIn(place, upstream, dy_out, row_buf, (row_send, row_recv, row_local))
    later = [
        Gather(place, full, full.at[place.me], sems, k)
        for k, full in enumerate((w2_full, w1_full, wo_full))
    ]

    @pl.when(step == 0)
    def _():
        place.barrier()
        for item in later:
            item.start(2, 3)
        for item in later:
            item.start(4, 5)
        rows.start()
        for item in later:
            item.to_core(6, 0, 1)
        rows.own(seq_size)

    x_rows = x_ref[...]
    depth = x_rows.shape[1]
    mats = [ref[...].reshape(depth, LANES) for ref in (wq_ref, wk_ref, wv_ref)]
    both = dot(x_rows, jnp.concatenate(mats, axis=1), 1, 0)
    q_ref[...] = (both[:, :LANES] + bq_ref[...]).astype(BF16)
    k_ref[...] = both[:, LANES : 2 * LANES].astype(BF16)
    v_ref[...] = (both[:, 2 * LANES :] + bv_ref[...]).astype(BF16)
    attend_kernel(bias_ref, q_ref, k_ref, v_ref, ctx_ref, probs_ref, rows_blk=rows_blk)

    @pl.when(step == last - 1)
    def _():
        for item in later:
            item.arrive(2, 3)
            item.to_core(2, 3)

    @pl.when(step == last)
    def _():
        for item in later:
            item.arrive(4, 5)
            item.to_core(4, 5)
        for item in later:
            item.finish(range(2, 6), range(7))
        rows.finish()


def forward_all(seq_size, bias, rows, qkv_full, bq, bv, upstream, w2_full, w1_full, wo_full):
    seq_len, feats = rows.shape
    seq_count, blk, _ = upstream.shape
    pairs = feats // LANES
    shard = qkv_full.shape[1]
    any_spec = pl.BlockSpec(memory_space=pl.ANY)
    dma = pltpu.SemaphoreType.DMA
    cols = pl.BlockSpec((seq_len, LANES), lambda g: (0, g))

    def mat(which):
        return pl.BlockSpec((8, shard, LANES), lambda g, w=which: (0, 0, w * pairs + g))

    vec = pl.BlockSpec((1, LANES), lambda g: (0, g))
    fulls = [w2_full, w1_full, wo_full]
    flat = jax.ShapeDtypeStruct((seq_len, feats), BF16)
    return pl.pallas_call(
        functools.partial(forward_kernel, seq_size, seq_count, min(512, seq_len)),
        grid=(pairs,),
        in_specs=[
            pl.BlockSpec((1, seq_len), lambda g: (0, 0)),
            pl.BlockSpec((seq_len, feats), lambda g: (0, 0)),
            mat(0), mat(1), mat(2), vec, vec,
        ]
        + [any_spec] * 4,
        out_specs=[cols] * 4
        + [pl.BlockSpec((2, seq_len, seq_len), lambda g: (g, 0, 0))]
        + [any_spec] * 4,
        out_shape=[flat] * 4
        + [jax.ShapeDtypeStruct((feats // HEAD, seq_len, seq_len), BF16), flat]
        + [jax.ShapeDtypeStruct(item.shape, BF16) for item in fulls],
        scratch_shapes=[
            pltpu.VMEM((blk, feats), BF16),
            dma((seq_count,)), dma((seq_size,)), dma((seq_size,)),
            dma((3, 6)), dma((3, 6)), dma((3, 7)), dma((3, 7)),
        ],
        input_output_aliases={8: 6, 9: 7, 10: 8},
        compiler_params=pltpu.CompilerParams(
            collective_id=3, has_side_effects=True, vmem_limit_bytes=VMEM_LIMIT
        ),
    )(bias, rows, qkv_full, qkv_full, qkv_full, bq, bv, upstream, *fulls)


class Reduce:
    def __init__(self, place, source, total, bufs, sems, index):
        self.place, self.source, self.total, self.index = place, source, total, index
        self.own, self.other, self.first_x, self.first_y, self.second, self.arrived = bufs
        (
            self.own_sem, self.core_send, self.core_recv, self.one_send, self.one_recv,
            self.two_send, self.two_recv, self.z_send, self.z_recv,
        ) = sems
        at = place
        self.apart = [(r % 2) * at.to_x + (r // 2) * at.to_y for r in range(4)]
        self.rows = self.own.shape[1]
        self.half = self.rows // 2

    def keep_copy(self, r):
        return pltpu.make_async_copy(
            self.source(self.place.me + self.apart[r]), self.own.at[r],
            self.own_sem.at[self.index, r],
        )

    def core_copy(self, r):
        at = self.place
        return remote(
            self.source(at.me + at.to_core + self.apart[r]), self.other.at[r],
            self.core_send.at[self.index, r], self.core_recv.at[self.index, r], at.core_dev,
        )

    def one_copy(self, way, k):
        half = self.half
        if way == 0:
            src, dst = self.own.at[(1, 3)[k], pl.ds(0, half)], self.first_x.at[k]
        else:
            src, dst = self.own.at[(2, 3)[k], pl.ds(half, half)], self.first_y.at[k]
        return remote(
            src, dst, self.one_send.at[self.index, way, k], self.one_recv.at[self.index, way, k],
            (self.place.x_dev, self.place.y_dev)[way],
        )

    def two_copy(self, way):
        src = self.own.at[(2, 1)[way], pl.ds(way * self.half, self.half)]
        return remote(
            src, self.second.at[way], self.two_send.at[self.index, way],
            self.two_recv.at[self.index, way], (self.place.y_dev, self.place.x_dev)[way],
        )

    def z_copy(self, way, src):
        at = self.place
        return remote(
            src, self.arrived.at[way], self.z_send.at[self.index, way],
            self.z_recv.at[self.index, way], (at.me, at.here + (1, -1)[way]),
        )

    def hops(self, way):
        at = self.place
        return at.here if way == 0 else at.seq_size - 1 - at.here

    def add(self, dest, first, *others, start=0, count=None):
        count = self.rows if count is None else count

        def body(i, carry):
            to = pl.ds(pl.multiple_of(start + i * 16, 16), 16)
            frm = pl.ds(pl.multiple_of(i * 16, 16), 16)
            if len(others) == 1:
                dest[to, :] = first[to, :] + others[0][frm, :]
            else:
                value = first[to, :].astype(F32)
                for other in others:
                    value = value + other[frm, :].astype(F32)
                dest[to, :] = value.astype(dest.dtype)
            return carry

        lax.fori_loop(0, count // 16, body, 0, unroll=True)

    def begin(self):
        for r in (3, 1, 2, 0):
            self.core_copy(r).start()
            self.keep_copy(r).start()

    def core_stage(self):
        for r in (3, 1, 2, 0):
            self.keep_copy(r).wait()
            self.core_copy(r).wait_recv()
            self.add(self.own.at[r], self.own.at[r], self.other.at[r])
            if r == 3:
                self.one_copy(0, 1).start()
                self.one_copy(1, 1).start()
            elif r == 1:
                self.one_copy(0, 0).start()
            elif r == 2:
                self.one_copy(1, 0).start()

    def one_stage(self):
        firsts = (self.first_x, self.first_y)
        for k in (1, 0):
            for way in range(2):
                self.one_copy(way, k).wait_recv()
                dest = self.own.at[(2, 1)[way] if k else 0]
                self.add(dest, dest, firsts[way].at[k], start=way * self.half, count=self.half)
                if k:
                    self.two_copy(way).start()

    def two_stage(self):
        mine = self.own.at[0]
        for way in range(2):
            self.two_copy(way).wait_recv()
            self.add(mine, mine, self.second.at[way], start=way * self.half, count=self.half)
        self.z_hop(0)

    def z_hop(self, hop):
        mine = self.own.at[0]
        for way in range(2):
            passed = self.other.at[way]

            @pl.when(self.hops(way) == hop)
            def _():
                if hop == 0:
                    self.z_copy(way, mine).start()
                else:
                    self.z_copy(way, passed).wait_recv()
                    if hop < self.place.seq_size - 1:
                        self.add(passed, mine, self.arrived.at[way])
                        self.z_copy(way, passed).start()

    def finish(self):
        total = self.own.at[3]
        last = self.place.seq_size - 1
        mine = self.own.at[0]
        up, down = self.arrived.at[0], self.arrived.at[1]
        here = self.place.here
        self.one_copy(0, 1).wait_send()
        self.one_copy(1, 1).wait_send()

        @pl.when(here == 0)
        def _():
            self.add(total, mine, down)

        @pl.when(here == last)
        def _():
            self.add(total, mine, up)

        @pl.when((here > 0) & (here < last))
        def _():
            self.add(total, mine, up, down)

        self.total_copy().start()

    def total_copy(self):
        return pltpu.make_async_copy(
            self.own.at[3], self.total, self.own_sem.at[self.index, 3]
        )

    def drain(self):
        for r in range(4):
            self.core_copy(r).wait_send()
        for way in range(2):
            self.one_copy(way, 0).wait_send()
            self.two_copy(way).wait_send()

            @pl.when(self.hops(way) < self.place.seq_size - 1)
            def _():
                self.z_copy(way, self.own.at[0]).wait_send()

        self.total_copy().wait()

    @staticmethod
    def scratch(count, rows, width):
        return [
            pltpu.VMEM((count, lead, rows // split, width), BF16)
            for lead, split in ((4, 1), (4, 1), (2, 2), (2, 2), (2, 2), (2, 1))
        ]

    @staticmethod
    def semaphores(count):
        dma = pltpu.SemaphoreType.DMA
        return [
            dma((count, 4)), dma((count, 4)), dma((count, 4)),
            dma((count, 2, 2)), dma((count, 2, 2)), dma((count, 2)), dma((count, 2)),
            dma((count, 2)), dma((count, 2)),
        ]


class RowsOut:
    def __init__(self, place, rows, blocks, sems):
        self.place, self.rows, self.blocks = place, rows, blocks
        self.send_sem, self.recv_sem, self.local_sem = sems
        self.blk = blocks.shape[1]

    def part(self, pos):
        return self.rows.at[pl.ds(pos * self.blk, self.blk)]

    def copy(self, pos):
        at = self.place
        return remote(
            self.part(pos), self.blocks.at[at.my_seq], self.send_sem.at[pos],
            self.recv_sem.at[at.my_seq], (at.me, pos),
        )

    def keep(self, pos):
        return pltpu.make_async_copy(
            self.part(pos), self.blocks.at[self.place.my_seq], self.local_sem.at[0]
        )

    def start(self, pos):
        at = self.place

        @pl.when(at.is_owner & (at.here != pos))
        def _():
            self.copy(pos).start()

        @pl.when(at.is_owner & (at.here == pos))
        def _():
            self.keep(pos).start()

    def finish(self):
        at = self.place
        for seq in range(at.seq_count):

            @pl.when(at.here != seq + at.shift)
            def _():
                remote(
                    self.part(0), self.blocks.at[seq], self.send_sem.at[0], self.recv_sem.at[seq],
                    (at.me, (at.here + 1) % at.seq_size),
                ).wait_recv()

        @pl.when(at.is_owner)
        def _():
            self.keep(0).wait()
            for pos in range(at.seq_size):

                @pl.when(at.here != pos)
                def _():
                    self.copy(pos).wait_send()


INV_SQRT2 = 0.7071067811865476
INV_SQRT_2PI = 0.3989422804014327
BQ, BV, BO, G1, B1, C2, G2, B2, C1 = range(9)


def normalize(resid):
    centre = resid - jnp.mean(resid, axis=-1, keepdims=True)
    inv = lax.rsqrt(jnp.mean(centre * centre, axis=-1, keepdims=True) + EPS)
    return centre * inv, inv


def normalize_back(normed, inv, grad_normed):
    mean_grad = jnp.mean(grad_normed, axis=-1, keepdims=True)
    mean_both = jnp.mean(grad_normed * normed, axis=-1, keepdims=True)
    return inv * (grad_normed - mean_grad - normed * mean_both)


def gelu_parts(pre):
    cumulative = 0.5 * (1.0 + lax.erf(pre * INV_SQRT2))
    slope = cumulative + pre * (INV_SQRT_2PI * jnp.exp(-0.5 * pre * pre))
    return pre * cumulative, slope


def feed_kernel(
    rows_blk, ctx_ref, x_ref, wo_ref, vec_ref, w1_ref, w2_ref, dy_ref,
    act_ref, slope_ref, out_ref, resid_ref, normed_ref, inv_ref, vec_out,
    hidden_low,
):
    step = pl.program_id(0)
    seq_len, feats = x_ref.shape
    width = act_ref.shape[1]
    blocks = [pl.ds(i * rows_blk, rows_blk) for i in range(seq_len // rows_blk)]

    def vec(k):
        return vec_ref[k : k + 1, :]

    @pl.when(step == 0)
    def _():
        merge = wo_ref[...].reshape(feats, feats)
        for rows in blocks:
            resid = x_ref[rows, :].astype(F32) + (dot(ctx_ref[rows, :], merge, 1, 0) + vec(BO))
            normed, inv = normalize(resid)
            normed_ref[rows, :] = normed
            inv_ref[rows, :] = jnp.broadcast_to(inv, (rows_blk, LANES))
            hidden_low[rows, :] = (normed * vec(G1) + vec(B1)).astype(BF16)

    expand = w1_ref[...].reshape(feats, width)
    shrink = w2_ref[...].reshape(width, feats)
    shift = vec_ref[pl.ds(C1 + step, 1), :]
    for rows in blocks:
        act, slope = gelu_parts(dot(hidden_low[rows, :], expand, 1, 0) + shift)
        act_low = act.astype(BF16)
        act_ref[rows, :] = act_low
        slope_ref[rows, :] = slope.astype(BF16)
        part = dot(act_low, shrink, 1, 0)

        @pl.when(step == 0)
        def _():
            resid_ref[rows, :] = part

        @pl.when(step > 0)
        def _():
            resid_ref[rows, :] += part

    @pl.when(step == pl.num_programs(0) - 1)
    def _():
        sums = [jnp.zeros((1, feats), F32)] * 3
        for rows in blocks:
            hidden = normed_ref[rows, :] * vec(G1) + vec(B1)
            normed, inv = normalize(hidden + (resid_ref[rows, :] + vec(C2)))
            out_ref[rows, :] = (normed * vec(G2) + vec(B2)).astype(BF16)
            dy = dy_ref[rows, :].astype(F32)
            grad = normalize_back(normed, inv, vec(G2) * dy)
            resid_ref[rows, :] = grad
            terms = (dy * normed, dy, grad.astype(BF16).astype(F32))
            sums = [
                total + jnp.sum(term, axis=0, keepdims=True) for total, term in zip(sums, terms)
            ]
        for k, total in enumerate(sums):
            vec_out[k : k + 1, :] = total


def feed_forward(ctx, inputs, wo_full, vecs, w1_full, w2_full, dy):
    seq_len, feats = inputs.shape
    shard = w1_full.shape[1]
    hidden = w1_full.shape[2]
    steps = hidden // feats
    once = pl.Buffered(1)

    def whole(shape, mode=None):
        return pl.BlockSpec(shape, lambda j: (0,) * len(shape), pipeline_mode=mode)

    rows, rows_f32 = (seq_len, feats), jax.ShapeDtypeStruct((seq_len, feats), F32)
    cols = pl.BlockSpec(rows, lambda j: (0, j))
    wide = jax.ShapeDtypeStruct((seq_len, hidden), BF16)
    return pl.pallas_call(
        functools.partial(feed_kernel, min(256, seq_len)),
        grid=(steps,),
        in_specs=[
            whole(rows, once), whole(rows, once), whole(wo_full.shape, once),
            whole(vecs.shape, once),
            pl.BlockSpec((8, shard, feats), lambda j: (0, 0, j)),
            pl.BlockSpec((8 // steps, w2_full.shape[1], feats), lambda j: (j, 0, 0)),
            whole(rows, once),
        ],
        out_specs=[cols, cols, whole(rows), whole(rows), whole(rows), whole((seq_len, LANES)),
                   whole((8, feats))],
        out_shape=[
            wide, wide, jax.ShapeDtypeStruct(rows, BF16), rows_f32, rows_f32,
            jax.ShapeDtypeStruct((seq_len, LANES), F32), jax.ShapeDtypeStruct((8, feats), F32),
        ],
        scratch_shapes=[pltpu.VMEM(rows, BF16)],
        compiler_params=pltpu.CompilerParams(vmem_limit_bytes=VMEM_LIMIT),
    )(ctx, inputs, wo_full, vecs, w1_full, w2_full, dy)


def feed_back_kernel(seq_size, seq_count, rows_blk, *refs):
    refs = list(refs)

    def take(count):
        got = refs[:count]
        del refs[:count]
        return got

    act_ref, slope_ref, w1_ref, w2_ref, resid_ref, normed_ref, inv_ref, ctx_ref = take(8)
    wo_ref, vec_ref, vec_in, out_rows = take(4)
    d_w1, resid_out, grad_ctx, d_wo, vec_out, w2_total, out_blocks = take(7)
    grad_ffn, hidden_low, d_w2, vec_sums = take(4)
    count = 4
    bufs = take(6)
    sems = take(9)
    out_sems = take(3)

    step = pl.program_id(0)
    half_steps = pl.num_programs(0) // 2
    seq_len, feats = resid_ref.shape
    chunk = d_w2.shape[1] // count
    place = Place(seq_size, seq_count)
    outs = RowsOut(place, out_rows, out_blocks, out_sems)
    jobs = [
        Reduce(
            place, lambda shard, c=c: d_w2.at[shard, pl.ds(c * chunk, chunk)],
            w2_total.at[pl.ds(c * chunk, chunk)], [buf.at[c] for buf in bufs], sems, c,
        )
        for c in range(count)
    ]
    blocks = [pl.ds(i * rows_blk, rows_blk) for i in range(seq_len // rows_blk)]

    def vec(k):
        return vec_ref[k : k + 1, :]

    @pl.when(step == 0)
    def _():
        place.barrier()
        for pos in range(seq_size):
            outs.start(pos)
        for rows in blocks:
            grad_ffn[rows, :] = resid_ref[rows, :].astype(BF16)
            hidden_low[rows, :] = (normed_ref[rows, :] * vec(G1) + vec(B1)).astype(BF16)

    @pl.when(step < half_steps)
    def _():
        shards = 8 // half_steps
        part = dot(act_ref[...], grad_ffn[...], 0, 0).astype(BF16)
        d_w2[pl.ds(step * shards, shards)] = part.reshape(shards, d_w2.shape[1], feats)

    @pl.when(step == half_steps - 1)
    def _():
        for job in jobs:
            job.begin()

    @pl.when(step >= half_steps)
    def _():
        width = act_ref.shape[1]
        shrink = w2_ref[...].reshape(width, feats)
        expand = w1_ref[...].reshape(feats, width)
        ones = jnp.ones((8, rows_blk), BF16)
        total = jnp.zeros((8, width), F32)
        outer = jnp.zeros((feats, width), F32)
        for rows in blocks:
            grad_act = dot(grad_ffn[rows, :], shrink, 1, 1)
            grad_pre = (grad_act * slope_ref[rows, :].astype(F32)).astype(BF16)
            total = total + dot(ones, grad_pre, 1, 0)
            outer = outer + dot(hidden_low[rows, :], grad_pre, 0, 0)
            part = dot(grad_pre, expand, 1, 1)

            @pl.when(step == half_steps)
            def _():
                resid_out[rows, :] = resid_ref[rows, :] + part

            @pl.when(step > half_steps)
            def _():
                resid_out[rows, :] += part

        d_w1[0] = outer.astype(BF16).reshape(d_w1.shape[1:])
        vec_sums[pl.ds(step - half_steps, 1), :] = total[0:1, :]

    @pl.when(step == half_steps)
    def _():
        for job in jobs:
            job.core_stage()

    @pl.when(step == half_steps + 1)
    def _():
        jobs[0].one_stage()
        jobs[1].one_stage()

    @pl.when(step == half_steps + 2)
    def _():
        jobs[2].one_stage()
        jobs[3].one_stage()
        jobs[0].two_stage()

    @pl.when(step == pl.num_programs(0) - 1)
    def _():
        for job in jobs[1:]:
            job.two_stage()
        jobs[0].z_hop(1)
        merge = wo_ref[...].reshape(feats, feats)
        sums = [jnp.zeros((1, feats), F32)] * 3
        outer = jnp.zeros((feats, feats), F32)
        for rows in blocks:
            grad_hidden = resid_out[rows, :]
            normed = normed_ref[rows, :]
            grad = normalize_back(normed, inv_ref[rows, 0:1], vec(G1) * grad_hidden)
            resid_out[rows, :] = grad
            low = grad.astype(BF16)
            grad_ctx[rows, :] = dot(low, merge, 1, 1).astype(BF16)
            outer = outer + dot(ctx_ref[rows, :], low, 0, 0)
            terms = (grad_hidden * normed, grad_hidden, low.astype(F32))
            sums = [
                total + jnp.sum(term, axis=0, keepdims=True) for total, term in zip(sums, terms)
            ]
        d_wo[...] = outer.astype(BF16).reshape(d_wo.shape)
        jobs[1].z_hop(1)
        jobs[0].z_hop(2)
        row = lax.broadcasted_iota(jnp.int32, (16, 1), 0)
        lines = sums + [vec_in[k : k + 1, :] for k in range(3)]
        lines = lines + [vec_sums[k : k + 1, :] for k in range(4)]
        packed = jnp.zeros((16, feats), F32)
        for k, line in enumerate(lines):
            packed = jnp.where(row == k, line, packed)
        vec_out[...] = packed.astype(BF16)

        tail = [functools.partial(Reduce.z_hop, hop=hop) for hop in range(1, seq_size)]
        tail.append(Reduce.finish)
        plan = [(job, max(0, k - 1), tail[max(0, 2 - k) :]) for k, job in enumerate(jobs)]
        for time in range(max(wait + len(stages) for _, wait, stages in plan)):
            for job, wait, stages in plan:
                if 0 <= time - wait < len(stages):
                    stages[time - wait](job)
        for job in jobs:
            job.drain()
        outs.finish()


def feed_back(
    seq_size, seq_count, act, slope, w1_full, w2_full, resid, normed, inv, ctx, wo_full, vecs,
    vec_in, out_rows,
):
    seq_len, feats = ctx.shape
    shard, w2_rows = w1_full.shape[1], w2_full.shape[1]
    steps = act.shape[1] // feats
    blk = seq_len // seq_size
    once = pl.Buffered(1)
    any_spec = pl.BlockSpec(memory_space=pl.ANY)
    dma = pltpu.SemaphoreType.DMA

    def whole(shape, mode=None):
        return pl.BlockSpec(shape, lambda j: (0,) * len(shape), pipeline_mode=mode)

    def first(j):
        return jnp.minimum(j, steps - 1)

    def second(j):
        return jnp.maximum(j - steps, 0)

    rows = (seq_len, feats)
    return pl.pallas_call(
        functools.partial(feed_back_kernel, seq_size, seq_count, min(256, seq_len)),
        grid=(2 * steps,),
        in_specs=[
            pl.BlockSpec(rows, lambda j: (0, first(j))),
            pl.BlockSpec(rows, lambda j: (0, second(j))),
            pl.BlockSpec((8, shard, feats), lambda j: (0, 0, second(j))),
            pl.BlockSpec((8 // steps, w2_rows, feats), lambda j: (second(j), 0, 0)),
            whole(rows, once), whole(rows, once), whole(inv.shape, once), whole(rows, once),
            whole(wo_full.shape, once), whole(vecs.shape, once), whole(vec_in.shape, once),
            any_spec,
        ],
        out_specs=[
            pl.BlockSpec((1, 8, shard, feats), lambda j: (second(j), 0, 0, 0)),
            whole(rows), whole(rows), whole(wo_full.shape), whole((16, feats)),
            any_spec, any_spec,
        ],
        out_shape=[
            jax.ShapeDtypeStruct((steps, 8, shard, feats), BF16),
            jax.ShapeDtypeStruct(rows, F32), jax.ShapeDtypeStruct(rows, BF16),
            jax.ShapeDtypeStruct(wo_full.shape, BF16), jax.ShapeDtypeStruct((16, feats), BF16),
            jax.ShapeDtypeStruct((w2_rows, feats), BF16),
            jax.ShapeDtypeStruct((seq_count, blk, feats), BF16),
        ],
        scratch_shapes=[
            pltpu.VMEM(rows, BF16), pltpu.VMEM(rows, BF16), pltpu.VMEM((8, w2_rows, feats), BF16),
            pltpu.VMEM((8, feats), F32),
        ]
        + Reduce.scratch(4, w2_rows // 4, feats)
        + Reduce.semaphores(4)
        + [dma((seq_size,)), dma((seq_count,)), dma((1,))],
        compiler_params=pltpu.CompilerParams(
            collective_id=4, has_side_effects=True, vmem_limit_bytes=VMEM_MAX
        ),
    )(
        act, slope, w1_full, w2_full, resid, normed, inv, ctx, wo_full, vecs, vec_in, out_rows
    )


def backward_kernel(seq_size, seq_count, rows_blk, *refs):
    refs = list(refs)

    def take(count):
        got = refs[:count]
        del refs[:count]
        return got

    q_ref, k_ref, v_ref, ctx_ref, grad_ref, probs_ref, vec_ref = take(7)
    x_in, qkv_in, resid_in, d_w1, d_wo = take(5)
    w1_total, wo_total, wq_total, wk_total, wv_total, vec_total, token_out = take(7)
    key_acc, value_acc, grads_all, x_rows, qkv_mat, resid, token_rows = take(7)
    mats = take(3)
    (vec_src,) = take(1)
    w1_count = d_w1.shape[0]
    mat_count = w1_count + 4
    bufs = take(6)
    vec_bufs = take(6)
    sems = take(9)
    (load_sem,) = take(1)
    token_sems = take(3)

    step = pl.program_id(0)
    place = Place(seq_size, seq_count)
    seq_len, feats = x_rows.shape

    def outer_source(c):
        if c < w1_count:
            return lambda shard: d_w1.at[c, shard]
        if c == w1_count:
            return lambda shard: d_wo.at[shard]
        return lambda shard: mats[c - w1_count - 1].at[shard]

    outer_totals = [w1_total.at[:, pl.ds(c * feats, feats)] for c in range(w1_count)]
    outer_totals += [wo_total, wq_total, wk_total, wv_total]
    jobs = [
        Reduce(place, outer_source(c), outer_totals[c], [buf.at[c] for buf in bufs], sems, c)
        for c in range(mat_count)
    ]
    jobs.append(
        Reduce(
            place, lambda shard: vec_src.at[shard], vec_total, [buf.at[0] for buf in vec_bufs],
            sems, mat_count,
        )
    )
    ready = w1_count + 1
    blk = seq_len // seq_size
    loads = [
        pltpu.make_async_copy(src, dst, load_sem.at[k])
        for k, (src, dst) in enumerate(((x_in, x_rows), (qkv_in, qkv_mat), (resid_in, resid)))
    ]
    tokens = RowsOut(place, token_rows, token_out, token_sems)

    @pl.when(step == 0)
    def _():
        place.barrier()
        for job in jobs[:ready]:
            job.begin()
        for load in loads:
            load.start()
        jobs[0].core_stage()

    column = pl.multiple_of(step * LANES, LANES)

    def store(which, rows, values):
        grads_all[which, rows, pl.ds(column, LANES)] = values

    attend_back_pair(
        q_ref, k_ref, v_ref, ctx_ref, grad_ref, probs_ref, store, key_acc, value_acc, rows_blk
    )

    core, one, two = Reduce.core_stage, Reduce.one_stage, Reduce.two_stage
    hops = [functools.partial(Reduce.z_hop, hop=hop) for hop in range(1, seq_size)]
    tail = hops + [Reduce.finish]
    ticks = (
        ((core, 1), (core, 2)),
        ((one, 0), (core, 3), (core, 4)),
        ((one, 1), (one, 2)),
        ((two, 0), (one, 3)),
        ((two, 1), (two, 2), (one, 4), (hops[0], 0)),
    )
    for at_step, stages in enumerate(ticks):

        @pl.when(step == at_step)
        def _():
            for stage, chunk in stages:
                stage(jobs[chunk])

    @pl.when(step == pl.num_programs(0) - 1)
    def _():
        for load in loads:
            load.wait()
        for chunk in (3, 4):
            two(jobs[chunk])
        hops[0](jobs[1])
        hops[0](jobs[2])
        hops[1](jobs[0])
        after = (
            ((hops[0], 3), (hops[1], 1), (hops[2], 0)),
            ((hops[0], 4), (hops[1], 2), (hops[2], 1), (Reduce.finish, 0)),
            ((hops[1], 3), (hops[2], 2), (Reduce.finish, 1)),
            ((hops[1], 4), (hops[2], 3), (Reduce.finish, 2)),
        )
        for pos in range(seq_size):
            rows = pl.ds(pos * blk, blk)
            part = resid[rows, :]
            for which in range(3):
                mat = qkv_mat[:, :, which * feats : (which + 1) * feats].reshape(feats, feats)
                part = part + dot(grads_all[which, rows, :], mat, 1, 1)
            token_rows[rows, :] = part.astype(BF16)
            tokens.start(pos)
            for stage, chunk in after[pos]:
                stage(jobs[chunk])
        for which in range(3):
            outer_sum = dot(x_rows[...], grads_all[which], 0, 0).astype(BF16)
            mats[which][...] = outer_sum.reshape(mats[which].shape)
            jobs[ready + which].begin()
            if which:
                core(jobs[ready + which - 1])
        ones = jnp.ones((16, seq_len), BF16)
        grad_bq = dot(ones, grads_all[0], 1, 0)
        grad_bv = dot(ones, grads_all[2], 1, 0)
        row = lax.broadcasted_iota(jnp.int32, (16, 1), 0)
        biases = jnp.where(row == 0, grad_bq, grad_bv).astype(BF16)
        for shard in range(8):
            vec_src[shard, 0:16, :] = vec_ref[...]
            vec_src[shard, 16:32, :] = biases
        jobs[-1].begin()
        core(jobs[-2])
        core(jobs[-1])

        plan = [(jobs[3], 0, [Reduce.finish]), (jobs[4], 0, tail[2:])]
        for k, job in enumerate(jobs[ready:]):
            plan.append((job, k, [one, two] + tail))
        for time in range(max(wait + len(stages) for _, wait, stages in plan)):
            for job, wait, stages in plan:
                if 0 <= time - wait < len(stages):
                    stages[time - wait](job)
        for job in jobs:
            job.drain()
        tokens.finish()


def backward_all(
    seq_size, seq_count, query, key, value, ctx, grad_ctx, probs, vecs, inputs, qkv_full, resid,
    d_w1, d_wo,
):
    seq_len, feats = ctx.shape
    blk = seq_len // seq_size
    shard = qkv_full.shape[1]
    w1_count = d_w1.shape[0]
    count = w1_count + 4
    any_spec = pl.BlockSpec(memory_space=pl.ANY)
    cols = pl.BlockSpec((seq_len, LANES), lambda g: (0, g))
    dma = pltpu.SemaphoreType.DMA
    mat = jax.ShapeDtypeStruct((shard, feats), BF16)
    return pl.pallas_call(
        functools.partial(backward_kernel, seq_size, seq_count, min(512, seq_len)),
        grid=(feats // LANES,),
        in_specs=[cols] * 5
        + [
            pl.BlockSpec((2, seq_len, seq_len), lambda g: (g, 0, 0)),
            pl.BlockSpec(vecs.shape, lambda g: (0, 0)),
        ]
        + [any_spec] * 5,
        out_specs=[any_spec] * 7,
        out_shape=[jax.ShapeDtypeStruct((shard, w1_count * feats), BF16), mat, mat, mat, mat]
        + [
            jax.ShapeDtypeStruct((32, feats), BF16),
            jax.ShapeDtypeStruct((seq_count, blk, feats), BF16),
        ],
        scratch_shapes=[pltpu.VMEM((2, HEAD, seq_len), F32)] * 2
        + [
            pltpu.VMEM((3, seq_len, feats), BF16),
            pltpu.VMEM((seq_len, feats), BF16),
            pltpu.VMEM(qkv_full.shape, BF16),
            pltpu.VMEM((seq_len, feats), F32),
            pltpu.VMEM((seq_len, feats), BF16),
        ]
        + [pltpu.VMEM((8, shard, feats), BF16)] * 3
        + [pltpu.VMEM((8, 32, feats), BF16)]
        + Reduce.scratch(count, shard, feats)
        + Reduce.scratch(1, 32, feats)
        + Reduce.semaphores(count + 1)
        + [dma((3,)), dma((seq_size,)), dma((seq_count,)), dma((1,))],
        compiler_params=pltpu.CompilerParams(
            collective_id=1, has_side_effects=True, vmem_limit_bytes=VMEM_MAX
        ),
    )(query, key, value, ctx, grad_ctx, probs, vecs, inputs, qkv_full, resid, d_w1, d_wo)


def widen_kernel(*refs):
    count = len(refs) // 2
    for source, dest in zip(refs[:count], refs[count:]):
        dest[...] = source[...].astype(F32)


def widen(arrays):
    return pl.pallas_call(
        widen_kernel,
        out_shape=[jax.ShapeDtypeStruct(item.shape, F32) for item in arrays],
        compiler_params=pltpu.CompilerParams(vmem_limit_bytes=VMEM_LIMIT),
    )(*arrays)


def column_sum(rows):
    return jnp.sum(rows, axis=0, dtype=F32)


def per_device(mesh_shape, tokens, lengths, *rest):
    weights, upstream = rest[:15], rest[15]
    dp_size, seq_size = mesh_shape
    seq_count, row_count, feats = tokens.shape
    dp_index = lax.axis_index("dp")
    here = lax.axis_index("seq")
    spare = seq_size - seq_count

    def owner_shift(dp):
        return spare * (dp % 2)

    my_seq = jnp.clip(here - owner_shift(dp_index), 0, seq_count - 1)

    def owned_by(dp, pos):
        seq = pos - owner_shift(dp)
        return 0 <= seq < seq_count

    def shift_pairs(step, to_owner):
        pairs = []
        for dp in range(dp_size):
            for pos in range(seq_size):
                dest = (pos + step) % seq_size
                if owned_by(dp, dest if to_owner else pos):
                    pairs.append((dp * seq_size + pos, dp * seq_size + dest))
        return pairs

    def gather(piece):
        return lax.all_gather(piece, "dp", axis=0, tiled=True)

    def to_owners(blocks):
        pieces = []
        for step in range(seq_size):
            dest = (here + step) % seq_size
            seq = jnp.clip(dest - owner_shift(dp_index), 0, seq_count - 1)
            piece = lax.dynamic_index_in_dim(blocks, seq, 0, keepdims=False)
            if step == 0:
                owner = (here >= owner_shift(dp_index)) & (here < owner_shift(dp_index) + seq_count)
                piece = jnp.where(owner, piece, jnp.zeros_like(piece))
            else:
                piece = lax.ppermute(piece, ("dp", "seq"), shift_pairs(step, True))
            pieces.append(piece)
        order = (here - jnp.arange(seq_size)) % seq_size
        return jnp.take(jnp.stack(pieces), order, axis=0).reshape(-1, feats)

    def from_owners(rows):
        pieces = rows.reshape(seq_size, row_count, feats)
        arrived = []
        for step in range(seq_size):
            piece = lax.dynamic_index_in_dim(pieces, (here - step) % seq_size, 0, keepdims=False)
            if step:
                piece = lax.ppermute(piece, ("dp", "seq"), shift_pairs(seq_size - step, False))
            arrived.append(piece)
        stack = jnp.stack(arrived)
        order = (jnp.arange(seq_count) + owner_shift(dp_index) - here) % seq_size
        return jnp.take(stack, order, axis=0)

    wq, bq, wk, wv, bv, wo, bo, g1, b1, w1, c1, w2, c2, g2, b2 = weights
    shard_rows = feats // dp_size
    direct = dp_size == 8 and shard_rows % 32 == 0
    vec_parts = (bq, bv, bo, g1, b1, c2, g2, b2, c1)
    vec_sizes = [item.shape[0] for item in vec_parts]
    vec_len = sum(vec_sizes)
    vec_rows = -(-vec_len // (32 * LANES)) * 32
    packed = jnp.concatenate(vec_parts).astype(BF16)
    seq_len = seq_size * row_count
    position = lax.iota(jnp.int32, seq_len)
    valid_len = lax.dynamic_index_in_dim(lengths, my_seq, 0, keepdims=False)
    key_bias = jnp.where(position < valid_len, 0.0, 8.0 * NEG_FILL).astype(F32).reshape(1, seq_len)

    if direct:
        packed = jnp.pad(packed, (0, vec_rows * LANES - vec_len)).reshape(vec_rows, LANES)
        inputs, qkv_full, packed, w2_part, w1_part, wo_part = start_all(
            seq_size, tokens, (wq, wk, wv), packed, w2, w1, wo
        )
        packed = packed.reshape(dp_size, vec_rows * LANES)
        qkv_mat = qkv_full.reshape(feats, 3 * feats)
    else:
        qkv_mat = gather(jnp.concatenate([wq, wk, wv], axis=1).astype(BF16))
        packed = lax.all_gather(packed, "dp", axis=0, tiled=False)
        merge_mat, expand_mat, reduce_mat = [gather(item.astype(BF16)) for item in (wo, w1, w2)]
    vecs = []
    start = 0
    for size in vec_sizes:
        vecs.append(packed[:, start : start + size].reshape(1, -1).astype(F32))
        start += size
    bq, bv, bo, g1, b1, c2, g2, b2, c1 = vecs

    if direct:
        query, key, value, ctx, probs, dy, w2_full, w1_full, wo_full = forward_all(
            seq_size, key_bias, inputs, qkv_full, bq, bv, upstream, w2_part, w1_part, wo_part
        )
        vec_rows = jnp.concatenate([item.reshape(-1, feats) for item in vecs])
        vec_rows = jnp.pad(vec_rows, ((0, 16 - vec_rows.shape[0]), (0, 0)))
        act, slope, out_rows, grad_resid2, normed1, inv1, second_sums = feed_forward(
            ctx, inputs, wo_full, vec_rows, w1_full, w2_full, dy
        )
        d_w1, grad_resid1, grad_ctx, d_wo, vec_sums, sum_w2, output = feed_back(
            seq_size, seq_count, act, slope, w1_full, w2_full, grad_resid2, normed1, inv1, ctx,
            wo_full, vec_rows, second_sums, out_rows,
        )
        *sums, vec_sum, token_grad = backward_all(
            seq_size, seq_count, query, key, value, ctx, grad_ctx, probs, vec_sums, inputs,
            qkv_full, grad_resid1, d_w1, d_wo,
        )
        sum_w2, sum_w1, s_wo, s_wq, s_wk, s_wv, vec_sum = widen([sum_w2] + sums + [vec_sum])

        def own_part(first, length):
            rows = vec_sum[first : first + -(-length * dp_size // feats)].reshape(-1)
            return lax.dynamic_slice(rows, (dp_index * length,), (length,))

        s_g1, s_b1, s_bo, s_g2, s_b2, s_c2 = [own_part(k, shard_rows) for k in range(6)]
        s_c1 = own_part(6, c1.shape[1] // dp_size)
        s_bq, s_bv = own_part(16, shard_rows), own_part(17, shard_rows)
    else:
        inputs = to_owners(tokens)
        dy = to_owners(upstream).astype(F32)
        qkv = dot(inputs, qkv_mat, 1, 0)
        query = (qkv[:, :feats] + bq).astype(BF16)
        key = qkv[:, feats : 2 * feats].astype(BF16)
        value = (qkv[:, 2 * feats :] + bv).astype(BF16)
        ctx, probs = attend(key_bias, query, key, value)
        normed1, inv1 = normalize(inputs.astype(F32) + dot(ctx, merge_mat, 1, 0) + bo)
        hidden = normed1 * g1 + b1
        hidden_low = hidden.astype(BF16)
        pre = dot(hidden_low, expand_mat, 1, 0) + c1
        phi_cum = 0.5 * (1.0 + lax.erf(pre * INV_SQRT2))
        act = (pre * phi_cum).astype(BF16)
        slope = (phi_cum + pre * (INV_SQRT_2PI * jnp.exp(-0.5 * pre * pre))).astype(BF16)
        normed2, inv2 = normalize(hidden + dot(act, reduce_mat, 1, 0) + c2)
        result = (normed2 * g2 + b2).astype(BF16)
        output = from_owners(result)

        d_g2 = column_sum(dy * normed2)
        d_b2 = column_sum(dy)
        grad_resid2 = normalize_back(normed2, inv2, g2 * dy)
        grad_ffn = grad_resid2.astype(BF16)
        d_w2 = dot(act, grad_ffn, 0, 0).astype(BF16)
        d_c2 = column_sum(grad_ffn)
        grad_pre = (dot(grad_ffn, reduce_mat, 1, 1) * slope.astype(F32)).astype(BF16)
        d_w1 = dot(hidden_low, grad_pre, 0, 0).astype(BF16)
        d_c1 = column_sum(grad_pre)
        grad_hidden = grad_resid2 + dot(grad_pre, expand_mat, 1, 1)
        d_g1 = column_sum(grad_hidden * normed1)
        d_b1 = column_sum(grad_hidden)
        grad_resid1 = normalize_back(normed1, inv1, g1 * grad_hidden)
        grad_att = grad_resid1.astype(BF16)
        d_wo = dot(ctx, grad_att, 0, 0).astype(BF16)
        d_bo = column_sum(grad_att)
        grad_ctx = dot(grad_att, merge_mat, 1, 1).astype(BF16)
        grad_qkv = attend_back(query, key, value, ctx, grad_ctx, probs)
        token_rows = grad_resid1
        d_qkv = []
        for which in range(3):
            mat = qkv_mat[:, which * feats : (which + 1) * feats]
            token_rows = token_rows + dot(grad_qkv[which], mat, 1, 1)
            d_qkv.append(dot(inputs, grad_qkv[which], 0, 0).astype(BF16))
        d_bq = column_sum(grad_qkv[0])
        d_bv = column_sum(grad_qkv[2])
        token_grad = from_owners(token_rows.astype(BF16))
        vec_grads = (d_bq, d_bv, d_bo, d_g1, d_b1, d_c2, d_g2, d_b2, d_c1)
        vec_pack = jnp.concatenate([item.reshape(dp_size, -1) for item in vec_grads], axis=1)
        vec_cols = -(-vec_len // (shard_rows * LANES)) * LANES
        vec_pack = jnp.pad(vec_pack, ((0, 0), (0, shard_rows * vec_cols - vec_len)))
        vec_pack = vec_pack.reshape(feats, vec_cols).astype(BF16)

        def reduce(full):
            own = lax.psum_scatter(full, "dp", scatter_dimension=0, tiled=True)
            return lax.psum(own, "seq").astype(F32)

        sum_w2 = reduce(d_w2)
        sum_w1 = reduce(d_w1)
        sum_rest = reduce(jnp.concatenate([d_wo] + d_qkv + [vec_pack], axis=1))
        s_wo, s_wq, s_wk, s_wv = [sum_rest[:, i * feats : (i + 1) * feats] for i in range(4)]
        flat = sum_rest[:, 4 * feats :].reshape(-1)
        out_vecs = []
        start = 0
        for size in vec_sizes:
            out_vecs.append(flat[start : start + size])
            start += size
        s_bq, s_bv, s_bo, s_g1, s_b1, s_c2, s_g2, s_b2, s_c1 = out_vecs
    return (
        output,
        token_grad,
        s_wq,
        s_bq,
        s_wk,
        s_wv,
        s_bv,
        s_wo,
        s_bo,
        s_g1,
        s_b1,
        sum_w1,
        s_c1,
        sum_w2,
        s_c2,
        s_g2,
        s_b2,
    )


def solution(mesh):
    rows, mat, vec = P("dp", "seq", None), P("dp", None), P("dp")
    params = (mat, vec, mat, mat, vec, mat, vec, vec, vec, mat, vec, mat, vec, vec, vec)
    return jax.shard_map(
        functools.partial(per_device, (mesh.shape["dp"], mesh.shape["seq"])),
        mesh=mesh,
        in_specs=(rows, vec) + params + (rows,),
        out_specs=(rows, rows) + params,
        check_vma=False,
    )
```

```python
import functools

import jax
import jax.numpy as jnp
from jax import lax
from jax.experimental import pallas as pl
from jax.experimental.pallas import tpu as pltpu
from jax.sharding import PartitionSpec as P

HEAD = 64
LANES = 128
EPS = 1e-12
NEG_FILL = -1000000000.0
SCALE2 = 0.125 * 1.4426950408889634
F32 = jnp.float32
BF16 = jnp.bfloat16
VMEM_LIMIT = 60 * 1024 * 1024
VMEM_MAX = 67043328


def dot(left, right, left_dim, right_dim):
    return lax.dot_general(
        left, right, (((left_dim,), (right_dim,)), ((), ())), preferred_element_type=F32
    )


def attend_kernel(bias_ref, q_ref, k_ref, v_ref, ctx_ref, probs_ref, *, rows_blk):
    seq_len = q_ref.shape[0]
    lane = lax.broadcasted_iota(jnp.int32, (1, LANES), 1)
    bias = bias_ref[...]
    for blk in range(seq_len // rows_blk):
        rows = pl.ds(blk * rows_blk, rows_blk)
        query = q_ref[rows, :]
        mixed = []
        for head in range(2):
            mine = (lane < HEAD) if head == 0 else (lane >= HEAD)
            query_h = jnp.where(mine, query, jnp.zeros_like(query))
            score = dot(query_h, k_ref[...], 1, 1) + bias
            top = jnp.max(score, axis=1, keepdims=True)
            expo = jnp.exp2((score - top) * SCALE2)
            total = jnp.sum(expo, axis=1, keepdims=True)
            probs = (expo * (1.0 / total)).astype(BF16)
            probs_ref[head, rows, :] = probs
            mixed.append(dot(probs, v_ref[...], 1, 0))
        ctx_ref[rows, :] = jnp.where(lane < HEAD, mixed[0], mixed[1]).astype(BF16)


def attend(bias, query, key, value):
    seq_len, feats = query.shape
    cols = pl.BlockSpec((seq_len, LANES), lambda g: (0, g))
    return pl.pallas_call(
        functools.partial(attend_kernel, rows_blk=min(512, seq_len)),
        grid=(feats // LANES,),
        in_specs=[pl.BlockSpec((1, seq_len), lambda g: (0, 0)), cols, cols, cols],
        out_specs=[cols, pl.BlockSpec((2, seq_len, seq_len), lambda g: (g, 0, 0))],
        out_shape=[
            jax.ShapeDtypeStruct((seq_len, feats), BF16),
            jax.ShapeDtypeStruct((feats // HEAD, seq_len, seq_len), BF16),
        ],
        compiler_params=pltpu.CompilerParams(vmem_limit_bytes=VMEM_LIMIT),
    )(bias, query, key, value)


def attend_back_pair(
    q_ref, k_ref, v_ref, ctx_ref, grad_ref, probs_ref, store, key_acc, value_acc, rows_blk,
    between=None,
):
    seq_len = q_ref.shape[0]
    lane = lax.broadcasted_iota(jnp.int32, (1, LANES), 1)
    for blk in range(seq_len // rows_blk):
        rows = pl.ds(blk * rows_blk, rows_blk)
        query = q_ref[rows, :]
        grad = grad_ref[rows, :]
        overlap = ctx_ref[rows, :].astype(F32) * grad.astype(F32)
        query_t = query.T
        grad_t = grad.T
        grad_query = []
        for head in range(2):
            mine = (lane < HEAD) if head == 0 else (lane >= HEAD)
            part = slice(head * HEAD, (head + 1) * HEAD)
            grad_h = jnp.where(mine, grad, jnp.zeros_like(grad))
            inner = jnp.sum(jnp.where(mine, overlap, 0.0), axis=1, keepdims=True)
            probs = probs_ref[head, rows, :]
            grad_probs = dot(grad_h, v_ref[...], 1, 1)
            grad_score = (probs.astype(F32) * (grad_probs - inner)).astype(BF16)
            grad_query.append(dot(grad_score, k_ref[...], 1, 0))
            grad_key = dot(query_t[part], grad_score, 1, 0)
            grad_value = dot(grad_t[part], probs, 1, 0)
            if blk == 0:
                key_acc[head] = grad_key
                value_acc[head] = grad_value
            else:
                key_acc[head] += grad_key
                value_acc[head] += grad_value
        mixed = jnp.where(lane < HEAD, grad_query[0], grad_query[1])
        store(0, rows, (0.125 * mixed).astype(BF16))
        if between is not None:
            between(blk)
    everything = pl.ds(0, seq_len)
    grad_key = jnp.concatenate([key_acc[0], key_acc[1]], axis=0)
    store(1, everything, (0.125 * grad_key).T.astype(BF16))
    grad_value = jnp.concatenate([value_acc[0], value_acc[1]], axis=0)
    store(2, everything, grad_value.T.astype(BF16))


def attend_back_kernel(
    q_ref, k_ref, v_ref, ctx_ref, grad_ref, probs_ref, out_ref, key_acc, value_acc, *, rows_blk
):
    def store(which, rows, values):
        out_ref[which, rows, :] = values

    attend_back_pair(
        q_ref, k_ref, v_ref, ctx_ref, grad_ref, probs_ref, store, key_acc, value_acc, rows_blk
    )


def attend_back(query, key, value, ctx, grad_ctx, probs):
    seq_len, feats = ctx.shape
    cols = pl.BlockSpec((seq_len, LANES), lambda g: (0, g))
    return pl.pallas_call(
        functools.partial(attend_back_kernel, rows_blk=min(512, seq_len)),
        grid=(feats // LANES,),
        in_specs=[cols] * 5 + [pl.BlockSpec((2, seq_len, seq_len), lambda g: (g, 0, 0))],
        out_specs=pl.BlockSpec((3, seq_len, LANES), lambda g: (0, 0, g)),
        out_shape=jax.ShapeDtypeStruct((3, seq_len, feats), BF16),
        scratch_shapes=[pltpu.VMEM((2, HEAD, seq_len), F32)] * 2,
        compiler_params=pltpu.CompilerParams(vmem_limit_bytes=VMEM_LIMIT),
    )(query, key, value, ctx, grad_ctx, probs)


MESH = pl.DeviceIdType.MESH


def remote(src, dst, send, recv, device):
    return pltpu.make_async_remote_copy(
        src_ref=src, dst_ref=dst, send_sem=send, recv_sem=recv,
        device_id=device, device_id_type=MESH,
    )


class Place:
    def __init__(self, seq_size, seq_count):
        self.me = me = lax.axis_index("dp")
        self.here = here = lax.axis_index("seq")
        core, x_at, y_at = me % 2, (me // 2) % 2, (me // 4) % 2
        self.to_core, self.to_x, self.to_y = 1 - 2 * core, 2 - 4 * x_at, 4 - 8 * y_at
        self.core_dev = (me + self.to_core, here)
        self.x_dev = (me + self.to_x, here)
        self.y_dev = (me + self.to_y, here)
        self.shift = (seq_size - seq_count) * core
        self.my_seq = here - self.shift
        self.is_owner = (self.my_seq >= 0) & (self.my_seq < seq_count)
        self.seq_size, self.seq_count = seq_size, seq_count

    def barrier(self):
        barrier = pltpu.get_barrier_semaphore()
        for device in (self.core_dev, self.x_dev, self.y_dev):
            pl.semaphore_signal(barrier, inc=1, device_id=device, device_id_type=MESH)
        for step in range(1, self.seq_size):
            pl.semaphore_signal(
                barrier, inc=1, device_id=(self.me, (self.here + step) % self.seq_size),
                device_id_type=MESH,
            )
        pl.semaphore_wait(barrier, 3 + self.seq_size - 1)


class Gather:
    def __init__(self, place, full, own, sems, index):
        self.place, self.full, self.own, self.index = place, full, own, index
        self.send_sem, self.recv_sem, self.core_send, self.core_recv = sems

    def half(self, which):
        count = self.full.shape[1] // 2
        return pl.ds(which * count, count)

    def piece(self, p):
        at = self.place
        rows = self.half(p % 2)
        shard = at.me + (0, 0, 0, 0, at.to_x, at.to_y)[p]
        src = self.own.at[rows] if p < 4 else self.full.at[shard, rows]
        device = (at.x_dev, at.y_dev, at.y_dev, at.x_dev, at.y_dev, at.x_dev)[p]
        return remote(
            src, self.full.at[shard, rows],
            self.send_sem.at[self.index, p], self.recv_sem.at[self.index, p], device,
        )

    def core_piece(self, p):
        at = self.place
        if p == 6:
            src, dst = self.own, self.full.at[at.me]
        else:
            across = at.to_x + at.to_y
            shard = at.me + (at.to_x, at.to_y, at.to_y, at.to_x, across, across)[p]
            src = dst = self.full.at[shard, self.half(p % 2)]
        return remote(
            src, dst, self.core_send.at[self.index, p], self.core_recv.at[self.index, p],
            at.core_dev,
        )

    def start(self, *pieces):
        for p in pieces:
            self.piece(p).start()

    def arrive(self, *pieces):
        for p in pieces:
            self.piece(p).wait_recv()

    def to_core(self, *pieces):
        for p in pieces:
            self.core_piece(p).start()

    def finish(self, pieces, core_pieces):
        for p in core_pieces:
            self.core_piece(p).wait_recv()
        for p in pieces:
            self.piece(p).wait_send()
        for p in core_pieces:
            self.core_piece(p).wait_send()


class RowsIn:
    def __init__(self, place, blocks, whole, buf, sems):
        self.place, self.blocks, self.whole, self.buf = place, blocks, whole, buf
        self.send_sem, self.recv_sem, self.local_sem = sems
        self.rows = blocks.shape[1]

    def to(self, seq, source):
        at = self.place
        return remote(
            self.blocks.at[seq], self.whole.at[pl.ds(source * self.rows, self.rows)],
            self.send_sem.at[seq], self.recv_sem.at[source], (at.me, seq + at.shift),
        )

    def own(self, count):
        at = self.place

        def out(pos, k):
            return pltpu.make_async_copy(
                self.buf, self.whole.at[pl.ds(pos * self.rows, self.rows)], self.local_sem.at[k]
            )

        @pl.when(at.is_owner)
        def _():
            load = pltpu.make_async_copy(self.blocks.at[at.my_seq], self.buf, self.local_sem.at[0])
            load.start()
            load.wait()
            out(at.here, 1).start()
            out(at.here, 1).wait()

        @pl.when(jnp.logical_not(at.is_owner))
        def _():
            self.buf[...] = jnp.zeros_like(self.buf)
            for pos in range(at.seq_size):
                out(pos, pos).start()
            for pos in range(at.seq_size):
                out(pos, pos).wait()

    def start(self):
        at = self.place
        for seq in range(at.seq_count):

            @pl.when(at.here != seq + at.shift)
            def _():
                self.to(seq, at.here).start()

    def finish(self):
        at = self.place

        @pl.when(at.is_owner)
        def _():
            for pos in range(at.seq_size):

                @pl.when(at.here != pos)
                def _():
                    remote(
                        self.blocks.at[0], self.whole.at[pl.ds(pos * self.rows, self.rows)],
                        self.send_sem.at[0], self.recv_sem.at[pos],
                        (at.me, (at.here + 1) % at.seq_size),
                    ).wait_recv()

        for seq in range(at.seq_count):

            @pl.when(at.here != seq + at.shift)
            def _():
                self.to(seq, at.here).wait_send()


def start_kernel(
    seq_size, seq_count, tokens, wq, wk, wv, w2, w1, wo, *refs,
):
    vec_refs, refs = refs[:9], refs[9:]
    rows_out, qkv_full, vec_full, w2_full, w1_full, wo_full = refs[:6]
    qkv_low, w2_low, w1_low, wo_low, row_buf, vec_wide, vecs = refs[6:13]
    row_send, row_recv, row_local, sem_a, sem_b, sem_c, sem_d, own_sem = refs[13:]
    place = Place(seq_size, seq_count)
    sems = (sem_a, sem_b, sem_c, sem_d)
    rows = RowsIn(place, tokens, rows_out, row_buf, (row_send, row_recv, row_local))
    first = [
        Gather(place, qkv_full, qkv_low, sems, 0),
        Gather(place, vec_full, vecs, sems, 1),
    ]
    later = [
        Gather(place, w2_full, w2_low, sems, 2),
        Gather(place, w1_full, w1_low, sems, 3),
        Gather(place, wo_full, wo_low, sems, 4),
    ]
    place.barrier()
    rows.start()
    feats = wq.shape[1]
    vec_wide[...] = jnp.zeros_like(vec_wide)
    for k, item in enumerate(vec_refs[:8]):
        vec_wide[k : k + 1, 0 : item.shape[1]] = item[...]
    for k in range(vec_refs[8].shape[1] // LANES):
        vec_wide[8 + k : 9 + k, :] = vec_refs[8][:, k * LANES : (k + 1) * LANES]
    vecs[...] = vec_wide[...].astype(BF16)
    for k, item in enumerate((wq, wk, wv)):
        qkv_low[:, k * feats : (k + 1) * feats] = item[...].astype(BF16)
    for item in first:
        item.start(0, 1)
    for item in first:
        item.start(2, 3)
        item.to_core(6)
    w2_low[...] = w2[...].astype(BF16)
    w1_low[...] = w1[...].astype(BF16)
    wo_low[...] = wo[...].astype(BF16)
    keep = [
        pltpu.make_async_copy(item.own, item.full.at[place.me], own_sem.at[item.index])
        for item in first + later
    ]
    for copy in keep:
        copy.start()
    for item in first:
        item.arrive(0, 1)
        item.start(4, 5)
        item.to_core(0, 1)
    for item in later:
        item.start(0, 1)
    rows.own(seq_size)
    for item in first:
        item.arrive(2, 3)
        item.to_core(2, 3)
    for item in first:
        item.arrive(4, 5)
        item.to_core(4, 5)
    for item in first:
        item.finish(range(6), range(7))
    for item in later:
        item.arrive(0, 1)
        for p in (0, 1):
            item.piece(p).wait_send()
    for copy in keep:
        copy.wait()
    rows.finish()


def start_all(seq_size, tokens, qkv_parts, vecs, w2, w1, wo):
    seq_count, blk, feats = tokens.shape
    any_spec = pl.BlockSpec(memory_space=pl.ANY)
    vmem_spec = pl.BlockSpec(memory_space=pltpu.VMEM)
    dma = pltpu.SemaphoreType.DMA
    shard = qkv_parts[0].shape[0]

    def full(rows, cols):
        return jax.ShapeDtypeStruct((8, rows, cols), BF16)

    return pl.pallas_call(
        functools.partial(start_kernel, seq_size, seq_count),
        in_specs=[any_spec] + [vmem_spec] * (6 + len(vecs)),
        out_specs=[any_spec] * 6,
        out_shape=[
            jax.ShapeDtypeStruct((seq_size * blk, feats), BF16),
            full(shard, 3 * feats), full(32, LANES), full(*w2.shape), full(*w1.shape),
            full(*wo.shape),
        ],
        scratch_shapes=[
            pltpu.VMEM((shard, 3 * feats), BF16), pltpu.VMEM(w2.shape, BF16),
            pltpu.VMEM(w1.shape, BF16), pltpu.VMEM(wo.shape, BF16), pltpu.VMEM((blk, feats), BF16),
            pltpu.VMEM((32, LANES), F32), pltpu.VMEM((32, LANES), BF16),
            dma((seq_count,)), dma((seq_size,)), dma((seq_size,)),
            dma((5, 6)), dma((5, 6)), dma((5, 7)), dma((5, 7)), dma((5,)),
        ],
        compiler_params=pltpu.CompilerParams(
            collective_id=2, has_side_effects=True, vmem_limit_bytes=VMEM_LIMIT
        ),
    )(tokens, *qkv_parts, w2, w1, wo, *vecs)


BQ, BV, BO, G1, B1, C2, G2, B2, C1 = range(9)


def unpack_vectors(full, out):
    shards, _, _ = full.shape
    feats = out.shape[1]
    part = feats // shards
    lane = lax.broadcasted_iota(jnp.int32, (LANES, feats), 0)
    column = lax.broadcasted_iota(jnp.int32, (LANES, feats), 1)
    rows = jnp.zeros((16, feats), F32)
    for k in range(shards):
        place = ((lane < part) & (column == lane + k * part)).astype(BF16)
        rows = rows + dot(full[k, 0:16, :], place, 1, 0)
    out[...] = rows
    long = feats * 4 // shards
    for k in range(shards):
        row, start = C1 + k * long // feats, k * long % feats
        for j in range(long // LANES):
            out[row : row + 1, start + j * LANES : start + (j + 1) * LANES] = full[
                k, 8 + j : 9 + j, :
            ].astype(F32)


def forward_kernel(
    seq_size, seq_count, rows_blk,
    len_ref, x_ref, wq_ref, wk_ref, wv_ref, vec_full, upstream, w2_in, w1_in, wo_in,
    q_ref, k_ref, v_ref, ctx_ref, probs_ref, vec_out, dy_out, w2_full, w1_full, wo_full,
    bias_ref, row_buf, row_send, row_recv, row_local, sem_a, sem_b, sem_c, sem_d,
):
    step = pl.program_id(0)
    last = pl.num_programs(0) - 1
    place = Place(seq_size, seq_count)
    sems = (sem_a, sem_b, sem_c, sem_d)
    rows = RowsIn(place, upstream, dy_out, row_buf, (row_send, row_recv, row_local))
    later = [
        Gather(place, full, full.at[place.me], sems, k)
        for k, full in enumerate((w2_full, w1_full, wo_full))
    ]

    @pl.when(step == 0)
    def _():
        place.barrier()
        for item in later:
            item.start(2, 3)
        for item in later:
            item.start(4, 5)
        rows.start()
        for item in later:
            item.to_core(6, 0, 1)
        rows.own(seq_size)
        unpack_vectors(vec_full, vec_out)
        valid = len_ref[jnp.clip(place.my_seq, 0, seq_count - 1)]
        position = lax.broadcasted_iota(jnp.int32, bias_ref.shape, 1)
        bias_ref[...] = jnp.where(position < valid, 0.0, 8.0 * NEG_FILL)

    x_rows = x_ref[...]
    depth = x_rows.shape[1]
    column = pl.ds(pl.multiple_of(step * LANES, LANES), LANES)
    mats = [ref[...].reshape(depth, LANES) for ref in (wq_ref, wk_ref, wv_ref)]
    both = dot(x_rows, jnp.concatenate(mats, axis=1), 1, 0)
    q_ref[...] = (both[:, :LANES] + vec_out[BQ : BQ + 1, column]).astype(BF16)
    k_ref[...] = both[:, LANES : 2 * LANES].astype(BF16)
    v_ref[...] = (both[:, 2 * LANES :] + vec_out[BV : BV + 1, column]).astype(BF16)
    attend_kernel(bias_ref, q_ref, k_ref, v_ref, ctx_ref, probs_ref, rows_blk=rows_blk)

    @pl.when(step == last - 1)
    def _():
        for item in later:
            item.arrive(2, 3)
            item.to_core(2, 3)

    @pl.when(step == last)
    def _():
        for item in later:
            item.arrive(4, 5)
            item.to_core(4, 5)
        for item in later:
            item.finish(range(2, 6), range(7))
        rows.finish()


def forward_all(seq_size, lengths, rows, qkv_full, vec_full, upstream, w2_full, w1_full, wo_full):
    seq_len, feats = rows.shape
    seq_count, blk, _ = upstream.shape
    pairs = feats // LANES
    shard = qkv_full.shape[1]
    any_spec = pl.BlockSpec(memory_space=pl.ANY)
    dma = pltpu.SemaphoreType.DMA
    cols = pl.BlockSpec((seq_len, LANES), lambda g: (0, g))

    def mat(which):
        return pl.BlockSpec((8, shard, LANES), lambda g, w=which: (0, 0, w * pairs + g))

    fulls = [w2_full, w1_full, wo_full]
    flat = jax.ShapeDtypeStruct((seq_len, feats), BF16)
    return pl.pallas_call(
        functools.partial(forward_kernel, seq_size, seq_count, min(512, seq_len)),
        grid=(pairs,),
        in_specs=[
            pl.BlockSpec(memory_space=pltpu.SMEM),
            pl.BlockSpec((seq_len, feats), lambda g: (0, 0)),
            mat(0), mat(1), mat(2), pl.BlockSpec(vec_full.shape, lambda g: (0, 0, 0)),
        ]
        + [any_spec] * 4,
        out_specs=[cols] * 4
        + [
            pl.BlockSpec((2, seq_len, seq_len), lambda g: (g, 0, 0)),
            pl.BlockSpec((16, feats), lambda g: (0, 0)),
        ]
        + [any_spec] * 4,
        out_shape=[flat] * 4
        + [
            jax.ShapeDtypeStruct((feats // HEAD, seq_len, seq_len), BF16),
            jax.ShapeDtypeStruct((16, feats), F32),
            flat,
        ]
        + [jax.ShapeDtypeStruct(item.shape, BF16) for item in fulls],
        scratch_shapes=[
            pltpu.VMEM((1, seq_len), F32), pltpu.VMEM((blk, feats), BF16),
            dma((seq_count,)), dma((seq_size,)), dma((seq_size,)),
            dma((3, 6)), dma((3, 6)), dma((3, 7)), dma((3, 7)),
        ],
        input_output_aliases={7: 7, 8: 8, 9: 9},
        compiler_params=pltpu.CompilerParams(
            collective_id=3, has_side_effects=True, vmem_limit_bytes=VMEM_LIMIT
        ),
    )(lengths, rows, qkv_full, qkv_full, qkv_full, vec_full, upstream, *fulls)


def add_rows(dest, first, *others, start=0, count=None):
    count = dest.shape[0] if count is None else count

    def body(i, carry):
        to = pl.ds(pl.multiple_of(start + i * 16, 16), 16)
        frm = pl.ds(pl.multiple_of(i * 16, 16), 16)
        if len(others) == 1:
            dest[to, :] = first[to, :] + others[0][frm, :]
        else:
            value = first[to, :].astype(F32)
            for other in others:
                value = value + other[frm, :].astype(F32)
            dest[to, :] = value.astype(dest.dtype)
        return carry

    lax.fori_loop(0, count // 16, body, 0, unroll=True)


class Chain:
    def __init__(self, place, mine, passed, arrived, total, sems, index):
        self.place, self.mine, self.passed, self.arrived = place, mine, passed, arrived
        self.total, self.index = total, index
        self.z_send, self.z_recv = sems

    def copy(self, way, src):
        at = self.place
        return remote(
            src, self.arrived.at[way], self.z_send.at[self.index, way],
            self.z_recv.at[self.index, way], (at.me, at.here + (1, -1)[way]),
        )

    def hops(self, way):
        at = self.place
        return at.here if way == 0 else at.seq_size - 1 - at.here

    def hop(self, hop):
        for way in range(2):
            passed = self.passed.at[way]

            @pl.when(self.hops(way) == hop)
            def _():
                if hop == 0:
                    self.copy(way, self.mine).start()
                else:
                    self.copy(way, passed).wait_recv()
                    if hop < self.place.seq_size - 1:
                        add_rows(passed, self.mine, self.arrived.at[way])
                        self.copy(way, passed).start()

    def finish(self):
        last = self.place.seq_size - 1
        up, down = self.arrived.at[0], self.arrived.at[1]
        here = self.place.here

        @pl.when(here == 0)
        def _():
            add_rows(self.total, self.mine, down)

        @pl.when(here == last)
        def _():
            add_rows(self.total, self.mine, up)

        @pl.when((here > 0) & (here < last))
        def _():
            add_rows(self.total, self.mine, up, down)

    def drain(self):
        for way in range(2):

            @pl.when(self.hops(way) < self.place.seq_size - 1)
            def _():
                self.copy(way, self.mine).wait_send()

    @staticmethod
    def semaphores(count):
        dma = pltpu.SemaphoreType.DMA
        return [dma((count, 2)), dma((count, 2))]


class Carried:
    def __init__(self, place, source, result, bufs, sems, copy_sems, index, slot):
        mine, passed, arrived, total = bufs
        self.chain = Chain(place, mine, passed, arrived, total, sems, index)
        self.load = pltpu.make_async_copy(source, mine, copy_sems.at[slot, 0])
        self.out = pltpu.make_async_copy(total, result, copy_sems.at[slot, 1])

    def begin(self):
        self.load.wait()
        self.chain.hop(0)

    def hop(self, hop):
        self.chain.hop(hop)

    def finish(self):
        self.chain.finish()
        self.out.start()

    def drain(self):
        self.chain.drain()
        self.out.wait()


class Reduce:
    def __init__(self, place, source, result, bufs, sems, index, z_arrived=None, z_sems=None):
        self.place, self.source, self.index = place, source, index
        self.own, self.other, self.first_x, self.first_y, self.second = bufs
        (
            self.own_sem, self.core_send, self.core_recv, self.one_send, self.one_recv,
            self.two_send, self.two_recv,
        ) = sems
        at = place
        self.apart = [(r % 2) * at.to_x + (r // 2) * at.to_y for r in range(4)]
        self.rows = self.own.shape[1]
        self.half = self.rows // 2
        self.chain, total = None, self.own.at[0]
        if z_arrived is not None:
            total = self.own.at[3]
            self.chain = Chain(place, self.own.at[0], self.other, z_arrived, total, z_sems, index)
        self.out = pltpu.make_async_copy(total, result, self.own_sem.at[index, 3])

    def keep_copy(self, r):
        return pltpu.make_async_copy(
            self.source(self.place.me + self.apart[r]), self.own.at[r],
            self.own_sem.at[self.index, r],
        )

    def core_copy(self, r):
        at = self.place
        return remote(
            self.source(at.me + at.to_core + self.apart[r]), self.other.at[r],
            self.core_send.at[self.index, r], self.core_recv.at[self.index, r], at.core_dev,
        )

    def one_copy(self, way, k):
        half = self.half
        if way == 0:
            src, dst = self.own.at[(1, 3)[k], pl.ds(0, half)], self.first_x.at[k]
        else:
            src, dst = self.own.at[(2, 3)[k], pl.ds(half, half)], self.first_y.at[k]
        return remote(
            src, dst, self.one_send.at[self.index, way, k], self.one_recv.at[self.index, way, k],
            (self.place.x_dev, self.place.y_dev)[way],
        )

    def two_copy(self, way):
        src = self.own.at[(2, 1)[way], pl.ds(way * self.half, self.half)]
        return remote(
            src, self.second.at[way], self.two_send.at[self.index, way],
            self.two_recv.at[self.index, way], (self.place.y_dev, self.place.x_dev)[way],
        )

    def begin(self):
        for r in (3, 1, 2, 0):
            self.core_copy(r).start()
            self.keep_copy(r).start()

    def core_stage(self):
        for r in (3, 1, 2, 0):
            self.keep_copy(r).wait()
            self.core_copy(r).wait_recv()
            add_rows(self.own.at[r], self.own.at[r], self.other.at[r])
            if r == 3:
                self.one_copy(0, 1).start()
                self.one_copy(1, 1).start()
            elif r == 1:
                self.one_copy(0, 0).start()
            elif r == 2:
                self.one_copy(1, 0).start()

    def one_stage(self):
        firsts = (self.first_x, self.first_y)
        for k in (1, 0):
            for way in range(2):
                self.one_copy(way, k).wait_recv()
                dest = self.own.at[(2, 1)[way] if k else 0]
                add_rows(dest, dest, firsts[way].at[k], start=way * self.half, count=self.half)
                if k:
                    self.two_copy(way).start()

    def two_stage(self):
        mine = self.own.at[0]
        for way in range(2):
            self.two_copy(way).wait_recv()
            add_rows(mine, mine, self.second.at[way], start=way * self.half, count=self.half)
        if self.chain is not None:
            self.chain.hop(0)

    def hop(self, hop):
        self.chain.hop(hop)

    def finish(self):
        if self.chain is not None:
            self.one_copy(0, 1).wait_send()
            self.one_copy(1, 1).wait_send()
            self.chain.finish()
        self.out.start()

    def drain(self):
        for r in range(4):
            self.core_copy(r).wait_send()
        for way in range(2):
            self.one_copy(way, 0).wait_send()
            if self.chain is None:
                self.one_copy(way, 1).wait_send()
            self.two_copy(way).wait_send()
        if self.chain is not None:
            self.chain.drain()
        self.out.wait()

    @staticmethod
    def scratch(count, rows, width):
        return [
            pltpu.VMEM((count, lead, rows // split, width), BF16)
            for lead, split in ((4, 1), (4, 1), (2, 2), (2, 2), (2, 2))
        ]

    @staticmethod
    def semaphores(count):
        dma = pltpu.SemaphoreType.DMA
        return [
            dma((count, 4)), dma((count, 4)), dma((count, 4)),
            dma((count, 2, 2)), dma((count, 2, 2)), dma((count, 2)), dma((count, 2)),
        ]


class RowsOut:
    def __init__(self, place, rows, blocks, sems):
        self.place, self.rows, self.blocks = place, rows, blocks
        self.send_sem, self.recv_sem, self.local_sem = sems
        self.blk = blocks.shape[1]

    def part(self, pos):
        return self.rows.at[pl.ds(pos * self.blk, self.blk)]

    def copy(self, pos):
        at = self.place
        return remote(
            self.part(pos), self.blocks.at[at.my_seq], self.send_sem.at[pos],
            self.recv_sem.at[at.my_seq], (at.me, pos),
        )

    def keep(self, pos):
        return pltpu.make_async_copy(
            self.part(pos), self.blocks.at[self.place.my_seq], self.local_sem.at[0]
        )

    def start(self, pos):
        at = self.place

        @pl.when(at.is_owner & (at.here != pos))
        def _():
            self.copy(pos).start()

        @pl.when(at.is_owner & (at.here == pos))
        def _():
            self.keep(pos).start()

    def finish(self):
        at = self.place
        for seq in range(at.seq_count):

            @pl.when(at.here != seq + at.shift)
            def _():
                remote(
                    self.part(0), self.blocks.at[seq], self.send_sem.at[0], self.recv_sem.at[seq],
                    (at.me, (at.here + 1) % at.seq_size),
                ).wait_recv()

        @pl.when(at.is_owner)
        def _():
            self.keep(0).wait()
            for pos in range(at.seq_size):

                @pl.when(at.here != pos)
                def _():
                    self.copy(pos).wait_send()


INV_SQRT2 = 0.7071067811865476
INV_SQRT_2PI = 0.3989422804014327


def normalize(resid):
    centre = resid - jnp.mean(resid, axis=-1, keepdims=True)
    inv = lax.rsqrt(jnp.mean(centre * centre, axis=-1, keepdims=True) + EPS)
    return centre * inv, inv


def normalize_back(normed, inv, grad_normed):
    mean_grad = jnp.mean(grad_normed, axis=-1, keepdims=True)
    mean_both = jnp.mean(grad_normed * normed, axis=-1, keepdims=True)
    return inv * (grad_normed - mean_grad - normed * mean_both)


def gelu_parts(pre):
    cumulative = 0.5 * (1.0 + lax.erf(pre * INV_SQRT2))
    slope = cumulative + pre * (INV_SQRT_2PI * jnp.exp(-0.5 * pre * pre))
    return pre * cumulative, slope


def feed_kernel(
    rows_blk, ctx_ref, x_ref, wo_ref, vec_ref, w1_ref, w2_ref, dy_ref,
    act_ref, slope_ref, out_ref, resid_ref, normed_ref, inv_ref, vec_out,
    hidden_low,
):
    step = pl.program_id(0)
    seq_len, feats = x_ref.shape
    width = act_ref.shape[1]
    blocks = [pl.ds(i * rows_blk, rows_blk) for i in range(seq_len // rows_blk)]

    def vec(k):
        return vec_ref[k : k + 1, :]

    @pl.when(step == 0)
    def _():
        merge = wo_ref[...].reshape(feats, feats)
        for rows in blocks:
            resid = x_ref[rows, :].astype(F32) + (dot(ctx_ref[rows, :], merge, 1, 0) + vec(BO))
            normed, inv = normalize(resid)
            normed_ref[rows, :] = normed
            inv_ref[rows, :] = jnp.broadcast_to(inv, (rows_blk, LANES))
            hidden_low[rows, :] = (normed * vec(G1) + vec(B1)).astype(BF16)

    expand = w1_ref[...].reshape(feats, width)
    shrink = w2_ref[...].reshape(width, feats)
    shift = vec_ref[pl.ds(C1 + step, 1), :]
    for rows in blocks:
        act, slope = gelu_parts(dot(hidden_low[rows, :], expand, 1, 0) + shift)
        act_low = act.astype(BF16)
        act_ref[rows, :] = act_low
        slope_ref[rows, :] = slope.astype(BF16)
        part = dot(act_low, shrink, 1, 0)

        @pl.when(step == 0)
        def _():
            resid_ref[rows, :] = part

        @pl.when(step > 0)
        def _():
            resid_ref[rows, :] += part

    @pl.when(step == pl.num_programs(0) - 1)
    def _():
        sums = [jnp.zeros((1, feats), F32)] * 3
        for rows in blocks:
            hidden = normed_ref[rows, :] * vec(G1) + vec(B1)
            normed, inv = normalize(hidden + (resid_ref[rows, :] + vec(C2)))
            out_ref[rows, :] = (normed * vec(G2) + vec(B2)).astype(BF16)
            dy = dy_ref[rows, :].astype(F32)
            grad = normalize_back(normed, inv, vec(G2) * dy)
            resid_ref[rows, :] = grad
            terms = (dy * normed, dy, grad.astype(BF16).astype(F32))
            sums = [
                total + jnp.sum(term, axis=0, keepdims=True) for total, term in zip(sums, terms)
            ]
        for k, total in enumerate(sums):
            vec_out[k : k + 1, :] = total


def feed_forward(ctx, inputs, wo_full, vecs, w1_full, w2_full, dy):
    seq_len, feats = inputs.shape
    shard = w1_full.shape[1]
    hidden = w1_full.shape[2]
    steps = hidden // feats
    once = pl.Buffered(1)

    def whole(shape, mode=None):
        return pl.BlockSpec(shape, lambda j: (0,) * len(shape), pipeline_mode=mode)

    rows, rows_f32 = (seq_len, feats), jax.ShapeDtypeStruct((seq_len, feats), F32)
    cols = pl.BlockSpec(rows, lambda j: (0, j))
    wide = jax.ShapeDtypeStruct((seq_len, hidden), BF16)
    return pl.pallas_call(
        functools.partial(feed_kernel, min(256, seq_len)),
        grid=(steps,),
        in_specs=[
            whole(rows, once), whole(rows, once), whole(wo_full.shape, once),
            whole(vecs.shape, once),
            pl.BlockSpec((8, shard, feats), lambda j: (0, 0, j)),
            pl.BlockSpec((8 // steps, w2_full.shape[1], feats), lambda j: (j, 0, 0)),
            whole(rows, once),
        ],
        out_specs=[cols, cols, whole(rows), whole(rows), whole(rows), whole((seq_len, LANES)),
                   whole((8, feats))],
        out_shape=[
            wide, wide, jax.ShapeDtypeStruct(rows, BF16), rows_f32, rows_f32,
            jax.ShapeDtypeStruct((seq_len, LANES), F32), jax.ShapeDtypeStruct((8, feats), F32),
        ],
        scratch_shapes=[pltpu.VMEM(rows, BF16)],
        compiler_params=pltpu.CompilerParams(vmem_limit_bytes=VMEM_LIMIT),
    )(ctx, inputs, wo_full, vecs, w1_full, w2_full, dy)


def feed_back_kernel(seq_size, seq_count, rows_blk, *refs):
    refs = list(refs)

    def take(count):
        got = refs[:count]
        del refs[:count]
        return got

    act_ref, slope_ref, w1_ref, w2_ref, resid_ref, normed_ref, inv_ref, ctx_ref = take(8)
    wo_ref, vec_ref, vec_in, out_rows = take(4)
    d_w1, resid_out, grad_ctx, d_wo, vec_out, w2_part, out_blocks = take(7)
    grad_ffn, hidden_low, d_w2, vec_sums = take(4)
    count = 4
    bufs = take(5)
    sems = take(7)
    out_sems = take(3)

    step = pl.program_id(0)
    half_steps = pl.num_programs(0) // 2
    seq_len, feats = resid_ref.shape
    chunk = d_w2.shape[1] // count
    place = Place(seq_size, seq_count)
    outs = RowsOut(place, out_rows, out_blocks, out_sems)
    jobs = [
        Reduce(
            place, lambda shard, c=c: d_w2.at[shard, pl.ds(c * chunk, chunk)],
            w2_part.at[pl.ds(c * chunk, chunk)], [buf.at[c] for buf in bufs], sems, c,
        )
        for c in range(count)
    ]
    blocks = [pl.ds(i * rows_blk, rows_blk) for i in range(seq_len // rows_blk)]

    def vec(k):
        return vec_ref[k : k + 1, :]

    @pl.when(step == 0)
    def _():
        place.barrier()
        for pos in range(seq_size):
            outs.start(pos)
        for rows in blocks:
            grad_ffn[rows, :] = resid_ref[rows, :].astype(BF16)
            hidden_low[rows, :] = (normed_ref[rows, :] * vec(G1) + vec(B1)).astype(BF16)

    @pl.when(step < half_steps)
    def _():
        shards = 8 // half_steps
        part = dot(act_ref[...], grad_ffn[...], 0, 0).astype(BF16)
        d_w2[pl.ds(step * shards, shards)] = part.reshape(shards, d_w2.shape[1], feats)

    @pl.when(step == half_steps - 1)
    def _():
        for job in jobs:
            job.begin()

    @pl.when(step >= half_steps)
    def _():
        width = act_ref.shape[1]
        shrink = w2_ref[...].reshape(width, feats)
        expand = w1_ref[...].reshape(feats, width)
        ones = jnp.ones((8, rows_blk), BF16)
        total = jnp.zeros((8, width), F32)
        outer = jnp.zeros((feats, width), F32)
        for rows in blocks:
            grad_act = dot(grad_ffn[rows, :], shrink, 1, 1)
            grad_pre = (grad_act * slope_ref[rows, :].astype(F32)).astype(BF16)
            total = total + dot(ones, grad_pre, 1, 0)
            outer = outer + dot(hidden_low[rows, :], grad_pre, 0, 0)
            part = dot(grad_pre, expand, 1, 1)

            @pl.when(step == half_steps)
            def _():
                resid_out[rows, :] = resid_ref[rows, :] + part

            @pl.when(step > half_steps)
            def _():
                resid_out[rows, :] += part

        d_w1[0] = outer.astype(BF16).reshape(d_w1.shape[1:])
        vec_sums[pl.ds(step - half_steps, 1), :] = total[0:1, :]

    @pl.when(step == half_steps)
    def _():
        for job in jobs:
            job.core_stage()

    @pl.when(step == half_steps + 1)
    def _():
        jobs[0].one_stage()
        jobs[1].one_stage()

    @pl.when(step == half_steps + 2)
    def _():
        jobs[2].one_stage()
        jobs[3].one_stage()
        jobs[0].two_stage()

    @pl.when(step == pl.num_programs(0) - 1)
    def _():
        jobs[1].two_stage()
        merge = wo_ref[...].reshape(feats, feats)
        sums = [jnp.zeros((1, feats), F32)] * 3
        outer = jnp.zeros((feats, feats), F32)
        for rows in blocks:
            grad_hidden = resid_out[rows, :]
            normed = normed_ref[rows, :]
            grad = normalize_back(normed, inv_ref[rows, 0:1], vec(G1) * grad_hidden)
            resid_out[rows, :] = grad
            low = grad.astype(BF16)
            grad_ctx[rows, :] = dot(low, merge, 1, 1).astype(BF16)
            outer = outer + dot(ctx_ref[rows, :], low, 0, 0)
            terms = (grad_hidden * normed, grad_hidden, low.astype(F32))
            sums = [
                total + jnp.sum(term, axis=0, keepdims=True) for total, term in zip(sums, terms)
            ]
        d_wo[...] = outer.astype(BF16).reshape(d_wo.shape)
        row = lax.broadcasted_iota(jnp.int32, (16, 1), 0)
        lines = sums + [vec_in[k : k + 1, :] for k in range(3)]
        lines = lines + [vec_sums[k : k + 1, :] for k in range(4)]
        packed = jnp.zeros((16, feats), F32)
        for k, line in enumerate(lines):
            packed = jnp.where(row == k, line, packed)
        vec_out[...] = packed.astype(BF16)

        for job in jobs[:2]:
            job.finish()
        for job in jobs[2:]:
            job.two_stage()
            job.finish()
        for job in jobs:
            job.drain()
        outs.finish()


def feed_back(
    seq_size, seq_count, act, slope, w1_full, w2_full, resid, normed, inv, ctx, wo_full, vecs,
    vec_in, out_rows,
):
    seq_len, feats = ctx.shape
    shard, w2_rows = w1_full.shape[1], w2_full.shape[1]
    steps = act.shape[1] // feats
    blk = seq_len // seq_size
    once = pl.Buffered(1)
    any_spec = pl.BlockSpec(memory_space=pl.ANY)
    dma = pltpu.SemaphoreType.DMA

    def whole(shape, mode=None):
        return pl.BlockSpec(shape, lambda j: (0,) * len(shape), pipeline_mode=mode)

    def first(j):
        return jnp.minimum(j, steps - 1)

    def second(j):
        return jnp.maximum(j - steps, 0)

    rows = (seq_len, feats)
    return pl.pallas_call(
        functools.partial(feed_back_kernel, seq_size, seq_count, min(256, seq_len)),
        grid=(2 * steps,),
        in_specs=[
            pl.BlockSpec(rows, lambda j: (0, first(j))),
            pl.BlockSpec(rows, lambda j: (0, second(j))),
            pl.BlockSpec((8, shard, feats), lambda j: (0, 0, second(j))),
            pl.BlockSpec((8 // steps, w2_rows, feats), lambda j: (second(j), 0, 0)),
            whole(rows, once), whole(rows, once), whole(inv.shape, once), whole(rows, once),
            whole(wo_full.shape, once), whole(vecs.shape, once), whole(vec_in.shape, once),
            any_spec,
        ],
        out_specs=[
            pl.BlockSpec((1, 8, shard, feats), lambda j: (second(j), 0, 0, 0)),
            whole(rows), whole(rows), whole(wo_full.shape), whole((16, feats)),
            any_spec, any_spec,
        ],
        out_shape=[
            jax.ShapeDtypeStruct((steps, 8, shard, feats), BF16),
            jax.ShapeDtypeStruct(rows, F32), jax.ShapeDtypeStruct(rows, BF16),
            jax.ShapeDtypeStruct(wo_full.shape, BF16), jax.ShapeDtypeStruct((16, feats), BF16),
            jax.ShapeDtypeStruct((w2_rows, feats), BF16),
            jax.ShapeDtypeStruct((seq_count, blk, feats), BF16),
        ],
        scratch_shapes=[
            pltpu.VMEM(rows, BF16), pltpu.VMEM(rows, BF16), pltpu.VMEM((8, w2_rows, feats), BF16),
            pltpu.VMEM((8, feats), F32),
        ]
        + Reduce.scratch(4, w2_rows // 4, feats)
        + Reduce.semaphores(4)
        + [dma((seq_size,)), dma((seq_count,)), dma((1,))],
        compiler_params=pltpu.CompilerParams(
            collective_id=4, has_side_effects=True, vmem_limit_bytes=VMEM_MAX
        ),
    )(
        act, slope, w1_full, w2_full, resid, normed, inv, ctx, wo_full, vecs, vec_in, out_rows
    )


def pair_column(feats, which, pair):
    return (pair // 2) * feats + (pair % 2) * 3 * LANES + which * LANES


def backward_kernel(seq_size, seq_count, rows_blk, *refs):
    refs = list(refs)

    def take(count):
        got = refs[:count]
        del refs[:count]
        return got

    q_ref, k_ref, v_ref, ctx_ref, grad_ref, probs_ref, vec_ref = take(7)
    x_in, qkv_in, resid_in, d_w1, d_wo, w2_part = take(6)
    w2_total, w1_total, wo_total, qkv_total, vec_total, token_out = take(6)
    key_acc, value_acc, grads, x_rows, qkv_mat, resid, token_rows = take(7)
    mats, bias_rows, vec_src = take(3)
    w1_count = d_w1.shape[0]
    mat_count = w1_count + 4
    bufs = take(5)
    (arrived,) = take(1)
    vec_bufs = take(5)
    (vec_arrived,) = take(1)
    carried_bufs = take(4)
    sems = take(7)
    z_sems = take(2)
    load_sem, carried_sems = take(2)
    token_sems = take(3)

    step = pl.program_id(0)
    last = pl.num_programs(0) - 1
    place = Place(seq_size, seq_count)
    seq_len, feats = x_rows.shape

    def outer_source(c):
        if c < w1_count:
            return lambda shard: d_w1.at[c, shard]
        if c == w1_count:
            return lambda shard: d_wo.at[shard]
        return lambda shard: mats.at[c - w1_count - 1, shard]

    totals = [w1_total.at[:, pl.ds(c * feats, feats)] for c in range(w1_count)]
    totals += [wo_total] + [qkv_total.at[:, pl.ds(c * feats, feats)] for c in range(3)]
    jobs = [
        Reduce(
            place, outer_source(c), totals[c], [buf.at[c] for buf in bufs], sems, c,
            arrived.at[c], z_sems,
        )
        for c in range(mat_count)
    ]
    jobs.append(
        Reduce(
            place, lambda shard: vec_src.at[shard], vec_total, [buf.at[0] for buf in vec_bufs],
            sems, mat_count, vec_arrived.at[0], z_sems,
        )
    )
    chunk = w2_part.shape[0] // 4
    carried = []
    for c in range(4):
        rows = pl.ds(c * chunk, chunk)
        carried.append(
            Carried(
                place, w2_part.at[rows], w2_total.at[rows], [buf.at[c] for buf in carried_bufs],
                z_sems, carried_sems, mat_count + 1 + c, c,
            )
        )
    w0, w1, w2, w3, wo, qkv_a, qkv_b, qkv_c, vec = jobs
    t0, t1, t2, t3 = carried
    blk = seq_len // seq_size
    loads = [
        pltpu.make_async_copy(src, dst, load_sem.at[k])
        for k, (src, dst) in enumerate(((x_in, x_rows), (qkv_in, qkv_mat), (resid_in, resid)))
    ]
    tokens = RowsOut(place, token_rows, token_out, token_sems)

    core, one, two = Reduce.core_stage, Reduce.one_stage, Reduce.two_stage

    def hop1(job):
        job.hop(1)

    def hop2(job):
        job.hop(2)

    def end(job):
        job.hop(3)
        job.finish()

    ticks = (
        ((core, w0), (core, w1)),
        ((core, w2), (hop1, t0)),
        ((one, w0), (hop1, t1)),
        ((one, w1), (core, w3), (hop1, t2), (hop2, t0)),
        ((one, w2), (hop1, t3), (hop2, t1)),
        ((two, w0), (two, w1), (core, wo), (hop2, t2), (end, t0)),
        ((one, w3), (core, qkv_a), (hop2, t3), (end, t1)),
        ((two, w2), (hop1, w0), (end, t2)),
        ((one, wo), (hop1, w1), (end, t3)),
        ((two, w3), (core, qkv_b), (one, qkv_a), (hop1, w2), (hop2, w0)),
        ((two, wo), (hop2, w1)),
        ((one, qkv_b), (hop1, w3), (hop2, w2), (end, w0)),
    )
    after = (
        ((two, qkv_a), (end, w1)),
        ((core, qkv_c), (hop1, wo)),
        ((core, vec), (two, qkv_b), (hop2, w3)),
        ((end, w2), (hop1, qkv_a)),
    )
    rest = (
        (one, qkv_c), (one, vec), (hop2, wo), (hop1, qkv_b), (end, w3),
        (two, qkv_c), (two, vec), (hop2, qkv_a), (end, wo),
        (hop1, qkv_c), (hop1, vec), (hop2, qkv_b), (end, qkv_a),
        (hop2, qkv_c), (hop2, vec), (end, qkv_b),
        (end, qkv_c), (end, vec),
    )

    @pl.when(step == 0)
    def _():
        place.barrier()
        for job in carried:
            job.load.start()
        for job in (w0, w1, w2, w3, wo):
            job.begin()
        for load in loads:
            load.start()
        for job in carried:
            job.begin()

    @pl.when(step == 2)
    def _():
        qkv_a.begin()

    @pl.when(step == 4)
    def _():
        qkv_b.begin()

    def store(which, rows, values):
        grads[rows, which * LANES : (which + 1) * LANES] = values

    def between(half):
        for at_step in range(len(ticks) // 2):

            @pl.when(step == at_step)
            def _():
                for stage, job in ticks[2 * at_step + half]:
                    stage(job)

    attend_back_pair(
        q_ref, k_ref, v_ref, ctx_ref, grad_ref, probs_ref, store, key_acc, value_acc, rows_blk,
        between,
    )

    @pl.when(step == 0)
    def _():
        for load in loads:
            load.wait()

    width = 3 * LANES
    column = pl.multiple_of(step * LANES, LANES)
    half = pl.multiple_of((step % 2) * width, LANES)
    outer = dot(x_rows[...], grads[...], 0, 0).astype(BF16)
    mats[step // 2, :, :, pl.ds(half, width)] = outer.reshape(8, feats // 8, width)
    sums = dot(jnp.ones((16, seq_len), BF16), grads[...], 1, 0)
    bias_rows[0, :, pl.ds(column, LANES)] = sums[:, :LANES]
    bias_rows[1, :, pl.ds(column, LANES)] = sums[:, 2 * LANES :]
    mat = jnp.concatenate(
        [
            qkv_mat[:, :, pl.ds(pl.multiple_of(which * feats + column, LANES), LANES)].reshape(
                feats, LANES
            )
            for which in range(3)
        ],
        axis=1,
    )

    @pl.when(step < last)
    def _():
        for pos in range(seq_size):
            rows = pl.ds(pos * blk, blk)
            resid[rows, :] += dot(grads[rows, :], mat, 1, 1)

    @pl.when(step == last)
    def _():
        qkv_c.begin()
        row = lax.broadcasted_iota(jnp.int32, (16, 1), 0)
        biases = jnp.where(row == 0, bias_rows[0], bias_rows[1]).astype(BF16)
        for shard in range(8):
            vec_src[shard, 0:16, :] = vec_ref[...]
            vec_src[shard, 16:32, :] = biases
        vec.begin()
        for pos in range(seq_size):
            rows = pl.ds(pos * blk, blk)
            total = resid[rows, :] + dot(grads[rows, :], mat, 1, 1)
            token_rows[rows, :] = total.astype(BF16)
            tokens.start(pos)
            for stage, job in after[pos]:
                stage(job)
        for stage, job in rest:
            stage(job)
        for job in jobs + carried:
            job.drain()
        tokens.finish()


def backward_all(
    seq_size, seq_count, query, key, value, ctx, grad_ctx, probs, vecs, inputs, qkv_full, resid,
    d_w1, d_wo, w2_part,
):
    seq_len, feats = ctx.shape
    blk = seq_len // seq_size
    shard = qkv_full.shape[1]
    w1_count = d_w1.shape[0]
    count = w1_count + 4
    chunk = w2_part.shape[0] // 4
    any_spec = pl.BlockSpec(memory_space=pl.ANY)
    cols = pl.BlockSpec((seq_len, LANES), lambda g: (0, g))
    dma = pltpu.SemaphoreType.DMA

    def low(*shape):
        return jax.ShapeDtypeStruct(shape, BF16)

    return pl.pallas_call(
        functools.partial(backward_kernel, seq_size, seq_count, seq_len // 2),
        grid=(feats // LANES,),
        in_specs=[cols] * 5
        + [
            pl.BlockSpec((2, seq_len, seq_len), lambda g: (g, 0, 0)),
            pl.BlockSpec(vecs.shape, lambda g: (0, 0)),
        ]
        + [any_spec] * 6,
        out_specs=[any_spec] * 6,
        out_shape=[
            low(*w2_part.shape), low(shard, w1_count * feats), low(shard, feats),
            low(shard, 3 * feats), low(32, feats), low(seq_count, blk, feats),
        ],
        scratch_shapes=[pltpu.VMEM((2, HEAD, seq_len), F32)] * 2
        + [
            pltpu.VMEM((seq_len, 3 * LANES), BF16),
            pltpu.VMEM((seq_len, feats), BF16),
            pltpu.VMEM(qkv_full.shape, BF16),
            pltpu.VMEM((seq_len, feats), F32),
            pltpu.VMEM((seq_len, feats), BF16),
            pltpu.VMEM((3, 8, shard, feats), BF16),
            pltpu.VMEM((2, 16, feats), F32),
            pltpu.VMEM((8, 32, feats), BF16),
        ]
        + Reduce.scratch(count, shard, feats)
        + [pltpu.VMEM((count, 2, shard, feats), BF16)]
        + Reduce.scratch(1, 32, feats)
        + [pltpu.VMEM((1, 2, 32, feats), BF16)]
        + [
            pltpu.VMEM((4, chunk, feats), BF16), pltpu.VMEM((4, 2, chunk, feats), BF16),
            pltpu.VMEM((4, 2, chunk, feats), BF16), pltpu.VMEM((4, chunk, feats), BF16),
        ]
        + Reduce.semaphores(count + 1)
        + Chain.semaphores(count + 5)
        + [dma((3,)), dma((4, 2)), dma((seq_size,)), dma((seq_count,)), dma((1,))],
        compiler_params=pltpu.CompilerParams(
            collective_id=1, has_side_effects=True, vmem_limit_bytes=VMEM_MAX
        ),
    )(
        query, key, value, ctx, grad_ctx, probs, vecs, inputs, qkv_full, resid, d_w1, d_wo, w2_part
    )


def widen_kernel(w2_in, w1_in, wo_in, qkv_in, vec_in, *outs):
    w2_out, w1_out, wo_out = outs[:3]
    mats, vecs = outs[3:6], outs[6:]
    feats = wo_in.shape[1]
    w2_out[...] = w2_in[...].astype(F32)
    w1_out[...] = w1_in[...].astype(F32)
    wo_out[...] = wo_in[...].astype(F32)
    for which, mat in enumerate(mats):
        for pair in range(feats // LANES):
            start = pair_column(feats, which, pair)
            mat[:, pair * LANES : (pair + 1) * LANES] = qkv_in[:, start : start + LANES].astype(F32)
    me = lax.axis_index("dp")
    part = feats // 8
    rows = vec_in[...].astype(F32)
    own = jnp.zeros((rows.shape[0], part), F32)
    long = jnp.zeros((1, 4 * part), F32)
    for k in range(8):
        own = jnp.where(me == k, rows[:, k * part : (k + 1) * part], own)
        row, start = 6 + k // 2, (k % 2) * 4 * part
        long = jnp.where(me == k, rows[row : row + 1, start : start + 4 * part], long)
    for k, row in enumerate((16, 17, 2, 0, 1, 5, 3, 4)):
        vecs[k][...] = own[row : row + 1, :]
    vecs[8][...] = long


def widen(w2_sum, w1_sum, wo_sum, qkv_sum, vec_sum):
    feats = wo_sum.shape[1]
    part = feats // 8

    def wide(*shape):
        return jax.ShapeDtypeStruct(shape, F32)

    return pl.pallas_call(
        widen_kernel,
        out_shape=[wide(*w2_sum.shape), wide(*w1_sum.shape)]
        + [wide(*wo_sum.shape)] * 4
        + [wide(1, part)] * 8
        + [wide(1, 4 * part)],
        compiler_params=pltpu.CompilerParams(vmem_limit_bytes=VMEM_LIMIT),
    )(w2_sum, w1_sum, wo_sum, qkv_sum, vec_sum)


def column_sum(rows):
    return jnp.sum(rows, axis=0, dtype=F32)


def per_device(mesh_shape, tokens, lengths, *rest):
    weights, upstream = rest[:15], rest[15]
    dp_size, seq_size = mesh_shape
    seq_count, row_count, feats = tokens.shape
    dp_index = lax.axis_index("dp")
    here = lax.axis_index("seq")
    spare = seq_size - seq_count

    def owner_shift(dp):
        return spare * (dp % 2)

    my_seq = jnp.clip(here - owner_shift(dp_index), 0, seq_count - 1)

    def owned_by(dp, pos):
        seq = pos - owner_shift(dp)
        return 0 <= seq < seq_count

    def shift_pairs(step, to_owner):
        pairs = []
        for dp in range(dp_size):
            for pos in range(seq_size):
                dest = (pos + step) % seq_size
                if owned_by(dp, dest if to_owner else pos):
                    pairs.append((dp * seq_size + pos, dp * seq_size + dest))
        return pairs

    def gather(piece):
        return lax.all_gather(piece, "dp", axis=0, tiled=True)

    def to_owners(blocks):
        pieces = []
        for step in range(seq_size):
            dest = (here + step) % seq_size
            seq = jnp.clip(dest - owner_shift(dp_index), 0, seq_count - 1)
            piece = lax.dynamic_index_in_dim(blocks, seq, 0, keepdims=False)
            if step == 0:
                owner = (here >= owner_shift(dp_index)) & (here < owner_shift(dp_index) + seq_count)
                piece = jnp.where(owner, piece, jnp.zeros_like(piece))
            else:
                piece = lax.ppermute(piece, ("dp", "seq"), shift_pairs(step, True))
            pieces.append(piece)
        order = (here - jnp.arange(seq_size)) % seq_size
        return jnp.take(jnp.stack(pieces), order, axis=0).reshape(-1, feats)

    def from_owners(rows):
        pieces = rows.reshape(seq_size, row_count, feats)
        arrived = []
        for step in range(seq_size):
            piece = lax.dynamic_index_in_dim(pieces, (here - step) % seq_size, 0, keepdims=False)
            if step:
                piece = lax.ppermute(piece, ("dp", "seq"), shift_pairs(seq_size - step, False))
            arrived.append(piece)
        stack = jnp.stack(arrived)
        order = (jnp.arange(seq_count) + owner_shift(dp_index) - here) % seq_size
        return jnp.take(stack, order, axis=0)

    wq, bq, wk, wv, bv, wo, bo, g1, b1, w1, c1, w2, c2, g2, b2 = weights
    shard_rows = feats // dp_size
    seq_len = seq_size * row_count
    direct = (dp_size, seq_size, feats, seq_len) == (8, 4, 768, 1024) and seq_count == 3
    vec_parts = (bq, bv, bo, g1, b1, c2, g2, b2, c1)
    vec_sizes = [item.shape[0] for item in vec_parts]
    vec_len = sum(vec_sizes)
    if not direct:
        packed = jnp.concatenate(vec_parts).astype(BF16)
        position = lax.iota(jnp.int32, seq_len)
        valid_len = lax.dynamic_index_in_dim(lengths, my_seq, 0, keepdims=False)
        key_bias = jnp.where(position < valid_len, 0.0, 8.0 * NEG_FILL).astype(F32)
        key_bias = key_bias.reshape(1, seq_len)
        qkv_mat = gather(jnp.concatenate([wq, wk, wv], axis=1).astype(BF16))
        packed = lax.all_gather(packed, "dp", axis=0, tiled=False)
        merge_mat, expand_mat, reduce_mat = [gather(item.astype(BF16)) for item in (wo, w1, w2)]
        vecs = []
        start = 0
        for size in vec_sizes:
            vecs.append(packed[:, start : start + size].reshape(1, -1).astype(F32))
            start += size
        bq, bv, bo, g1, b1, c2, g2, b2, c1 = vecs

    if direct:
        inputs, qkv_full, vec_full, w2_part, w1_part, wo_part = start_all(
            seq_size, tokens, (wq, wk, wv), [item.reshape(1, -1) for item in vec_parts], w2, w1, wo
        )
        query, key, value, ctx, probs, vec_rows, dy, w2_full, w1_full, wo_full = forward_all(
            seq_size, lengths, inputs, qkv_full, vec_full, upstream, w2_part, w1_part, wo_part
        )
        act, slope, out_rows, grad_resid2, normed1, inv1, second_sums = feed_forward(
            ctx, inputs, wo_full, vec_rows, w1_full, w2_full, dy
        )
        d_w1, grad_resid1, grad_ctx, d_wo, vec_sums, part_w2, output = feed_back(
            seq_size, seq_count, act, slope, w1_full, w2_full, grad_resid2, normed1, inv1, ctx,
            wo_full, vec_rows, second_sums, out_rows,
        )
        *sums, token_grad = backward_all(
            seq_size, seq_count, query, key, value, ctx, grad_ctx, probs, vec_sums, inputs,
            qkv_full, grad_resid1, d_w1, d_wo, part_w2,
        )
        sum_w2, sum_w1, s_wo, s_wq, s_wk, s_wv, *vec_sums = widen(*sums)
        vec_sums = [item.reshape(-1) for item in vec_sums]
        s_bq, s_bv, s_bo, s_g1, s_b1, s_c2, s_g2, s_b2, s_c1 = vec_sums
    else:
        inputs = to_owners(tokens)
        dy = to_owners(upstream).astype(F32)
        qkv = dot(inputs, qkv_mat, 1, 0)
        query = (qkv[:, :feats] + bq).astype(BF16)
        key = qkv[:, feats : 2 * feats].astype(BF16)
        value = (qkv[:, 2 * feats :] + bv).astype(BF16)
        ctx, probs = attend(key_bias, query, key, value)
        normed1, inv1 = normalize(inputs.astype(F32) + dot(ctx, merge_mat, 1, 0) + bo)
        hidden = normed1 * g1 + b1
        hidden_low = hidden.astype(BF16)
        pre = dot(hidden_low, expand_mat, 1, 0) + c1
        phi_cum = 0.5 * (1.0 + lax.erf(pre * INV_SQRT2))
        act = (pre * phi_cum).astype(BF16)
        slope = (phi_cum + pre * (INV_SQRT_2PI * jnp.exp(-0.5 * pre * pre))).astype(BF16)
        normed2, inv2 = normalize(hidden + dot(act, reduce_mat, 1, 0) + c2)
        result = (normed2 * g2 + b2).astype(BF16)
        output = from_owners(result)

        d_g2 = column_sum(dy * normed2)
        d_b2 = column_sum(dy)
        grad_resid2 = normalize_back(normed2, inv2, g2 * dy)
        grad_ffn = grad_resid2.astype(BF16)
        d_w2 = dot(act, grad_ffn, 0, 0).astype(BF16)
        d_c2 = column_sum(grad_ffn)
        grad_pre = (dot(grad_ffn, reduce_mat, 1, 1) * slope.astype(F32)).astype(BF16)
        d_w1 = dot(hidden_low, grad_pre, 0, 0).astype(BF16)
        d_c1 = column_sum(grad_pre)
        grad_hidden = grad_resid2 + dot(grad_pre, expand_mat, 1, 1)
        d_g1 = column_sum(grad_hidden * normed1)
        d_b1 = column_sum(grad_hidden)
        grad_resid1 = normalize_back(normed1, inv1, g1 * grad_hidden)
        grad_att = grad_resid1.astype(BF16)
        d_wo = dot(ctx, grad_att, 0, 0).astype(BF16)
        d_bo = column_sum(grad_att)
        grad_ctx = dot(grad_att, merge_mat, 1, 1).astype(BF16)
        grad_qkv = attend_back(query, key, value, ctx, grad_ctx, probs)
        token_rows = grad_resid1
        d_qkv = []
        for which in range(3):
            mat = qkv_mat[:, which * feats : (which + 1) * feats]
            token_rows = token_rows + dot(grad_qkv[which], mat, 1, 1)
            d_qkv.append(dot(inputs, grad_qkv[which], 0, 0).astype(BF16))
        d_bq = column_sum(grad_qkv[0])
        d_bv = column_sum(grad_qkv[2])
        token_grad = from_owners(token_rows.astype(BF16))
        vec_grads = (d_bq, d_bv, d_bo, d_g1, d_b1, d_c2, d_g2, d_b2, d_c1)
        vec_pack = jnp.concatenate([item.reshape(dp_size, -1) for item in vec_grads], axis=1)
        vec_cols = -(-vec_len // (shard_rows * LANES)) * LANES
        vec_pack = jnp.pad(vec_pack, ((0, 0), (0, shard_rows * vec_cols - vec_len)))
        vec_pack = vec_pack.reshape(feats, vec_cols).astype(BF16)

        def reduce(full):
            own = lax.psum_scatter(full, "dp", scatter_dimension=0, tiled=True)
            return lax.psum(own, "seq").astype(F32)

        sum_w2 = reduce(d_w2)
        sum_w1 = reduce(d_w1)
        sum_rest = reduce(jnp.concatenate([d_wo] + d_qkv + [vec_pack], axis=1))
        s_wo, s_wq, s_wk, s_wv = [sum_rest[:, i * feats : (i + 1) * feats] for i in range(4)]
        flat = sum_rest[:, 4 * feats :].reshape(-1)
        out_vecs = []
        start = 0
        for size in vec_sizes:
            out_vecs.append(flat[start : start + size])
            start += size
        s_bq, s_bv, s_bo, s_g1, s_b1, s_c2, s_g2, s_b2, s_c1 = out_vecs
    return (
        output,
        token_grad,
        s_wq,
        s_bq,
        s_wk,
        s_wv,
        s_bv,
        s_wo,
        s_bo,
        s_g1,
        s_b1,
        sum_w1,
        s_c1,
        sum_w2,
        s_c2,
        s_g2,
        s_b2,
    )


def solution(mesh):
    rows, mat, vec = P("dp", "seq", None), P("dp", None), P("dp")
    params = (mat, vec, mat, mat, vec, mat, vec, vec, vec, mat, vec, mat, vec, vec, vec)
    return jax.shard_map(
        functools.partial(per_device, (mesh.shape["dp"], mesh.shape["seq"])),
        mesh=mesh,
        in_specs=(rows, vec) + params + (rows,),
        out_specs=(rows, rows) + params,
        check_vma=False,
    )
```

```python
import functools

import jax
import jax.numpy as jnp
from jax import lax
from jax.experimental import pallas as pl
from jax.experimental.pallas import tpu as pltpu
from jax.sharding import PartitionSpec as P

HEAD = 64
LANES = 128
EPS = 1e-12
NEG_FILL = -1000000000.0
SCALE2 = 0.125 * 1.4426950408889634
F32 = jnp.float32
BF16 = jnp.bfloat16
VMEM_LIMIT = 60 * 1024 * 1024
VMEM_MAX = 67043328


def dot(left, right, left_dim, right_dim):
    return lax.dot_general(
        left, right, (((left_dim,), (right_dim,)), ((), ())), preferred_element_type=F32
    )


def attend_kernel(bias_ref, q_ref, k_ref, v_ref, ctx_ref, probs_ref, *, rows_blk):
    seq_len = q_ref.shape[0]
    lane = lax.broadcasted_iota(jnp.int32, (1, LANES), 1)
    bias = bias_ref[...]
    for blk in range(seq_len // rows_blk):
        rows = pl.ds(blk * rows_blk, rows_blk)
        query = q_ref[rows, :]
        mixed = []
        for head in range(2):
            mine = (lane < HEAD) if head == 0 else (lane >= HEAD)
            query_h = jnp.where(mine, query, jnp.zeros_like(query))
            score = dot(query_h, k_ref[...], 1, 1) + bias
            top = jnp.max(score, axis=1, keepdims=True)
            expo = jnp.exp2((score - top) * SCALE2)
            total = jnp.sum(expo, axis=1, keepdims=True)
            probs = (expo * (1.0 / total)).astype(BF16)
            probs_ref[head, rows, :] = probs
            mixed.append(dot(probs, v_ref[...], 1, 0))
        ctx_ref[rows, :] = jnp.where(lane < HEAD, mixed[0], mixed[1]).astype(BF16)


def attend(bias, query, key, value):
    seq_len, feats = query.shape
    cols = pl.BlockSpec((seq_len, LANES), lambda g: (0, g))
    return pl.pallas_call(
        functools.partial(attend_kernel, rows_blk=min(512, seq_len)),
        grid=(feats // LANES,),
        in_specs=[pl.BlockSpec((1, seq_len), lambda g: (0, 0)), cols, cols, cols],
        out_specs=[cols, pl.BlockSpec((2, seq_len, seq_len), lambda g: (g, 0, 0))],
        out_shape=[
            jax.ShapeDtypeStruct((seq_len, feats), BF16),
            jax.ShapeDtypeStruct((feats // HEAD, seq_len, seq_len), BF16),
        ],
        compiler_params=pltpu.CompilerParams(vmem_limit_bytes=VMEM_LIMIT),
    )(bias, query, key, value)


def attend_back_pair(
    q_ref, k_ref, v_ref, ctx_ref, grad_ref, probs_ref, store, key_acc, value_acc, rows_blk,
    between=None,
):
    seq_len = q_ref.shape[0]
    lane = lax.broadcasted_iota(jnp.int32, (1, LANES), 1)
    for blk in range(seq_len // rows_blk):
        rows = pl.ds(blk * rows_blk, rows_blk)
        query = q_ref[rows, :]
        grad = grad_ref[rows, :]
        overlap = ctx_ref[rows, :].astype(F32) * grad.astype(F32)
        query_t = query.T
        grad_t = grad.T
        grad_query = []
        for head in range(2):
            mine = (lane < HEAD) if head == 0 else (lane >= HEAD)
            part = slice(head * HEAD, (head + 1) * HEAD)
            grad_h = jnp.where(mine, grad, jnp.zeros_like(grad))
            inner = jnp.sum(jnp.where(mine, overlap, 0.0), axis=1, keepdims=True)
            probs = probs_ref[head, rows, :]
            grad_probs = dot(grad_h, v_ref[...], 1, 1)
            grad_score = (probs.astype(F32) * (grad_probs - inner)).astype(BF16)
            grad_query.append(dot(grad_score, k_ref[...], 1, 0))
            grad_key = dot(query_t[part], grad_score, 1, 0)
            grad_value = dot(grad_t[part], probs, 1, 0)
            if blk == 0:
                key_acc[head] = grad_key
                value_acc[head] = grad_value
            else:
                key_acc[head] += grad_key
                value_acc[head] += grad_value
        mixed = jnp.where(lane < HEAD, grad_query[0], grad_query[1])
        store(0, rows, (0.125 * mixed).astype(BF16))
        if between is not None:
            between(blk)
    everything = pl.ds(0, seq_len)
    grad_key = jnp.concatenate([key_acc[0], key_acc[1]], axis=0)
    store(1, everything, (0.125 * grad_key).T.astype(BF16))
    grad_value = jnp.concatenate([value_acc[0], value_acc[1]], axis=0)
    store(2, everything, grad_value.T.astype(BF16))


def attend_back_kernel(
    q_ref, k_ref, v_ref, ctx_ref, grad_ref, probs_ref, out_ref, key_acc, value_acc, *, rows_blk
):
    def store(which, rows, values):
        out_ref[which, rows, :] = values

    attend_back_pair(
        q_ref, k_ref, v_ref, ctx_ref, grad_ref, probs_ref, store, key_acc, value_acc, rows_blk
    )


def attend_back(query, key, value, ctx, grad_ctx, probs):
    seq_len, feats = ctx.shape
    cols = pl.BlockSpec((seq_len, LANES), lambda g: (0, g))
    return pl.pallas_call(
        functools.partial(attend_back_kernel, rows_blk=min(512, seq_len)),
        grid=(feats // LANES,),
        in_specs=[cols] * 5 + [pl.BlockSpec((2, seq_len, seq_len), lambda g: (g, 0, 0))],
        out_specs=pl.BlockSpec((3, seq_len, LANES), lambda g: (0, 0, g)),
        out_shape=jax.ShapeDtypeStruct((3, seq_len, feats), BF16),
        scratch_shapes=[pltpu.VMEM((2, HEAD, seq_len), F32)] * 2,
        compiler_params=pltpu.CompilerParams(vmem_limit_bytes=VMEM_LIMIT),
    )(query, key, value, ctx, grad_ctx, probs)


MESH = pl.DeviceIdType.MESH


def remote(src, dst, send, recv, device):
    return pltpu.make_async_remote_copy(
        src_ref=src, dst_ref=dst, send_sem=send, recv_sem=recv,
        device_id=device, device_id_type=MESH,
    )


class Place:
    def __init__(self, seq_size, seq_count):
        self.me = me = lax.axis_index("dp")
        self.here = here = lax.axis_index("seq")
        core, x_at, y_at = me % 2, (me // 2) % 2, (me // 4) % 2
        self.to_core, self.to_x, self.to_y = 1 - 2 * core, 2 - 4 * x_at, 4 - 8 * y_at
        self.core_dev = (me + self.to_core, here)
        self.x_dev = (me + self.to_x, here)
        self.y_dev = (me + self.to_y, here)
        self.shift = (seq_size - seq_count) * core
        self.my_seq = here - self.shift
        self.is_owner = (self.my_seq >= 0) & (self.my_seq < seq_count)
        self.seq_size, self.seq_count = seq_size, seq_count

    def barrier(self):
        barrier = pltpu.get_barrier_semaphore()
        for device in (self.core_dev, self.x_dev, self.y_dev):
            pl.semaphore_signal(barrier, inc=1, device_id=device, device_id_type=MESH)
        for step in range(1, self.seq_size):
            pl.semaphore_signal(
                barrier, inc=1, device_id=(self.me, (self.here + step) % self.seq_size),
                device_id_type=MESH,
            )
        pl.semaphore_wait(barrier, 3 + self.seq_size - 1)


class Gather:
    def __init__(self, place, full, own, sems, index):
        self.place, self.full, self.own, self.index = place, full, own, index
        self.send_sem, self.recv_sem, self.core_send, self.core_recv = sems

    def half(self, which):
        count = self.full.shape[1] // 2
        return pl.ds(which * count, count)

    def piece(self, p):
        at = self.place
        rows = self.half(p % 2)
        shard = at.me + (0, 0, 0, 0, at.to_x, at.to_y)[p]
        src = self.own.at[rows] if p < 4 else self.full.at[shard, rows]
        device = (at.x_dev, at.y_dev, at.y_dev, at.x_dev, at.y_dev, at.x_dev)[p]
        return remote(
            src, self.full.at[shard, rows],
            self.send_sem.at[self.index, p], self.recv_sem.at[self.index, p], device,
        )

    def core_piece(self, p):
        at = self.place
        if p == 6:
            src, dst = self.own, self.full.at[at.me]
        else:
            across = at.to_x + at.to_y
            shard = at.me + (at.to_x, at.to_y, at.to_y, at.to_x, across, across)[p]
            src = dst = self.full.at[shard, self.half(p % 2)]
        return remote(
            src, dst, self.core_send.at[self.index, p], self.core_recv.at[self.index, p],
            at.core_dev,
        )

    def start(self, *pieces):
        for p in pieces:
            self.piece(p).start()

    def arrive(self, *pieces):
        for p in pieces:
            self.piece(p).wait_recv()

    def to_core(self, *pieces):
        for p in pieces:
            self.core_piece(p).start()

    def finish(self, pieces, core_pieces):
        for p in core_pieces:
            self.core_piece(p).wait_recv()
        for p in pieces:
            self.piece(p).wait_send()
        for p in core_pieces:
            self.core_piece(p).wait_send()


class RowsIn:
    def __init__(self, place, blocks, whole, buf, sems):
        self.place, self.blocks, self.whole, self.buf = place, blocks, whole, buf
        self.send_sem, self.recv_sem, self.local_sem = sems
        self.rows = blocks.shape[1]

    def to(self, seq, source):
        at = self.place
        return remote(
            self.blocks.at[seq], self.whole.at[pl.ds(source * self.rows, self.rows)],
            self.send_sem.at[seq], self.recv_sem.at[source], (at.me, seq + at.shift),
        )

    def own(self, count):
        at = self.place

        def out(pos, k):
            return pltpu.make_async_copy(
                self.buf, self.whole.at[pl.ds(pos * self.rows, self.rows)], self.local_sem.at[k]
            )

        @pl.when(at.is_owner)
        def _():
            load = pltpu.make_async_copy(self.blocks.at[at.my_seq], self.buf, self.local_sem.at[0])
            load.start()
            load.wait()
            out(at.here, 1).start()
            out(at.here, 1).wait()

        @pl.when(jnp.logical_not(at.is_owner))
        def _():
            self.buf[...] = jnp.zeros_like(self.buf)
            for pos in range(at.seq_size):
                out(pos, pos).start()
            for pos in range(at.seq_size):
                out(pos, pos).wait()

    def start(self):
        at = self.place
        for seq in range(at.seq_count):

            @pl.when(at.here != seq + at.shift)
            def _():
                self.to(seq, at.here).start()

    def finish(self):
        at = self.place

        @pl.when(at.is_owner)
        def _():
            for pos in range(at.seq_size):

                @pl.when(at.here != pos)
                def _():
                    remote(
                        self.blocks.at[0], self.whole.at[pl.ds(pos * self.rows, self.rows)],
                        self.send_sem.at[0], self.recv_sem.at[pos],
                        (at.me, (at.here + 1) % at.seq_size),
                    ).wait_recv()

        for seq in range(at.seq_count):

            @pl.when(at.here != seq + at.shift)
            def _():
                self.to(seq, at.here).wait_send()


def start_kernel(
    seq_size, seq_count, tokens, wq, wk, wv, w2, w1, wo, *refs,
):
    vec_refs, refs = refs[:9], refs[9:]
    rows_out, qkv_full, vec_full, w2_full, w1_full, wo_full = refs[:6]
    qkv_low, w2_low, w1_low, wo_low, row_buf, vec_wide, vecs = refs[6:13]
    row_send, row_recv, row_local, sem_a, sem_b, sem_c, sem_d, own_sem = refs[13:]
    place = Place(seq_size, seq_count)
    sems = (sem_a, sem_b, sem_c, sem_d)
    rows = RowsIn(place, tokens, rows_out, row_buf, (row_send, row_recv, row_local))
    first = [
        Gather(place, qkv_full, qkv_low, sems, 0),
        Gather(place, vec_full, vecs, sems, 1),
    ]
    later = [
        Gather(place, w2_full, w2_low, sems, 2),
        Gather(place, w1_full, w1_low, sems, 3),
        Gather(place, wo_full, wo_low, sems, 4),
    ]
    place.barrier()
    rows.start()
    feats = wq.shape[1]
    vec_wide[...] = jnp.zeros_like(vec_wide)
    for k, item in enumerate(vec_refs[:8]):
        vec_wide[k : k + 1, 0 : item.shape[1]] = item[...]
    for k in range(vec_refs[8].shape[1] // LANES):
        vec_wide[8 + k : 9 + k, :] = vec_refs[8][:, k * LANES : (k + 1) * LANES]
    vecs[...] = vec_wide[...].astype(BF16)
    for k, item in enumerate((wq, wk, wv)):
        qkv_low[:, k * feats : (k + 1) * feats] = item[...].astype(BF16)
    for item in first:
        item.start(0, 1)
    for item in first:
        item.start(2, 3)
        item.to_core(6)
    w2_low[...] = w2[...].astype(BF16)
    w1_low[...] = w1[...].astype(BF16)
    wo_low[...] = wo[...].astype(BF16)
    keep = [
        pltpu.make_async_copy(item.own, item.full.at[place.me], own_sem.at[item.index])
        for item in first + later
    ]
    for copy in keep:
        copy.start()
    for item in first:
        item.arrive(0, 1)
        item.start(4, 5)
        item.to_core(0, 1)
    for item in later:
        item.start(0, 1)
    rows.own(seq_size)
    for item in first:
        item.arrive(2, 3)
        item.to_core(2, 3)
    for item in first:
        item.arrive(4, 5)
        item.to_core(4, 5)
    for item in first:
        item.finish(range(6), range(7))
    for item in later:
        item.arrive(0, 1)
        for p in (0, 1):
            item.piece(p).wait_send()
    for copy in keep:
        copy.wait()
    rows.finish()


def start_all(seq_size, tokens, qkv_parts, vecs, w2, w1, wo):
    seq_count, blk, feats = tokens.shape
    any_spec = pl.BlockSpec(memory_space=pl.ANY)
    vmem_spec = pl.BlockSpec(memory_space=pltpu.VMEM)
    dma = pltpu.SemaphoreType.DMA
    shard = qkv_parts[0].shape[0]

    def full(rows, cols):
        return jax.ShapeDtypeStruct((8, rows, cols), BF16)

    return pl.pallas_call(
        functools.partial(start_kernel, seq_size, seq_count),
        in_specs=[any_spec] + [vmem_spec] * (6 + len(vecs)),
        out_specs=[any_spec] * 6,
        out_shape=[
            jax.ShapeDtypeStruct((seq_size * blk, feats), BF16),
            full(shard, 3 * feats), full(32, LANES), full(*w2.shape), full(*w1.shape),
            full(*wo.shape),
        ],
        scratch_shapes=[
            pltpu.VMEM((shard, 3 * feats), BF16), pltpu.VMEM(w2.shape, BF16),
            pltpu.VMEM(w1.shape, BF16), pltpu.VMEM(wo.shape, BF16), pltpu.VMEM((blk, feats), BF16),
            pltpu.VMEM((32, LANES), F32), pltpu.VMEM((32, LANES), BF16),
            dma((seq_count,)), dma((seq_size,)), dma((seq_size,)),
            dma((5, 6)), dma((5, 6)), dma((5, 7)), dma((5, 7)), dma((5,)),
        ],
        compiler_params=pltpu.CompilerParams(
            collective_id=2, has_side_effects=True, vmem_limit_bytes=VMEM_LIMIT
        ),
    )(tokens, *qkv_parts, w2, w1, wo, *vecs)


BQ, BV, BO, G1, B1, C2, G2, B2, C1 = range(9)


def unpack_vectors(full, out):
    shards, _, _ = full.shape
    feats = out.shape[1]
    part = feats // shards
    lane = lax.broadcasted_iota(jnp.int32, (LANES, feats), 0)
    column = lax.broadcasted_iota(jnp.int32, (LANES, feats), 1)
    rows = jnp.zeros((16, feats), F32)
    for k in range(shards):
        place = ((lane < part) & (column == lane + k * part)).astype(BF16)
        rows = rows + dot(full[k, 0:16, :], place, 1, 0)
    out[...] = rows
    long = feats * 4 // shards
    for k in range(shards):
        row, start = C1 + k * long // feats, k * long % feats
        for j in range(long // LANES):
            out[row : row + 1, start + j * LANES : start + (j + 1) * LANES] = full[
                k, 8 + j : 9 + j, :
            ].astype(F32)


def forward_kernel(
    seq_size, seq_count, rows_blk,
    len_ref, x_ref, wq_ref, wk_ref, wv_ref, vec_full, upstream, w2_in, w1_in, wo_in,
    q_ref, k_ref, v_ref, ctx_ref, probs_ref, vec_out, dy_out, w2_full, w1_full, wo_full,
    bias_ref, row_buf, row_send, row_recv, row_local, sem_a, sem_b, sem_c, sem_d,
):
    step = pl.program_id(0)
    last = pl.num_programs(0) - 1
    place = Place(seq_size, seq_count)
    sems = (sem_a, sem_b, sem_c, sem_d)
    rows = RowsIn(place, upstream, dy_out, row_buf, (row_send, row_recv, row_local))
    later = [
        Gather(place, full, full.at[place.me], sems, k)
        for k, full in enumerate((w2_full, w1_full, wo_full))
    ]

    @pl.when(step == 0)
    def _():
        place.barrier()
        for item in later:
            item.start(2, 3)
        for item in later:
            item.start(4, 5)
        rows.start()
        for item in later:
            item.to_core(6, 0, 1)
        rows.own(seq_size)
        unpack_vectors(vec_full, vec_out)
        valid = len_ref[jnp.clip(place.my_seq, 0, seq_count - 1)]
        position = lax.broadcasted_iota(jnp.int32, bias_ref.shape, 1)
        bias_ref[...] = jnp.where(position < valid, 0.0, 8.0 * NEG_FILL)

    x_rows = x_ref[...]
    depth = x_rows.shape[1]
    column = pl.ds(pl.multiple_of(step * LANES, LANES), LANES)
    mats = [ref[...].reshape(depth, LANES) for ref in (wq_ref, wk_ref, wv_ref)]
    both = dot(x_rows, jnp.concatenate(mats, axis=1), 1, 0)
    q_ref[...] = (both[:, :LANES] + vec_out[BQ : BQ + 1, column]).astype(BF16)
    k_ref[...] = both[:, LANES : 2 * LANES].astype(BF16)
    v_ref[...] = (both[:, 2 * LANES :] + vec_out[BV : BV + 1, column]).astype(BF16)
    attend_kernel(bias_ref, q_ref, k_ref, v_ref, ctx_ref, probs_ref, rows_blk=rows_blk)

    @pl.when(step == last - 1)
    def _():
        for item in later:
            item.arrive(2, 3)
            item.to_core(2, 3)

    @pl.when(step == last)
    def _():
        for item in later:
            item.arrive(4, 5)
            item.to_core(4, 5)
        for item in later:
            item.finish(range(2, 6), range(7))
        rows.finish()


def forward_all(seq_size, lengths, rows, qkv_full, vec_full, upstream, w2_full, w1_full, wo_full):
    seq_len, feats = rows.shape
    seq_count, blk, _ = upstream.shape
    pairs = feats // LANES
    shard = qkv_full.shape[1]
    any_spec = pl.BlockSpec(memory_space=pl.ANY)
    dma = pltpu.SemaphoreType.DMA
    cols = pl.BlockSpec((seq_len, LANES), lambda g: (0, g))

    def mat(which):
        return pl.BlockSpec((8, shard, LANES), lambda g, w=which: (0, 0, w * pairs + g))

    fulls = [w2_full, w1_full, wo_full]
    flat = jax.ShapeDtypeStruct((seq_len, feats), BF16)
    return pl.pallas_call(
        functools.partial(forward_kernel, seq_size, seq_count, min(512, seq_len)),
        grid=(pairs,),
        in_specs=[
            pl.BlockSpec(memory_space=pltpu.SMEM),
            pl.BlockSpec((seq_len, feats), lambda g: (0, 0)),
            mat(0), mat(1), mat(2), pl.BlockSpec(vec_full.shape, lambda g: (0, 0, 0)),
        ]
        + [any_spec] * 4,
        out_specs=[cols] * 4
        + [
            pl.BlockSpec((2, seq_len, seq_len), lambda g: (g, 0, 0)),
            pl.BlockSpec((16, feats), lambda g: (0, 0)),
        ]
        + [any_spec] * 4,
        out_shape=[flat] * 4
        + [
            jax.ShapeDtypeStruct((feats // HEAD, seq_len, seq_len), BF16),
            jax.ShapeDtypeStruct((16, feats), F32),
            flat,
        ]
        + [jax.ShapeDtypeStruct(item.shape, BF16) for item in fulls],
        scratch_shapes=[
            pltpu.VMEM((1, seq_len), F32), pltpu.VMEM((blk, feats), BF16),
            dma((seq_count,)), dma((seq_size,)), dma((seq_size,)),
            dma((3, 6)), dma((3, 6)), dma((3, 7)), dma((3, 7)),
        ],
        input_output_aliases={7: 7, 8: 8, 9: 9},
        compiler_params=pltpu.CompilerParams(
            collective_id=3, has_side_effects=True, vmem_limit_bytes=VMEM_LIMIT
        ),
    )(lengths, rows, qkv_full, qkv_full, qkv_full, vec_full, upstream, *fulls)


def add_rows(dest, first, *others, start=0, count=None):
    count = dest.shape[0] if count is None else count
    size = 48 if count % 48 == 0 else min(count, 64)

    def body(i, carry):
        for k in range(size // 16):
            to = pl.ds(pl.multiple_of(start + i * size + k * 16, 16), 16)
            frm = pl.ds(pl.multiple_of(i * size + k * 16, 16), 16)
            if len(others) == 1:
                dest[to, :] = first[to, :] + others[0][frm, :]
            else:
                value = first[to, :].astype(F32)
                for other in others:
                    value = value + other[frm, :].astype(F32)
                dest[to, :] = value.astype(dest.dtype)
        return carry

    lax.fori_loop(0, count // size, body, 0, unroll=count == size)


class Chain:
    def __init__(self, place, mine, passed, arrived, total, sems, index):
        self.place, self.mine, self.passed, self.arrived = place, mine, passed, arrived
        self.total, self.index = total, index
        self.z_send, self.z_recv = sems

    def copy(self, way, src):
        at = self.place
        return remote(
            src, self.arrived.at[way], self.z_send.at[self.index, way],
            self.z_recv.at[self.index, way], (at.me, at.here + 1 - 2 * way),
        )

    def hops(self, way):
        at = self.place
        return at.here if way == 0 else at.seq_size - 1 - at.here

    def hop(self, hop):
        here, last = self.place.here, self.place.seq_size - 1

        @pl.when((here == hop) | (here == last - hop))
        def _():
            way = jnp.where(here == hop, 0, 1)
            passed = self.passed.at[way]
            if hop == 0:
                self.copy(way, self.mine).start()
            else:
                self.copy(way, passed).wait_recv()
                if hop < last:
                    add_rows(passed, self.mine, self.arrived.at[way])
                    self.copy(way, passed).start()

    def finish(self):
        last = self.place.seq_size - 1
        here = self.place.here
        inner = (here > 0) & (here < last)

        @pl.when(jnp.logical_not(inner))
        def _():
            add_rows(self.total, self.mine, self.arrived.at[jnp.where(here == 0, 1, 0)])

        @pl.when(inner)
        def _():
            add_rows(self.total, self.mine, self.arrived.at[0], self.arrived.at[1])

    def drain(self):
        for way in range(2):

            @pl.when(self.hops(way) < self.place.seq_size - 1)
            def _():
                self.copy(way, self.mine).wait_send()

    @staticmethod
    def semaphores(count):
        dma = pltpu.SemaphoreType.DMA
        return [dma((count, 2)), dma((count, 2))]


class Carried:
    def __init__(self, place, source, result, bufs, sems, copy_sems, index, slot):
        mine, passed, arrived, total = bufs
        self.chain = Chain(place, mine, passed, arrived, total, sems, index)
        self.load = pltpu.make_async_copy(source, mine, copy_sems.at[slot, 0])
        self.out = pltpu.make_async_copy(total, result, copy_sems.at[slot, 1])

    def begin(self):
        self.load.wait()
        self.chain.hop(0)

    def hop(self, hop):
        self.chain.hop(hop)

    def finish(self):
        self.chain.finish()
        self.out.start()

    def drain(self):
        self.chain.drain()
        self.out.wait()


class Reduce:
    def __init__(self, place, source, result, bufs, sems, index, z_arrived=None, z_sems=None):
        self.place, self.source, self.index = place, source, index
        self.own, self.other, self.first_x, self.first_y, self.second = bufs
        (
            self.own_sem, self.core_send, self.core_recv, self.one_send, self.one_recv,
            self.two_send, self.two_recv,
        ) = sems
        at = place
        self.apart = [(r % 2) * at.to_x + (r // 2) * at.to_y for r in range(4)]
        self.rows = self.own.shape[1]
        self.half = self.rows // 2
        self.chain, total = None, self.own.at[0]
        if z_arrived is not None:
            total = self.own.at[3]
            self.chain = Chain(place, self.own.at[0], self.other, z_arrived, total, z_sems, index)
        self.out = pltpu.make_async_copy(total, result, self.own_sem.at[index, 3])

    def keep_copy(self, r):
        return pltpu.make_async_copy(
            self.source(self.place.me + self.apart[r]), self.own.at[r],
            self.own_sem.at[self.index, r],
        )

    def core_copy(self, r):
        at = self.place
        return remote(
            self.source(at.me + at.to_core + self.apart[r]), self.other.at[r],
            self.core_send.at[self.index, r], self.core_recv.at[self.index, r], at.core_dev,
        )

    def one_copy(self, way, k):
        half = self.half
        if way == 0:
            src, dst = self.own.at[(1, 3)[k], pl.ds(0, half)], self.first_x.at[k]
        else:
            src, dst = self.own.at[(2, 3)[k], pl.ds(half, half)], self.first_y.at[k]
        return remote(
            src, dst, self.one_send.at[self.index, way, k], self.one_recv.at[self.index, way, k],
            (self.place.x_dev, self.place.y_dev)[way],
        )

    def two_copy(self, way):
        src = self.own.at[(2, 1)[way], pl.ds(way * self.half, self.half)]
        return remote(
            src, self.second.at[way], self.two_send.at[self.index, way],
            self.two_recv.at[self.index, way], (self.place.y_dev, self.place.x_dev)[way],
        )

    def begin(self):
        for r in (3, 1, 2, 0):
            self.core_copy(r).start()
            self.keep_copy(r).start()

    def core_stage(self):
        for r in (3, 1, 2, 0):
            self.keep_copy(r).wait()
            self.core_copy(r).wait_recv()
            add_rows(self.own.at[r], self.own.at[r], self.other.at[r])
            if r == 3:
                self.one_copy(0, 1).start()
                self.one_copy(1, 1).start()
            elif r == 1:
                self.one_copy(0, 0).start()
            elif r == 2:
                self.one_copy(1, 0).start()

    def one_stage(self):
        firsts = (self.first_x, self.first_y)
        for k in (1, 0):
            for way in range(2):
                self.one_copy(way, k).wait_recv()
                dest = self.own.at[(2, 1)[way] if k else 0]
                add_rows(dest, dest, firsts[way].at[k], start=way * self.half, count=self.half)
                if k:
                    self.two_copy(way).start()

    def two_stage(self):
        mine = self.own.at[0]
        for way in range(2):
            self.two_copy(way).wait_recv()
            add_rows(mine, mine, self.second.at[way], start=way * self.half, count=self.half)
        if self.chain is not None:
            self.chain.hop(0)

    def hop(self, hop):
        self.chain.hop(hop)

    def finish(self):
        if self.chain is not None:
            self.one_copy(0, 1).wait_send()
            self.one_copy(1, 1).wait_send()
            self.chain.finish()
        self.out.start()

    def drain(self):
        for r in range(4):
            self.core_copy(r).wait_send()
        for way in range(2):
            self.one_copy(way, 0).wait_send()
            if self.chain is None:
                self.one_copy(way, 1).wait_send()
            self.two_copy(way).wait_send()
        if self.chain is not None:
            self.chain.drain()
        self.out.wait()

    @staticmethod
    def scratch(count, rows, width):
        return [
            pltpu.VMEM((count, lead, rows // split, width), BF16)
            for lead, split in ((4, 1), (4, 1), (2, 2), (2, 2), (2, 2))
        ]

    @staticmethod
    def semaphores(count):
        dma = pltpu.SemaphoreType.DMA
        return [
            dma((count, 4)), dma((count, 4)), dma((count, 4)),
            dma((count, 2, 2)), dma((count, 2, 2)), dma((count, 2)), dma((count, 2)),
        ]


class RowsOut:
    def __init__(self, place, rows, blocks, sems):
        self.place, self.rows, self.blocks = place, rows, blocks
        self.send_sem, self.recv_sem, self.local_sem = sems
        self.blk = blocks.shape[1]

    def part(self, pos):
        return self.rows.at[pl.ds(pos * self.blk, self.blk)]

    def copy(self, pos):
        at = self.place
        return remote(
            self.part(pos), self.blocks.at[at.my_seq], self.send_sem.at[pos],
            self.recv_sem.at[at.my_seq], (at.me, pos),
        )

    def keep(self, pos):
        return pltpu.make_async_copy(
            self.part(pos), self.blocks.at[self.place.my_seq], self.local_sem.at[0]
        )

    def start(self, pos):
        at = self.place

        @pl.when(at.is_owner & (at.here != pos))
        def _():
            self.copy(pos).start()

        @pl.when(at.is_owner & (at.here == pos))
        def _():
            self.keep(pos).start()

    def finish(self):
        at = self.place
        for seq in range(at.seq_count):

            @pl.when(at.here != seq + at.shift)
            def _():
                remote(
                    self.part(0), self.blocks.at[seq], self.send_sem.at[0], self.recv_sem.at[seq],
                    (at.me, (at.here + 1) % at.seq_size),
                ).wait_recv()

        @pl.when(at.is_owner)
        def _():
            self.keep(0).wait()
            for pos in range(at.seq_size):

                @pl.when(at.here != pos)
                def _():
                    self.copy(pos).wait_send()


INV_SQRT2 = 0.7071067811865476
INV_SQRT_2PI = 0.3989422804014327


def normalize(resid):
    centre = resid - jnp.mean(resid, axis=-1, keepdims=True)
    inv = lax.rsqrt(jnp.mean(centre * centre, axis=-1, keepdims=True) + EPS)
    return centre * inv, inv


def normalize_back(normed, inv, grad_normed):
    mean_grad = jnp.mean(grad_normed, axis=-1, keepdims=True)
    mean_both = jnp.mean(grad_normed * normed, axis=-1, keepdims=True)
    return inv * (grad_normed - mean_grad - normed * mean_both)


def gelu_parts(pre):
    cumulative = 0.5 * (1.0 + lax.erf(pre * INV_SQRT2))
    slope = cumulative + pre * (INV_SQRT_2PI * jnp.exp(-0.5 * pre * pre))
    return pre * cumulative, slope


def feed_kernel(
    rows_blk, ctx_ref, x_ref, wo_ref, vec_ref, w1_ref, w2_ref, dy_ref,
    act_ref, slope_ref, out_ref, resid_ref, normed_ref, inv_ref, vec_out,
    hidden_low,
):
    step = pl.program_id(0)
    seq_len, feats = x_ref.shape
    width = slope_ref.shape[1]
    parts = act_ref.shape[0]
    blocks = [pl.ds(i * rows_blk, rows_blk) for i in range(seq_len // rows_blk)]

    def vec(k):
        return vec_ref[k : k + 1, :]

    @pl.when(step == 0)
    def _():
        merge = wo_ref[...].reshape(feats, feats)
        for rows in blocks:
            resid = x_ref[rows, :].astype(F32) + (dot(ctx_ref[rows, :], merge, 1, 0) + vec(BO))
            normed, inv = normalize(resid)
            normed_ref[rows, :] = normed
            inv_ref[rows, :] = jnp.broadcast_to(inv, (rows_blk, LANES))
            hidden_low[rows, :] = (normed * vec(G1) + vec(B1)).astype(BF16)
            resid_ref[rows, :] = jnp.zeros((rows_blk, feats), F32)

    expand = w1_ref[...].reshape(feats, width)
    shrink = w2_ref[...].reshape(width, feats)
    shift = vec_ref[pl.ds(C1 + step, 1), :]
    for rows in blocks:
        act, slope = gelu_parts(dot(hidden_low[rows, :], expand, 1, 0) + shift)
        act_low = act.astype(BF16)
        for k in range(width // LANES):
            column = k // parts * LANES
            act_ref[k % parts, rows, column : column + LANES] = act_low[
                :, k * LANES : (k + 1) * LANES
            ]
        slope_ref[rows, :] = slope.astype(BF16)
        resid_ref[rows, :] += dot(act_low, shrink, 1, 0)

    @pl.when(step == pl.num_programs(0) - 1)
    def _():
        sums = [jnp.zeros((1, feats), F32)] * 3
        for rows in blocks:
            hidden = normed_ref[rows, :] * vec(G1) + vec(B1)
            normed, inv = normalize(hidden + (resid_ref[rows, :] + vec(C2)))
            out_ref[rows, :] = (normed * vec(G2) + vec(B2)).astype(BF16)
            dy = dy_ref[rows, :].astype(F32)
            grad = normalize_back(normed, inv, vec(G2) * dy)
            resid_ref[rows, :] = grad
            terms = (dy * normed, dy, grad.astype(BF16).astype(F32))
            sums = [
                total + jnp.sum(term, axis=0, keepdims=True) for total, term in zip(sums, terms)
            ]
        for k, total in enumerate(sums):
            vec_out[k : k + 1, :] = total


def feed_forward(ctx, inputs, wo_full, vecs, w1_full, w2_full, dy):
    seq_len, feats = inputs.shape
    shard = w1_full.shape[1]
    hidden = w1_full.shape[2]
    steps = hidden // feats
    once = pl.Buffered(1)

    def whole(shape, mode=None):
        return pl.BlockSpec(shape, lambda j: (0,) * len(shape), pipeline_mode=mode)

    rows, rows_f32 = (seq_len, feats), jax.ShapeDtypeStruct((seq_len, feats), F32)
    cols = pl.BlockSpec(rows, lambda j: (0, j))
    wide = jax.ShapeDtypeStruct((seq_len, hidden), BF16)
    parts = w2_full.shape[1] // LANES
    act_block = pl.BlockSpec((parts, seq_len, feats // parts), lambda j: (0, 0, j))
    act_shape = jax.ShapeDtypeStruct((parts, seq_len, hidden // parts), BF16)
    return pl.pallas_call(
        functools.partial(feed_kernel, min(256, seq_len)),
        grid=(steps,),
        in_specs=[
            whole(rows, once), whole(rows, once), whole(wo_full.shape, once),
            whole(vecs.shape, once),
            pl.BlockSpec((8, shard, feats), lambda j: (0, 0, j)),
            pl.BlockSpec((8 // steps, w2_full.shape[1], feats), lambda j: (j, 0, 0)),
            whole(rows, once),
        ],
        out_specs=[act_block, cols, whole(rows), whole(rows), whole(rows), whole((seq_len, LANES)),
                   whole((8, feats))],
        out_shape=[
            act_shape, wide, jax.ShapeDtypeStruct(rows, BF16), rows_f32, rows_f32,
            jax.ShapeDtypeStruct((seq_len, LANES), F32), jax.ShapeDtypeStruct((8, feats), F32),
        ],
        scratch_shapes=[pltpu.VMEM(rows, BF16)],
        compiler_params=pltpu.CompilerParams(vmem_limit_bytes=VMEM_LIMIT),
    )(ctx, inputs, wo_full, vecs, w1_full, w2_full, dy)


def feed_back_kernel(seq_size, seq_count, rows_blk, *refs):
    refs = list(refs)

    def take(count):
        got = refs[:count]
        del refs[:count]
        return got

    act_ref, slope_ref, w1_ref, w2_ref, resid_ref, normed_ref, inv_ref, ctx_ref = take(8)
    wo_ref, vec_ref, vec_in, out_rows = take(4)
    d_w1, resid_out, grad_ctx, d_wo, vec_out, w2_part, w1_part, out_blocks = take(8)
    grad_ffn, hidden_low, grad_pre, d_w2, early, vec_sums = take(6)
    w2_bufs = take(5)
    w2_sems = take(7)
    w1_bufs = take(5)
    w1_sems = take(7)
    out_sems = take(3)

    step = pl.program_id(0)
    last = pl.num_programs(0) - 1
    seq_len, feats = resid_ref.shape
    parts, chunk = d_w2.shape[0], d_w2.shape[2]
    early_count = early.shape[0]
    place = Place(seq_size, seq_count)
    outs = RowsOut(place, out_rows, out_blocks, out_sems)
    jobs = [
        Reduce(
            place, lambda shard, c=c: d_w2.at[c, shard], w2_part.at[pl.ds(c * chunk, chunk)],
            [buf.at[c] for buf in w2_bufs], w2_sems, c,
        )
        for c in range(parts)
    ]
    jobs += [
        Reduce(
            place, lambda shard, c=c: early.at[c, shard], w1_part.at[c],
            [buf.at[c] for buf in w1_bufs], w1_sems, c,
        )
        for c in range(early_count)
    ]
    t0, t1, t2, w0, w1 = jobs
    begin, core = Reduce.begin, Reduce.core_stage
    one, two = Reduce.one_stage, Reduce.two_stage
    ticks = (
        ((begin, t0),),
        ((begin, t1), (core, t0)),
        ((begin, t2), (core, t1)),
        ((one, t0), (core, t2), (begin, w0)),
        ((one, t1), (two, t0), (core, w0), (begin, w1)),
        ((one, t2), (two, t1), (core, w1)),
    )

    def run(stages):
        for stage, job in stages:
            stage(job)

    blocks = [pl.ds(i * rows_blk, rows_blk) for i in range(seq_len // rows_blk)]

    def vec(k):
        return vec_ref[k : k + 1, :]

    @pl.when(step == 0)
    def _():
        place.barrier()
        for pos in range(seq_size):
            outs.start(pos)
        for rows in blocks:
            grad_ffn[rows, :] = resid_ref[rows, :].astype(BF16)
            hidden_low[rows, :] = (normed_ref[rows, :] * vec(G1) + vec(B1)).astype(BF16)
            resid_out[rows, :] = resid_ref[rows, :]

    @pl.when(step < parts)
    def _():
        part = dot(act_ref[0], grad_ffn[...], 0, 0).astype(BF16)
        d_w2[step] = part.reshape(d_w2.shape[1:])

    @pl.when(step >= parts)
    def _():
        width = slope_ref.shape[1]
        shrink = w2_ref[...].reshape(width, feats)
        expand = w1_ref[...].reshape(feats, width)
        for rows in blocks:
            grad_act = dot(grad_ffn[rows, :], shrink, 1, 1)
            low = (grad_act * slope_ref[rows, :].astype(F32)).astype(BF16)
            grad_pre[rows, :] = low
            resid_out[rows, :] += dot(low, expand, 1, 1)
        total = dot(jnp.ones((8, seq_len), BF16), grad_pre[...], 1, 0)
        outer = dot(hidden_low[...], grad_pre[...], 0, 0)
        low = outer.astype(BF16).reshape(early.shape[1:])

        @pl.when(step < parts + early_count)
        def _():
            early[jnp.minimum(step - parts, early_count - 1)] = low

        @pl.when(step >= parts + early_count)
        def _():
            d_w1[0] = low

        vec_sums[pl.ds(step - parts, 1), :] = total[0:1, :]

    for at_step, stages in enumerate(ticks):

        @pl.when(step == at_step)
        def _():
            run(stages)

    @pl.when(step == last)
    def _():
        run(((one, w0), (two, t2)))
        for job in jobs[:parts]:
            job.finish()
        merge = wo_ref[...].reshape(feats, feats)
        sums = [jnp.zeros((1, feats), F32)] * 3
        for rows in blocks:
            grad_hidden = resid_out[rows, :]
            normed = normed_ref[rows, :]
            grad = normalize_back(normed, inv_ref[rows, 0:1], vec(G1) * grad_hidden)
            resid_out[rows, :] = grad
            low = grad.astype(BF16)
            grad_ctx[rows, :] = dot(low, merge, 1, 1).astype(BF16)
            grad_pre[rows, :] = low
            terms = (grad_hidden * normed, grad_hidden, low.astype(F32))
            sums = [
                total + jnp.sum(term, axis=0, keepdims=True) for total, term in zip(sums, terms)
            ]
        d_wo[...] = dot(ctx_ref[...], grad_pre[...], 0, 0).astype(BF16).reshape(d_wo.shape)
        row = lax.broadcasted_iota(jnp.int32, (16, 1), 0)
        lines = sums + [vec_in[k : k + 1, :] for k in range(3)]
        lines = lines + [vec_sums[k : k + 1, :] for k in range(4)]
        packed = jnp.zeros((16, feats), F32)
        for k, line in enumerate(lines):
            packed = jnp.where(row == k, line, packed)
        vec_out[...] = packed.astype(BF16)

        run(((one, w1), (two, w0), (Reduce.finish, w0), (two, w1), (Reduce.finish, w1)))
        for job in jobs:
            job.drain()
        outs.finish()


def feed_back(
    seq_size, seq_count, act, slope, w1_full, w2_full, resid, normed, inv, ctx, wo_full, vecs,
    vec_in, out_rows,
):
    seq_len, feats = ctx.shape
    shard, w2_rows = w1_full.shape[1], w2_full.shape[1]
    steps = slope.shape[1] // feats
    parts = act.shape[0]
    early = 2
    blk = seq_len // seq_size
    once = pl.Buffered(1)
    any_spec = pl.BlockSpec(memory_space=pl.ANY)
    dma = pltpu.SemaphoreType.DMA

    def whole(shape, mode=None):
        return pl.BlockSpec(shape, lambda j: (0,) * len(shape), pipeline_mode=mode)

    def first(j):
        return jnp.minimum(j, parts - 1)

    def second(j):
        return jnp.maximum(j - parts, 0)

    rows = (seq_len, feats)
    return pl.pallas_call(
        functools.partial(feed_back_kernel, seq_size, seq_count, min(256, seq_len)),
        grid=(parts + steps,),
        in_specs=[
            pl.BlockSpec((1,) + act.shape[1:], lambda j: (first(j), 0, 0)),
            pl.BlockSpec(rows, lambda j: (0, second(j))),
            pl.BlockSpec((8, shard, feats), lambda j: (0, 0, second(j))),
            pl.BlockSpec((8 // steps, w2_rows, feats), lambda j: (second(j), 0, 0)),
            whole(rows, once), whole(rows, once), whole(inv.shape, once), whole(rows, once),
            whole(wo_full.shape, once), whole(vecs.shape, once), whole(vec_in.shape, once),
            any_spec,
        ],
        out_specs=[
            pl.BlockSpec((1, 8, shard, feats), lambda j: (jnp.maximum(j - parts - early, 0), 0, 0, 0)),
            whole(rows), whole(rows), whole(wo_full.shape), whole((16, feats)),
            any_spec, any_spec, any_spec,
        ],
        out_shape=[
            jax.ShapeDtypeStruct((steps - early, 8, shard, feats), BF16),
            jax.ShapeDtypeStruct(rows, F32), jax.ShapeDtypeStruct(rows, BF16),
            jax.ShapeDtypeStruct(wo_full.shape, BF16), jax.ShapeDtypeStruct((16, feats), BF16),
            jax.ShapeDtypeStruct((w2_rows, feats), BF16),
            jax.ShapeDtypeStruct((early, shard, feats), BF16),
            jax.ShapeDtypeStruct((seq_count, blk, feats), BF16),
        ],
        scratch_shapes=[
            pltpu.VMEM(rows, BF16), pltpu.VMEM(rows, BF16), pltpu.VMEM(rows, BF16),
            pltpu.VMEM((parts, 8, w2_rows // parts, feats), BF16),
            pltpu.VMEM((early, 8, shard, feats), BF16),
            pltpu.VMEM((8, feats), F32),
        ]
        + Reduce.scratch(parts, w2_rows // parts, feats)
        + Reduce.semaphores(parts)
        + Reduce.scratch(early, shard, feats)
        + Reduce.semaphores(early)
        + [dma((seq_size,)), dma((seq_count,)), dma((1,))],
        compiler_params=pltpu.CompilerParams(
            collective_id=4, has_side_effects=True, vmem_limit_bytes=VMEM_MAX
        ),
    )(
        act, slope, w1_full, w2_full, resid, normed, inv, ctx, wo_full, vecs, vec_in, out_rows
    )


def pair_column(feats, which, pair):
    return (pair // 2) * feats + (pair % 2) * 3 * LANES + which * LANES


def backward_kernel(seq_size, seq_count, rows_blk, *refs):
    refs = list(refs)

    def take(count):
        got = refs[:count]
        del refs[:count]
        return got

    q_ref, k_ref, v_ref, ctx_ref, grad_ref, probs_ref, vec_ref = take(7)
    x_in, qkv_in, resid_in, d_w1, d_wo, w2_part, w1_part = take(7)
    w2_total, w1_total, wo_total, qkv_total, vec_total, token_out = take(6)
    key_acc, value_acc, grads, x_rows, qkv_mat, resid, token_rows = take(7)
    mats, bias_rows, vec_src = take(3)
    w1_count = d_w1.shape[0]
    early_count = w1_part.shape[0]
    mat_count = w1_count + 4
    bufs = take(5)
    (arrived,) = take(1)
    vec_bufs = take(5)
    (vec_arrived,) = take(1)
    w2_bufs = take(4)
    w1_bufs = take(4)
    sems = take(7)
    z_sems = take(2)
    load_sem, carried_sems = take(2)
    token_sems = take(3)

    step = pl.program_id(0)
    last = pl.num_programs(0) - 1
    place = Place(seq_size, seq_count)
    seq_len, feats = x_rows.shape

    def outer_source(c):
        if c < w1_count:
            return lambda shard: d_w1.at[c, shard]
        if c == w1_count:
            return lambda shard: d_wo.at[shard]
        return lambda shard: mats.at[c - w1_count - 1, shard]

    w1_totals = [w1_total.at[:, pl.ds(c * feats, feats)] for c in range(early_count + w1_count)]
    totals = w1_totals[early_count:]
    totals += [wo_total] + [qkv_total.at[:, pl.ds(c * feats, feats)] for c in range(3)]
    jobs = [
        Reduce(
            place, outer_source(c), totals[c], [buf.at[c] for buf in bufs], sems, c,
            arrived.at[c], z_sems,
        )
        for c in range(mat_count)
    ]
    jobs.append(
        Reduce(
            place, lambda shard: vec_src.at[shard], vec_total, [buf.at[0] for buf in vec_bufs],
            sems, mat_count, vec_arrived.at[0], z_sems,
        )
    )
    parts = w2_bufs[0].shape[0]
    chunk = w2_part.shape[0] // parts
    pieces = [
        (w2_part.at[pl.ds(c * chunk, chunk)], w2_total.at[pl.ds(c * chunk, chunk)], w2_bufs, c)
        for c in range(parts)
    ]
    pieces += [(w1_part.at[c], w1_totals[c], w1_bufs, c) for c in range(early_count)]
    carried = [
        Carried(
            place, source, result, [buf.at[c] for buf in held], z_sems, carried_sems,
            mat_count + 1 + slot, slot,
        )
        for slot, (source, result, held, c) in enumerate(pieces)
    ]
    w2, w3, wo, qkv_a, qkv_b, qkv_c, vec = jobs
    t0, t1, t2, t3, t4 = carried
    blk = seq_len // seq_size
    loads = [
        pltpu.make_async_copy(src, dst, load_sem.at[k])
        for k, (src, dst) in enumerate(((x_in, x_rows), (qkv_in, qkv_mat), (resid_in, resid)))
    ]
    tokens = RowsOut(place, token_rows, token_out, token_sems)

    core, one, two = Reduce.core_stage, Reduce.one_stage, Reduce.two_stage

    def hop1(job):
        job.hop(1)

    def hop2(job):
        job.hop(2)

    def end(job):
        job.hop(3)
        job.finish()

    ticks = (
        ((core, w2), (core, w3)),
        ((core, wo), (hop1, t0)),
        ((one, w2),),
        ((one, w3), (hop1, t1), (hop2, t0)),
        ((one, wo), (core, qkv_a), (hop1, t2)),
        ((two, w2), (two, w3), (hop1, t3), (hop2, t1), (end, t0)),
        ((two, wo), (hop2, t2)),
        ((one, qkv_a), (hop1, t4), (hop2, t3), (end, t1)),
        ((core, qkv_b), (two, qkv_a), (hop1, w2), (end, t2)),
        ((hop1, w3), (hop2, t4), (end, t3)),
        ((one, qkv_b), (hop1, wo), (hop2, w2)),
        ((two, qkv_b), (hop1, qkv_a), (hop2, w3), (end, t4)),
    )
    after = (
        ((hop2, wo), (end, w2)),
        ((core, qkv_c),),
        ((core, vec), (hop1, qkv_b), (end, w3)),
        ((hop2, qkv_a),),
    )
    rest = (
        (one, qkv_c), (one, vec), (end, wo), (hop2, qkv_b), (end, qkv_a),
        (two, qkv_c), (two, vec), (hop1, qkv_c), (hop1, vec), (end, qkv_b),
        (hop2, qkv_c), (hop2, vec), (end, qkv_c), (end, vec),
    )

    @pl.when(step == 0)
    def _():
        place.barrier()
        for job in carried:
            job.load.start()
        for job in (w2, w3, wo):
            job.begin()
        for load in loads:
            load.start()
        for job in carried:
            job.begin()

    @pl.when(step == 2)
    def _():
        qkv_a.begin()

    @pl.when(step == 4)
    def _():
        qkv_b.begin()

    def store(which, rows, values):
        grads[rows, which * LANES : (which + 1) * LANES] = values

    def between(half):
        for at_step in range(len(ticks) // 2):

            @pl.when(step == at_step)
            def _():
                for stage, job in ticks[2 * at_step + half]:
                    stage(job)

    attend_back_pair(
        q_ref, k_ref, v_ref, ctx_ref, grad_ref, probs_ref, store, key_acc, value_acc, rows_blk,
        between,
    )

    @pl.when(step == 0)
    def _():
        for load in loads:
            load.wait()

    width = 3 * LANES
    column = pl.multiple_of(step * LANES, LANES)
    half = pl.multiple_of((step % 2) * width, LANES)
    outer = dot(x_rows[...], grads[...], 0, 0).astype(BF16)
    mats[step // 2, :, :, pl.ds(half, width)] = outer.reshape(8, feats // 8, width)
    sums = dot(jnp.ones((16, seq_len), BF16), grads[...], 1, 0)
    bias_rows[0, :, pl.ds(column, LANES)] = sums[:, :LANES]
    bias_rows[1, :, pl.ds(column, LANES)] = sums[:, 2 * LANES :]
    mat = jnp.concatenate(
        [
            qkv_mat[:, :, pl.ds(pl.multiple_of(which * feats + column, LANES), LANES)].reshape(
                feats, LANES
            )
            for which in range(3)
        ],
        axis=1,
    )

    @pl.when(step < last)
    def _():
        for pos in range(seq_size):
            rows = pl.ds(pos * blk, blk)
            resid[rows, :] += dot(grads[rows, :], mat, 1, 1)

    @pl.when(step == last)
    def _():
        qkv_c.begin()
        row = lax.broadcasted_iota(jnp.int32, (16, 1), 0)
        biases = jnp.where(row == 0, bias_rows[0], bias_rows[1]).astype(BF16)
        for shard in range(8):
            vec_src[shard, 0:16, :] = vec_ref[...]
            vec_src[shard, 16:32, :] = biases
        vec.begin()
        for pos in range(seq_size):
            rows = pl.ds(pos * blk, blk)
            total = resid[rows, :] + dot(grads[rows, :], mat, 1, 1)
            token_rows[rows, :] = total.astype(BF16)
            tokens.start(pos)
            for stage, job in after[pos]:
                stage(job)
        for stage, job in rest:
            stage(job)
        for job in jobs + carried:
            job.drain()
        tokens.finish()


def backward_all(
    seq_size, seq_count, query, key, value, ctx, grad_ctx, probs, vecs, inputs, qkv_full, resid,
    d_w1, d_wo, w2_part, w1_part,
):
    seq_len, feats = ctx.shape
    blk = seq_len // seq_size
    shard = qkv_full.shape[1]
    w1_count = d_w1.shape[0]
    early = w1_part.shape[0]
    count = w1_count + 4
    parts = w2_part.shape[0] // LANES
    any_spec = pl.BlockSpec(memory_space=pl.ANY)
    cols = pl.BlockSpec((seq_len, LANES), lambda g: (0, g))
    dma = pltpu.SemaphoreType.DMA

    def low(*shape):
        return jax.ShapeDtypeStruct(shape, BF16)

    return pl.pallas_call(
        functools.partial(backward_kernel, seq_size, seq_count, seq_len // 2),
        grid=(feats // LANES,),
        in_specs=[cols] * 5
        + [
            pl.BlockSpec((2, seq_len, seq_len), lambda g: (g, 0, 0)),
            pl.BlockSpec(vecs.shape, lambda g: (0, 0)),
        ]
        + [any_spec] * 7,
        out_specs=[any_spec] * 6,
        out_shape=[
            low(*w2_part.shape), low(shard, (early + w1_count) * feats), low(shard, feats),
            low(shard, 3 * feats), low(32, feats), low(seq_count, blk, feats),
        ],
        scratch_shapes=[pltpu.VMEM((2, HEAD, seq_len), F32)] * 2
        + [
            pltpu.VMEM((seq_len, 3 * LANES), BF16),
            pltpu.VMEM((seq_len, feats), BF16),
            pltpu.VMEM(qkv_full.shape, BF16),
            pltpu.VMEM((seq_len, feats), F32),
            pltpu.VMEM((seq_len, feats), BF16),
            pltpu.VMEM((3, 8, shard, feats), BF16),
            pltpu.VMEM((2, 16, feats), F32),
            pltpu.VMEM((8, 32, feats), BF16),
        ]
        + Reduce.scratch(count, shard, feats)
        + [pltpu.VMEM((count, 2, shard, feats), BF16)]
        + Reduce.scratch(1, 32, feats)
        + [pltpu.VMEM((1, 2, 32, feats), BF16)]
        + [
            pltpu.VMEM((parts,) + lead + (LANES, feats), BF16) for lead in ((), (2,), (2,), ())
        ]
        + [pltpu.VMEM((early,) + lead + (shard, feats), BF16) for lead in ((), (2,), (2,), ())]
        + Reduce.semaphores(count + 1)
        + Chain.semaphores(count + 1 + parts + early)
        + [dma((3,)), dma((parts + early, 2)), dma((seq_size,)), dma((seq_count,)), dma((1,))],
        compiler_params=pltpu.CompilerParams(
            collective_id=1, has_side_effects=True, vmem_limit_bytes=VMEM_MAX
        ),
    )(
        query, key, value, ctx, grad_ctx, probs, vecs, inputs, qkv_full, resid, d_w1, d_wo,
        w2_part, w1_part,
    )


def widen_kernel(w2_in, w1_in, wo_in, qkv_in, vec_in, *outs):
    w2_out, w1_out, wo_out = outs[:3]
    mats, vecs = outs[3:6], outs[6:]
    feats = wo_in.shape[1]
    w2_out[...] = w2_in[...].astype(F32)
    w1_out[...] = w1_in[...].astype(F32)
    wo_out[...] = wo_in[...].astype(F32)
    for which, mat in enumerate(mats):
        for pair in range(feats // LANES):
            start = pair_column(feats, which, pair)
            mat[:, pair * LANES : (pair + 1) * LANES] = qkv_in[:, start : start + LANES].astype(F32)
    me = lax.axis_index("dp")
    part = feats // 8
    rows = vec_in[...].astype(F32)
    own = jnp.zeros((rows.shape[0], part), F32)
    long = jnp.zeros((1, 4 * part), F32)
    for k in range(8):
        own = jnp.where(me == k, rows[:, k * part : (k + 1) * part], own)
        row, start = 6 + k // 2, (k % 2) * 4 * part
        long = jnp.where(me == k, rows[row : row + 1, start : start + 4 * part], long)
    for k, row in enumerate((16, 17, 2, 0, 1, 5, 3, 4)):
        vecs[k][...] = own[row : row + 1, :]
    vecs[8][...] = long


def widen(w2_sum, w1_sum, wo_sum, qkv_sum, vec_sum):
    feats = wo_sum.shape[1]
    part = feats // 8

    def wide(*shape):
        return jax.ShapeDtypeStruct(shape, F32)

    return pl.pallas_call(
        widen_kernel,
        out_shape=[wide(*w2_sum.shape), wide(*w1_sum.shape)]
        + [wide(*wo_sum.shape)] * 4
        + [wide(1, part)] * 8
        + [wide(1, 4 * part)],
        compiler_params=pltpu.CompilerParams(vmem_limit_bytes=VMEM_LIMIT),
    )(w2_sum, w1_sum, wo_sum, qkv_sum, vec_sum)


def column_sum(rows):
    return jnp.sum(rows, axis=0, dtype=F32)


def per_device(mesh_shape, tokens, lengths, *rest):
    weights, upstream = rest[:15], rest[15]
    dp_size, seq_size = mesh_shape
    seq_count, row_count, feats = tokens.shape
    dp_index = lax.axis_index("dp")
    here = lax.axis_index("seq")
    spare = seq_size - seq_count

    def owner_shift(dp):
        return spare * (dp % 2)

    my_seq = jnp.clip(here - owner_shift(dp_index), 0, seq_count - 1)

    def owned_by(dp, pos):
        seq = pos - owner_shift(dp)
        return 0 <= seq < seq_count

    def shift_pairs(step, to_owner):
        pairs = []
        for dp in range(dp_size):
            for pos in range(seq_size):
                dest = (pos + step) % seq_size
                if owned_by(dp, dest if to_owner else pos):
                    pairs.append((dp * seq_size + pos, dp * seq_size + dest))
        return pairs

    def gather(piece):
        return lax.all_gather(piece, "dp", axis=0, tiled=True)

    def to_owners(blocks):
        pieces = []
        for step in range(seq_size):
            dest = (here + step) % seq_size
            seq = jnp.clip(dest - owner_shift(dp_index), 0, seq_count - 1)
            piece = lax.dynamic_index_in_dim(blocks, seq, 0, keepdims=False)
            if step == 0:
                owner = (here >= owner_shift(dp_index)) & (here < owner_shift(dp_index) + seq_count)
                piece = jnp.where(owner, piece, jnp.zeros_like(piece))
            else:
                piece = lax.ppermute(piece, ("dp", "seq"), shift_pairs(step, True))
            pieces.append(piece)
        order = (here - jnp.arange(seq_size)) % seq_size
        return jnp.take(jnp.stack(pieces), order, axis=0).reshape(-1, feats)

    def from_owners(rows):
        pieces = rows.reshape(seq_size, row_count, feats)
        arrived = []
        for step in range(seq_size):
            piece = lax.dynamic_index_in_dim(pieces, (here - step) % seq_size, 0, keepdims=False)
            if step:
                piece = lax.ppermute(piece, ("dp", "seq"), shift_pairs(seq_size - step, False))
            arrived.append(piece)
        stack = jnp.stack(arrived)
        order = (jnp.arange(seq_count) + owner_shift(dp_index) - here) % seq_size
        return jnp.take(stack, order, axis=0)

    wq, bq, wk, wv, bv, wo, bo, g1, b1, w1, c1, w2, c2, g2, b2 = weights
    shard_rows = feats // dp_size
    seq_len = seq_size * row_count
    direct = (dp_size, seq_size, feats, seq_len) == (8, 4, 768, 1024) and seq_count == 3
    vec_parts = (bq, bv, bo, g1, b1, c2, g2, b2, c1)
    vec_sizes = [item.shape[0] for item in vec_parts]
    vec_len = sum(vec_sizes)
    if not direct:
        packed = jnp.concatenate(vec_parts).astype(BF16)
        position = lax.iota(jnp.int32, seq_len)
        valid_len = lax.dynamic_index_in_dim(lengths, my_seq, 0, keepdims=False)
        key_bias = jnp.where(position < valid_len, 0.0, 8.0 * NEG_FILL).astype(F32)
        key_bias = key_bias.reshape(1, seq_len)
        qkv_mat = gather(jnp.concatenate([wq, wk, wv], axis=1).astype(BF16))
        packed = lax.all_gather(packed, "dp", axis=0, tiled=False)
        merge_mat, expand_mat, reduce_mat = [gather(item.astype(BF16)) for item in (wo, w1, w2)]
        vecs = []
        start = 0
        for size in vec_sizes:
            vecs.append(packed[:, start : start + size].reshape(1, -1).astype(F32))
            start += size
        bq, bv, bo, g1, b1, c2, g2, b2, c1 = vecs

    if direct:
        inputs, qkv_full, vec_full, w2_part, w1_part, wo_part = start_all(
            seq_size, tokens, (wq, wk, wv), [item.reshape(1, -1) for item in vec_parts], w2, w1, wo
        )
        query, key, value, ctx, probs, vec_rows, dy, w2_full, w1_full, wo_full = forward_all(
            seq_size, lengths, inputs, qkv_full, vec_full, upstream, w2_part, w1_part, wo_part
        )
        act, slope, out_rows, grad_resid2, normed1, inv1, second_sums = feed_forward(
            ctx, inputs, wo_full, vec_rows, w1_full, w2_full, dy
        )
        d_w1, grad_resid1, grad_ctx, d_wo, vec_sums, part_w2, part_w1, output = feed_back(
            seq_size, seq_count, act, slope, w1_full, w2_full, grad_resid2, normed1, inv1, ctx,
            wo_full, vec_rows, second_sums, out_rows,
        )
        *sums, token_grad = backward_all(
            seq_size, seq_count, query, key, value, ctx, grad_ctx, probs, vec_sums, inputs,
            qkv_full, grad_resid1, d_w1, d_wo, part_w2, part_w1,
        )
        sum_w2, sum_w1, s_wo, s_wq, s_wk, s_wv, *vec_sums = widen(*sums)
        vec_sums = [item.reshape(-1) for item in vec_sums]
        s_bq, s_bv, s_bo, s_g1, s_b1, s_c2, s_g2, s_b2, s_c1 = vec_sums
    else:
        inputs = to_owners(tokens)
        dy = to_owners(upstream).astype(F32)
        qkv = dot(inputs, qkv_mat, 1, 0)
        query = (qkv[:, :feats] + bq).astype(BF16)
        key = qkv[:, feats : 2 * feats].astype(BF16)
        value = (qkv[:, 2 * feats :] + bv).astype(BF16)
        ctx, probs = attend(key_bias, query, key, value)
        normed1, inv1 = normalize(inputs.astype(F32) + dot(ctx, merge_mat, 1, 0) + bo)
        hidden = normed1 * g1 + b1
        hidden_low = hidden.astype(BF16)
        pre = dot(hidden_low, expand_mat, 1, 0) + c1
        phi_cum = 0.5 * (1.0 + lax.erf(pre * INV_SQRT2))
        act = (pre * phi_cum).astype(BF16)
        slope = (phi_cum + pre * (INV_SQRT_2PI * jnp.exp(-0.5 * pre * pre))).astype(BF16)
        normed2, inv2 = normalize(hidden + dot(act, reduce_mat, 1, 0) + c2)
        result = (normed2 * g2 + b2).astype(BF16)
        output = from_owners(result)

        d_g2 = column_sum(dy * normed2)
        d_b2 = column_sum(dy)
        grad_resid2 = normalize_back(normed2, inv2, g2 * dy)
        grad_ffn = grad_resid2.astype(BF16)
        d_w2 = dot(act, grad_ffn, 0, 0).astype(BF16)
        d_c2 = column_sum(grad_ffn)
        grad_pre = (dot(grad_ffn, reduce_mat, 1, 1) * slope.astype(F32)).astype(BF16)
        d_w1 = dot(hidden_low, grad_pre, 0, 0).astype(BF16)
        d_c1 = column_sum(grad_pre)
        grad_hidden = grad_resid2 + dot(grad_pre, expand_mat, 1, 1)
        d_g1 = column_sum(grad_hidden * normed1)
        d_b1 = column_sum(grad_hidden)
        grad_resid1 = normalize_back(normed1, inv1, g1 * grad_hidden)
        grad_att = grad_resid1.astype(BF16)
        d_wo = dot(ctx, grad_att, 0, 0).astype(BF16)
        d_bo = column_sum(grad_att)
        grad_ctx = dot(grad_att, merge_mat, 1, 1).astype(BF16)
        grad_qkv = attend_back(query, key, value, ctx, grad_ctx, probs)
        token_rows = grad_resid1
        d_qkv = []
        for which in range(3):
            mat = qkv_mat[:, which * feats : (which + 1) * feats]
            token_rows = token_rows + dot(grad_qkv[which], mat, 1, 1)
            d_qkv.append(dot(inputs, grad_qkv[which], 0, 0).astype(BF16))
        d_bq = column_sum(grad_qkv[0])
        d_bv = column_sum(grad_qkv[2])
        token_grad = from_owners(token_rows.astype(BF16))
        vec_grads = (d_bq, d_bv, d_bo, d_g1, d_b1, d_c2, d_g2, d_b2, d_c1)
        vec_pack = jnp.concatenate([item.reshape(dp_size, -1) for item in vec_grads], axis=1)
        vec_cols = -(-vec_len // (shard_rows * LANES)) * LANES
        vec_pack = jnp.pad(vec_pack, ((0, 0), (0, shard_rows * vec_cols - vec_len)))
        vec_pack = vec_pack.reshape(feats, vec_cols).astype(BF16)

        def reduce(full):
            own = lax.psum_scatter(full, "dp", scatter_dimension=0, tiled=True)
            return lax.psum(own, "seq").astype(F32)

        sum_w2 = reduce(d_w2)
        sum_w1 = reduce(d_w1)
        sum_rest = reduce(jnp.concatenate([d_wo] + d_qkv + [vec_pack], axis=1))
        s_wo, s_wq, s_wk, s_wv = [sum_rest[:, i * feats : (i + 1) * feats] for i in range(4)]
        flat = sum_rest[:, 4 * feats :].reshape(-1)
        out_vecs = []
        start = 0
        for size in vec_sizes:
            out_vecs.append(flat[start : start + size])
            start += size
        s_bq, s_bv, s_bo, s_g1, s_b1, s_c2, s_g2, s_b2, s_c1 = out_vecs
    return (
        output,
        token_grad,
        s_wq,
        s_bq,
        s_wk,
        s_wv,
        s_bv,
        s_wo,
        s_bo,
        s_g1,
        s_b1,
        sum_w1,
        s_c1,
        sum_w2,
        s_c2,
        s_g2,
        s_b2,
    )


def solution(mesh):
    rows, mat, vec = P("dp", "seq", None), P("dp", None), P("dp")
    params = (mat, vec, mat, mat, vec, mat, vec, vec, vec, mat, vec, mat, vec, vec, vec)
    return jax.shard_map(
        functools.partial(per_device, (mesh.shape["dp"], mesh.shape["seq"])),
        mesh=mesh,
        in_specs=(rows, vec) + params + (rows,),
        out_specs=(rows, rows) + params,
        check_vma=False,
    )
```

```python
import functools

import jax
import jax.numpy as jnp
from jax import lax
from jax.experimental import pallas as pl
from jax.experimental.pallas import tpu as pltpu
from jax.sharding import PartitionSpec as P

HEAD = 64
LANES = 128
EPS = 1e-12
NEG_FILL = -1000000000.0
SCALE2 = 0.125 * 1.4426950408889634
F32 = jnp.float32
BF16 = jnp.bfloat16
VMEM_LIMIT = 60 * 1024 * 1024
VMEM_MAX = 67043328


def dot(left, right, left_dim, right_dim):
    return lax.dot_general(
        left, right, (((left_dim,), (right_dim,)), ((), ())), preferred_element_type=F32
    )


def attend_kernel(bias_ref, q_ref, k_ref, v_ref, ctx_ref, probs_ref, *, rows_blk):
    seq_len = q_ref.shape[0]
    lane = lax.broadcasted_iota(jnp.int32, (1, LANES), 1)
    bias = bias_ref[...]
    for blk in range(seq_len // rows_blk):
        rows = pl.ds(blk * rows_blk, rows_blk)
        query = q_ref[rows, :]
        mixed = []
        for head in range(2):
            mine = (lane < HEAD) if head == 0 else (lane >= HEAD)
            query_h = jnp.where(mine, query, jnp.zeros_like(query))
            score = dot(query_h, k_ref[...], 1, 1) + bias
            top = jnp.max(score, axis=1, keepdims=True)
            expo = jnp.exp2((score - top) * SCALE2)
            total = jnp.sum(expo, axis=1, keepdims=True)
            probs = (expo * (1.0 / total)).astype(BF16)
            probs_ref[head, rows, :] = probs
            mixed.append(dot(probs, v_ref[...], 1, 0))
        ctx_ref[rows, :] = jnp.where(lane < HEAD, mixed[0], mixed[1]).astype(BF16)


def attend(bias, query, key, value):
    seq_len, feats = query.shape
    cols = pl.BlockSpec((seq_len, LANES), lambda g: (0, g))
    return pl.pallas_call(
        functools.partial(attend_kernel, rows_blk=min(512, seq_len)),
        grid=(feats // LANES,),
        in_specs=[pl.BlockSpec((1, seq_len), lambda g: (0, 0)), cols, cols, cols],
        out_specs=[cols, pl.BlockSpec((2, seq_len, seq_len), lambda g: (g, 0, 0))],
        out_shape=[
            jax.ShapeDtypeStruct((seq_len, feats), BF16),
            jax.ShapeDtypeStruct((feats // HEAD, seq_len, seq_len), BF16),
        ],
        compiler_params=pltpu.CompilerParams(vmem_limit_bytes=VMEM_LIMIT),
    )(bias, query, key, value)


def attend_back_pair(
    q_ref, k_ref, v_ref, ctx_ref, grad_ref, probs_ref, store, key_acc, value_acc, rows_blk,
    between=None,
):
    seq_len = q_ref.shape[0]
    lane = lax.broadcasted_iota(jnp.int32, (1, LANES), 1)
    for blk in range(seq_len // rows_blk):
        rows = pl.ds(blk * rows_blk, rows_blk)
        query = q_ref[rows, :]
        grad = grad_ref[rows, :]
        overlap = ctx_ref[rows, :].astype(F32) * grad.astype(F32)
        query_t = query.T
        grad_t = grad.T
        grad_query = []
        for head in range(2):
            mine = (lane < HEAD) if head == 0 else (lane >= HEAD)
            part = slice(head * HEAD, (head + 1) * HEAD)
            grad_h = jnp.where(mine, grad, jnp.zeros_like(grad))
            inner = jnp.sum(jnp.where(mine, overlap, 0.0), axis=1, keepdims=True)
            probs = probs_ref[head, rows, :]
            grad_probs = dot(grad_h, v_ref[...], 1, 1)
            grad_score = (probs.astype(F32) * (grad_probs - inner)).astype(BF16)
            grad_query.append(dot(grad_score, k_ref[...], 1, 0))
            grad_key = dot(query_t[part], grad_score, 1, 0)
            grad_value = dot(grad_t[part], probs, 1, 0)
            if blk == 0:
                key_acc[head] = grad_key
                value_acc[head] = grad_value
            else:
                key_acc[head] += grad_key
                value_acc[head] += grad_value
        mixed = jnp.where(lane < HEAD, grad_query[0], grad_query[1])
        store(0, rows, (0.125 * mixed).astype(BF16))
        if between is not None:
            between(blk)
    everything = pl.ds(0, seq_len)
    grad_key = jnp.concatenate([key_acc[0], key_acc[1]], axis=0)
    store(1, everything, (0.125 * grad_key).T.astype(BF16))
    grad_value = jnp.concatenate([value_acc[0], value_acc[1]], axis=0)
    store(2, everything, grad_value.T.astype(BF16))


def attend_back_kernel(
    q_ref, k_ref, v_ref, ctx_ref, grad_ref, probs_ref, out_ref, key_acc, value_acc, *, rows_blk
):
    def store(which, rows, values):
        out_ref[which, rows, :] = values

    attend_back_pair(
        q_ref, k_ref, v_ref, ctx_ref, grad_ref, probs_ref, store, key_acc, value_acc, rows_blk
    )


def attend_back(query, key, value, ctx, grad_ctx, probs):
    seq_len, feats = ctx.shape
    cols = pl.BlockSpec((seq_len, LANES), lambda g: (0, g))
    return pl.pallas_call(
        functools.partial(attend_back_kernel, rows_blk=min(512, seq_len)),
        grid=(feats // LANES,),
        in_specs=[cols] * 5 + [pl.BlockSpec((2, seq_len, seq_len), lambda g: (g, 0, 0))],
        out_specs=pl.BlockSpec((3, seq_len, LANES), lambda g: (0, 0, g)),
        out_shape=jax.ShapeDtypeStruct((3, seq_len, feats), BF16),
        scratch_shapes=[pltpu.VMEM((2, HEAD, seq_len), F32)] * 2,
        compiler_params=pltpu.CompilerParams(vmem_limit_bytes=VMEM_LIMIT),
    )(query, key, value, ctx, grad_ctx, probs)


MESH = pl.DeviceIdType.MESH


def remote(src, dst, send, recv, device):
    return pltpu.make_async_remote_copy(
        src_ref=src, dst_ref=dst, send_sem=send, recv_sem=recv,
        device_id=device, device_id_type=MESH,
    )


class Place:
    def __init__(self, seq_size, seq_count):
        self.me = me = lax.axis_index("dp")
        self.here = here = lax.axis_index("seq")
        core, x_at, y_at = me % 2, (me // 2) % 2, (me // 4) % 2
        self.to_core, self.to_x, self.to_y = 1 - 2 * core, 2 - 4 * x_at, 4 - 8 * y_at
        self.core_dev = (me + self.to_core, here)
        self.x_dev = (me + self.to_x, here)
        self.y_dev = (me + self.to_y, here)
        self.shift = (seq_size - seq_count) * core
        self.my_seq = here - self.shift
        self.is_owner = (self.my_seq >= 0) & (self.my_seq < seq_count)
        self.seq_size, self.seq_count = seq_size, seq_count

    def barrier(self):
        barrier = pltpu.get_barrier_semaphore()
        for device in (self.core_dev, self.x_dev, self.y_dev):
            pl.semaphore_signal(barrier, inc=1, device_id=device, device_id_type=MESH)
        for step in range(1, self.seq_size):
            pl.semaphore_signal(
                barrier, inc=1, device_id=(self.me, (self.here + step) % self.seq_size),
                device_id_type=MESH,
            )
        pl.semaphore_wait(barrier, 3 + self.seq_size - 1)


class Gather:
    def __init__(self, place, full, own, sems, index):
        self.place, self.full, self.own, self.index = place, full, own, index
        self.send_sem, self.recv_sem, self.core_send, self.core_recv = sems

    def half(self, which):
        count = self.full.shape[1] // 2
        return pl.ds(which * count, count)

    def piece(self, p):
        at = self.place
        rows = self.half(p % 2)
        shard = at.me + (0, 0, 0, 0, at.to_x, at.to_y)[p]
        src = self.own.at[rows] if p < 4 else self.full.at[shard, rows]
        device = (at.x_dev, at.y_dev, at.y_dev, at.x_dev, at.y_dev, at.x_dev)[p]
        return remote(
            src, self.full.at[shard, rows],
            self.send_sem.at[self.index, p], self.recv_sem.at[self.index, p], device,
        )

    def core_piece(self, p):
        at = self.place
        if p == 6:
            src, dst = self.own, self.full.at[at.me]
        else:
            across = at.to_x + at.to_y
            shard = at.me + (at.to_x, at.to_y, at.to_y, at.to_x, across, across)[p]
            src = dst = self.full.at[shard, self.half(p % 2)]
        return remote(
            src, dst, self.core_send.at[self.index, p], self.core_recv.at[self.index, p],
            at.core_dev,
        )

    def start(self, *pieces):
        for p in pieces:
            self.piece(p).start()

    def arrive(self, *pieces):
        for p in pieces:
            self.piece(p).wait_recv()

    def to_core(self, *pieces):
        for p in pieces:
            self.core_piece(p).start()

    def finish(self, pieces, core_pieces):
        for p in core_pieces:
            self.core_piece(p).wait_recv()
        for p in pieces:
            self.piece(p).wait_send()
        for p in core_pieces:
            self.core_piece(p).wait_send()


class RowsIn:
    def __init__(self, place, blocks, whole, buf, sems):
        self.place, self.blocks, self.whole, self.buf = place, blocks, whole, buf
        self.send_sem, self.recv_sem, self.local_sem = sems
        self.rows = blocks.shape[1]

    def to(self, seq, source):
        at = self.place
        return remote(
            self.blocks.at[seq], self.whole.at[pl.ds(source * self.rows, self.rows)],
            self.send_sem.at[seq], self.recv_sem.at[source], (at.me, seq + at.shift),
        )

    def own(self, count):
        at = self.place

        def out(pos, k):
            return pltpu.make_async_copy(
                self.buf, self.whole.at[pl.ds(pos * self.rows, self.rows)], self.local_sem.at[k]
            )

        @pl.when(at.is_owner)
        def _():
            load = pltpu.make_async_copy(self.blocks.at[at.my_seq], self.buf, self.local_sem.at[0])
            load.start()
            load.wait()
            out(at.here, 1).start()
            out(at.here, 1).wait()

        @pl.when(jnp.logical_not(at.is_owner))
        def _():
            self.buf[...] = jnp.zeros_like(self.buf)
            for pos in range(at.seq_size):
                out(pos, pos).start()
            for pos in range(at.seq_size):
                out(pos, pos).wait()

    def start(self):
        at = self.place
        for seq in range(at.seq_count):

            @pl.when(at.here != seq + at.shift)
            def _():
                self.to(seq, at.here).start()

    def finish(self):
        at = self.place

        @pl.when(at.is_owner)
        def _():
            for pos in range(at.seq_size):

                @pl.when(at.here != pos)
                def _():
                    remote(
                        self.blocks.at[0], self.whole.at[pl.ds(pos * self.rows, self.rows)],
                        self.send_sem.at[0], self.recv_sem.at[pos],
                        (at.me, (at.here + 1) % at.seq_size),
                    ).wait_recv()

        for seq in range(at.seq_count):

            @pl.when(at.here != seq + at.shift)
            def _():
                self.to(seq, at.here).wait_send()


def start_kernel(
    seq_size, seq_count, tokens, wq, wk, wv, w2, w1, wo, *refs,
):
    vec_refs, refs = refs[:9], refs[9:]
    rows_out, qkv_full, vec_full, w2_full, w1_full, wo_full = refs[:6]
    qkv_low, w2_low, w1_low, wo_low, row_buf, vec_wide, vecs = refs[6:13]
    row_send, row_recv, row_local, sem_a, sem_b, sem_c, sem_d, own_sem = refs[13:]
    place = Place(seq_size, seq_count)
    sems = (sem_a, sem_b, sem_c, sem_d)
    rows = RowsIn(place, tokens, rows_out, row_buf, (row_send, row_recv, row_local))
    first = [
        Gather(place, qkv_full, qkv_low, sems, 0),
        Gather(place, vec_full, vecs, sems, 1),
    ]
    later = [
        Gather(place, w2_full, w2_low, sems, 2),
        Gather(place, w1_full, w1_low, sems, 3),
        Gather(place, wo_full, wo_low, sems, 4),
    ]
    place.barrier()
    rows.start()
    feats = wq.shape[1]
    vec_wide[...] = jnp.zeros_like(vec_wide)
    for k, item in enumerate(vec_refs[:8]):
        vec_wide[k : k + 1, 0 : item.shape[1]] = item[...]
    for k in range(vec_refs[8].shape[0] // LANES):
        vec_wide[8 + k : 9 + k, :] = vec_refs[8][k * LANES : (k + 1) * LANES].reshape(1, LANES)
    vecs[...] = vec_wide[...].astype(BF16)
    for k, item in enumerate((wq, wk, wv)):
        qkv_low[:, k * feats : (k + 1) * feats] = item[...].astype(BF16)
    for item in first:
        item.start(0, 1)
    for item in first:
        item.start(2, 3)
        item.to_core(6)
    w2_low[...] = w2[...].astype(BF16)
    w1_low[...] = w1[...].astype(BF16)
    wo_low[...] = wo[...].astype(BF16)
    keep = [
        pltpu.make_async_copy(item.own, item.full.at[place.me], own_sem.at[item.index])
        for item in first + later
    ]
    for copy in keep:
        copy.start()
    for item in first:
        item.arrive(0, 1)
        item.start(4, 5)
        item.to_core(0, 1)
    for item in later:
        item.start(0, 1)
    rows.own(seq_size)
    for item in first:
        item.arrive(2, 3)
        item.to_core(2, 3)
    for item in first:
        item.arrive(4, 5)
        item.to_core(4, 5)
    for item in first:
        item.finish(range(6), range(7))
    for item in later:
        item.arrive(0, 1)
        for p in (0, 1):
            item.piece(p).wait_send()
    for copy in keep:
        copy.wait()
    rows.finish()


def start_all(seq_size, tokens, qkv_parts, vecs, w2, w1, wo):
    seq_count, blk, feats = tokens.shape
    any_spec = pl.BlockSpec(memory_space=pl.ANY)
    vmem_spec = pl.BlockSpec(memory_space=pltpu.VMEM)
    dma = pltpu.SemaphoreType.DMA
    shard = qkv_parts[0].shape[0]

    def full(rows, cols):
        return jax.ShapeDtypeStruct((8, rows, cols), BF16)

    return pl.pallas_call(
        functools.partial(start_kernel, seq_size, seq_count),
        in_specs=[any_spec] + [vmem_spec] * (6 + len(vecs)),
        out_specs=[any_spec] * 6,
        out_shape=[
            jax.ShapeDtypeStruct((seq_size * blk, feats), BF16),
            full(shard, 3 * feats), full(32, LANES), full(*w2.shape), full(*w1.shape),
            full(*wo.shape),
        ],
        scratch_shapes=[
            pltpu.VMEM((shard, 3 * feats), BF16), pltpu.VMEM(w2.shape, BF16),
            pltpu.VMEM(w1.shape, BF16), pltpu.VMEM(wo.shape, BF16), pltpu.VMEM((blk, feats), BF16),
            pltpu.VMEM((32, LANES), F32), pltpu.VMEM((32, LANES), BF16),
            dma((seq_count,)), dma((seq_size,)), dma((seq_size,)),
            dma((5, 6)), dma((5, 6)), dma((5, 7)), dma((5, 7)), dma((5,)),
        ],
        compiler_params=pltpu.CompilerParams(
            collective_id=2, has_side_effects=True, vmem_limit_bytes=VMEM_LIMIT
        ),
    )(tokens, *qkv_parts, w2, w1, wo, *vecs)


BQ, BV, BO, G1, B1, C2, G2, B2, C1 = range(9)


def unpack_vectors(full, out):
    shards, _, _ = full.shape
    feats = out.shape[1]
    part = feats // shards
    lane = lax.broadcasted_iota(jnp.int32, (LANES, feats), 0)
    column = lax.broadcasted_iota(jnp.int32, (LANES, feats), 1)
    rows = jnp.zeros((16, feats), F32)
    for k in range(shards):
        place = ((lane < part) & (column == lane + k * part)).astype(BF16)
        rows = rows + dot(full[k, 0:16, :], place, 1, 0)
    out[...] = rows
    long = feats * 4 // shards
    for k in range(shards):
        row, start = C1 + k * long // feats, k * long % feats
        for j in range(long // LANES):
            out[row : row + 1, start + j * LANES : start + (j + 1) * LANES] = full[
                k, 8 + j : 9 + j, :
            ].astype(F32)


def forward_kernel(
    seq_size, seq_count, rows_blk,
    len_ref, x_ref, wq_ref, wk_ref, wv_ref, vec_full, upstream, w2_in, w1_in, wo_in,
    q_ref, k_ref, v_ref, ctx_ref, probs_ref, vec_out, dy_out, w2_full, w1_full, wo_full,
    bias_ref, row_buf, row_send, row_recv, row_local, sem_a, sem_b, sem_c, sem_d,
):
    step = pl.program_id(0)
    last = pl.num_programs(0) - 1
    place = Place(seq_size, seq_count)
    sems = (sem_a, sem_b, sem_c, sem_d)
    rows = RowsIn(place, upstream, dy_out, row_buf, (row_send, row_recv, row_local))
    later = [
        Gather(place, full, full.at[place.me], sems, k)
        for k, full in enumerate((w2_full, w1_full, wo_full))
    ]

    @pl.when(step == 0)
    def _():
        place.barrier()
        for item in later:
            item.start(2, 3)
        for item in later:
            item.start(4, 5)
        rows.start()
        for item in later:
            item.to_core(6, 0, 1)
        rows.own(seq_size)
        unpack_vectors(vec_full, vec_out)
        valid = len_ref[jnp.clip(place.my_seq, 0, seq_count - 1)]
        position = lax.broadcasted_iota(jnp.int32, bias_ref.shape, 1)
        bias_ref[...] = jnp.where(position < valid, 0.0, 8.0 * NEG_FILL)

    x_rows = x_ref[...]
    depth = x_rows.shape[1]
    column = pl.ds(pl.multiple_of(step * LANES, LANES), LANES)
    mats = [ref[...].reshape(depth, LANES) for ref in (wq_ref, wk_ref, wv_ref)]
    both = dot(x_rows, jnp.concatenate(mats, axis=1), 1, 0)
    q_ref[...] = (both[:, :LANES] + vec_out[BQ : BQ + 1, column]).astype(BF16)
    k_ref[...] = both[:, LANES : 2 * LANES].astype(BF16)
    v_ref[...] = (both[:, 2 * LANES :] + vec_out[BV : BV + 1, column]).astype(BF16)
    attend_kernel(bias_ref, q_ref, k_ref, v_ref, ctx_ref, probs_ref, rows_blk=rows_blk)

    @pl.when(step == last - 3)
    def _():
        for item in later:
            item.arrive(2, 3)
            item.to_core(2, 3)

    @pl.when(step == last - 1)
    def _():
        for item in later[:2]:
            item.arrive(4, 5)
            item.to_core(4, 5)

    @pl.when(step == last)
    def _():
        for item in later[2:]:
            item.arrive(4, 5)
            item.to_core(4, 5)
        for item in later:
            item.finish(range(2, 6), range(7))
        rows.finish()


def forward_all(seq_size, lengths, rows, qkv_full, vec_full, upstream, w2_full, w1_full, wo_full):
    seq_len, feats = rows.shape
    seq_count, blk, _ = upstream.shape
    pairs = feats // LANES
    shard = qkv_full.shape[1]
    any_spec = pl.BlockSpec(memory_space=pl.ANY)
    dma = pltpu.SemaphoreType.DMA
    cols = pl.BlockSpec((seq_len, LANES), lambda g: (0, g))

    def mat(which):
        return pl.BlockSpec((8, shard, LANES), lambda g, w=which: (0, 0, w * pairs + g))

    fulls = [w2_full, w1_full, wo_full]
    flat = jax.ShapeDtypeStruct((seq_len, feats), BF16)
    return pl.pallas_call(
        functools.partial(forward_kernel, seq_size, seq_count, min(512, seq_len)),
        grid=(pairs,),
        in_specs=[
            pl.BlockSpec(memory_space=pltpu.SMEM),
            pl.BlockSpec((seq_len, feats), lambda g: (0, 0)),
            mat(0), mat(1), mat(2), pl.BlockSpec(vec_full.shape, lambda g: (0, 0, 0)),
        ]
        + [any_spec] * 4,
        out_specs=[cols] * 4
        + [
            pl.BlockSpec((2, seq_len, seq_len), lambda g: (g, 0, 0)),
            pl.BlockSpec((16, feats), lambda g: (0, 0)),
        ]
        + [any_spec] * 4,
        out_shape=[flat] * 4
        + [
            jax.ShapeDtypeStruct((feats // HEAD, seq_len, seq_len), BF16),
            jax.ShapeDtypeStruct((16, feats), F32),
            flat,
        ]
        + [jax.ShapeDtypeStruct(item.shape, BF16) for item in fulls],
        scratch_shapes=[
            pltpu.VMEM((1, seq_len), F32), pltpu.VMEM((blk, feats), BF16),
            dma((seq_count,)), dma((seq_size,)), dma((seq_size,)),
            dma((3, 6)), dma((3, 6)), dma((3, 7)), dma((3, 7)),
        ],
        input_output_aliases={7: 7, 8: 8, 9: 9},
        compiler_params=pltpu.CompilerParams(
            collective_id=3, has_side_effects=True, vmem_limit_bytes=VMEM_LIMIT
        ),
    )(lengths, rows, qkv_full, qkv_full, qkv_full, vec_full, upstream, *fulls)


def add_rows(dest, first, *others, start=0, count=None):
    count = dest.shape[0] if count is None else count
    size = 48 if count % 48 == 0 else min(count, 64)

    def body(i, carry):
        for k in range(size // 16):
            to = pl.ds(pl.multiple_of(start + i * size + k * 16, 16), 16)
            frm = pl.ds(pl.multiple_of(i * size + k * 16, 16), 16)
            if len(others) == 1:
                dest[to, :] = first[to, :] + others[0][frm, :]
            else:
                value = first[to, :].astype(F32)
                for other in others:
                    value = value + other[frm, :].astype(F32)
                dest[to, :] = value.astype(dest.dtype)
        return carry

    lax.fori_loop(0, count // size, body, 0, unroll=count == size)


class Chain:
    def __init__(self, place, mine, passed, arrived, total, sems, index):
        self.place, self.mine, self.passed, self.arrived = place, mine, passed, arrived
        self.total, self.index = total, index
        self.z_send, self.z_recv = sems

    def copy(self, way, src):
        at = self.place
        return remote(
            src, self.arrived.at[way], self.z_send.at[self.index, way],
            self.z_recv.at[self.index, way], (at.me, at.here + 1 - 2 * way),
        )

    def hops(self, way):
        at = self.place
        return at.here if way == 0 else at.seq_size - 1 - at.here

    def hop(self, hop):
        here, last = self.place.here, self.place.seq_size - 1

        @pl.when((here == hop) | (here == last - hop))
        def _():
            way = jnp.where(here == hop, 0, 1)
            passed = self.passed.at[way]
            if hop == 0:
                self.copy(way, self.mine).start()
            else:
                self.copy(way, passed).wait_recv()
                if hop < last:
                    add_rows(passed, self.mine, self.arrived.at[way])
                    self.copy(way, passed).start()

    def finish(self):
        last = self.place.seq_size - 1
        here = self.place.here
        inner = (here > 0) & (here < last)

        @pl.when(jnp.logical_not(inner))
        def _():
            add_rows(self.total, self.mine, self.arrived.at[jnp.where(here == 0, 1, 0)])

        @pl.when(inner)
        def _():
            add_rows(self.total, self.mine, self.arrived.at[0], self.arrived.at[1])

    def drain(self):
        for way in range(2):

            @pl.when(self.hops(way) < self.place.seq_size - 1)
            def _():
                self.copy(way, self.mine).wait_send()

    @staticmethod
    def semaphores(count):
        dma = pltpu.SemaphoreType.DMA
        return [dma((count, 2)), dma((count, 2))]


class Carried:
    def __init__(self, place, source, result, bufs, sems, copy_sems, index, slot):
        mine, passed, arrived, total = bufs
        self.chain = Chain(place, mine, passed, arrived, total, sems, index)
        self.load = pltpu.make_async_copy(source, mine, copy_sems.at[slot, 0])
        self.out = pltpu.make_async_copy(total, result, copy_sems.at[slot, 1])

    def begin(self):
        self.load.wait()
        self.chain.hop(0)

    def hop(self, hop):
        self.chain.hop(hop)

    def finish(self):
        self.chain.finish()
        self.out.start()

    def drain(self):
        self.chain.drain()
        self.out.wait()


class Reduce:
    def __init__(self, place, source, result, bufs, sems, index, z_arrived=None, z_sems=None):
        self.place, self.source, self.index = place, source, index
        self.own, self.other, self.first_x, self.first_y, self.second = bufs
        (
            self.own_sem, self.core_send, self.core_recv, self.one_send, self.one_recv,
            self.two_send, self.two_recv,
        ) = sems
        at = place
        self.apart = [(r % 2) * at.to_x + (r // 2) * at.to_y for r in range(4)]
        self.rows = self.own.shape[1]
        self.half = self.rows // 2
        self.chain, total = None, self.own.at[0]
        if z_arrived is not None:
            total = self.own.at[3]
            self.chain = Chain(place, self.own.at[0], self.other, z_arrived, total, z_sems, index)
        self.out = pltpu.make_async_copy(total, result, self.own_sem.at[index, 3])

    def keep_copy(self, r):
        return pltpu.make_async_copy(
            self.source(self.place.me + self.apart[r]), self.own.at[r],
            self.own_sem.at[self.index, r],
        )

    def core_copy(self, r):
        at = self.place
        return remote(
            self.source(at.me + at.to_core + self.apart[r]), self.other.at[r],
            self.core_send.at[self.index, r], self.core_recv.at[self.index, r], at.core_dev,
        )

    def one_copy(self, way, k):
        half = self.half
        if way == 0:
            src, dst = self.own.at[(1, 3)[k], pl.ds(0, half)], self.first_x.at[k]
        else:
            src, dst = self.own.at[(2, 3)[k], pl.ds(half, half)], self.first_y.at[k]
        return remote(
            src, dst, self.one_send.at[self.index, way, k], self.one_recv.at[self.index, way, k],
            (self.place.x_dev, self.place.y_dev)[way],
        )

    def two_copy(self, way):
        src = self.own.at[(2, 1)[way], pl.ds(way * self.half, self.half)]
        return remote(
            src, self.second.at[way], self.two_send.at[self.index, way],
            self.two_recv.at[self.index, way], (self.place.y_dev, self.place.x_dev)[way],
        )

    def begin(self):
        for r in (3, 1, 2, 0):
            self.core_copy(r).start()
            self.keep_copy(r).start()

    def core_stage(self):
        for r in (3, 1, 2, 0):
            self.keep_copy(r).wait()
            self.core_copy(r).wait_recv()
            add_rows(self.own.at[r], self.own.at[r], self.other.at[r])
            if r == 3:
                self.one_copy(0, 1).start()
                self.one_copy(1, 1).start()
            elif r == 1:
                self.one_copy(0, 0).start()
            elif r == 2:
                self.one_copy(1, 0).start()

    def one_stage(self):
        firsts = (self.first_x, self.first_y)
        for k in (1, 0):
            for way in range(2):
                self.one_copy(way, k).wait_recv()
                dest = self.own.at[(2, 1)[way] if k else 0]
                add_rows(dest, dest, firsts[way].at[k], start=way * self.half, count=self.half)
                if k:
                    self.two_copy(way).start()

    def two_stage(self):
        mine = self.own.at[0]
        for way in range(2):
            self.two_copy(way).wait_recv()
            add_rows(mine, mine, self.second.at[way], start=way * self.half, count=self.half)
        if self.chain is not None:
            self.chain.hop(0)

    def hop(self, hop):
        self.chain.hop(hop)

    def finish(self):
        if self.chain is not None:
            self.one_copy(0, 1).wait_send()
            self.one_copy(1, 1).wait_send()
            self.chain.finish()
        self.out.start()

    def drain(self):
        for r in range(4):
            self.core_copy(r).wait_send()
        for way in range(2):
            self.one_copy(way, 0).wait_send()
            if self.chain is None:
                self.one_copy(way, 1).wait_send()
            self.two_copy(way).wait_send()
        if self.chain is not None:
            self.chain.drain()
        self.out.wait()

    @staticmethod
    def scratch(count, rows, width):
        return [
            pltpu.VMEM((count, lead, rows // split, width), BF16)
            for lead, split in ((4, 1), (4, 1), (2, 2), (2, 2), (2, 2))
        ]

    @staticmethod
    def semaphores(count):
        dma = pltpu.SemaphoreType.DMA
        return [
            dma((count, 4)), dma((count, 4)), dma((count, 4)),
            dma((count, 2, 2)), dma((count, 2, 2)), dma((count, 2)), dma((count, 2)),
        ]


class RowsOut:
    def __init__(self, place, rows, blocks, sems):
        self.place, self.rows, self.blocks = place, rows, blocks
        self.send_sem, self.recv_sem, self.local_sem = sems
        self.blk = blocks.shape[1]

    def part(self, pos):
        return self.rows.at[pl.ds(pos * self.blk, self.blk)]

    def copy(self, pos):
        at = self.place
        return remote(
            self.part(pos), self.blocks.at[at.my_seq], self.send_sem.at[pos],
            self.recv_sem.at[at.my_seq], (at.me, pos),
        )

    def keep(self, pos):
        return pltpu.make_async_copy(
            self.part(pos), self.blocks.at[self.place.my_seq], self.local_sem.at[0]
        )

    def start(self, pos):
        at = self.place

        @pl.when(at.is_owner & (at.here != pos))
        def _():
            self.copy(pos).start()

        @pl.when(at.is_owner & (at.here == pos))
        def _():
            self.keep(pos).start()

    def finish(self):
        at = self.place
        for seq in range(at.seq_count):

            @pl.when(at.here != seq + at.shift)
            def _():
                remote(
                    self.part(0), self.blocks.at[seq], self.send_sem.at[0], self.recv_sem.at[seq],
                    (at.me, (at.here + 1) % at.seq_size),
                ).wait_recv()

        @pl.when(at.is_owner)
        def _():
            self.keep(0).wait()
            for pos in range(at.seq_size):

                @pl.when(at.here != pos)
                def _():
                    self.copy(pos).wait_send()


INV_SQRT2 = 0.7071067811865476
INV_SQRT_2PI = 0.3989422804014327


def normalize(resid):
    centre = resid - jnp.mean(resid, axis=-1, keepdims=True)
    inv = lax.rsqrt(jnp.mean(centre * centre, axis=-1, keepdims=True) + EPS)
    return centre * inv, inv


def normalize_back(normed, inv, grad_normed):
    mean_grad = jnp.mean(grad_normed, axis=-1, keepdims=True)
    mean_both = jnp.mean(grad_normed * normed, axis=-1, keepdims=True)
    return inv * (grad_normed - mean_grad - normed * mean_both)


def gelu_parts(pre):
    cumulative = 0.5 * (1.0 + lax.erf(pre * INV_SQRT2))
    slope = cumulative + pre * (INV_SQRT_2PI * jnp.exp(-0.5 * pre * pre))
    return pre * cumulative, slope


def feed_kernel(
    rows_blk, ctx_ref, x_ref, wo_ref, vec_ref, w1_ref, w2_ref, dy_ref,
    act_ref, slope_ref, out_ref, resid_ref, normed_ref, inv_ref, vec_out,
    hidden_low,
):
    step = pl.program_id(0)
    seq_len, feats = x_ref.shape
    width = slope_ref.shape[1]
    parts = act_ref.shape[0]
    blocks = [pl.ds(i * rows_blk, rows_blk) for i in range(seq_len // rows_blk)]

    def vec(k):
        return vec_ref[k : k + 1, :]

    @pl.when(step == 0)
    def _():
        merge = wo_ref[...].reshape(feats, feats)
        for rows in blocks:
            resid = x_ref[rows, :].astype(F32) + (dot(ctx_ref[rows, :], merge, 1, 0) + vec(BO))
            normed, inv = normalize(resid)
            normed_ref[rows, :] = normed
            inv_ref[rows, :] = jnp.broadcast_to(inv, (rows_blk, LANES))
            hidden_low[rows, :] = (normed * vec(G1) + vec(B1)).astype(BF16)
            resid_ref[rows, :] = jnp.zeros((rows_blk, feats), F32)

    expand = w1_ref[...].reshape(feats, width)
    shrink = w2_ref[...].reshape(width, feats)
    shift = vec_ref[pl.ds(C1 + step, 1), :]
    for rows in blocks:
        act, slope = gelu_parts(dot(hidden_low[rows, :], expand, 1, 0) + shift)
        act_low = act.astype(BF16)
        for k in range(width // LANES):
            column = k // parts * LANES
            act_ref[k % parts, rows, column : column + LANES] = act_low[
                :, k * LANES : (k + 1) * LANES
            ]
        slope_ref[rows, :] = slope.astype(BF16)
        resid_ref[rows, :] += dot(act_low, shrink, 1, 0)

    @pl.when(step == pl.num_programs(0) - 1)
    def _():
        sums = [jnp.zeros((1, feats), F32)] * 3
        for rows in blocks:
            hidden = normed_ref[rows, :] * vec(G1) + vec(B1)
            normed, inv = normalize(hidden + (resid_ref[rows, :] + vec(C2)))
            out_ref[rows, :] = (normed * vec(G2) + vec(B2)).astype(BF16)
            dy = dy_ref[rows, :].astype(F32)
            grad = normalize_back(normed, inv, vec(G2) * dy)
            resid_ref[rows, :] = grad
            terms = (dy * normed, dy, grad.astype(BF16).astype(F32))
            sums = [
                total + jnp.sum(term, axis=0, keepdims=True) for total, term in zip(sums, terms)
            ]
        for k, total in enumerate(sums):
            vec_out[k : k + 1, :] = total


def feed_forward(ctx, inputs, wo_full, vecs, w1_full, w2_full, dy):
    seq_len, feats = inputs.shape
    shard = w1_full.shape[1]
    hidden = w1_full.shape[2]
    steps = hidden // feats
    once = pl.Buffered(1)

    def whole(shape, mode=None):
        return pl.BlockSpec(shape, lambda j: (0,) * len(shape), pipeline_mode=mode)

    rows, rows_f32 = (seq_len, feats), jax.ShapeDtypeStruct((seq_len, feats), F32)
    cols = pl.BlockSpec(rows, lambda j: (0, j))
    wide = jax.ShapeDtypeStruct((seq_len, hidden), BF16)
    parts = w2_full.shape[1] // LANES
    act_block = pl.BlockSpec((parts, seq_len, feats // parts), lambda j: (0, 0, j))
    act_shape = jax.ShapeDtypeStruct((parts, seq_len, hidden // parts), BF16)
    return pl.pallas_call(
        functools.partial(feed_kernel, min(256, seq_len)),
        grid=(steps,),
        in_specs=[
            whole(rows, once), whole(rows, once), whole(wo_full.shape, once),
            whole(vecs.shape, once),
            pl.BlockSpec((8, shard, feats), lambda j: (0, 0, j)),
            pl.BlockSpec((8 // steps, w2_full.shape[1], feats), lambda j: (j, 0, 0)),
            whole(rows, once),
        ],
        out_specs=[act_block, cols, whole(rows), whole(rows), whole(rows), whole((seq_len, LANES)),
                   whole((8, feats))],
        out_shape=[
            act_shape, wide, jax.ShapeDtypeStruct(rows, BF16), rows_f32, rows_f32,
            jax.ShapeDtypeStruct((seq_len, LANES), F32), jax.ShapeDtypeStruct((8, feats), F32),
        ],
        scratch_shapes=[pltpu.VMEM(rows, BF16)],
        compiler_params=pltpu.CompilerParams(vmem_limit_bytes=VMEM_LIMIT),
    )(ctx, inputs, wo_full, vecs, w1_full, w2_full, dy)


def feed_back_kernel(seq_size, seq_count, rows_blk, *refs):
    refs = list(refs)

    def take(count):
        got = refs[:count]
        del refs[:count]
        return got

    act_ref, slope_ref, w1_ref, w2_ref, resid_ref, normed_ref, inv_ref, ctx_ref = take(8)
    wo_ref, vec_ref, vec_in, out_rows = take(4)
    d_w1, resid_out, grad_ctx, d_wo, vec_out, w2_part, w1_part, out_blocks = take(8)
    grad_ffn, hidden_low, grad_pre, d_w2, early, vec_sums = take(6)
    w2_bufs = take(5)
    w2_sems = take(7)
    w1_bufs = take(5)
    w1_sems = take(7)
    out_sems = take(3)

    step = pl.program_id(0)
    last = pl.num_programs(0) - 1
    seq_len, feats = resid_ref.shape
    parts, chunk = d_w2.shape[0], d_w2.shape[2]
    early_count = early.shape[0]
    place = Place(seq_size, seq_count)
    outs = RowsOut(place, out_rows, out_blocks, out_sems)
    jobs = [
        Reduce(
            place, lambda shard, c=c: d_w2.at[c, shard], w2_part.at[pl.ds(c * chunk, chunk)],
            [buf.at[c] for buf in w2_bufs], w2_sems, c,
        )
        for c in range(parts)
    ]
    jobs += [
        Reduce(
            place, lambda shard, c=c: early.at[c, shard], w1_part.at[c],
            [buf.at[c] for buf in w1_bufs], w1_sems, c,
        )
        for c in range(early_count)
    ]
    t0, t1, t2, w0, w1 = jobs
    begin, core = Reduce.begin, Reduce.core_stage
    one, two = Reduce.one_stage, Reduce.two_stage
    ticks = (
        ((begin, t0),),
        ((begin, t1), (core, t0)),
        ((begin, t2), (core, t1)),
        ((one, t0), (core, t2), (begin, w0)),
        ((one, t1), (two, t0), (core, w0), (begin, w1)),
        ((one, t2), (two, t1), (core, w1)),
    )

    def run(stages):
        for stage, job in stages:
            stage(job)

    blocks = [pl.ds(i * rows_blk, rows_blk) for i in range(seq_len // rows_blk)]

    def vec(k):
        return vec_ref[k : k + 1, :]

    @pl.when(step == 0)
    def _():
        place.barrier()
        for pos in range(seq_size):
            outs.start(pos)
        for rows in blocks:
            grad_ffn[rows, :] = resid_ref[rows, :].astype(BF16)
            hidden_low[rows, :] = (normed_ref[rows, :] * vec(G1) + vec(B1)).astype(BF16)
            resid_out[rows, :] = resid_ref[rows, :]

    @pl.when(step < parts)
    def _():
        part = dot(act_ref[0], grad_ffn[...], 0, 0).astype(BF16)
        d_w2[step] = part.reshape(d_w2.shape[1:])

    @pl.when(step >= parts)
    def _():
        width = slope_ref.shape[1]
        shrink = w2_ref[...].reshape(width, feats)
        expand = w1_ref[...].reshape(feats, width)
        for rows in blocks:
            grad_act = dot(grad_ffn[rows, :], shrink, 1, 1)
            low = (grad_act * slope_ref[rows, :].astype(F32)).astype(BF16)
            grad_pre[rows, :] = low
            resid_out[rows, :] += dot(low, expand, 1, 1)
        total = dot(jnp.ones((8, seq_len), BF16), grad_pre[...], 1, 0)
        outer = dot(hidden_low[...], grad_pre[...], 0, 0)
        low = outer.astype(BF16).reshape(early.shape[1:])

        @pl.when(step < parts + early_count)
        def _():
            early[jnp.minimum(step - parts, early_count - 1)] = low

        @pl.when(step >= parts + early_count)
        def _():
            d_w1[0] = low

        vec_sums[pl.ds(step - parts, 1), :] = total[0:1, :]

    for at_step, stages in enumerate(ticks):

        @pl.when(step == at_step)
        def _():
            run(stages)

    @pl.when(step == last)
    def _():
        run(((one, w0), (Reduce.finish, t0), (Reduce.finish, t1)))
        merge = wo_ref[...].reshape(feats, feats)
        sums = [jnp.zeros((1, feats), F32)] * 3
        for k, rows in enumerate(blocks):
            if k == len(blocks) - 1:
                run(((two, t2), (Reduce.finish, t2)))
            grad_hidden = resid_out[rows, :]
            normed = normed_ref[rows, :]
            grad = normalize_back(normed, inv_ref[rows, 0:1], vec(G1) * grad_hidden)
            resid_out[rows, :] = grad
            low = grad.astype(BF16)
            grad_ctx[rows, :] = dot(low, merge, 1, 1).astype(BF16)
            grad_pre[rows, :] = low
            terms = (grad_hidden * normed, grad_hidden, low.astype(F32))
            sums = [
                total + jnp.sum(term, axis=0, keepdims=True) for total, term in zip(sums, terms)
            ]
        run(((one, w1),))
        d_wo[...] = dot(ctx_ref[...], grad_pre[...], 0, 0).astype(BF16).reshape(d_wo.shape)
        row = lax.broadcasted_iota(jnp.int32, (16, 1), 0)
        lines = sums + [vec_in[k : k + 1, :] for k in range(3)]
        lines = lines + [vec_sums[k : k + 1, :] for k in range(4)]
        packed = jnp.zeros((16, feats), F32)
        for k, line in enumerate(lines):
            packed = jnp.where(row == k, line, packed)
        vec_out[...] = packed.astype(BF16)

        run(((two, w0), (Reduce.finish, w0), (two, w1), (Reduce.finish, w1)))
        for job in jobs:
            job.drain()
        outs.finish()


def feed_back(
    seq_size, seq_count, act, slope, w1_full, w2_full, resid, normed, inv, ctx, wo_full, vecs,
    vec_in, out_rows,
):
    seq_len, feats = ctx.shape
    shard, w2_rows = w1_full.shape[1], w2_full.shape[1]
    steps = slope.shape[1] // feats
    parts = act.shape[0]
    early = 2
    blk = seq_len // seq_size
    once = pl.Buffered(1)
    any_spec = pl.BlockSpec(memory_space=pl.ANY)
    dma = pltpu.SemaphoreType.DMA

    def whole(shape, mode=None):
        return pl.BlockSpec(shape, lambda j: (0,) * len(shape), pipeline_mode=mode)

    def first(j):
        return jnp.minimum(j, parts - 1)

    def second(j):
        return jnp.maximum(j - parts, 0)

    rows = (seq_len, feats)
    return pl.pallas_call(
        functools.partial(feed_back_kernel, seq_size, seq_count, min(256, seq_len)),
        grid=(parts + steps,),
        in_specs=[
            pl.BlockSpec((1,) + act.shape[1:], lambda j: (first(j), 0, 0)),
            pl.BlockSpec(rows, lambda j: (0, second(j))),
            pl.BlockSpec((8, shard, feats), lambda j: (0, 0, second(j))),
            pl.BlockSpec((8 // steps, w2_rows, feats), lambda j: (second(j), 0, 0)),
            whole(rows, once), whole(rows, once), whole(inv.shape, once), whole(rows, once),
            whole(wo_full.shape, once), whole(vecs.shape, once), whole(vec_in.shape, once),
            any_spec,
        ],
        out_specs=[
            pl.BlockSpec((1, 8, shard, feats), lambda j: (jnp.maximum(j - parts - early, 0), 0, 0, 0)),
            whole(rows), whole(rows), whole(wo_full.shape), whole((16, feats)),
            any_spec, any_spec, any_spec,
        ],
        out_shape=[
            jax.ShapeDtypeStruct((steps - early, 8, shard, feats), BF16),
            jax.ShapeDtypeStruct(rows, F32), jax.ShapeDtypeStruct(rows, BF16),
            jax.ShapeDtypeStruct(wo_full.shape, BF16), jax.ShapeDtypeStruct((16, feats), BF16),
            jax.ShapeDtypeStruct((w2_rows, feats), BF16),
            jax.ShapeDtypeStruct((early, shard, feats), BF16),
            jax.ShapeDtypeStruct((seq_count, blk, feats), BF16),
        ],
        scratch_shapes=[
            pltpu.VMEM(rows, BF16), pltpu.VMEM(rows, BF16), pltpu.VMEM(rows, BF16),
            pltpu.VMEM((parts, 8, w2_rows // parts, feats), BF16),
            pltpu.VMEM((early, 8, shard, feats), BF16),
            pltpu.VMEM((8, feats), F32),
        ]
        + Reduce.scratch(parts, w2_rows // parts, feats)
        + Reduce.semaphores(parts)
        + Reduce.scratch(early, shard, feats)
        + Reduce.semaphores(early)
        + [dma((seq_size,)), dma((seq_count,)), dma((1,))],
        compiler_params=pltpu.CompilerParams(
            collective_id=4, has_side_effects=True, vmem_limit_bytes=VMEM_MAX
        ),
    )(
        act, slope, w1_full, w2_full, resid, normed, inv, ctx, wo_full, vecs, vec_in, out_rows
    )


def pair_column(feats, which, pair):
    return (pair // 2) * feats + (pair % 2) * 3 * LANES + which * LANES


def backward_kernel(seq_size, seq_count, rows_blk, *refs):
    refs = list(refs)

    def take(count):
        got = refs[:count]
        del refs[:count]
        return got

    q_ref, k_ref, v_ref, ctx_ref, grad_ref, probs_ref, vec_ref = take(7)
    x_in, qkv_in, resid_in, d_w1, d_wo, w2_part, w1_part = take(7)
    w2_total, w1_total, wo_total, qkv_total, vec_total, token_out = take(6)
    key_acc, value_acc, grads, x_rows, qkv_mat, resid, token_rows = take(7)
    mats, bias_rows, vec_src = take(3)
    w1_count = d_w1.shape[0]
    early_count = w1_part.shape[0]
    mat_count = w1_count + 4
    bufs = take(5)
    (arrived,) = take(1)
    vec_bufs = take(5)
    (vec_arrived,) = take(1)
    w2_bufs = take(4)
    w1_bufs = take(4)
    sems = take(7)
    z_sems = take(2)
    load_sem, carried_sems = take(2)
    token_sems = take(3)

    step = pl.program_id(0)
    last = pl.num_programs(0) - 1
    place = Place(seq_size, seq_count)
    seq_len, feats = x_rows.shape

    def outer_source(c):
        if c < w1_count:
            return lambda shard: d_w1.at[c, shard]
        if c == w1_count:
            return lambda shard: d_wo.at[shard]
        return lambda shard: mats.at[c - w1_count - 1, shard]

    w1_totals = [w1_total.at[:, pl.ds(c * feats, feats)] for c in range(early_count + w1_count)]
    totals = w1_totals[early_count:]
    totals += [wo_total] + [qkv_total.at[:, pl.ds(c * feats, feats)] for c in range(3)]
    jobs = [
        Reduce(
            place, outer_source(c), totals[c], [buf.at[c] for buf in bufs], sems, c,
            arrived.at[c], z_sems,
        )
        for c in range(mat_count)
    ]
    jobs.append(
        Reduce(
            place, lambda shard: vec_src.at[shard], vec_total, [buf.at[0] for buf in vec_bufs],
            sems, mat_count, vec_arrived.at[0], z_sems,
        )
    )
    parts = w2_bufs[0].shape[0]
    chunk = w2_part.shape[0] // parts
    pieces = [
        (w2_part.at[pl.ds(c * chunk, chunk)], w2_total.at[pl.ds(c * chunk, chunk)], w2_bufs, c)
        for c in range(parts)
    ]
    pieces += [(w1_part.at[c], w1_totals[c], w1_bufs, c) for c in range(early_count)]
    carried = [
        Carried(
            place, source, result, [buf.at[c] for buf in held], z_sems, carried_sems,
            mat_count + 1 + slot, slot,
        )
        for slot, (source, result, held, c) in enumerate(pieces)
    ]
    w2, w3, wo, qkv_a, qkv_b, qkv_c, vec = jobs
    t0, t1, t2, t3, t4 = carried
    blk = seq_len // seq_size
    loads = [
        pltpu.make_async_copy(src, dst, load_sem.at[k])
        for k, (src, dst) in enumerate(((x_in, x_rows), (qkv_in, qkv_mat), (resid_in, resid)))
    ]
    tokens = RowsOut(place, token_rows, token_out, token_sems)

    core, one, two = Reduce.core_stage, Reduce.one_stage, Reduce.two_stage

    def hop1(job):
        job.hop(1)

    def hop2(job):
        job.hop(2)

    def end(job):
        job.hop(3)
        job.finish()

    ticks = (
        ((core, w2), (core, w3)),
        ((core, wo), (hop1, t0)),
        ((one, w2),),
        ((one, w3), (hop1, t1), (hop2, t0)),
        ((one, wo), (core, qkv_a), (hop1, t2)),
        ((two, w2), (two, w3), (hop1, t3), (hop2, t1), (end, t0)),
        ((two, wo), (hop2, t2)),
        ((one, qkv_a), (hop1, t4), (hop2, t3), (end, t1)),
        ((core, qkv_b), (two, qkv_a), (hop1, w2), (end, t2)),
        ((hop1, w3), (hop2, t4), (end, t3)),
        ((one, qkv_b), (hop1, wo), (hop2, w2)),
        ((two, qkv_b), (hop1, qkv_a), (hop2, w3), (end, t4)),
    )
    after = (
        ((hop2, wo), (end, w2)),
        ((core, qkv_c),),
        ((core, vec), (hop1, qkv_b), (end, w3)),
        ((hop2, qkv_a),),
    )
    rest = (
        (one, qkv_c), (one, vec), (two, qkv_c), (two, vec), (end, wo), (hop2, qkv_b),
        (end, qkv_a), (hop1, qkv_c), (hop1, vec), (end, qkv_b),
        (hop2, qkv_c), (hop2, vec), (end, qkv_c), (end, vec),
    )

    @pl.when(step == 0)
    def _():
        place.barrier()
        for job in carried:
            job.load.start()
        for job in (w2, w3, wo):
            job.begin()
        for load in loads:
            load.start()
        for job in carried:
            job.begin()

    @pl.when(step == 2)
    def _():
        qkv_a.begin()

    @pl.when(step == 4)
    def _():
        qkv_b.begin()

    def store(which, rows, values):
        grads[rows, which * LANES : (which + 1) * LANES] = values

    def between(half):
        for at_step in range(len(ticks) // 2):

            @pl.when(step == at_step)
            def _():
                for stage, job in ticks[2 * at_step + half]:
                    stage(job)

    attend_back_pair(
        q_ref, k_ref, v_ref, ctx_ref, grad_ref, probs_ref, store, key_acc, value_acc, rows_blk,
        between,
    )

    @pl.when(step == 0)
    def _():
        for load in loads:
            load.wait()

    width = 3 * LANES
    column = pl.multiple_of(step * LANES, LANES)
    half = pl.multiple_of((step % 2) * width, LANES)
    outer = dot(x_rows[...], grads[...], 0, 0).astype(BF16)
    mats[step // 2, :, :, pl.ds(half, width)] = outer.reshape(8, feats // 8, width)
    sums = dot(jnp.ones((16, seq_len), BF16), grads[...], 1, 0)
    bias_rows[0, :, pl.ds(column, LANES)] = sums[:, :LANES]
    bias_rows[1, :, pl.ds(column, LANES)] = sums[:, 2 * LANES :]
    mat = jnp.concatenate(
        [
            qkv_mat[:, :, pl.ds(pl.multiple_of(which * feats + column, LANES), LANES)].reshape(
                feats, LANES
            )
            for which in range(3)
        ],
        axis=1,
    )

    @pl.when(step < last)
    def _():
        for pos in range(seq_size):
            rows = pl.ds(pos * blk, blk)
            resid[rows, :] += dot(grads[rows, :], mat, 1, 1)

    @pl.when(step == last)
    def _():
        qkv_c.begin()
        row = lax.broadcasted_iota(jnp.int32, (16, 1), 0)
        biases = jnp.where(row == 0, bias_rows[0], bias_rows[1]).astype(BF16)
        for shard in range(8):
            vec_src[shard, 0:16, :] = vec_ref[...]
            vec_src[shard, 16:32, :] = biases
        vec.begin()
        for pos in range(seq_size):
            rows = pl.ds(pos * blk, blk)
            total = resid[rows, :] + dot(grads[rows, :], mat, 1, 1)
            token_rows[rows, :] = total.astype(BF16)
            tokens.start(pos)
            for stage, job in after[pos]:
                stage(job)
        for stage, job in rest:
            stage(job)
        for job in jobs + carried:
            job.drain()
        tokens.finish()


def backward_all(
    seq_size, seq_count, query, key, value, ctx, grad_ctx, probs, vecs, inputs, qkv_full, resid,
    d_w1, d_wo, w2_part, w1_part,
):
    seq_len, feats = ctx.shape
    blk = seq_len // seq_size
    shard = qkv_full.shape[1]
    w1_count = d_w1.shape[0]
    early = w1_part.shape[0]
    count = w1_count + 4
    parts = w2_part.shape[0] // LANES
    any_spec = pl.BlockSpec(memory_space=pl.ANY)
    cols = pl.BlockSpec((seq_len, LANES), lambda g: (0, g))
    dma = pltpu.SemaphoreType.DMA

    def low(*shape):
        return jax.ShapeDtypeStruct(shape, BF16)

    return pl.pallas_call(
        functools.partial(backward_kernel, seq_size, seq_count, seq_len // 2),
        grid=(feats // LANES,),
        in_specs=[cols] * 5
        + [
            pl.BlockSpec((2, seq_len, seq_len), lambda g: (g, 0, 0)),
            pl.BlockSpec(vecs.shape, lambda g: (0, 0)),
        ]
        + [any_spec] * 7,
        out_specs=[any_spec] * 6,
        out_shape=[
            low(*w2_part.shape), low(shard, (early + w1_count) * feats), low(shard, feats),
            low(shard, 3 * feats), low(32, feats), low(seq_count, blk, feats),
        ],
        scratch_shapes=[pltpu.VMEM((2, HEAD, seq_len), F32)] * 2
        + [
            pltpu.VMEM((seq_len, 3 * LANES), BF16),
            pltpu.VMEM((seq_len, feats), BF16),
            pltpu.VMEM(qkv_full.shape, BF16),
            pltpu.VMEM((seq_len, feats), F32),
            pltpu.VMEM((seq_len, feats), BF16),
            pltpu.VMEM((3, 8, shard, feats), BF16),
            pltpu.VMEM((2, 16, feats), F32),
            pltpu.VMEM((8, 32, feats), BF16),
        ]
        + Reduce.scratch(count, shard, feats)
        + [pltpu.VMEM((count, 2, shard, feats), BF16)]
        + Reduce.scratch(1, 32, feats)
        + [pltpu.VMEM((1, 2, 32, feats), BF16)]
        + [
            pltpu.VMEM((parts,) + lead + (LANES, feats), BF16) for lead in ((), (2,), (2,), ())
        ]
        + [pltpu.VMEM((early,) + lead + (shard, feats), BF16) for lead in ((), (2,), (2,), ())]
        + Reduce.semaphores(count + 1)
        + Chain.semaphores(count + 1 + parts + early)
        + [dma((3,)), dma((parts + early, 2)), dma((seq_size,)), dma((seq_count,)), dma((1,))],
        compiler_params=pltpu.CompilerParams(
            collective_id=1, has_side_effects=True, vmem_limit_bytes=VMEM_MAX
        ),
    )(
        query, key, value, ctx, grad_ctx, probs, vecs, inputs, qkv_full, resid, d_w1, d_wo,
        w2_part, w1_part,
    )


def widen_kernel(w2_in, w1_in, wo_in, qkv_in, vec_in, *outs):
    w2_out, w1_out, wo_out = outs[:3]
    mats, vecs = outs[3:6], outs[6:]
    feats = wo_in.shape[1]
    w2_out[...] = w2_in[...].astype(F32)
    w1_out[...] = w1_in[...].astype(F32)
    wo_out[...] = wo_in[...].astype(F32)
    for which, mat in enumerate(mats):
        for pair in range(feats // LANES):
            start = pair_column(feats, which, pair)
            mat[:, pair * LANES : (pair + 1) * LANES] = qkv_in[:, start : start + LANES].astype(F32)
    me = lax.axis_index("dp")
    part = feats // 8
    rows = vec_in[...].astype(F32)
    own = jnp.zeros((rows.shape[0], part), F32)
    long = jnp.zeros((1, 4 * part), F32)
    for k in range(8):
        own = jnp.where(me == k, rows[:, k * part : (k + 1) * part], own)
        row, start = 6 + k // 2, (k % 2) * 4 * part
        long = jnp.where(me == k, rows[row : row + 1, start : start + 4 * part], long)
    for k, row in enumerate((16, 17, 2, 0, 1, 5, 3, 4)):
        vecs[k][...] = own[row : row + 1, :]
    vecs[8][...] = long.reshape(4 * part)


def widen(w2_sum, w1_sum, wo_sum, qkv_sum, vec_sum):
    feats = wo_sum.shape[1]
    part = feats // 8

    def wide(*shape):
        return jax.ShapeDtypeStruct(shape, F32)

    return pl.pallas_call(
        widen_kernel,
        out_shape=[wide(*w2_sum.shape), wide(*w1_sum.shape)]
        + [wide(*wo_sum.shape)] * 4
        + [wide(1, part)] * 8
        + [wide(4 * part)],
        compiler_params=pltpu.CompilerParams(vmem_limit_bytes=VMEM_LIMIT),
    )(w2_sum, w1_sum, wo_sum, qkv_sum, vec_sum)


def column_sum(rows):
    return jnp.sum(rows, axis=0, dtype=F32)


def per_device(mesh_shape, tokens, lengths, *rest):
    weights, upstream = rest[:15], rest[15]
    dp_size, seq_size = mesh_shape
    seq_count, row_count, feats = tokens.shape
    dp_index = lax.axis_index("dp")
    here = lax.axis_index("seq")
    spare = seq_size - seq_count

    def owner_shift(dp):
        return spare * (dp % 2)

    my_seq = jnp.clip(here - owner_shift(dp_index), 0, seq_count - 1)

    def owned_by(dp, pos):
        seq = pos - owner_shift(dp)
        return 0 <= seq < seq_count

    def shift_pairs(step, to_owner):
        pairs = []
        for dp in range(dp_size):
            for pos in range(seq_size):
                dest = (pos + step) % seq_size
                if owned_by(dp, dest if to_owner else pos):
                    pairs.append((dp * seq_size + pos, dp * seq_size + dest))
        return pairs

    def gather(piece):
        return lax.all_gather(piece, "dp", axis=0, tiled=True)

    def to_owners(blocks):
        pieces = []
        for step in range(seq_size):
            dest = (here + step) % seq_size
            seq = jnp.clip(dest - owner_shift(dp_index), 0, seq_count - 1)
            piece = lax.dynamic_index_in_dim(blocks, seq, 0, keepdims=False)
            if step == 0:
                owner = (here >= owner_shift(dp_index)) & (here < owner_shift(dp_index) + seq_count)
                piece = jnp.where(owner, piece, jnp.zeros_like(piece))
            else:
                piece = lax.ppermute(piece, ("dp", "seq"), shift_pairs(step, True))
            pieces.append(piece)
        order = (here - jnp.arange(seq_size)) % seq_size
        return jnp.take(jnp.stack(pieces), order, axis=0).reshape(-1, feats)

    def from_owners(rows):
        pieces = rows.reshape(seq_size, row_count, feats)
        arrived = []
        for step in range(seq_size):
            piece = lax.dynamic_index_in_dim(pieces, (here - step) % seq_size, 0, keepdims=False)
            if step:
                piece = lax.ppermute(piece, ("dp", "seq"), shift_pairs(seq_size - step, False))
            arrived.append(piece)
        stack = jnp.stack(arrived)
        order = (jnp.arange(seq_count) + owner_shift(dp_index) - here) % seq_size
        return jnp.take(stack, order, axis=0)

    wq, bq, wk, wv, bv, wo, bo, g1, b1, w1, c1, w2, c2, g2, b2 = weights
    shard_rows = feats // dp_size
    seq_len = seq_size * row_count
    direct = (dp_size, seq_size, feats, seq_len) == (8, 4, 768, 1024) and seq_count == 3
    vec_parts = (bq, bv, bo, g1, b1, c2, g2, b2, c1)
    vec_sizes = [item.shape[0] for item in vec_parts]
    vec_len = sum(vec_sizes)
    if not direct:
        packed = jnp.concatenate(vec_parts).astype(BF16)
        position = lax.iota(jnp.int32, seq_len)
        valid_len = lax.dynamic_index_in_dim(lengths, my_seq, 0, keepdims=False)
        key_bias = jnp.where(position < valid_len, 0.0, 8.0 * NEG_FILL).astype(F32)
        key_bias = key_bias.reshape(1, seq_len)
        qkv_mat = gather(jnp.concatenate([wq, wk, wv], axis=1).astype(BF16))
        packed = lax.all_gather(packed, "dp", axis=0, tiled=False)
        merge_mat, expand_mat, reduce_mat = [gather(item.astype(BF16)) for item in (wo, w1, w2)]
        vecs = []
        start = 0
        for size in vec_sizes:
            vecs.append(packed[:, start : start + size].reshape(1, -1).astype(F32))
            start += size
        bq, bv, bo, g1, b1, c2, g2, b2, c1 = vecs

    if direct:
        inputs, qkv_full, vec_full, w2_part, w1_part, wo_part = start_all(
            seq_size, tokens, (wq, wk, wv),
            [item.reshape(1, -1) for item in vec_parts[:-1]] + [c1], w2, w1, wo,
        )
        query, key, value, ctx, probs, vec_rows, dy, w2_full, w1_full, wo_full = forward_all(
            seq_size, lengths, inputs, qkv_full, vec_full, upstream, w2_part, w1_part, wo_part
        )
        act, slope, out_rows, grad_resid2, normed1, inv1, second_sums = feed_forward(
            ctx, inputs, wo_full, vec_rows, w1_full, w2_full, dy
        )
        d_w1, grad_resid1, grad_ctx, d_wo, vec_sums, part_w2, part_w1, output = feed_back(
            seq_size, seq_count, act, slope, w1_full, w2_full, grad_resid2, normed1, inv1, ctx,
            wo_full, vec_rows, second_sums, out_rows,
        )
        *sums, token_grad = backward_all(
            seq_size, seq_count, query, key, value, ctx, grad_ctx, probs, vec_sums, inputs,
            qkv_full, grad_resid1, d_w1, d_wo, part_w2, part_w1,
        )
        sum_w2, sum_w1, s_wo, s_wq, s_wk, s_wv, *vec_sums = widen(*sums)
        vec_sums = [item.reshape(-1) for item in vec_sums]
        s_bq, s_bv, s_bo, s_g1, s_b1, s_c2, s_g2, s_b2, s_c1 = vec_sums
    else:
        inputs = to_owners(tokens)
        dy = to_owners(upstream).astype(F32)
        qkv = dot(inputs, qkv_mat, 1, 0)
        query = (qkv[:, :feats] + bq).astype(BF16)
        key = qkv[:, feats : 2 * feats].astype(BF16)
        value = (qkv[:, 2 * feats :] + bv).astype(BF16)
        ctx, probs = attend(key_bias, query, key, value)
        normed1, inv1 = normalize(inputs.astype(F32) + dot(ctx, merge_mat, 1, 0) + bo)
        hidden = normed1 * g1 + b1
        hidden_low = hidden.astype(BF16)
        pre = dot(hidden_low, expand_mat, 1, 0) + c1
        phi_cum = 0.5 * (1.0 + lax.erf(pre * INV_SQRT2))
        act = (pre * phi_cum).astype(BF16)
        slope = (phi_cum + pre * (INV_SQRT_2PI * jnp.exp(-0.5 * pre * pre))).astype(BF16)
        normed2, inv2 = normalize(hidden + dot(act, reduce_mat, 1, 0) + c2)
        result = (normed2 * g2 + b2).astype(BF16)
        output = from_owners(result)

        d_g2 = column_sum(dy * normed2)
        d_b2 = column_sum(dy)
        grad_resid2 = normalize_back(normed2, inv2, g2 * dy)
        grad_ffn = grad_resid2.astype(BF16)
        d_w2 = dot(act, grad_ffn, 0, 0).astype(BF16)
        d_c2 = column_sum(grad_ffn)
        grad_pre = (dot(grad_ffn, reduce_mat, 1, 1) * slope.astype(F32)).astype(BF16)
        d_w1 = dot(hidden_low, grad_pre, 0, 0).astype(BF16)
        d_c1 = column_sum(grad_pre)
        grad_hidden = grad_resid2 + dot(grad_pre, expand_mat, 1, 1)
        d_g1 = column_sum(grad_hidden * normed1)
        d_b1 = column_sum(grad_hidden)
        grad_resid1 = normalize_back(normed1, inv1, g1 * grad_hidden)
        grad_att = grad_resid1.astype(BF16)
        d_wo = dot(ctx, grad_att, 0, 0).astype(BF16)
        d_bo = column_sum(grad_att)
        grad_ctx = dot(grad_att, merge_mat, 1, 1).astype(BF16)
        grad_qkv = attend_back(query, key, value, ctx, grad_ctx, probs)
        token_rows = grad_resid1
        d_qkv = []
        for which in range(3):
            mat = qkv_mat[:, which * feats : (which + 1) * feats]
            token_rows = token_rows + dot(grad_qkv[which], mat, 1, 1)
            d_qkv.append(dot(inputs, grad_qkv[which], 0, 0).astype(BF16))
        d_bq = column_sum(grad_qkv[0])
        d_bv = column_sum(grad_qkv[2])
        token_grad = from_owners(token_rows.astype(BF16))
        vec_grads = (d_bq, d_bv, d_bo, d_g1, d_b1, d_c2, d_g2, d_b2, d_c1)
        vec_pack = jnp.concatenate([item.reshape(dp_size, -1) for item in vec_grads], axis=1)
        vec_cols = -(-vec_len // (shard_rows * LANES)) * LANES
        vec_pack = jnp.pad(vec_pack, ((0, 0), (0, shard_rows * vec_cols - vec_len)))
        vec_pack = vec_pack.reshape(feats, vec_cols).astype(BF16)

        def reduce(full):
            own = lax.psum_scatter(full, "dp", scatter_dimension=0, tiled=True)
            return lax.psum(own, "seq").astype(F32)

        sum_w2 = reduce(d_w2)
        sum_w1 = reduce(d_w1)
        sum_rest = reduce(jnp.concatenate([d_wo] + d_qkv + [vec_pack], axis=1))
        s_wo, s_wq, s_wk, s_wv = [sum_rest[:, i * feats : (i + 1) * feats] for i in range(4)]
        flat = sum_rest[:, 4 * feats :].reshape(-1)
        out_vecs = []
        start = 0
        for size in vec_sizes:
            out_vecs.append(flat[start : start + size])
            start += size
        s_bq, s_bv, s_bo, s_g1, s_b1, s_c2, s_g2, s_b2, s_c1 = out_vecs
    return (
        output,
        token_grad,
        s_wq,
        s_bq,
        s_wk,
        s_wv,
        s_bv,
        s_wo,
        s_bo,
        s_g1,
        s_b1,
        sum_w1,
        s_c1,
        sum_w2,
        s_c2,
        s_g2,
        s_b2,
    )


def solution(mesh):
    rows, mat, vec = P("dp", "seq", None), P("dp", None), P("dp")
    params = (mat, vec, mat, mat, vec, mat, vec, vec, vec, mat, vec, mat, vec, vec, vec)
    return jax.shard_map(
        functools.partial(per_device, (mesh.shape["dp"], mesh.shape["seq"])),
        mesh=mesh,
        in_specs=(rows, vec) + params + (rows,),
        out_specs=(rows, rows) + params,
        check_vma=False,
    )
```

```python
import functools

import jax
import jax.numpy as jnp
from jax import lax
from jax.experimental import pallas as pl
from jax.experimental.pallas import tpu as pltpu
from jax.sharding import PartitionSpec as P

HEAD = 64
LANES = 128
EPS = 1e-12
NEG_FILL = -1000000000.0
SCALE2 = 0.125 * 1.4426950408889634
F32 = jnp.float32
BF16 = jnp.bfloat16
VMEM_LIMIT = 60 * 1024 * 1024
VMEM_MAX = 67043328


def dot(left, right, left_dim, right_dim):
    return lax.dot_general(
        left, right, (((left_dim,), (right_dim,)), ((), ())), preferred_element_type=F32
    )


def attend_kernel(bias_ref, q_ref, k_ref, v_ref, ctx_ref, probs_ref, *, rows_blk):
    seq_len = q_ref.shape[0]
    lane = lax.broadcasted_iota(jnp.int32, (1, LANES), 1)
    bias = bias_ref[...]
    for blk in range(seq_len // rows_blk):
        rows = pl.ds(blk * rows_blk, rows_blk)
        query = q_ref[rows, :]
        mixed = []
        for head in range(2):
            mine = (lane < HEAD) if head == 0 else (lane >= HEAD)
            query_h = jnp.where(mine, query, jnp.zeros_like(query))
            score = dot(query_h, k_ref[...], 1, 1) + bias
            top = jnp.max(score, axis=1, keepdims=True)
            expo = jnp.exp2((score - top) * SCALE2)
            total = jnp.sum(expo, axis=1, keepdims=True)
            probs = (expo * (1.0 / total)).astype(BF16)
            probs_ref[head, rows, :] = probs
            mixed.append(dot(probs, v_ref[...], 1, 0))
        ctx_ref[rows, :] = jnp.where(lane < HEAD, mixed[0], mixed[1]).astype(BF16)


def attend(bias, query, key, value):
    seq_len, feats = query.shape
    cols = pl.BlockSpec((seq_len, LANES), lambda g: (0, g))
    return pl.pallas_call(
        functools.partial(attend_kernel, rows_blk=min(512, seq_len)),
        grid=(feats // LANES,),
        in_specs=[pl.BlockSpec((1, seq_len), lambda g: (0, 0)), cols, cols, cols],
        out_specs=[cols, pl.BlockSpec((2, seq_len, seq_len), lambda g: (g, 0, 0))],
        out_shape=[
            jax.ShapeDtypeStruct((seq_len, feats), BF16),
            jax.ShapeDtypeStruct((feats // HEAD, seq_len, seq_len), BF16),
        ],
        compiler_params=pltpu.CompilerParams(vmem_limit_bytes=VMEM_LIMIT),
    )(bias, query, key, value)


def attend_back_pair(
    q_ref, k_ref, v_ref, ctx_ref, grad_ref, probs_ref, store, key_acc, value_acc, rows_blk,
    between=None,
):
    seq_len = q_ref.shape[0]
    lane = lax.broadcasted_iota(jnp.int32, (1, LANES), 1)
    for blk in range(seq_len // rows_blk):
        rows = pl.ds(blk * rows_blk, rows_blk)
        query = q_ref[rows, :]
        grad = grad_ref[rows, :]
        overlap = ctx_ref[rows, :].astype(F32) * grad.astype(F32)
        query_t = query.T
        grad_t = grad.T
        grad_query = []
        for head in range(2):
            mine = (lane < HEAD) if head == 0 else (lane >= HEAD)
            part = slice(head * HEAD, (head + 1) * HEAD)
            grad_h = jnp.where(mine, grad, jnp.zeros_like(grad))
            inner = jnp.sum(jnp.where(mine, overlap, 0.0), axis=1, keepdims=True)
            probs = probs_ref[head, rows, :]
            grad_probs = dot(grad_h, v_ref[...], 1, 1)
            grad_score = (probs.astype(F32) * (grad_probs - inner)).astype(BF16)
            grad_query.append(dot(grad_score, k_ref[...], 1, 0))
            grad_key = dot(query_t[part], grad_score, 1, 0)
            grad_value = dot(grad_t[part], probs, 1, 0)
            if blk == 0:
                key_acc[head] = grad_key
                value_acc[head] = grad_value
            else:
                key_acc[head] += grad_key
                value_acc[head] += grad_value
        mixed = jnp.where(lane < HEAD, grad_query[0], grad_query[1])
        store(0, rows, (0.125 * mixed).astype(BF16))
        if between is not None:
            between(blk)
    everything = pl.ds(0, seq_len)
    grad_key = jnp.concatenate([key_acc[0], key_acc[1]], axis=0)
    store(1, everything, (0.125 * grad_key).T.astype(BF16))
    grad_value = jnp.concatenate([value_acc[0], value_acc[1]], axis=0)
    store(2, everything, grad_value.T.astype(BF16))


def attend_back_kernel(
    q_ref, k_ref, v_ref, ctx_ref, grad_ref, probs_ref, out_ref, key_acc, value_acc, *, rows_blk
):
    def store(which, rows, values):
        out_ref[which, rows, :] = values

    attend_back_pair(
        q_ref, k_ref, v_ref, ctx_ref, grad_ref, probs_ref, store, key_acc, value_acc, rows_blk
    )


def attend_back(query, key, value, ctx, grad_ctx, probs):
    seq_len, feats = ctx.shape
    cols = pl.BlockSpec((seq_len, LANES), lambda g: (0, g))
    return pl.pallas_call(
        functools.partial(attend_back_kernel, rows_blk=min(512, seq_len)),
        grid=(feats // LANES,),
        in_specs=[cols] * 5 + [pl.BlockSpec((2, seq_len, seq_len), lambda g: (g, 0, 0))],
        out_specs=pl.BlockSpec((3, seq_len, LANES), lambda g: (0, 0, g)),
        out_shape=jax.ShapeDtypeStruct((3, seq_len, feats), BF16),
        scratch_shapes=[pltpu.VMEM((2, HEAD, seq_len), F32)] * 2,
        compiler_params=pltpu.CompilerParams(vmem_limit_bytes=VMEM_LIMIT),
    )(query, key, value, ctx, grad_ctx, probs)


MESH = pl.DeviceIdType.MESH


def remote(src, dst, send, recv, device):
    return pltpu.make_async_remote_copy(
        src_ref=src, dst_ref=dst, send_sem=send, recv_sem=recv,
        device_id=device, device_id_type=MESH,
    )


class Place:
    def __init__(self, seq_size, seq_count):
        self.me = me = lax.axis_index("dp")
        self.here = here = lax.axis_index("seq")
        core, x_at, y_at = me % 2, (me // 2) % 2, (me // 4) % 2
        self.to_core, self.to_x, self.to_y = 1 - 2 * core, 2 - 4 * x_at, 4 - 8 * y_at
        self.core_dev = (me + self.to_core, here)
        self.x_dev = (me + self.to_x, here)
        self.y_dev = (me + self.to_y, here)
        self.shift = (seq_size - seq_count) * core
        self.my_seq = here - self.shift
        self.is_owner = (self.my_seq >= 0) & (self.my_seq < seq_count)
        self.seq_size, self.seq_count = seq_size, seq_count

    def barrier(self):
        barrier = pltpu.get_barrier_semaphore()
        for device in (self.core_dev, self.x_dev, self.y_dev):
            pl.semaphore_signal(barrier, inc=1, device_id=device, device_id_type=MESH)
        for step in range(1, self.seq_size):
            pl.semaphore_signal(
                barrier, inc=1, device_id=(self.me, (self.here + step) % self.seq_size),
                device_id_type=MESH,
            )
        pl.semaphore_wait(barrier, 3 + self.seq_size - 1)


class Gather:
    def __init__(self, place, full, own, sems, index):
        self.place, self.full, self.own, self.index = place, full, own, index
        self.send_sem, self.recv_sem, self.core_send, self.core_recv = sems

    def half(self, which):
        count = self.full.shape[1] // 2
        return pl.ds(which * count, count)

    def piece(self, p):
        at = self.place
        rows = self.half(p % 2)
        shard = at.me + (0, 0, 0, 0, at.to_x, at.to_y)[p]
        src = self.own.at[rows] if p < 4 else self.full.at[shard, rows]
        device = (at.x_dev, at.y_dev, at.y_dev, at.x_dev, at.y_dev, at.x_dev)[p]
        return remote(
            src, self.full.at[shard, rows],
            self.send_sem.at[self.index, p], self.recv_sem.at[self.index, p], device,
        )

    def core_piece(self, p):
        at = self.place
        if p == 6:
            src, dst = self.own, self.full.at[at.me]
        else:
            across = at.to_x + at.to_y
            shard = at.me + (at.to_x, at.to_y, at.to_y, at.to_x, across, across)[p]
            src = dst = self.full.at[shard, self.half(p % 2)]
        return remote(
            src, dst, self.core_send.at[self.index, p], self.core_recv.at[self.index, p],
            at.core_dev,
        )

    def start(self, *pieces):
        for p in pieces:
            self.piece(p).start()

    def arrive(self, *pieces):
        for p in pieces:
            self.piece(p).wait_recv()

    def to_core(self, *pieces):
        for p in pieces:
            self.core_piece(p).start()

    def finish(self, pieces, core_pieces):
        for p in core_pieces:
            self.core_piece(p).wait_recv()
        for p in pieces:
            self.piece(p).wait_send()
        for p in core_pieces:
            self.core_piece(p).wait_send()


class RowsIn:
    def __init__(self, place, blocks, whole, buf, sems):
        self.place, self.blocks, self.whole, self.buf = place, blocks, whole, buf
        self.send_sem, self.recv_sem, self.local_sem = sems
        self.rows = blocks.shape[1]

    def to(self, seq, source):
        at = self.place
        return remote(
            self.blocks.at[seq], self.whole.at[pl.ds(source * self.rows, self.rows)],
            self.send_sem.at[seq], self.recv_sem.at[source], (at.me, seq + at.shift),
        )

    def own(self, count):
        at = self.place

        def out(pos, k):
            return pltpu.make_async_copy(
                self.buf, self.whole.at[pl.ds(pos * self.rows, self.rows)], self.local_sem.at[k]
            )

        @pl.when(at.is_owner)
        def _():
            load = pltpu.make_async_copy(self.blocks.at[at.my_seq], self.buf, self.local_sem.at[0])
            load.start()
            load.wait()
            out(at.here, 1).start()
            out(at.here, 1).wait()

        @pl.when(jnp.logical_not(at.is_owner))
        def _():
            self.buf[...] = jnp.zeros_like(self.buf)
            for pos in range(at.seq_size):
                out(pos, pos).start()
            for pos in range(at.seq_size):
                out(pos, pos).wait()

    def start(self):
        at = self.place
        for seq in range(at.seq_count):

            @pl.when(at.here != seq + at.shift)
            def _():
                self.to(seq, at.here).start()

    def finish(self):
        at = self.place

        @pl.when(at.is_owner)
        def _():
            for pos in range(at.seq_size):

                @pl.when(at.here != pos)
                def _():
                    remote(
                        self.blocks.at[0], self.whole.at[pl.ds(pos * self.rows, self.rows)],
                        self.send_sem.at[0], self.recv_sem.at[pos],
                        (at.me, (at.here + 1) % at.seq_size),
                    ).wait_recv()

        for seq in range(at.seq_count):

            @pl.when(at.here != seq + at.shift)
            def _():
                self.to(seq, at.here).wait_send()


def start_kernel(
    seq_size, seq_count, tokens, wq, wk, wv, w2, w1, wo, *refs,
):
    vec_refs, refs = refs[:9], refs[9:]
    rows_out, qkv_full, vec_full, w2_full, w1_full, wo_full = refs[:6]
    qkv_low, w2_low, w1_low, wo_low, row_buf, vec_wide, vecs = refs[6:13]
    row_send, row_recv, row_local, sem_a, sem_b, sem_c, sem_d, own_sem = refs[13:]
    place = Place(seq_size, seq_count)
    sems = (sem_a, sem_b, sem_c, sem_d)
    rows = RowsIn(place, tokens, rows_out, row_buf, (row_send, row_recv, row_local))
    first = [
        Gather(place, qkv_full, qkv_low, sems, 0),
        Gather(place, vec_full, vecs, sems, 1),
    ]
    later = [
        Gather(place, w2_full, w2_low, sems, 2),
        Gather(place, w1_full, w1_low, sems, 3),
        Gather(place, wo_full, wo_low, sems, 4),
    ]
    place.barrier()
    rows.start()
    feats = wq.shape[1]
    vec_wide[...] = jnp.zeros_like(vec_wide)
    for k, item in enumerate(vec_refs[:8]):
        vec_wide[k : k + 1, 0 : item.shape[1]] = item[...]
    for k in range(vec_refs[8].shape[0] // LANES):
        vec_wide[8 + k : 9 + k, :] = vec_refs[8][k * LANES : (k + 1) * LANES].reshape(1, LANES)
    vecs[...] = vec_wide[...].astype(BF16)
    for k, item in enumerate((wq, wk, wv)):
        qkv_low[:, k * feats : (k + 1) * feats] = item[...].astype(BF16)
    for item in first:
        item.start(0, 1)
    for item in first:
        item.start(2, 3)
        item.to_core(6)
    w2_low[...] = w2[...].astype(BF16)
    w1_low[...] = w1[...].astype(BF16)
    wo_low[...] = wo[...].astype(BF16)
    keep = [
        pltpu.make_async_copy(item.own, item.full.at[place.me], own_sem.at[item.index])
        for item in first + later
    ]
    for copy in keep:
        copy.start()
    for item in first:
        item.arrive(0, 1)
        item.start(4, 5)
        item.to_core(0, 1)
    for item in later:
        item.start(0, 1)
    rows.own(seq_size)
    for item in first:
        item.arrive(2, 3)
        item.to_core(2, 3)
    for item in first:
        item.arrive(4, 5)
        item.to_core(4, 5)
    for item in first:
        item.finish(range(6), range(7))
    for item in later:
        item.arrive(0, 1)
        for p in (0, 1):
            item.piece(p).wait_send()
    for copy in keep:
        copy.wait()
    rows.finish()


def start_all(seq_size, tokens, qkv_parts, vecs, w2, w1, wo):
    seq_count, blk, feats = tokens.shape
    any_spec = pl.BlockSpec(memory_space=pl.ANY)
    vmem_spec = pl.BlockSpec(memory_space=pltpu.VMEM)
    dma = pltpu.SemaphoreType.DMA
    shard = qkv_parts[0].shape[0]

    def full(rows, cols):
        return jax.ShapeDtypeStruct((8, rows, cols), BF16)

    return pl.pallas_call(
        functools.partial(start_kernel, seq_size, seq_count),
        in_specs=[any_spec] + [vmem_spec] * (6 + len(vecs)),
        out_specs=[any_spec] * 6,
        out_shape=[
            jax.ShapeDtypeStruct((seq_size * blk, feats), BF16),
            full(shard, 3 * feats), full(32, LANES), full(*w2.shape), full(*w1.shape),
            full(*wo.shape),
        ],
        scratch_shapes=[
            pltpu.VMEM((shard, 3 * feats), BF16), pltpu.VMEM(w2.shape, BF16),
            pltpu.VMEM(w1.shape, BF16), pltpu.VMEM(wo.shape, BF16), pltpu.VMEM((blk, feats), BF16),
            pltpu.VMEM((32, LANES), F32), pltpu.VMEM((32, LANES), BF16),
            dma((seq_count,)), dma((seq_size,)), dma((seq_size,)),
            dma((5, 6)), dma((5, 6)), dma((5, 7)), dma((5, 7)), dma((5,)),
        ],
        compiler_params=pltpu.CompilerParams(
            collective_id=2, has_side_effects=True, vmem_limit_bytes=VMEM_LIMIT
        ),
    )(tokens, *qkv_parts, w2, w1, wo, *vecs)


BQ, BV, BO, G1, B1, C2, G2, B2, C1 = range(9)


def unpack_vectors(full, out):
    shards, _, _ = full.shape
    feats = out.shape[1]
    part = feats // shards
    lane = lax.broadcasted_iota(jnp.int32, (LANES, feats), 0)
    column = lax.broadcasted_iota(jnp.int32, (LANES, feats), 1)
    rows = jnp.zeros((16, feats), F32)
    for k in range(shards):
        place = ((lane < part) & (column == lane + k * part)).astype(BF16)
        rows = rows + dot(full[k, 0:16, :], place, 1, 0)
    out[...] = rows
    long = feats * 4 // shards
    for k in range(shards):
        row, start = C1 + k * long // feats, k * long % feats
        for j in range(long // LANES):
            out[row : row + 1, start + j * LANES : start + (j + 1) * LANES] = full[
                k, 8 + j : 9 + j, :
            ].astype(F32)


def forward_kernel(
    seq_size, seq_count, rows_blk,
    len_ref, x_ref, wq_ref, wk_ref, wv_ref, vec_full, upstream, w2_in, w1_in, wo_in,
    q_ref, k_ref, v_ref, ctx_ref, probs_ref, vec_out, dy_out, w2_full, w1_full, wo_full,
    bias_ref, row_buf, row_send, row_recv, row_local, sem_a, sem_b, sem_c, sem_d,
):
    step = pl.program_id(0)
    last = pl.num_programs(0) - 1
    place = Place(seq_size, seq_count)
    sems = (sem_a, sem_b, sem_c, sem_d)
    rows = RowsIn(place, upstream, dy_out, row_buf, (row_send, row_recv, row_local))
    later = [
        Gather(place, full, full.at[place.me], sems, k)
        for k, full in enumerate((w2_full, w1_full, wo_full))
    ]

    @pl.when(step == 0)
    def _():
        place.barrier()
        for item in later:
            item.start(2, 3)
        for item in later:
            item.start(4, 5)
        rows.start()
        for item in later:
            item.to_core(6, 0, 1)
        rows.own(seq_size)
        unpack_vectors(vec_full, vec_out)
        valid = len_ref[jnp.clip(place.my_seq, 0, seq_count - 1)]
        position = lax.broadcasted_iota(jnp.int32, bias_ref.shape, 1)
        bias_ref[...] = jnp.where(position < valid, 0.0, 8.0 * NEG_FILL)

    x_rows = x_ref[...]
    depth = x_rows.shape[1]
    column = pl.ds(pl.multiple_of(step * LANES, LANES), LANES)
    mats = [ref[...].reshape(depth, LANES) for ref in (wq_ref, wk_ref, wv_ref)]
    both = dot(x_rows, jnp.concatenate(mats, axis=1), 1, 0)
    q_ref[...] = (both[:, :LANES] + vec_out[BQ : BQ + 1, column]).astype(BF16)
    k_ref[...] = both[:, LANES : 2 * LANES].astype(BF16)
    v_ref[...] = (both[:, 2 * LANES :] + vec_out[BV : BV + 1, column]).astype(BF16)
    attend_kernel(bias_ref, q_ref, k_ref, v_ref, ctx_ref, probs_ref, rows_blk=rows_blk)

    @pl.when(step == last - 3)
    def _():
        for item in later:
            item.arrive(2, 3)
            item.to_core(2, 3)

    @pl.when(step == last - 1)
    def _():
        for item in later[:2]:
            item.arrive(4, 5)
            item.to_core(4, 5)

    @pl.when(step == last)
    def _():
        for item in later[2:]:
            item.arrive(4, 5)
            item.to_core(4, 5)
        for item in later:
            item.finish(range(2, 6), range(7))
        rows.finish()


def forward_all(seq_size, lengths, rows, qkv_full, vec_full, upstream, w2_full, w1_full, wo_full):
    seq_len, feats = rows.shape
    seq_count, blk, _ = upstream.shape
    pairs = feats // LANES
    shard = qkv_full.shape[1]
    any_spec = pl.BlockSpec(memory_space=pl.ANY)
    dma = pltpu.SemaphoreType.DMA
    cols = pl.BlockSpec((seq_len, LANES), lambda g: (0, g))

    def mat(which):
        return pl.BlockSpec((8, shard, LANES), lambda g, w=which: (0, 0, w * pairs + g))

    fulls = [w2_full, w1_full, wo_full]
    flat = jax.ShapeDtypeStruct((seq_len, feats), BF16)
    return pl.pallas_call(
        functools.partial(forward_kernel, seq_size, seq_count, min(512, seq_len)),
        grid=(pairs,),
        in_specs=[
            pl.BlockSpec(memory_space=pltpu.SMEM),
            pl.BlockSpec((seq_len, feats), lambda g: (0, 0)),
            mat(0), mat(1), mat(2), pl.BlockSpec(vec_full.shape, lambda g: (0, 0, 0)),
        ]
        + [any_spec] * 4,
        out_specs=[cols] * 4
        + [
            pl.BlockSpec((2, seq_len, seq_len), lambda g: (g, 0, 0)),
            pl.BlockSpec((16, feats), lambda g: (0, 0)),
        ]
        + [any_spec] * 4,
        out_shape=[flat] * 4
        + [
            jax.ShapeDtypeStruct((feats // HEAD, seq_len, seq_len), BF16),
            jax.ShapeDtypeStruct((16, feats), F32),
            flat,
        ]
        + [jax.ShapeDtypeStruct(item.shape, BF16) for item in fulls],
        scratch_shapes=[
            pltpu.VMEM((1, seq_len), F32), pltpu.VMEM((blk, feats), BF16),
            dma((seq_count,)), dma((seq_size,)), dma((seq_size,)),
            dma((3, 6)), dma((3, 6)), dma((3, 7)), dma((3, 7)),
        ],
        input_output_aliases={7: 7, 8: 8, 9: 9},
        compiler_params=pltpu.CompilerParams(
            collective_id=3, has_side_effects=True, vmem_limit_bytes=VMEM_LIMIT
        ),
    )(lengths, rows, qkv_full, qkv_full, qkv_full, vec_full, upstream, *fulls)


def add_rows(dest, first, *others, start=0, count=None):
    count = dest.shape[0] if count is None else count
    size = 48 if count == 48 else min(count, 32)

    def body(i, carry):
        for k in range(size // 16):
            to = pl.ds(pl.multiple_of(start + i * size + k * 16, 16), 16)
            frm = pl.ds(pl.multiple_of(i * size + k * 16, 16), 16)
            if len(others) == 1:
                dest[to, :] = first[to, :] + others[0][frm, :]
            else:
                value = first[to, :].astype(F32)
                for other in others:
                    value = value + other[frm, :].astype(F32)
                dest[to, :] = value.astype(dest.dtype)
        return carry

    lax.fori_loop(0, count // size, body, 0, unroll=count == size)


class Chain:
    def __init__(self, place, mine, passed, arrived, total, sems, index):
        self.place, self.mine, self.passed, self.arrived = place, mine, passed, arrived
        self.total, self.index = total, index
        self.z_send, self.z_recv = sems

    def copy(self, way, src):
        at = self.place
        return remote(
            src, self.arrived.at[way], self.z_send.at[self.index, way],
            self.z_recv.at[self.index, way], (at.me, at.here + 1 - 2 * way),
        )

    def hops(self, way):
        at = self.place
        return at.here if way == 0 else at.seq_size - 1 - at.here

    def hop(self, hop):
        here, last = self.place.here, self.place.seq_size - 1

        @pl.when((here == hop) | (here == last - hop))
        def _():
            way = jnp.where(here == hop, 0, 1)
            passed = self.passed.at[way]
            if hop == 0:
                self.copy(way, self.mine).start()
            else:
                self.copy(way, passed).wait_recv()
                if hop < last:
                    add_rows(passed, self.mine, self.arrived.at[way])
                    self.copy(way, passed).start()

    def finish(self):
        last = self.place.seq_size - 1
        here = self.place.here
        inner = (here > 0) & (here < last)

        @pl.when(jnp.logical_not(inner))
        def _():
            add_rows(self.total, self.mine, self.arrived.at[jnp.where(here == 0, 1, 0)])

        @pl.when(inner)
        def _():
            add_rows(self.total, self.mine, self.arrived.at[0], self.arrived.at[1])

    def drain(self):
        for way in range(2):

            @pl.when(self.hops(way) < self.place.seq_size - 1)
            def _():
                self.copy(way, self.mine).wait_send()

    @staticmethod
    def semaphores(count):
        dma = pltpu.SemaphoreType.DMA
        return [dma((count, 2)), dma((count, 2))]


class Carried:
    def __init__(self, place, source, result, bufs, sems, copy_sems, index, slot):
        mine, passed, arrived, total = bufs
        self.chain = Chain(place, mine, passed, arrived, total, sems, index)
        self.load = pltpu.make_async_copy(source, mine, copy_sems.at[slot, 0])
        self.out = pltpu.make_async_copy(total, result, copy_sems.at[slot, 1])

    def begin(self):
        self.load.wait()
        self.chain.hop(0)

    def hop(self, hop):
        self.chain.hop(hop)

    def finish(self):
        self.chain.finish()
        self.out.start()

    def drain(self):
        self.chain.drain()
        self.out.wait()


class Reduce:
    def __init__(self, place, source, result, bufs, sems, index, z_arrived=None, z_sems=None):
        self.place, self.source, self.index = place, source, index
        self.own, self.other, self.first_x, self.first_y, self.second = bufs
        (
            self.own_sem, self.core_send, self.core_recv, self.one_send, self.one_recv,
            self.two_send, self.two_recv,
        ) = sems
        at = place
        self.apart = [(r % 2) * at.to_x + (r // 2) * at.to_y for r in range(4)]
        self.rows = self.own.shape[1]
        self.half = self.rows // 2
        self.chain, total = None, self.own.at[0]
        if z_arrived is not None:
            total = self.own.at[3]
            self.chain = Chain(place, self.own.at[0], self.other, z_arrived, total, z_sems, index)
        self.out = pltpu.make_async_copy(total, result, self.own_sem.at[index, 3])

    def keep_copy(self, r):
        return pltpu.make_async_copy(
            self.source(self.place.me + self.apart[r]), self.own.at[r],
            self.own_sem.at[self.index, r],
        )

    def core_copy(self, r):
        at = self.place
        return remote(
            self.source(at.me + at.to_core + self.apart[r]), self.other.at[r],
            self.core_send.at[self.index, r], self.core_recv.at[self.index, r], at.core_dev,
        )

    def one_copy(self, way, k):
        half = self.half
        if way == 0:
            src, dst = self.own.at[(1, 3)[k], pl.ds(0, half)], self.first_x.at[k]
        else:
            src, dst = self.own.at[(2, 3)[k], pl.ds(half, half)], self.first_y.at[k]
        return remote(
            src, dst, self.one_send.at[self.index, way, k], self.one_recv.at[self.index, way, k],
            (self.place.x_dev, self.place.y_dev)[way],
        )

    def two_copy(self, way):
        src = self.own.at[(2, 1)[way], pl.ds(way * self.half, self.half)]
        return remote(
            src, self.second.at[way], self.two_send.at[self.index, way],
            self.two_recv.at[self.index, way], (self.place.y_dev, self.place.x_dev)[way],
        )

    def begin(self):
        for r in (3, 1, 2, 0):
            self.core_copy(r).start()
            self.keep_copy(r).start()

    def core_stage(self):
        for r in (3, 1, 2, 0):
            self.keep_copy(r).wait()
            self.core_copy(r).wait_recv()
            add_rows(self.own.at[r], self.own.at[r], self.other.at[r])
            if r == 3:
                self.one_copy(0, 1).start()
                self.one_copy(1, 1).start()
            elif r == 1:
                self.one_copy(0, 0).start()
            elif r == 2:
                self.one_copy(1, 0).start()

    def one_stage(self):
        firsts = (self.first_x, self.first_y)
        for k in (1, 0):
            for way in range(2):
                self.one_copy(way, k).wait_recv()
                dest = self.own.at[(2, 1)[way] if k else 0]
                add_rows(dest, dest, firsts[way].at[k], start=way * self.half, count=self.half)
                if k:
                    self.two_copy(way).start()

    def two_stage(self):
        mine = self.own.at[0]
        for way in range(2):
            self.two_copy(way).wait_recv()
            add_rows(mine, mine, self.second.at[way], start=way * self.half, count=self.half)
        if self.chain is not None:
            self.chain.hop(0)

    def hop(self, hop):
        self.chain.hop(hop)

    def finish(self):
        if self.chain is not None:
            self.one_copy(0, 1).wait_send()
            self.one_copy(1, 1).wait_send()
            self.chain.finish()
        self.out.start()

    def drain(self):
        for r in range(4):
            self.core_copy(r).wait_send()
        for way in range(2):
            self.one_copy(way, 0).wait_send()
            if self.chain is None:
                self.one_copy(way, 1).wait_send()
            self.two_copy(way).wait_send()
        if self.chain is not None:
            self.chain.drain()
        self.out.wait()

    @staticmethod
    def scratch(count, rows, width):
        return [
            pltpu.VMEM((count, lead, rows // split, width), BF16)
            for lead, split in ((4, 1), (4, 1), (2, 2), (2, 2), (2, 2))
        ]

    @staticmethod
    def semaphores(count):
        dma = pltpu.SemaphoreType.DMA
        return [
            dma((count, 4)), dma((count, 4)), dma((count, 4)),
            dma((count, 2, 2)), dma((count, 2, 2)), dma((count, 2)), dma((count, 2)),
        ]


class RowsOut:
    def __init__(self, place, rows, blocks, sems):
        self.place, self.rows, self.blocks = place, rows, blocks
        self.send_sem, self.recv_sem, self.local_sem = sems
        self.blk = blocks.shape[1]

    def part(self, pos):
        return self.rows.at[pl.ds(pos * self.blk, self.blk)]

    def copy(self, pos):
        at = self.place
        return remote(
            self.part(pos), self.blocks.at[at.my_seq], self.send_sem.at[pos],
            self.recv_sem.at[at.my_seq], (at.me, pos),
        )

    def keep(self, pos):
        return pltpu.make_async_copy(
            self.part(pos), self.blocks.at[self.place.my_seq], self.local_sem.at[0]
        )

    def start(self, pos):
        at = self.place

        @pl.when(at.is_owner & (at.here != pos))
        def _():
            self.copy(pos).start()

        @pl.when(at.is_owner & (at.here == pos))
        def _():
            self.keep(pos).start()

    def finish(self):
        at = self.place
        for seq in range(at.seq_count):

            @pl.when(at.here != seq + at.shift)
            def _():
                remote(
                    self.part(0), self.blocks.at[seq], self.send_sem.at[0], self.recv_sem.at[seq],
                    (at.me, (at.here + 1) % at.seq_size),
                ).wait_recv()

        @pl.when(at.is_owner)
        def _():
            self.keep(0).wait()
            for pos in range(at.seq_size):

                @pl.when(at.here != pos)
                def _():
                    self.copy(pos).wait_send()


INV_SQRT2 = 0.7071067811865476
INV_SQRT_2PI = 0.3989422804014327


def normalize(resid):
    centre = resid - jnp.mean(resid, axis=-1, keepdims=True)
    inv = lax.rsqrt(jnp.mean(centre * centre, axis=-1, keepdims=True) + EPS)
    return centre * inv, inv


def normalize_back(normed, inv, grad_normed):
    mean_grad = jnp.mean(grad_normed, axis=-1, keepdims=True)
    mean_both = jnp.mean(grad_normed * normed, axis=-1, keepdims=True)
    return inv * (grad_normed - mean_grad - normed * mean_both)


def gelu_parts(pre):
    cumulative = 0.5 * (1.0 + lax.erf(pre * INV_SQRT2))
    slope = cumulative + pre * (INV_SQRT_2PI * jnp.exp(-0.5 * pre * pre))
    return pre * cumulative, slope


def feed_kernel(
    rows_blk, ctx_ref, x_ref, wo_ref, vec_ref, w1_ref, w2_ref, dy_ref,
    act_ref, slope_ref, out_ref, resid_ref, normed_ref, inv_ref, vec_out,
    hidden_low,
):
    step = pl.program_id(0)
    seq_len, feats = x_ref.shape
    width = slope_ref.shape[1]
    parts = act_ref.shape[0]
    blocks = [pl.ds(i * rows_blk, rows_blk) for i in range(seq_len // rows_blk)]

    def vec(k):
        return vec_ref[k : k + 1, :]

    @pl.when(step == 0)
    def _():
        merge = wo_ref[...].reshape(feats, feats)
        for rows in blocks:
            resid = x_ref[rows, :].astype(F32) + (dot(ctx_ref[rows, :], merge, 1, 0) + vec(BO))
            normed, inv = normalize(resid)
            normed_ref[rows, :] = normed
            inv_ref[rows, :] = jnp.broadcast_to(inv, (rows_blk, LANES))
            hidden_low[rows, :] = (normed * vec(G1) + vec(B1)).astype(BF16)
            resid_ref[rows, :] = jnp.zeros((rows_blk, feats), F32)

    expand = w1_ref[...].reshape(feats, width)
    shrink = w2_ref[...].reshape(width, feats)
    shift = vec_ref[pl.ds(C1 + step, 1), :]
    for rows in blocks:
        act, slope = gelu_parts(dot(hidden_low[rows, :], expand, 1, 0) + shift)
        act_low = act.astype(BF16)
        for k in range(width // LANES):
            column = k // parts * LANES
            act_ref[k % parts, rows, column : column + LANES] = act_low[
                :, k * LANES : (k + 1) * LANES
            ]
        slope_ref[rows, :] = slope.astype(BF16)
        resid_ref[rows, :] += dot(act_low, shrink, 1, 0)

    @pl.when(step == pl.num_programs(0) - 1)
    def _():
        sums = [jnp.zeros((1, feats), F32)] * 3
        for rows in blocks:
            hidden = normed_ref[rows, :] * vec(G1) + vec(B1)
            normed, inv = normalize(hidden + (resid_ref[rows, :] + vec(C2)))
            out_ref[rows, :] = (normed * vec(G2) + vec(B2)).astype(BF16)
            dy = dy_ref[rows, :].astype(F32)
            grad = normalize_back(normed, inv, vec(G2) * dy)
            resid_ref[rows, :] = grad
            terms = (dy * normed, dy, grad.astype(BF16).astype(F32))
            sums = [
                total + jnp.sum(term, axis=0, keepdims=True) for total, term in zip(sums, terms)
            ]
        for k, total in enumerate(sums):
            vec_out[k : k + 1, :] = total


def feed_forward(ctx, inputs, wo_full, vecs, w1_full, w2_full, dy):
    seq_len, feats = inputs.shape
    shard = w1_full.shape[1]
    hidden = w1_full.shape[2]
    steps = hidden // feats
    once = pl.Buffered(1)

    def whole(shape, mode=None):
        return pl.BlockSpec(shape, lambda j: (0,) * len(shape), pipeline_mode=mode)

    rows, rows_f32 = (seq_len, feats), jax.ShapeDtypeStruct((seq_len, feats), F32)
    cols = pl.BlockSpec(rows, lambda j: (0, j))
    wide = jax.ShapeDtypeStruct((seq_len, hidden), BF16)
    parts = w2_full.shape[1] // LANES
    act_block = pl.BlockSpec((parts, seq_len, feats // parts), lambda j: (0, 0, j))
    act_shape = jax.ShapeDtypeStruct((parts, seq_len, hidden // parts), BF16)
    return pl.pallas_call(
        functools.partial(feed_kernel, min(256, seq_len)),
        grid=(steps,),
        in_specs=[
            whole(rows, once), whole(rows, once), whole(wo_full.shape, once),
            whole(vecs.shape, once),
            pl.BlockSpec((8, shard, feats), lambda j: (0, 0, j)),
            pl.BlockSpec((8 // steps, w2_full.shape[1], feats), lambda j: (j, 0, 0)),
            whole(rows, once),
        ],
        out_specs=[act_block, cols, whole(rows), whole(rows), whole(rows), whole((seq_len, LANES)),
                   whole((8, feats))],
        out_shape=[
            act_shape, wide, jax.ShapeDtypeStruct(rows, BF16), rows_f32, rows_f32,
            jax.ShapeDtypeStruct((seq_len, LANES), F32), jax.ShapeDtypeStruct((8, feats), F32),
        ],
        scratch_shapes=[pltpu.VMEM(rows, BF16)],
        compiler_params=pltpu.CompilerParams(vmem_limit_bytes=VMEM_LIMIT),
    )(ctx, inputs, wo_full, vecs, w1_full, w2_full, dy)


def feed_back_kernel(seq_size, seq_count, rows_blk, *refs):
    refs = list(refs)

    def take(count):
        got = refs[:count]
        del refs[:count]
        return got

    act_ref, slope_ref, w1_ref, w2_ref, resid_ref, normed_ref, inv_ref, ctx_ref = take(8)
    wo_ref, vec_ref, vec_in, out_rows = take(4)
    d_w1, resid_out, grad_ctx, d_wo, vec_out, w2_part, w1_part, out_blocks = take(8)
    grad_ffn, hidden_low, grad_pre, d_w2, early, vec_sums = take(6)
    w2_bufs = take(5)
    w2_sems = take(7)
    w1_bufs = take(5)
    w1_sems = take(7)
    out_sems = take(3)

    step = pl.program_id(0)
    last = pl.num_programs(0) - 1
    seq_len, feats = resid_ref.shape
    parts, chunk = d_w2.shape[0], d_w2.shape[2]
    early_count = early.shape[0]
    place = Place(seq_size, seq_count)
    outs = RowsOut(place, out_rows, out_blocks, out_sems)
    jobs = [
        Reduce(
            place, lambda shard, c=c: d_w2.at[c, shard], w2_part.at[pl.ds(c * chunk, chunk)],
            [buf.at[c] for buf in w2_bufs], w2_sems, c,
        )
        for c in range(parts)
    ]
    jobs += [
        Reduce(
            place, lambda shard, c=c: early.at[c, shard], w1_part.at[c],
            [buf.at[c] for buf in w1_bufs], w1_sems, c,
        )
        for c in range(early_count)
    ]
    t0, t1, t2, w0, w1 = jobs
    begin, core = Reduce.begin, Reduce.core_stage
    one, two = Reduce.one_stage, Reduce.two_stage
    ticks = (
        ((begin, t0),),
        ((begin, t1), (core, t0)),
        ((begin, t2), (core, t1)),
        ((one, t0), (core, t2), (begin, w0)),
        ((one, t1), (two, t0), (core, w0), (begin, w1)),
        ((one, t2), (two, t1), (core, w1)),
    )

    def run(stages):
        for stage, job in stages:
            stage(job)

    blocks = [pl.ds(i * rows_blk, rows_blk) for i in range(seq_len // rows_blk)]

    def vec(k):
        return vec_ref[k : k + 1, :]

    @pl.when(step == 0)
    def _():
        place.barrier()
        for pos in range(seq_size):
            outs.start(pos)
        for rows in blocks:
            grad_ffn[rows, :] = resid_ref[rows, :].astype(BF16)
            hidden_low[rows, :] = (normed_ref[rows, :] * vec(G1) + vec(B1)).astype(BF16)
            resid_out[rows, :] = resid_ref[rows, :]

    @pl.when(step < parts)
    def _():
        part = dot(act_ref[0], grad_ffn[...], 0, 0).astype(BF16)
        d_w2[step] = part.reshape(d_w2.shape[1:])

    @pl.when(step >= parts)
    def _():
        width = slope_ref.shape[1]
        shrink = w2_ref[...].reshape(width, feats)
        expand = w1_ref[...].reshape(feats, width)
        for rows in blocks:
            grad_act = dot(grad_ffn[rows, :], shrink, 1, 1)
            low = (grad_act * slope_ref[rows, :].astype(F32)).astype(BF16)
            grad_pre[rows, :] = low
            resid_out[rows, :] += dot(low, expand, 1, 1)
        total = dot(jnp.ones((8, seq_len), BF16), grad_pre[...], 1, 0)
        outer = dot(hidden_low[...], grad_pre[...], 0, 0)
        low = outer.astype(BF16).reshape(early.shape[1:])

        @pl.when(step < parts + early_count)
        def _():
            early[jnp.minimum(step - parts, early_count - 1)] = low

        @pl.when(step >= parts + early_count)
        def _():
            d_w1[0] = low

        vec_sums[pl.ds(step - parts, 1), :] = total[0:1, :]

    for at_step, stages in enumerate(ticks):

        @pl.when(step == at_step)
        def _():
            run(stages)

    @pl.when(step == last)
    def _():
        run(((one, w0), (Reduce.finish, t0), (Reduce.finish, t1)))
        merge = wo_ref[...].reshape(feats, feats)
        sums = [jnp.zeros((1, feats), F32)] * 3
        for k, rows in enumerate(blocks):
            if k == len(blocks) - 1:
                run(((two, t2), (Reduce.finish, t2)))
            grad_hidden = resid_out[rows, :]
            normed = normed_ref[rows, :]
            grad = normalize_back(normed, inv_ref[rows, 0:1], vec(G1) * grad_hidden)
            resid_out[rows, :] = grad
            low = grad.astype(BF16)
            grad_ctx[rows, :] = dot(low, merge, 1, 1).astype(BF16)
            grad_pre[rows, :] = low
            terms = (grad_hidden * normed, grad_hidden, low.astype(F32))
            sums = [
                total + jnp.sum(term, axis=0, keepdims=True) for total, term in zip(sums, terms)
            ]
        run(((one, w1),))
        d_wo[...] = dot(ctx_ref[...], grad_pre[...], 0, 0).astype(BF16).reshape(d_wo.shape)
        row = lax.broadcasted_iota(jnp.int32, (16, 1), 0)
        lines = sums + [vec_in[k : k + 1, :] for k in range(3)]
        lines = lines + [vec_sums[k : k + 1, :] for k in range(4)]
        packed = jnp.zeros((16, feats), F32)
        for k, line in enumerate(lines):
            packed = jnp.where(row == k, line, packed)
        vec_out[...] = packed.astype(BF16)

        run(((two, w0), (Reduce.finish, w0), (two, w1), (Reduce.finish, w1)))
        for job in jobs:
            job.drain()
        outs.finish()


def feed_back(
    seq_size, seq_count, act, slope, w1_full, w2_full, resid, normed, inv, ctx, wo_full, vecs,
    vec_in, out_rows,
):
    seq_len, feats = ctx.shape
    shard, w2_rows = w1_full.shape[1], w2_full.shape[1]
    steps = slope.shape[1] // feats
    parts = act.shape[0]
    early = 2
    blk = seq_len // seq_size
    once = pl.Buffered(1)
    any_spec = pl.BlockSpec(memory_space=pl.ANY)
    dma = pltpu.SemaphoreType.DMA

    def whole(shape, mode=None):
        return pl.BlockSpec(shape, lambda j: (0,) * len(shape), pipeline_mode=mode)

    def first(j):
        return jnp.minimum(j, parts - 1)

    def second(j):
        return jnp.maximum(j - parts, 0)

    rows = (seq_len, feats)
    return pl.pallas_call(
        functools.partial(feed_back_kernel, seq_size, seq_count, min(256, seq_len)),
        grid=(parts + steps,),
        in_specs=[
            pl.BlockSpec((1,) + act.shape[1:], lambda j: (first(j), 0, 0)),
            pl.BlockSpec(rows, lambda j: (0, second(j))),
            pl.BlockSpec((8, shard, feats), lambda j: (0, 0, second(j))),
            pl.BlockSpec((8 // steps, w2_rows, feats), lambda j: (second(j), 0, 0)),
            whole(rows, once), whole(rows, once), whole(inv.shape, once), whole(rows, once),
            whole(wo_full.shape, once), whole(vecs.shape, once), whole(vec_in.shape, once),
            any_spec,
        ],
        out_specs=[
            pl.BlockSpec((1, 8, shard, feats), lambda j: (jnp.maximum(j - parts - early, 0), 0, 0, 0)),
            whole(rows), whole(rows), whole(wo_full.shape), whole((16, feats)),
            any_spec, any_spec, any_spec,
        ],
        out_shape=[
            jax.ShapeDtypeStruct((steps - early, 8, shard, feats), BF16),
            jax.ShapeDtypeStruct(rows, F32), jax.ShapeDtypeStruct(rows, BF16),
            jax.ShapeDtypeStruct(wo_full.shape, BF16), jax.ShapeDtypeStruct((16, feats), BF16),
            jax.ShapeDtypeStruct((w2_rows, feats), BF16),
            jax.ShapeDtypeStruct((early, shard, feats), BF16),
            jax.ShapeDtypeStruct((seq_count, blk, feats), BF16),
        ],
        scratch_shapes=[
            pltpu.VMEM(rows, BF16), pltpu.VMEM(rows, BF16), pltpu.VMEM(rows, BF16),
            pltpu.VMEM((parts, 8, w2_rows // parts, feats), BF16),
            pltpu.VMEM((early, 8, shard, feats), BF16),
            pltpu.VMEM((8, feats), F32),
        ]
        + Reduce.scratch(parts, w2_rows // parts, feats)
        + Reduce.semaphores(parts)
        + Reduce.scratch(early, shard, feats)
        + Reduce.semaphores(early)
        + [dma((seq_size,)), dma((seq_count,)), dma((1,))],
        compiler_params=pltpu.CompilerParams(
            collective_id=4, has_side_effects=True, vmem_limit_bytes=VMEM_MAX
        ),
    )(
        act, slope, w1_full, w2_full, resid, normed, inv, ctx, wo_full, vecs, vec_in, out_rows
    )


def pair_column(feats, which, pair):
    return (pair // 2) * feats + (pair % 2) * 3 * LANES + which * LANES


def backward_kernel(seq_size, seq_count, rows_blk, *refs):
    refs = list(refs)

    def take(count):
        got = refs[:count]
        del refs[:count]
        return got

    q_ref, k_ref, v_ref, ctx_ref, grad_ref, probs_ref, vec_ref = take(7)
    x_in, qkv_in, resid_in, d_w1, d_wo, w2_part, w1_part = take(7)
    w2_total, w1_total, wo_total, qkv_total, vec_total, token_out = take(6)
    key_acc, value_acc, grads, x_rows, qkv_mat, resid, token_rows = take(7)
    mats, bias_rows, vec_src = take(3)
    w1_count = d_w1.shape[0]
    early_count = w1_part.shape[0]
    mat_count = w1_count + 4
    bufs = take(5)
    (arrived,) = take(1)
    vec_bufs = take(5)
    (vec_arrived,) = take(1)
    w2_bufs = take(4)
    w1_bufs = take(4)
    sems = take(7)
    z_sems = take(2)
    load_sem, carried_sems = take(2)
    token_sems = take(3)

    step = pl.program_id(0)
    last = pl.num_programs(0) - 1
    place = Place(seq_size, seq_count)
    seq_len, feats = x_rows.shape

    def outer_source(c):
        if c < w1_count:
            return lambda shard: d_w1.at[c, shard]
        if c == w1_count:
            return lambda shard: d_wo.at[shard]
        return lambda shard: mats.at[c - w1_count - 1, shard]

    w1_totals = [w1_total.at[:, pl.ds(c * feats, feats)] for c in range(early_count + w1_count)]
    totals = w1_totals[early_count:]
    totals += [wo_total] + [qkv_total.at[:, pl.ds(c * feats, feats)] for c in range(3)]
    jobs = [
        Reduce(
            place, outer_source(c), totals[c], [buf.at[c] for buf in bufs], sems, c,
            arrived.at[c], z_sems,
        )
        for c in range(mat_count)
    ]
    jobs.append(
        Reduce(
            place, lambda shard: vec_src.at[shard], vec_total, [buf.at[0] for buf in vec_bufs],
            sems, mat_count, vec_arrived.at[0], z_sems,
        )
    )
    parts = w2_bufs[0].shape[0]
    chunk = w2_part.shape[0] // parts
    pieces = [
        (w2_part.at[pl.ds(c * chunk, chunk)], w2_total.at[pl.ds(c * chunk, chunk)], w2_bufs, c)
        for c in range(parts)
    ]
    pieces += [(w1_part.at[c], w1_totals[c], w1_bufs, c) for c in range(early_count)]
    carried = [
        Carried(
            place, source, result, [buf.at[c] for buf in held], z_sems, carried_sems,
            mat_count + 1 + slot, slot,
        )
        for slot, (source, result, held, c) in enumerate(pieces)
    ]
    w2, w3, wo, qkv_a, qkv_b, qkv_c, vec = jobs
    t0, t1, t2, t3, t4 = carried
    blk = seq_len // seq_size
    loads = [
        pltpu.make_async_copy(src, dst, load_sem.at[k])
        for k, (src, dst) in enumerate(((x_in, x_rows), (qkv_in, qkv_mat), (resid_in, resid)))
    ]
    tokens = RowsOut(place, token_rows, token_out, token_sems)

    core, one, two = Reduce.core_stage, Reduce.one_stage, Reduce.two_stage

    def hop1(job):
        job.hop(1)

    def hop2(job):
        job.hop(2)

    def end(job):
        job.hop(3)
        job.finish()

    ticks = (
        ((core, w2), (core, w3)),
        ((core, wo), (hop1, t0)),
        ((one, w2),),
        ((one, w3), (hop1, t1), (hop2, t0)),
        ((one, wo), (core, qkv_a), (hop1, t2)),
        ((two, w2), (two, w3), (hop1, t3), (hop2, t1), (end, t0)),
        ((two, wo), (hop2, t2)),
        ((one, qkv_a), (hop1, t4), (hop2, t3), (end, t1)),
        ((core, qkv_b), (two, qkv_a), (hop1, w2), (end, t2)),
        ((hop1, w3), (hop2, t4), (end, t3)),
        ((one, qkv_b), (hop1, wo), (hop2, w2)),
        ((two, qkv_b), (hop1, qkv_a), (hop2, w3), (end, t4)),
    )
    after = (
        ((hop2, wo), (end, w2)),
        ((core, qkv_c),),
        ((core, vec), (hop1, qkv_b), (end, w3)),
        ((hop2, qkv_a),),
    )
    rest = (
        (one, qkv_c), (one, vec), (two, qkv_c), (two, vec), (end, wo), (hop2, qkv_b),
        (end, qkv_a), (hop1, qkv_c), (hop1, vec), (end, qkv_b),
        (hop2, qkv_c), (hop2, vec), (end, qkv_c), (end, vec),
    )

    @pl.when(step == 0)
    def _():
        place.barrier()
        for job in carried:
            job.load.start()
        for job in (w2, w3, wo):
            job.begin()
        for load in loads:
            load.start()
        for job in carried:
            job.begin()

    @pl.when(step == 2)
    def _():
        qkv_a.begin()

    @pl.when(step == 4)
    def _():
        qkv_b.begin()

    def store(which, rows, values):
        grads[rows, which * LANES : (which + 1) * LANES] = values

    def between(half):
        for at_step in range(len(ticks) // 2):

            @pl.when(step == at_step)
            def _():
                for stage, job in ticks[2 * at_step + half]:
                    stage(job)

    attend_back_pair(
        q_ref, k_ref, v_ref, ctx_ref, grad_ref, probs_ref, store, key_acc, value_acc, rows_blk,
        between,
    )

    @pl.when(step == 0)
    def _():
        for load in loads:
            load.wait()

    width = 3 * LANES
    column = pl.multiple_of(step * LANES, LANES)
    half = pl.multiple_of((step % 2) * width, LANES)
    outer = dot(x_rows[...], grads[...], 0, 0).astype(BF16)
    mats[step // 2, :, :, pl.ds(half, width)] = outer.reshape(8, feats // 8, width)
    sums = dot(jnp.ones((16, seq_len), BF16), grads[...], 1, 0)
    bias_rows[0, :, pl.ds(column, LANES)] = sums[:, :LANES]
    bias_rows[1, :, pl.ds(column, LANES)] = sums[:, 2 * LANES :]
    mat = jnp.concatenate(
        [
            qkv_mat[:, :, pl.ds(pl.multiple_of(which * feats + column, LANES), LANES)].reshape(
                feats, LANES
            )
            for which in range(3)
        ],
        axis=1,
    )

    @pl.when(step < last)
    def _():
        for pos in range(seq_size):
            rows = pl.ds(pos * blk, blk)
            resid[rows, :] += dot(grads[rows, :], mat, 1, 1)

    @pl.when(step == last)
    def _():
        qkv_c.begin()
        row = lax.broadcasted_iota(jnp.int32, (16, 1), 0)
        biases = jnp.where(row == 0, bias_rows[0], bias_rows[1]).astype(BF16)
        for shard in range(8):
            vec_src[shard, 0:16, :] = vec_ref[...]
            vec_src[shard, 16:32, :] = biases
        vec.begin()
        for pos in range(seq_size):
            rows = pl.ds(pos * blk, blk)
            total = resid[rows, :] + dot(grads[rows, :], mat, 1, 1)
            token_rows[rows, :] = total.astype(BF16)
            tokens.start(pos)
            for stage, job in after[pos]:
                stage(job)
        for stage, job in rest:
            stage(job)
        for job in jobs + carried:
            job.drain()
        tokens.finish()


def backward_all(
    seq_size, seq_count, query, key, value, ctx, grad_ctx, probs, vecs, inputs, qkv_full, resid,
    d_w1, d_wo, w2_part, w1_part,
):
    seq_len, feats = ctx.shape
    blk = seq_len // seq_size
    shard = qkv_full.shape[1]
    w1_count = d_w1.shape[0]
    early = w1_part.shape[0]
    count = w1_count + 4
    parts = w2_part.shape[0] // LANES
    any_spec = pl.BlockSpec(memory_space=pl.ANY)
    cols = pl.BlockSpec((seq_len, LANES), lambda g: (0, g))
    dma = pltpu.SemaphoreType.DMA

    def low(*shape):
        return jax.ShapeDtypeStruct(shape, BF16)

    return pl.pallas_call(
        functools.partial(backward_kernel, seq_size, seq_count, seq_len // 2),
        grid=(feats // LANES,),
        in_specs=[cols] * 5
        + [
            pl.BlockSpec((2, seq_len, seq_len), lambda g: (g, 0, 0)),
            pl.BlockSpec(vecs.shape, lambda g: (0, 0)),
        ]
        + [any_spec] * 7,
        out_specs=[any_spec] * 6,
        out_shape=[
            low(*w2_part.shape), low(shard, (early + w1_count) * feats), low(shard, feats),
            low(shard, 3 * feats), low(32, feats), low(seq_count, blk, feats),
        ],
        scratch_shapes=[pltpu.VMEM((2, HEAD, seq_len), F32)] * 2
        + [
            pltpu.VMEM((seq_len, 3 * LANES), BF16),
            pltpu.VMEM((seq_len, feats), BF16),
            pltpu.VMEM(qkv_full.shape, BF16),
            pltpu.VMEM((seq_len, feats), F32),
            pltpu.VMEM((seq_len, feats), BF16),
            pltpu.VMEM((3, 8, shard, feats), BF16),
            pltpu.VMEM((2, 16, feats), F32),
            pltpu.VMEM((8, 32, feats), BF16),
        ]
        + Reduce.scratch(count, shard, feats)
        + [pltpu.VMEM((count, 2, shard, feats), BF16)]
        + Reduce.scratch(1, 32, feats)
        + [pltpu.VMEM((1, 2, 32, feats), BF16)]
        + [
            pltpu.VMEM((parts,) + lead + (LANES, feats), BF16) for lead in ((), (2,), (2,), ())
        ]
        + [pltpu.VMEM((early,) + lead + (shard, feats), BF16) for lead in ((), (2,), (2,), ())]
        + Reduce.semaphores(count + 1)
        + Chain.semaphores(count + 1 + parts + early)
        + [dma((3,)), dma((parts + early, 2)), dma((seq_size,)), dma((seq_count,)), dma((1,))],
        compiler_params=pltpu.CompilerParams(
            collective_id=1, has_side_effects=True, vmem_limit_bytes=VMEM_MAX
        ),
    )(
        query, key, value, ctx, grad_ctx, probs, vecs, inputs, qkv_full, resid, d_w1, d_wo,
        w2_part, w1_part,
    )


def widen_kernel(w2_in, w1_in, wo_in, qkv_in, vec_in, *outs):
    w2_out, w1_out, wo_out = outs[:3]
    mats, vecs = outs[3:6], outs[6:]
    feats = wo_in.shape[1]
    w2_out[...] = w2_in[...].astype(F32)
    w1_out[...] = w1_in[...].astype(F32)
    wo_out[...] = wo_in[...].astype(F32)
    for which, mat in enumerate(mats):
        for pair in range(feats // LANES):
            start = pair_column(feats, which, pair)
            mat[:, pair * LANES : (pair + 1) * LANES] = qkv_in[:, start : start + LANES].astype(F32)
    me = lax.axis_index("dp")
    part = feats // 8
    rows = vec_in[...].astype(F32)
    own = jnp.zeros((rows.shape[0], part), F32)
    long = jnp.zeros((1, 4 * part), F32)
    for k in range(8):
        own = jnp.where(me == k, rows[:, k * part : (k + 1) * part], own)
        row, start = 6 + k // 2, (k % 2) * 4 * part
        long = jnp.where(me == k, rows[row : row + 1, start : start + 4 * part], long)
    for k, row in enumerate((16, 17, 2, 0, 1, 5, 3, 4)):
        vecs[k][...] = own[row : row + 1, :]
    vecs[8][...] = long.reshape(4 * part)


def widen(w2_sum, w1_sum, wo_sum, qkv_sum, vec_sum):
    feats = wo_sum.shape[1]
    part = feats // 8

    def wide(*shape):
        return jax.ShapeDtypeStruct(shape, F32)

    return pl.pallas_call(
        widen_kernel,
        out_shape=[wide(*w2_sum.shape), wide(*w1_sum.shape)]
        + [wide(*wo_sum.shape)] * 4
        + [wide(1, part)] * 8
        + [wide(4 * part)],
        compiler_params=pltpu.CompilerParams(vmem_limit_bytes=VMEM_LIMIT),
    )(w2_sum, w1_sum, wo_sum, qkv_sum, vec_sum)


def column_sum(rows):
    return jnp.sum(rows, axis=0, dtype=F32)


def per_device(mesh_shape, tokens, lengths, *rest):
    weights, upstream = rest[:15], rest[15]
    dp_size, seq_size = mesh_shape
    seq_count, row_count, feats = tokens.shape
    dp_index = lax.axis_index("dp")
    here = lax.axis_index("seq")
    spare = seq_size - seq_count

    def owner_shift(dp):
        return spare * (dp % 2)

    my_seq = jnp.clip(here - owner_shift(dp_index), 0, seq_count - 1)

    def owned_by(dp, pos):
        seq = pos - owner_shift(dp)
        return 0 <= seq < seq_count

    def shift_pairs(step, to_owner):
        pairs = []
        for dp in range(dp_size):
            for pos in range(seq_size):
                dest = (pos + step) % seq_size
                if owned_by(dp, dest if to_owner else pos):
                    pairs.append((dp * seq_size + pos, dp * seq_size + dest))
        return pairs

    def gather(piece):
        return lax.all_gather(piece, "dp", axis=0, tiled=True)

    def to_owners(blocks):
        pieces = []
        for step in range(seq_size):
            dest = (here + step) % seq_size
            seq = jnp.clip(dest - owner_shift(dp_index), 0, seq_count - 1)
            piece = lax.dynamic_index_in_dim(blocks, seq, 0, keepdims=False)
            if step == 0:
                owner = (here >= owner_shift(dp_index)) & (here < owner_shift(dp_index) + seq_count)
                piece = jnp.where(owner, piece, jnp.zeros_like(piece))
            else:
                piece = lax.ppermute(piece, ("dp", "seq"), shift_pairs(step, True))
            pieces.append(piece)
        order = (here - jnp.arange(seq_size)) % seq_size
        return jnp.take(jnp.stack(pieces), order, axis=0).reshape(-1, feats)

    def from_owners(rows):
        pieces = rows.reshape(seq_size, row_count, feats)
        arrived = []
        for step in range(seq_size):
            piece = lax.dynamic_index_in_dim(pieces, (here - step) % seq_size, 0, keepdims=False)
            if step:
                piece = lax.ppermute(piece, ("dp", "seq"), shift_pairs(seq_size - step, False))
            arrived.append(piece)
        stack = jnp.stack(arrived)
        order = (jnp.arange(seq_count) + owner_shift(dp_index) - here) % seq_size
        return jnp.take(stack, order, axis=0)

    wq, bq, wk, wv, bv, wo, bo, g1, b1, w1, c1, w2, c2, g2, b2 = weights
    shard_rows = feats // dp_size
    seq_len = seq_size * row_count
    direct = (dp_size, seq_size, feats, seq_len) == (8, 4, 768, 1024) and seq_count == 3
    vec_parts = (bq, bv, bo, g1, b1, c2, g2, b2, c1)
    vec_sizes = [item.shape[0] for item in vec_parts]
    vec_len = sum(vec_sizes)
    if not direct:
        packed = jnp.concatenate(vec_parts).astype(BF16)
        position = lax.iota(jnp.int32, seq_len)
        valid_len = lax.dynamic_index_in_dim(lengths, my_seq, 0, keepdims=False)
        key_bias = jnp.where(position < valid_len, 0.0, 8.0 * NEG_FILL).astype(F32)
        key_bias = key_bias.reshape(1, seq_len)
        qkv_mat = gather(jnp.concatenate([wq, wk, wv], axis=1).astype(BF16))
        packed = lax.all_gather(packed, "dp", axis=0, tiled=False)
        merge_mat, expand_mat, reduce_mat = [gather(item.astype(BF16)) for item in (wo, w1, w2)]
        vecs = []
        start = 0
        for size in vec_sizes:
            vecs.append(packed[:, start : start + size].reshape(1, -1).astype(F32))
            start += size
        bq, bv, bo, g1, b1, c2, g2, b2, c1 = vecs

    if direct:
        inputs, qkv_full, vec_full, w2_part, w1_part, wo_part = start_all(
            seq_size, tokens, (wq, wk, wv),
            [item.reshape(1, -1) for item in vec_parts[:-1]] + [c1], w2, w1, wo,
        )
        query, key, value, ctx, probs, vec_rows, dy, w2_full, w1_full, wo_full = forward_all(
            seq_size, lengths, inputs, qkv_full, vec_full, upstream, w2_part, w1_part, wo_part
        )
        act, slope, out_rows, grad_resid2, normed1, inv1, second_sums = feed_forward(
            ctx, inputs, wo_full, vec_rows, w1_full, w2_full, dy
        )
        d_w1, grad_resid1, grad_ctx, d_wo, vec_sums, part_w2, part_w1, output = feed_back(
            seq_size, seq_count, act, slope, w1_full, w2_full, grad_resid2, normed1, inv1, ctx,
            wo_full, vec_rows, second_sums, out_rows,
        )
        *sums, token_grad = backward_all(
            seq_size, seq_count, query, key, value, ctx, grad_ctx, probs, vec_sums, inputs,
            qkv_full, grad_resid1, d_w1, d_wo, part_w2, part_w1,
        )
        sum_w2, sum_w1, s_wo, s_wq, s_wk, s_wv, *vec_sums = widen(*sums)
        vec_sums = [item.reshape(-1) for item in vec_sums]
        s_bq, s_bv, s_bo, s_g1, s_b1, s_c2, s_g2, s_b2, s_c1 = vec_sums
    else:
        inputs = to_owners(tokens)
        dy = to_owners(upstream).astype(F32)
        qkv = dot(inputs, qkv_mat, 1, 0)
        query = (qkv[:, :feats] + bq).astype(BF16)
        key = qkv[:, feats : 2 * feats].astype(BF16)
        value = (qkv[:, 2 * feats :] + bv).astype(BF16)
        ctx, probs = attend(key_bias, query, key, value)
        normed1, inv1 = normalize(inputs.astype(F32) + dot(ctx, merge_mat, 1, 0) + bo)
        hidden = normed1 * g1 + b1
        hidden_low = hidden.astype(BF16)
        pre = dot(hidden_low, expand_mat, 1, 0) + c1
        phi_cum = 0.5 * (1.0 + lax.erf(pre * INV_SQRT2))
        act = (pre * phi_cum).astype(BF16)
        slope = (phi_cum + pre * (INV_SQRT_2PI * jnp.exp(-0.5 * pre * pre))).astype(BF16)
        normed2, inv2 = normalize(hidden + dot(act, reduce_mat, 1, 0) + c2)
        result = (normed2 * g2 + b2).astype(BF16)
        output = from_owners(result)

        d_g2 = column_sum(dy * normed2)
        d_b2 = column_sum(dy)
        grad_resid2 = normalize_back(normed2, inv2, g2 * dy)
        grad_ffn = grad_resid2.astype(BF16)
        d_w2 = dot(act, grad_ffn, 0, 0).astype(BF16)
        d_c2 = column_sum(grad_ffn)
        grad_pre = (dot(grad_ffn, reduce_mat, 1, 1) * slope.astype(F32)).astype(BF16)
        d_w1 = dot(hidden_low, grad_pre, 0, 0).astype(BF16)
        d_c1 = column_sum(grad_pre)
        grad_hidden = grad_resid2 + dot(grad_pre, expand_mat, 1, 1)
        d_g1 = column_sum(grad_hidden * normed1)
        d_b1 = column_sum(grad_hidden)
        grad_resid1 = normalize_back(normed1, inv1, g1 * grad_hidden)
        grad_att = grad_resid1.astype(BF16)
        d_wo = dot(ctx, grad_att, 0, 0).astype(BF16)
        d_bo = column_sum(grad_att)
        grad_ctx = dot(grad_att, merge_mat, 1, 1).astype(BF16)
        grad_qkv = attend_back(query, key, value, ctx, grad_ctx, probs)
        token_rows = grad_resid1
        d_qkv = []
        for which in range(3):
            mat = qkv_mat[:, which * feats : (which + 1) * feats]
            token_rows = token_rows + dot(grad_qkv[which], mat, 1, 1)
            d_qkv.append(dot(inputs, grad_qkv[which], 0, 0).astype(BF16))
        d_bq = column_sum(grad_qkv[0])
        d_bv = column_sum(grad_qkv[2])
        token_grad = from_owners(token_rows.astype(BF16))
        vec_grads = (d_bq, d_bv, d_bo, d_g1, d_b1, d_c2, d_g2, d_b2, d_c1)
        vec_pack = jnp.concatenate([item.reshape(dp_size, -1) for item in vec_grads], axis=1)
        vec_cols = -(-vec_len // (shard_rows * LANES)) * LANES
        vec_pack = jnp.pad(vec_pack, ((0, 0), (0, shard_rows * vec_cols - vec_len)))
        vec_pack = vec_pack.reshape(feats, vec_cols).astype(BF16)

        def reduce(full):
            own = lax.psum_scatter(full, "dp", scatter_dimension=0, tiled=True)
            return lax.psum(own, "seq").astype(F32)

        sum_w2 = reduce(d_w2)
        sum_w1 = reduce(d_w1)
        sum_rest = reduce(jnp.concatenate([d_wo] + d_qkv + [vec_pack], axis=1))
        s_wo, s_wq, s_wk, s_wv = [sum_rest[:, i * feats : (i + 1) * feats] for i in range(4)]
        flat = sum_rest[:, 4 * feats :].reshape(-1)
        out_vecs = []
        start = 0
        for size in vec_sizes:
            out_vecs.append(flat[start : start + size])
            start += size
        s_bq, s_bv, s_bo, s_g1, s_b1, s_c2, s_g2, s_b2, s_c1 = out_vecs
    return (
        output,
        token_grad,
        s_wq,
        s_bq,
        s_wk,
        s_wv,
        s_bv,
        s_wo,
        s_bo,
        s_g1,
        s_b1,
        sum_w1,
        s_c1,
        sum_w2,
        s_c2,
        s_g2,
        s_b2,
    )


def solution(mesh):
    rows, mat, vec = P("dp", "seq", None), P("dp", None), P("dp")
    params = (mat, vec, mat, mat, vec, mat, vec, vec, vec, mat, vec, mat, vec, vec, vec)
    return jax.shard_map(
        functools.partial(per_device, (mesh.shape["dp"], mesh.shape["seq"])),
        mesh=mesh,
        in_specs=(rows, vec) + params + (rows,),
        out_specs=(rows, rows) + params,
        check_vma=False,
    )
```
